32 devices in a mesh: seq: 8 (over z, x), exp: 4 (over y, core).
Axes of the slice: x: 2, y: 2, z: 4, core: 2. Of those that a mesh axis runs over, the one named last changes fastest.
Arguments:
- block_input: float32 [4096, 768], P(('seq', 'exp')), may hold values from -6 to 6
- seq_lengths: int32 [10], replicated, may hold values from 1 to 2048, 4096 in all
- expert_ids: int32 [4096, 1], P(('seq', 'exp')), may hold values from 0 to 3
- output_grad: float32 [4096, 768], P(('seq', 'exp')), may hold values from -6 to 6
- mixer_gain: float32 [768], replicated, may hold values from 0.5 to 1.5
- in_proj: float32 [768, 3072], replicated, may hold values from -0.21875 to 0.21875
- conv_weight: float32 [4, 1536], replicated, may hold values from -3 to 3
- conv_bias: float32 [1536], replicated, may hold values from -1.75 to 1.75
- state_proj: float32 [1536, 80], replicated, may hold values from -0.15625 to 0.15625
- step_proj: float32 [48, 1536], replicated, may hold values from -0.875 to 0.875
- step_bias: float32 [1536], replicated, may hold values from -7 to -2.5
- decay_log: float32 [1536, 16], replicated, may hold values from 0 to 2.77
- skip_gain: float32 [1536], replicated, may hold values from 0.5 to 1.5
- out_proj: float32 [1536, 768], replicated, may hold values from -0.3125 to 0.3125
- router_gain: float32 [768], replicated, may hold values from 0.5 to 1.5
- router: float32 [768, 4], replicated, may hold values from -0.15625 to 0.15625
- expert_up: float32 [4, 768, 3072], P('exp', None, 'seq'), may hold values from -0.21875 to 0.21875
- expert_down: float32 [4, 3072, 768], P('exp', 'seq'), may hold values from -0.875 to 0.875
Outputs:
- block_output: float32 [4096, 768], P(('seq', 'exp'))
- input_grad: float32 [4096, 768], P(('seq', 'exp'))
- grad_mixer_gain: float32 [768], replicated
- grad_in_proj: float32 [768, 3072], replicated
- grad_conv_weight: float32 [4, 1536], replicated
- grad_conv_bias: float32 [1536], replicated
- grad_state_proj: float32 [1536, 80], replicated
- grad_step_proj: float32 [48, 1536], replicated
- grad_step_bias: float32 [1536], replicated
- grad_decay_log: float32 [1536, 16], replicated
- grad_skip_gain: float32 [1536], replicated
- grad_out_proj: float32 [1536, 768], replicated
- grad_router_gain: float32 [768], replicated
- grad_router: float32 [768, 4], replicated
- grad_expert_up: float32 [4, 768, 3072], P('exp', None, 'seq')
- grad_expert_down: float32 [4, 3072, 768], P('exp', 'seq')
- expert_load: int32 [4], replicated
- dropped_load: int32 [4], replicated
The draws below stay inside these ranges and needn't reach their ends.
All inputs are finite; a program needn't handle non-finite values.
Results may differ from the reference program's by a relative error of at most 0.0003.
Values sent between devices are 32-bit elements; how exact they have to be, the bound alone decides.
No kernel may reach another device: no remote copies, remote signals or barrier semaphores. Data moves between devices by JAX's collectives and lax.ppermute only.
A program may use at most 448 MiB of HBM per device.

```python
import math
import jax
import jax.numpy as jnp
import numpy as np
from jax import lax

D = 768
DI = 1536
STATE = 16
RANK = 48
CONV = 4
FF = 3072
TOK_DEV = 128
EXPERTS = 4
TOKENS = 4096
CAP = 40
MAXLEN = 2048
SEQS = 10


def shard_levels(key, extent, shards, least, largest):
    level, own = 1.0, jax.random.fold_in(key, 6)
    for dim, blocks in shards:
        draws = jnp.exp(jax.random.uniform(jax.random.fold_in(own, dim), (blocks,), jnp.float32, least / len(shards), largest / len(shards)))
        level = level * jnp.repeat(draws, extent[dim] // blocks).reshape([-1 if axis == dim else 1 for axis in range(len(extent))])
    return level


def picks_of(stream_key, rows, amount, top, lift):
    ranking = jax.random.permutation(jax.random.fold_in(stream_key, 1), amount)
    pull = ranking
    for power in range(3):
        pull = pull * pull // amount
    pull = pull * lift // amount
    tickets = jax.random.randint(jax.random.fold_in(stream_key, 2), (rows, amount), 0, 4096) + pull
    sure = jax.random.permutation(jax.random.fold_in(stream_key, 3), rows)[jnp.arange(amount) % rows]
    tickets = jnp.where(jnp.arange(rows)[:, None] == sure[None, :], 1 << 14, tickets)
    priority = tickets * amount + jnp.arange(amount)
    return lax.top_k(priority.astype(jnp.int32), top)[1].astype(jnp.int32)


def profile(count, total, most, slope):
    loads = [(1 << 20) // math.isqrt(grade ** slope) + 1 for grade in range(2, count + 1)]
    surplus, counts = total - most - (count - 1), [1] * (count - 1)
    while surplus > 0:
        movable = [i for i in range(count - 1) if counts[i] < most]
        pool, remaining = sum([loads[i] for i in movable]), surplus
        for i in movable:
            more = min(most - counts[i], max(1, remaining * loads[i] // pool), surplus)
            counts[i] = counts[i] + more
            surplus = surplus - more
    return np.array([most] + counts)


def uneven_parts(own_key, count, total, most, skew):
    if count == 2:
        one = jax.random.randint(own_key, (), max(1, total - most), min(most, total - 1) + 1)
        return jnp.stack([one, total - one])
    sizes = jnp.asarray(profile(count, total, most, skew), jnp.int32)
    twos = (count - 1) // 2
    source_of, taker = sizes[1:1 + 2 * twos:2], sizes[2:2 + 2 * twos:2]
    room = jnp.minimum(source_of - 1, most - taker)
    passed = jax.random.randint(jax.random.fold_in(own_key, 1), (twos,), 0, 1 << 20) % (room + 1)
    sizes = sizes.at[1:1 + 2 * twos:2].set(source_of - passed).at[2:2 + 2 * twos:2].set(taker + passed)
    return sizes[jax.random.permutation(jax.random.fold_in(own_key, 2), count)]


def noise(key, shape, spread, most, cuts=(), kind=jnp.bfloat16):
    values = spread * jax.random.normal(key, shape, jnp.float32)
    if cuts:
        values = values * shard_levels(key, shape, cuts, -0.22, 0.18)
    return jnp.clip(values, -most, most).astype(kind)


def setup_inputs(seed: int = 0) -> dict:
    keys = jax.random.split(jax.random.key(seed), 19)
    block_input = noise(keys[0], (TOKENS, D), 1.0, 6.0, ((0, 32),), jnp.float32)
    seq_lengths = uneven_parts(keys[1], SEQS, TOKENS, MAXLEN, 2).astype(jnp.int32)
    expert_ids = picks_of(keys[2], TOKENS, EXPERTS, 1, 2048)
    output_grad = noise(keys[3], (TOKENS, D), 1.0, 6.0, ((0, 32),), jnp.float32)
    mixer_gain = jnp.clip(1.0 + 0.1 * jax.random.normal(keys[4], (D,), jnp.float32), 0.5, 1.5)
    in_proj = noise(keys[5], (D, 2 * DI), D ** -0.5, 0.21875, (), jnp.float32)
    conv_weight = noise(keys[6], (CONV, DI), CONV ** -0.5, 3.0, (), jnp.float32)
    conv_bias = noise(keys[7], (DI,), 0.3, 1.75, (), jnp.float32)
    state_proj = noise(keys[8], (DI, RANK + 2 * STATE), DI ** -0.5, 0.15625, (), jnp.float32)
    step_proj = noise(keys[9], (RANK, DI), RANK ** -0.5, 0.875, (), jnp.float32)
    step_bias = jnp.clip(jax.random.uniform(keys[10], (DI,), jnp.float32, -7.0, -2.5), -7.0, -2.5)
    decay_log = jnp.clip(jax.random.uniform(keys[11], (DI, STATE), jnp.float32, 0.0, 2.77), 0.0, 2.77)
    skip_gain = jnp.clip(jax.random.uniform(keys[12], (DI,), jnp.float32, 0.5, 1.5), 0.5, 1.5)
    out_proj = noise(keys[13], (DI, D), (DI // 4) ** -0.5, 0.3125, (), jnp.float32)
    router_gain = jnp.clip(1.0 + 0.1 * jax.random.normal(keys[14], (D,), jnp.float32), 0.5, 1.5)
    router = noise(keys[15], (D, EXPERTS), (2 * D) ** -0.5, 0.15625, (), jnp.float32)
    expert_up = noise(keys[16], (EXPERTS, D, FF), D ** -0.5, 0.21875, ((0, 4), (2, 8)), jnp.float32)
    expert_down = noise(keys[17], (EXPERTS, FF, D), (FF // 64) ** -0.5, 0.875, ((0, 4), (1, 8)), jnp.float32)
    return dict(block_input=block_input, seq_lengths=seq_lengths, expert_ids=expert_ids, output_grad=output_grad, mixer_gain=mixer_gain, in_proj=in_proj, conv_weight=conv_weight, conv_bias=conv_bias, state_proj=state_proj, step_proj=step_proj, step_bias=step_bias, decay_log=decay_log, skip_gain=skip_gain, out_proj=out_proj, router_gain=router_gain, router=router, expert_up=expert_up, expert_down=expert_down)


precise = lax.Precision.HIGHEST
epsilon = 1e-05

@jax.custom_vjp
def low(v):
    return lax.optimization_barrier(v.astype(jnp.bfloat16)).astype(jnp.float32)

@jax.custom_vjp
def low_back(v):
    return v

def low_keep(v):
    return (low(v), None)

def low_pass(kept, grad):
    return (grad,)

def back_keep(v):
    return (v, None)

def back_low(kept, grad):
    return (low(grad),)
low.defvjp(low_keep, low_pass)
low_back.defvjp(back_keep, back_low)

def rms_scale(values_in, gain):
    return values_in * lax.rsqrt(lax.optimization_barrier(jnp.mean(values_in * values_in, axis=1, keepdims=True)) + epsilon) * gain

def matmul_high(left, right):
    return jnp.dot(left, right, precision=precise, preferred_element_type=jnp.float32)

def one_token(carried, token):
    state_now, decay_rate = carried
    act_t, step_t, in_t, out_t, fresh_t = token
    decay_now = jnp.exp(step_t[:, None] * decay_rate) * (1.0 - fresh_t)
    state_now = decay_now * state_now + (step_t * act_t)[:, None] * in_t[None, :]
    return ((state_now, decay_rate), lax.optimization_barrier(jnp.sum(state_now * out_t[None, :], axis=1)))

def one_block(carried, pieces):
    return lax.scan(one_token, carried, pieces)

def reference(block_input, seq_lengths, expert_ids, output_grad, mixer_gain, in_proj, conv_weight, conv_bias, state_proj, step_proj, step_bias, decay_log, skip_gain, out_proj, router_gain, router, expert_up, expert_down):
    position = jnp.arange(TOKENS, dtype=jnp.int32)
    seq_starts = (jnp.cumsum(seq_lengths) - seq_lengths).astype(jnp.int32)
    start_flags = jnp.zeros((TOKENS,), jnp.int32).at[seq_starts].set(1)
    segment = (jnp.cumsum(start_flags) - 1).astype(jnp.int32)
    own_start = seq_starts[segment]
    fresh = start_flags.astype(jnp.float32)
    tap_pos = position[:, None] - (CONV - 1) + jnp.arange(CONV, dtype=jnp.int32)[None, :]
    tap_valid = (tap_pos >= own_start[:, None]).astype(jnp.float32)
    chosen_int = (expert_ids[:, 0:1] == jnp.arange(EXPERTS, dtype=jnp.int32)[None, :]).astype(jnp.int32)
    devices_n = TOKENS // TOK_DEV
    per_device = chosen_int.reshape(devices_n, TOK_DEV, EXPERTS)
    ahead_count = jnp.cumsum(per_device, axis=1) - per_device
    slot_rank = lax.optimization_barrier(jnp.sum(ahead_count * per_device, axis=2))
    kept_int = (slot_rank < CAP).astype(jnp.int32)
    slot_ids = (expert_ids[:, 0].reshape(devices_n, TOK_DEV) * CAP + jnp.minimum(slot_rank, CAP - 1)).astype(jnp.int32)
    kept = kept_int.astype(jnp.float32).reshape(TOKENS, 1)
    chosen = chosen_int.astype(jnp.float32)
    device_ids = jnp.broadcast_to(jnp.arange(devices_n, dtype=jnp.int32)[:, None], (devices_n, TOK_DEV))

    def forward(block_input, mixer_gain, in_proj, conv_weight, conv_bias, state_proj, step_proj, step_bias, decay_log, skip_gain, out_proj, router_gain, router, expert_up, expert_down):
        normed = rms_scale(block_input, mixer_gain)
        joined = matmul_high(normed, in_proj)
        inner_x = joined[:, :DI]
        gate_z = joined[:, DI:]
        padded = jnp.pad(inner_x, ((CONV - 1, 0), (0, 0)))
        summed = jnp.broadcast_to(conv_bias[None, :], (TOKENS, DI))
        for offset in range(CONV):
            summed = summed + padded[offset:offset + TOKENS] * tap_valid[:, offset:offset + 1] * conv_weight[offset][None, :]
        activated = jax.nn.silu(summed)
        projected = matmul_high(activated, state_proj)
        step_sizes = jax.nn.softplus(matmul_high(projected[:, :RANK], step_proj) + step_bias)
        in_state = projected[:, RANK:RANK + STATE]
        out_state = projected[:, RANK + STATE:]
        decay_rate = -jnp.exp(decay_log)
        blocks = TOKENS // TOK_DEV
        pieces = tuple((member.reshape((blocks, TOK_DEV) + member.shape[1:]) for member in (activated, step_sizes, in_state, out_state, fresh)))
        start = (jnp.zeros((DI, STATE), jnp.float32), decay_rate)
        finished, scan_out = lax.scan(jax.checkpoint(one_block), start, pieces)
        scan_out = scan_out.reshape(TOKENS, DI)
        mixed_gate = (scan_out + skip_gain * activated) * jax.nn.silu(gate_z)
        resid = block_input + matmul_high(mixed_gate, out_proj)
        normed_moe = rms_scale(resid, router_gain)
        probs = jax.nn.softmax(matmul_high(normed_moe, router), axis=1)
        gate = lax.optimization_barrier(jnp.sum(probs * chosen, axis=1))
        rows_dev = (normed_moe * kept).reshape(devices_n, TOK_DEV, D)
        buffers = jnp.zeros((devices_n, EXPERTS * CAP, D), jnp.float32).at[device_ids, slot_ids].add(rows_dev)
        grouped = buffers.reshape(devices_n, EXPERTS, CAP, D)
        hidden_pre = jnp.einsum('vecd,edf->vecf', grouped, expert_up, precision=precise)
        result = jnp.einsum('vecf,efd->vecd', jax.nn.gelu(hidden_pre), expert_down, precision=precise)
        returned = result.reshape(devices_n, EXPERTS * CAP, D)[device_ids, slot_ids].reshape(TOKENS, D) * kept
        return resid + gate[:, None] * returned
    block_output, pull_back = jax.vjp(forward, block_input, mixer_gain, in_proj, conv_weight, conv_bias, state_proj, step_proj, step_bias, decay_log, skip_gain, out_proj, router_gain, router, expert_up, expert_down)
    grads = pull_back(output_grad)
    expert_load = lax.optimization_barrier(jnp.sum(chosen_int, axis=0)).astype(jnp.int32)
    dropped_load = lax.optimization_barrier(jnp.sum(chosen_int * (1 - kept_int.reshape(TOKENS, 1)), axis=0)).astype(jnp.int32)
    return (block_output, grads[0], grads[1], grads[2], grads[3], grads[4], grads[5], grads[6], grads[7], grads[8], grads[9], grads[10], grads[11], grads[12], grads[13], grads[14], expert_load, dropped_load)
```

```python
import functools

import jax
import jax.numpy as jnp
from jax import lax
from jax.experimental import pallas as pl
from jax.experimental.pallas import tpu as pltpu
from jax.sharding import PartitionSpec as P

F32 = jnp.float32
BF16 = jnp.bfloat16
EPS = 1e-05
LOG2E = 1.4426950408889634
HALO = 16
RESET = 1e9
AXES = ("seq", "exp")
NN, NT, TN = ((1,), (0,)), ((1,), (1,)), ((0,), (0,))
VMEM_BYTES = 52 << 20


class Grid:
    def __init__(self):
        self.seq, self.exp = lax.axis_size("seq"), lax.axis_size("exp")
        self.outer = 4
        self.size = {
            "core": 2,
            "y": self.exp // 2,
            "inner": self.seq // self.outer,
            "outer": self.outer,
        }
        self.total = self.seq * self.exp
        index, step, self.step, self.at = lax.axis_index(AXES), 1, {}, {}
        for name in ("core", "y", "inner", "outer"):
            self.step[name] = step
            self.at[name] = (index // step) % self.size[name]
            step *= self.size[name]
        self.index = index

    def swap(self, block, name, mask):
        return self.swap_bits(block, mask * self.step[name])

    def swap_bits(self, block, bits):
        return lax.ppermute(block, AXES, [(i, i ^ bits) for i in range(self.total)])

    def along(self, block, distance):
        route = [(i - distance, i) for i in range(self.total) if 0 <= i - distance < self.total]
        return lax.ppermute(block, AXES, route)


def in_order(parts, place):
    bit = 1
    while bit < len(parts):
        turned = ((place // bit) % 2) == 1
        parts = [jnp.where(turned, parts[i ^ bit], parts[i]) for i in range(len(parts))]
        bit *= 2
    return parts


def scatter_rows(grid, block, name):
    count, place = grid.size[name], grid.at[name]
    if count == 1:
        return block
    rows = block.shape[0] // count
    piece = lambda s: lax.dynamic_slice_in_dim(block, (place ^ s) * rows, rows, 0)
    got = [grid.swap(piece(s), name, s) for s in range(1, count)]
    total = piece(0)
    for part in got:
        total = total + part
    return total


def gather_rows(grid, block, name):
    count = grid.size[name]
    if count == 1:
        return block
    parts = [block] + [grid.swap(block, name, s) for s in range(1, count)]
    return jnp.concatenate(in_order(parts, grid.at[name]), axis=0)


def sum_everywhere(grid, block):
    half = scatter_rows(grid, block, "core")
    rows, width = half.shape[0] // 2, half.shape[1]
    first = scatter_rows(grid, scatter_rows(grid, half[:rows], "inner"), "y")
    second = scatter_rows(grid, scatter_rows(grid, half[rows:], "y"), "inner")
    both = jnp.concatenate([first, second], axis=0)
    count, place = grid.size["outer"], grid.at["outer"]
    columns = width // count
    piece = lambda s: lax.dynamic_slice_in_dim(both, (place ^ s) * columns, columns, 1)
    got = [grid.swap(piece(s), "outer", s) for s in range(1, count)]
    total = piece(0)
    for part in got:
        total = total + part
    parts = [total] + [grid.swap(total, "outer", s) for s in range(1, count)]
    both = jnp.concatenate(in_order(parts, place), axis=1)
    own = both.shape[0] // 2
    first = gather_rows(grid, gather_rows(grid, both[:own], "y"), "inner")
    second = gather_rows(grid, gather_rows(grid, both[own:], "inner"), "y")
    return gather_rows(grid, jnp.concatenate([first, second], axis=0), "core")


def entering(grid, pair, rate, backward):
    states = pair.shape[0] - 1
    total, total_steps = pair[:states], pair[states:]
    ahead, ahead_steps = jnp.zeros_like(total), jnp.zeros_like(total_steps)
    bits = 1
    while bits < grid.total:
        got = grid.swap_bits(jnp.concatenate([total, total_steps], axis=0), bits)
        state, steps = got[:states], got[states:]
        later = ((grid.index // bits) % 2) == (0 if backward else 1)
        ahead = jnp.where(later, jnp.exp2(rate * ahead_steps) * state + ahead, ahead)
        ahead_steps = jnp.where(later, ahead_steps + steps, ahead_steps)
        early, late = jnp.where(later, state, total), jnp.where(later, total, state)
        total = jnp.exp2(rate * jnp.where(later, total_steps, steps)) * early + late
        total_steps = total_steps + steps
        bits *= 2
    return ahead


def pad_rows(block, rows):
    return jnp.pad(block, ((0, rows - block.shape[0]), (0, 0)))


def to_experts(grid, block, cap, tail):
    ny, width = grid.size["y"], 2 * cap
    slots = 2 * ny * cap
    held = [block[:width]]
    tails = [block[slots:]]
    for s in range(1, ny):
        part = block[s * width : (s + 1) * width]
        got = grid.swap(jnp.concatenate([part, block[slots:]], axis=0) if tail else part, "y", s)
        held.append(got[:width])
        tails.append(got[width:])
    mine = [h[:cap] for h in held]
    others = [h[cap:] for h in held]
    if tail:
        others.append(pad_rows(jnp.concatenate([t[2 * s + 1 : 2 * s + 2] for s, t in enumerate(tails)], axis=0), 8))
    got = grid.swap(jnp.concatenate(others, axis=0), "core", 1)
    out = mine + [got[: ny * cap]]
    if tail:
        ends = [t[2 * s : 2 * s + 1] for s, t in enumerate(tails)] + [got[ny * cap : ny * cap + ny]]
        out.append(pad_rows(jnp.concatenate(ends, axis=0), 8))
    return jnp.concatenate(out, axis=0)


def from_experts(grid, block, cap, tail):
    ny = grid.size["y"]
    half, slots = ny * cap, 2 * ny * cap
    send = block[half:slots]
    if tail:
        send = jnp.concatenate([send, pad_rows(block[slots + ny : slots + 2 * ny], 8)], axis=0)
    got = grid.swap(send, "core", 1)
    rows, ends = [], []
    for s in range(ny):
        pair = [block[s * cap : (s + 1) * cap], got[s * cap : (s + 1) * cap]]
        both = [block[slots + s : slots + s + 1], got[half + s : half + s + 1]] if tail else []
        if s:
            if tail:
                pair.append(pad_rows(jnp.concatenate(both, axis=0), 8))
            back = grid.swap(jnp.concatenate(pair, axis=0), "y", s)
            pair, both = [back[: 2 * cap]], [back[2 * cap : 2 * cap + 2]]
        rows += pair
        ends += both
    if tail:
        rows.append(pad_rows(jnp.concatenate(ends, axis=0), 8))
    return jnp.concatenate(rows, axis=0)


def split(value):
    high = value.astype(BF16)
    return high, (value - high.astype(F32)).astype(BF16)


def dot(left, right, dims):
    return lax.dot_general(left, right, (dims, ((), ())), preferred_element_type=F32)


def product(left, right, dims):
    return dot(left[0], right[0], dims) + (dot(left[0], right[1], dims) + dot(left[1], right[0], dims))


def pick(exact, value, dims):
    high, low = split(value)
    return dot(exact, high, dims) + dot(exact, low, dims)


def sigmoid(value):
    return 1.0 / (1.0 + jnp.exp(-value))


def softplus(value):
    small = jnp.exp(-jnp.abs(value))
    series = small * (1.0 - small * (0.5 - small * (1.0 / 3.0 - small * (0.25 - small * 0.2))))
    return jnp.maximum(value, 0.0) + jnp.where(small < 0.03, series, jnp.log(1.0 + small))


def iota(shape, dim):
    return lax.broadcasted_iota(jnp.int32, shape, dim)


def scale_of(value):
    return lax.rsqrt(jnp.mean(value * value, axis=1, keepdims=True) + EPS)


def over_lanes(ref, columns):
    rows = columns.shape[0]
    for t in range(columns.shape[1]):
        ref[t] = jnp.broadcast_to(columns[:, t : t + 1], (rows, 128))


def widen(value, width):
    return jnp.concatenate([value] * (width // 128), axis=1)


def call(kernel, outs, ins, grid=None, in_specs=None, out_specs=None, scratch=(), name=None):
    whole = pl.BlockSpec(memory_space=pltpu.VMEM)
    return pl.pallas_call(
        kernel,
        out_shape=outs,
        grid=grid or (),
        in_specs=in_specs or [whole] * len(ins),
        out_specs=out_specs or jax.tree.map(lambda _: whole, outs),
        scratch_shapes=scratch,
        name=name,
        compiler_params=pltpu.CompilerParams(vmem_limit_bytes=VMEM_BYTES),
    )(*ins)


def shape(*dims, dtype=F32):
    return jax.ShapeDtypeStruct(dims, dtype)


SMEM = pl.BlockSpec(memory_space=pltpu.SMEM)


def full(*dims):
    return pl.BlockSpec(dims, lambda c: (0,) * len(dims))


def route_kernel(experts, cap, me_ref, ids_ref, grad_ref, sent_ref, table_ref, rank_ref, load_ref):
    ids = ids_ref[...]
    tokens = ids.shape[0]
    chosen = (ids == iota((tokens, 128), 1)).astype(F32)
    before = (iota((tokens, tokens), 0) > iota((tokens, tokens), 1)).astype(BF16)
    rank = jnp.sum(dot(before, chosen.astype(BF16), NN) * chosen, axis=1, keepdims=True)
    kept = (rank < cap).astype(F32)
    place = jnp.where(rank < cap, ((ids ^ me_ref[0]) * cap).astype(F32) + rank, -1.0)
    row = jnp.broadcast_to(place, (tokens, tokens)).T
    slots = experts * cap
    table = (iota((slots, tokens), 0).astype(F32) == jnp.broadcast_to(row[0:1], (slots, tokens))).astype(F32)
    table = table.astype(BF16)
    table_ref[...] = table
    rank_ref[...] = rank
    sent_ref[...] = pick(table, grad_ref[...], NN)
    load_ref[...] = jnp.zeros_like(load_ref)
    load_ref[0:1, 0:128] = jnp.sum(chosen, axis=0, keepdims=True)
    load_ref[0:1, 128:256] = jnp.sum(chosen * (1.0 - kept), axis=0, keepdims=True)


def join_kernel(x_ref, halo_ref, gain_ref, weight_ref, joined_ref, high, low):
    @pl.when(pl.program_id(0) == 0)
    def _():
        x = jnp.concatenate([halo_ref[...], x_ref[...]], axis=0)
        high[...], low[...] = split(x * scale_of(x) * gain_ref[...])

    joined_ref[...] = product((high[...], low[...]), split(weight_ref[...]), NN)


def features_kernel(
    rank_n,
    states,
    inner_ref,
    since_ref,
    conv_w_ref,
    conv_b_ref,
    state_proj_ref,
    step_proj_ref,
    step_bias_ref,
    rate_ref,
    conv_ref,
    act_ref,
    pre_ref,
    steps_ref,
    masked_ref,
    drive_ref,
    proj_ref,
    pair_ref,
    in_lanes,
):
    tokens, width = act_ref.shape
    taps = conv_w_ref.shape[0]
    since = since_ref[...]
    conv = jnp.broadcast_to(conv_b_ref[...], (tokens, width))
    for k in range(taps):
        valid = (since >= taps - 1 - k).astype(F32)
        first = HALO - taps + 1 + k
        conv = conv + inner_ref[first : first + tokens, :] * valid * conv_w_ref[k : k + 1, :]
    act = conv * sigmoid(conv)
    conv_ref[...] = conv
    act_ref[...] = act
    proj = product(split(state_proj_ref[...]), split(act), NT)
    proj_ref[...] = proj
    pre = product(split(proj[:rank_n]), split(step_proj_ref[...]), TN) + step_bias_ref[...]
    pre_ref[...] = pre
    steps = softplus(pre)
    steps_ref[...] = steps
    masked = jnp.where(since == 0, RESET, steps)
    masked_ref[...] = masked
    drive_ref[...] = steps * act
    pair_ref[states : states + 1, :] = jnp.sum(masked, axis=0, keepdims=True)
    over_lanes(in_lanes, proj[rank_n : rank_n + states])
    chunk = 512
    for c in range(width // chunk):
        part = slice(c * chunk, (c + 1) * chunk)
        rate = rate_ref[:, part]

        def eight(group, state):
            for i in range(8):
                t = group * 8 + i
                decay = jnp.exp2(masked_ref[pl.ds(t, 1), part] * rate)
                state = decay * state + drive_ref[pl.ds(t, 1), part] * widen(in_lanes[t], chunk)
            return state

        pair_ref[0:states, part] = lax.fori_loop(0, tokens // 8, eight, jnp.zeros((states, chunk), F32))


def slot_tables(slots, cap, experts):
    slot = iota((slots, 8), 0)
    first = sum((slot >= cap * e).astype(jnp.int32) for e in range(1, experts))
    block = (first == iota((slots, 8), 1)).astype(F32)
    slot = iota((slots, 128), 0)
    first = sum(((slot >= cap * e).astype(jnp.int32) for e in range(1, experts)))
    within = (slot - first * cap == iota((slots, 128), 1)).astype(F32)
    return block, within


def scan_kernel(
    rank_n,
    states,
    experts,
    cap,
    me_ref,
    masked_ref,
    drive_ref,
    act_ref,
    gate_z_ref,
    start_ref,
    rate_ref,
    skip_ref,
    proj_ref,
    out_proj_ref,
    x_ref,
    gain_ref,
    router_ref,
    ids_ref,
    rank_ref,
    table_ref,
    scan_ref,
    history_ref,
    resid_ref,
    sent_ref,
    probs_ref,
    gate_ref,
    in_lanes,
    out_lanes,
    total,
):
    tokens, chunk = masked_ref.shape
    step = pl.program_id(0)

    @pl.when(step == 0)
    def _():
        over_lanes(in_lanes, proj_ref[rank_n : rank_n + states, :])
        over_lanes(out_lanes, proj_ref[rank_n + states : rank_n + 2 * states, :])
        total[...] = x_ref[...]

    rate = rate_ref[...]

    def eight(group, state):
        for i in range(8):
            t = group * 8 + i
            decay = jnp.exp2(masked_ref[pl.ds(t, 1), :] * rate)
            state = decay * state + drive_ref[pl.ds(t, 1), :] * widen(in_lanes[t], chunk)
            history_ref[t] = state
            scan_ref[pl.ds(t, 1), :] = jnp.sum(state * widen(out_lanes[t], chunk), axis=0, keepdims=True)
        return state

    lax.fori_loop(0, tokens // 8, eight, start_ref[...])
    gate_z = gate_z_ref[HALO:, :]
    mixed = (scan_ref[...] + skip_ref[...] * act_ref[...]) * (gate_z * sigmoid(gate_z))
    total[...] += product(split(mixed), split(out_proj_ref[...]), NN)

    @pl.when(step == pl.num_programs(0) - 1)
    def _():
        resid = total[...]
        resid_ref[...] = resid
        normed = resid * scale_of(resid) * gain_ref[...]
        logits = product(split(normed), split(router_ref[...]), NT)
        known = iota((tokens, 8), 1) < experts
        logits = jnp.where(known, logits, -1e30)
        raised = jnp.exp(logits - jnp.max(logits, axis=1, keepdims=True))
        raised = jnp.where(known, raised, 0.0)
        probs = raised / jnp.sum(raised, axis=1, keepdims=True)
        probs_ref[...] = probs
        ids = ids_ref[...]
        gate = jnp.sum(jnp.where(ids == iota((tokens, 8), 1), probs, 0.0), axis=1, keepdims=True)
        gate_ref[...] = gate
        slots = experts * cap
        sent_ref[0:slots, :] = pick(table_ref[...], normed, NN)
        sent_ref[slots:, :] = jnp.zeros((8, sent_ref.shape[1]), F32)
        rank = rank_ref[...].astype(jnp.int32)
        to_block = jnp.where(((ids ^ me_ref[0]) == iota((tokens, 8), 1)) & (rank < cap), gate, 0.0)
        at_rank = (rank == iota((tokens, 128), 1)).astype(BF16)
        high, low = split(to_block)
        rest = (to_block - high.astype(F32) - low.astype(F32)).astype(BF16)
        rows = dot(high, at_rank, TN) + (dot(low, at_rank, TN) + dot(rest, at_rank, TN))
        sent_ref[slots:, 0:128] = rows


def early_kernel(pieces, slices, *refs):
    grads, downs, out_ref = refs[:pieces], refs[pieces : pieces + slices], refs[-1]
    downs = [split(d[...]) for d in downs]
    for p in range(pieces):
        grad = split(grads[p][...])
        for i in range(slices):
            out_ref[p, i] = product(grad, downs[i], NT)


def gelu_parts(value):
    inner = 0.7978845608 * (value + 0.044715 * value * value * value)
    tanh = jnp.tanh(inner)
    slope = 0.5 * (1.0 + tanh) + 0.5 * value * (1.0 - tanh * tanh) * 0.7978845608 * (
        1.0 + 3.0 * 0.044715 * value * value
    )
    return 0.5 * value * (1.0 + tanh), slope


def expert_kernel(pieces, slices, experts, cap, *refs):
    tokens, ups, pulled = refs[:pieces], refs[pieces : pieces + slices], refs[pieces + slices]
    backs = refs[pieces + slices + 1 : 2 * pieces + slices + 1]
    hidden_ref, grad_ref = refs[-2:]
    slots = experts * cap
    ups = [split(u[...]) for u in ups]
    block, within = slot_tables(slots, cap, experts)
    within = within.astype(BF16)
    for p in range(pieces):
        rows = split(tokens[p][0:slots, :])
        back = jnp.zeros((slots, tokens[p].shape[1]), F32)
        to_gate = jnp.zeros((slots, 1), F32)
        for i in range(slices):
            hidden, slope = gelu_parts(product(rows, ups[i], NN))
            pull = pulled[p, i]
            grad = pull * slope
            hidden_ref[p, i] = hidden
            grad_ref[p, i] = grad
            to_gate += jnp.sum(hidden * pull, axis=1, keepdims=True)
            back += product(split(grad), ups[i], NT)
        backs[p][0:slots, :] = back
        backs[p][slots:, :] = jnp.zeros((8, tokens[p].shape[1]), F32)
        high, low = split(block * to_gate)
        rest = (block * to_gate - high.astype(F32) - low.astype(F32)).astype(BF16)
        backs[p][slots:, 0:128] = dot(high, within, TN) + (dot(low, within, TN) + dot(rest, within, TN))


def expert_grads_kernel(pieces, slices, experts, cap, *refs):
    tokens, grads = refs[:pieces], refs[pieces : 2 * pieces]
    downs = refs[2 * pieces : 2 * pieces + slices]
    hidden_ref, grad_ref = refs[2 * pieces + slices : 2 * pieces + slices + 2]
    outs = refs[2 * pieces + slices + 2 :]
    results, up_outs, down_outs = outs[:pieces], outs[pieces : pieces + slices], outs[pieces + slices :]
    slots = experts * cap
    downs = [split(d[...]) for d in downs]
    block, within = slot_tables(slots, cap, experts)
    within = within.astype(BF16)
    for p in range(pieces):
        ends = tokens[p][slots:, 0:128]
        high, low = split(ends)
        rest = (ends - high.astype(F32) - low.astype(F32)).astype(BF16)
        spread = dot(within, high, NT) + (dot(within, low, NT) + dot(within, rest, NT))
        gate = jnp.sum(spread * block, axis=1, keepdims=True)
        rows = split(tokens[p][0:slots, :] * gate)
        gated = split(grads[p][...] * gate)
        total = None
        for i in range(slices):
            hidden = split(hidden_ref[p, i])
            part = product(hidden, downs[i], NN)
            total = part if total is None else total + part
            up = product(rows, split(grad_ref[p, i]), TN)
            down = product(hidden, gated, TN)
            if p == 0:
                up_outs[i][...] = up
                down_outs[i][...] = down
            else:
                up_outs[i][...] += up
                down_outs[i][...] += down
        results[p][...] = total


def silu_parts(value):
    sig = sigmoid(value)
    return value * sig, sig * (1.0 + value * (1.0 - sig))


def mixer_back_kernel(
    rank_n,
    states,
    experts,
    cap,
    me_ref,
    back_ref,
    table_ref,
    gate_ref,
    probs_ref,
    ids_ref,
    rank_ref,
    resid_ref,
    grad_ref,
    gain_ref,
    router_ref,
    out_proj_ref,
    gate_z_ref,
    scan_ref,
    act_ref,
    skip_ref,
    masked_ref,
    rate_ref,
    proj_ref,
    steps_row_ref,
    grad_resid_ref,
    small_ref,
    grad_scan_ref,
    grad_gate_ref,
    grad_skip_ref,
    pair_ref,
    out_lanes,
    high,
    low,
):
    tokens, chunk = masked_ref.shape

    @pl.when(pl.program_id(0) == 0)
    def _():
        over_lanes(out_lanes, proj_ref[rank_n + states : rank_n + 2 * states, :])
        slots = experts * cap
        ids, rank = ids_ref[...], rank_ref[...].astype(jnp.int32)
        back = pick(table_ref[...], back_ref[0:slots, :], TN)
        at_rank = (rank == iota((tokens, 128), 1)).astype(BF16)
        ends = back_ref[slots:, 0:128]
        first, second = split(ends)
        third = (ends - first.astype(F32) - second.astype(F32)).astype(BF16)
        spread = dot(at_rank, first, NT) + (dot(at_rank, second, NT) + dot(at_rank, third, NT))
        mine = ((ids ^ me_ref[0]) == iota((tokens, 8), 1)) & (rank < cap)
        grad_gate = jnp.sum(jnp.where(mine, spread, 0.0), axis=1, keepdims=True)
        probs = probs_ref[...]
        grad_probs = jnp.where(ids == iota((tokens, 8), 1), grad_gate, 0.0)
        grad_logits = probs * (grad_probs - jnp.sum(probs * grad_probs, axis=1, keepdims=True))
        resid, gain = resid_ref[...], gain_ref[...]
        scale = scale_of(resid)
        normed = resid * scale * gain
        logits_two = split(grad_logits)
        grad_normed = gate_ref[...] * back + product(logits_two, split(router_ref[...]), NN)
        small_ref[...] = jnp.zeros_like(small_ref)
        small_ref[0:8, :] = product(logits_two, split(normed), TN)
        small_ref[8:9, :] = jnp.sum(grad_normed * resid * scale, axis=0, keepdims=True)
        pulled = gain * grad_normed
        grad_resid = (
            grad_ref[...]
            + scale * pulled
            - resid * (scale * scale * scale) * jnp.mean(pulled * resid, axis=1, keepdims=True)
        )
        grad_resid_ref[...] = grad_resid
        high[...], low[...] = split(grad_resid)

    grad_mixed = product((high[...], low[...]), split(out_proj_ref[...]), NT)
    silu, slope = silu_parts(gate_z_ref[HALO:, :])
    act = act_ref[...]
    grad_scan = grad_mixed * silu
    grad_scan_ref[...] = grad_scan
    grad_gate_ref[...] = grad_mixed * (scan_ref[...] + skip_ref[...] * act) * slope
    grad_skip_ref[...] = jnp.sum(grad_scan * act, axis=0, keepdims=True)
    rate = rate_ref[...]

    def eight(group, state):
        for i in range(8):
            t = tokens - 1 - (group * 8 + i)
            decay = jnp.exp2(masked_ref[pl.ds(t, 1), :] * rate)
            state = decay * (state + grad_scan_ref[pl.ds(t, 1), :] * widen(out_lanes[t], chunk))
        return state

    pair_ref[0:states, :] = lax.fori_loop(0, tokens // 8, eight, jnp.zeros((states, chunk), F32))
    pair_ref[states : states + 1, :] = steps_row_ref[...]


def out_grad_kernel(scan_ref, act_ref, skip_ref, gate_z_ref, grad_resid_ref, out_ref, high, low):
    @pl.when(pl.program_id(0) == 0)
    def _():
        high[...], low[...] = split(grad_resid_ref[...])

    gate_z = gate_z_ref[HALO:, :]
    mixed = (scan_ref[...] + skip_ref[...] * act_ref[...]) * (gate_z * sigmoid(gate_z))
    out_ref[...] = product(split(mixed), (high[...], low[...]), TN)


def gate_grad_kernel(x_ref, gain_ref, grad_gate_ref, weight_ref, out_ref, normed_ref, high, low):
    @pl.when(pl.program_id(0) == 0)
    def _():
        x = x_ref[...]
        high[...], low[...] = split(x * scale_of(x) * gain_ref[...])
        normed_ref[...] = jnp.zeros_like(normed_ref)

    grad = split(grad_gate_ref[...])
    out_ref[...] = product((high[...], low[...]), grad, TN)
    normed_ref[...] += product(grad, split(weight_ref[...]), NT)


def scan_back_kernel(
    rank_n,
    states,
    masked_ref,
    steps_ref,
    drive_ref,
    act_ref,
    pre_ref,
    grad_scan_ref,
    skip_ref,
    history_ref,
    start_ref,
    end_ref,
    rate_ref,
    proj_ref,
    step_proj_ref,
    grad_act_ref,
    grad_pre_ref,
    grad_decay_ref,
    grad_proj_ref,
    in_lanes,
    out_lanes,
    grad_drive,
    grad_steps,
):
    tokens, chunk = masked_ref.shape
    step = pl.program_id(0)

    @pl.when(step == 0)
    def _():
        over_lanes(in_lanes, proj_ref[rank_n : rank_n + states, :])
        over_lanes(out_lanes, proj_ref[rank_n + states : rank_n + 2 * states, :])
        grad_proj_ref[...] = jnp.zeros_like(grad_proj_ref)

    rate = rate_ref[...]
    lane = iota((states, tokens), 1)

    def one(t, before, carried):
        state, decays, grad_in, grad_out = carried
        masked = masked_ref[pl.ds(t, 1), :]
        grad = grad_scan_ref[pl.ds(t, 1), :]
        decay = jnp.exp2(masked * rate)
        state = state + grad * widen(out_lanes[t], chunk)
        at_out = jnp.sum(history_ref[t] * grad, axis=1, keepdims=True)
        at_in = jnp.sum(state * drive_ref[pl.ds(t, 1), :], axis=1, keepdims=True)
        grad_out = jnp.where(lane == t, at_out, grad_out)
        grad_in = jnp.where(lane == t, at_in, grad_in)
        grad_drive[pl.ds(t, 1), :] = jnp.sum(state * widen(in_lanes[t], chunk), axis=0, keepdims=True)
        state = decay * state
        pulled = state * before
        grad_steps[pl.ds(t, 1), :] = jnp.sum(pulled * rate, axis=0, keepdims=True)
        return state, decays + pulled * masked, grad_in, grad_out

    def four(group, carried):
        for i in range(4):
            t = tokens - 1 - (group * 4 + i)
            carried = one(t, history_ref[t - 1], carried)
        return carried

    nothing = jnp.zeros((states, tokens), F32)
    carried = lax.fori_loop(
        0, tokens // 4 - 1, four, (end_ref[...], jnp.zeros((states, chunk), F32), nothing, nothing)
    )
    for t in (3, 2, 1):
        carried = one(t, history_ref[t - 1], carried)
    _, decays, grad_in, grad_out = one(0, start_ref[...], carried)
    grad_decay_ref[...] = decays * (rate * (1.0 / LOG2E))
    steps, act = steps_ref[...], act_ref[...]
    grad_act_ref[...] = skip_ref[...] * grad_scan_ref[...] + grad_drive[...] * steps
    grad_pre = (grad_steps[...] * (1.0 / LOG2E) + grad_drive[...] * act) * sigmoid(pre_ref[...])
    grad_pre_ref[...] = grad_pre
    grad_proj_ref[0:rank_n, :] += product(split(step_proj_ref[...]), split(grad_pre), NT)
    grad_proj_ref[rank_n : rank_n + states, :] += grad_in
    grad_proj_ref[rank_n + states : rank_n + 2 * states, :] += grad_out


def input_back_kernel(
    rank_n,
    states,
    grad_proj_ref,
    proj_ref,
    state_proj_ref,
    act_ref,
    grad_act_ref,
    grad_pre_ref,
    conv_ref,
    inner_ref,
    conv_w_ref,
    since_ref,
    weight_ref,
    x_ref,
    halo_ref,
    gain_ref,
    grad_gate_normed_ref,
    grad_resid_ref,
    grad_decay_ref,
    grad_skip_ref,
    out_ref,
    input_ref,
    edge_ref,
    gain_row_ref,
    high,
    low,
    grad_inner,
    total,
):
    tokens, chunk = act_ref.shape
    depth = x_ref.shape[1]
    taps = conv_w_ref.shape[0]
    step = pl.program_id(0)

    @pl.when(step == 0)
    def _():
        x = jnp.concatenate([halo_ref[...], x_ref[...]], axis=0)
        high[...], low[...] = split(x * scale_of(x) * gain_ref[...])
        total[...] = jnp.zeros_like(total)

    act, grad_pre = split(act_ref[...]), grad_pre_ref[...]
    grad_pre_two = split(grad_pre)
    grad_proj = split(grad_proj_ref[...])
    grad_act = grad_act_ref[...] + product(grad_proj, split(state_proj_ref[...]), TN)
    _, slope = silu_parts(conv_ref[...])
    grad_conv = grad_act * slope
    since = since_ref[...]
    grad_inner[...] = jnp.zeros_like(grad_inner)
    base = depth
    out_ref[base : base + 2 * states + rank_n, :] = product(grad_proj, act, NN)
    base += 2 * states + rank_n
    out_ref[base : base + rank_n, :] = product(split(proj_ref[0:rank_n, :]), grad_pre_two, NN)
    base += rank_n
    out_ref[base : base + states, :] = grad_decay_ref[...]
    base += states
    rows = []
    for k in range(taps):
        valid = (since >= taps - 1 - k).astype(F32)
        first = HALO - taps + 1 + k
        held = grad_conv * valid
        rows.append(jnp.sum(held * inner_ref[first : first + tokens, :], axis=0, keepdims=True))
        grad_inner[first : first + tokens, :] += held * conv_w_ref[k : k + 1, :]
    rows.append(jnp.sum(grad_conv, axis=0, keepdims=True))
    rows.append(jnp.sum(grad_pre, axis=0, keepdims=True))
    rows.append(grad_skip_ref[...])
    out_ref[base:, :] = jnp.zeros((out_ref.shape[0] - base, chunk), F32)
    for i, row in enumerate(rows):
        out_ref[base + i : base + i + 1, :] = row
    grads = split(grad_inner[...])
    out_ref[0:depth, :] = product((high[...], low[...]), grads, TN)
    total[...] += product(grads, split(weight_ref[...]), NT)

    @pl.when(step == pl.num_programs(0) - 1)
    def _():
        gain = gain_ref[...]

        def rows_back(x, grad):
            scale = scale_of(x)
            pulled = gain * grad
            back = scale * pulled - x * (scale * scale * scale) * jnp.mean(pulled * x, axis=1, keepdims=True)
            return back, jnp.sum(grad * x * scale, axis=0, keepdims=True)

        edge, edge_gain = rows_back(halo_ref[...], total[0:HALO, :])
        own, own_gain = rows_back(x_ref[...], total[HALO:, :] + grad_gate_normed_ref[...])
        edge_ref[...] = edge
        input_ref[...] = grad_resid_ref[...] + own
        gain_row_ref[...] = edge_gain + own_gain


def per_device(
    block_input,
    seq_lengths,
    expert_ids,
    output_grad,
    mixer_gain,
    in_proj,
    conv_weight,
    conv_bias,
    state_proj,
    step_proj,
    step_bias,
    decay_log,
    skip_gain,
    out_proj,
    router_gain,
    router,
    expert_up,
    expert_down,
):
    grid = Grid()
    tokens, depth = block_input.shape
    taps, width = conv_weight.shape
    rank_n, states, experts = step_proj.shape[0], decay_log.shape[1], router.shape[1]
    cap = (5 * tokens + 4 * experts - 1) // (4 * experts)
    slots, hidden = experts * cap, expert_up.shape[2]
    chunk = 512
    chunks = width // chunk
    pieces, slices = grid.size["outer"], grid.size["inner"]
    me = lax.axis_index("exp").astype(jnp.int32).reshape(1)
    ext = HALO + tokens

    halo = grid.along(block_input[tokens - HALO :], 1)

    count = seq_lengths.shape[0]
    earlier = jnp.arange(count)[:, None] > jnp.arange(count)[None, :]
    starts = jnp.sum(jnp.where(earlier, seq_lengths[None, :], 0), axis=1)
    position = grid.index * tokens + jnp.arange(tokens, dtype=jnp.int32)
    own_start = jnp.max(jnp.where(starts[None, :] <= position[:, None], starts[None, :], 0), axis=1)
    since = (position - own_start)[:, None]
    rate = -jnp.exp(decay_log.T) * LOG2E
    state_proj_t = state_proj.T
    router_t = pad_rows(router.T, 8)
    row = lambda vector: vector.reshape(1, -1)

    sent_grads, table, rank, loads = call(
        functools.partial(route_kernel, experts, cap),
        [shape(slots, depth), shape(slots, tokens, dtype=BF16), shape(tokens, 1), shape(8, depth)],
        (me, expert_ids, output_grad),
        in_specs=[SMEM] + [pl.BlockSpec(memory_space=pltpu.VMEM)] * 2,
        name="route",
    )
    own_grads = to_experts(grid, sent_grads, cap, False)
    grad_pieces = [own_grads] + [grid.swap(own_grads, "outer", s) for s in range(1, pieces)]
    up, down = expert_up[0], expert_down[0]
    ups = [up] + [grid.swap(up, "inner", s) for s in range(1, slices)]
    downs = [down] + [grid.swap(down, "inner", s) for s in range(1, slices)]

    block = lambda c: (0, c)
    joined = call(
        join_kernel,
        shape(ext, 2 * width),
        (block_input, halo, row(mixer_gain), in_proj),
        grid=(2 * chunks,),
        in_specs=[full(tokens, depth), full(HALO, depth), full(1, depth), pl.BlockSpec((depth, chunk), block)],
        out_specs=pl.BlockSpec((ext, chunk), block),
        scratch=[pltpu.VMEM((ext, depth), BF16)] * 2,
        name="join",
    )
    conv, act, pre, steps, masked, drive, proj, pair = call(
        functools.partial(features_kernel, rank_n, states),
        [shape(tokens, width)] * 6 + [shape(rank_n + 2 * states, tokens), shape(states + 1, width)],
        (joined, since, conv_weight, row(conv_bias), state_proj_t, step_proj, row(step_bias), rate),
        grid=(1,),
        in_specs=[
            full(ext, width),
            full(tokens, 1),
            full(taps, width),
            full(1, width),
            full(rank_n + 2 * states, width),
            full(rank_n, width),
            full(1, width),
            full(states, width),
        ],
        out_specs=[full(tokens, width)] * 6 + [full(rank_n + 2 * states, tokens), full(states + 1, width)],
        scratch=[pltpu.VMEM((tokens, states, 128), F32)],
        name="features",
    )
    start = entering(grid, pair, rate, False)
    tok = pl.BlockSpec((tokens, chunk), block)
    gate_half = pl.BlockSpec((ext, chunk), lambda c: (0, chunks + c))
    one_row = pl.BlockSpec((1, chunk), block)
    state_rows = pl.BlockSpec((states, chunk), block)
    history_block = pl.BlockSpec((tokens, states, chunk), lambda c: (0, 0, c))
    out_rows = pl.BlockSpec((chunk, depth), lambda c: (c, 0))
    proj_full = full(rank_n + 2 * states, tokens)
    lanes = pltpu.VMEM((tokens, states, 128), F32)
    scan, history, resid, sent, probs, gate = call(
        functools.partial(scan_kernel, rank_n, states, experts, cap),
        [
            shape(tokens, width),
            shape(tokens, states, width),
            shape(tokens, depth),
            shape(slots + 8, depth),
            shape(tokens, 8),
            shape(tokens, 1),
        ],
        (
            me, masked, drive, act, joined, start, rate, row(skip_gain), proj, out_proj, block_input,
            row(router_gain), router_t, expert_ids, rank, table,
        ),
        grid=(chunks,),
        in_specs=[
            SMEM, tok, tok, tok, gate_half, state_rows, state_rows, one_row, proj_full, out_rows,
            full(tokens, depth), full(1, depth), full(8, depth), full(tokens, 1), full(tokens, 1),
            full(slots, tokens),
        ],
        out_specs=[
            tok, history_block, full(tokens, depth), full(slots + 8, depth), full(tokens, 8), full(tokens, 1),
        ],
        scratch=[lanes, lanes, pltpu.VMEM((tokens, depth), F32)],
        name="scan",
    )

    pulled = call(
        functools.partial(early_kernel, pieces, slices),
        shape(pieces, slices, slots, hidden),
        (*grad_pieces, *downs),
        name="early",
    )
    own_tokens = to_experts(grid, sent, cap, True)
    token_pieces = [own_tokens] + [grid.swap(own_tokens, "outer", s) for s in range(1, pieces)]
    *backs, hiddens, hidden_grads = call(
        functools.partial(expert_kernel, pieces, slices, experts, cap),
        [shape(slots + 8, depth)] * pieces + [shape(pieces, slices, slots, hidden)] * 2,
        (*token_pieces, *ups, pulled),
        name="expert",
    )
    back = backs[0]
    for s in range(1, pieces):
        back = back + grid.swap(backs[s], "outer", s)
    back = from_experts(grid, back, cap, True)
    outs = call(
        functools.partial(expert_grads_kernel, pieces, slices, experts, cap),
        [shape(slots, depth)] * pieces + [shape(depth, hidden)] * slices + [shape(hidden, depth)] * slices,
        (*token_pieces, *grad_pieces, *downs, hiddens, hidden_grads),
        name="expert_grads",
    )
    results, up_grads, down_grads = outs[:pieces], outs[pieces : pieces + slices], outs[pieces + slices :]
    grad_up, grad_down, result = up_grads[0], down_grads[0], results[0]
    for s in range(1, slices):
        grad_up = grad_up + grid.swap(up_grads[s], "inner", s)
        grad_down = grad_down + grid.swap(down_grads[s], "inner", s)
    for s in range(1, pieces):
        result = result + grid.swap(results[s], "outer", s)
    result = from_experts(grid, result, cap, False)

    grad_resid, small, grad_scan, grad_gate, grad_skip, back_pair = call(
        functools.partial(mixer_back_kernel, rank_n, states, experts, cap),
        [
            shape(tokens, depth),
            shape(16, depth),
            shape(tokens, width),
            shape(tokens, width),
            shape(1, width),
            shape(states + 1, width),
        ],
        (
            me, back, table, gate, probs, expert_ids, rank, resid, output_grad, row(router_gain), router_t,
            out_proj, joined, scan, act, row(skip_gain), masked, rate, proj, pair[states:],
        ),
        grid=(chunks,),
        in_specs=[
            SMEM, full(slots + 8, depth), full(slots, tokens), full(tokens, 1), full(tokens, 8),
            full(tokens, 1), full(tokens, 1), full(tokens, depth), full(tokens, depth), full(1, depth),
            full(8, depth), out_rows, gate_half, tok, tok, one_row, tok, state_rows, proj_full, one_row,
        ],
        out_specs=[
            full(tokens, depth), full(16, depth), tok, tok, one_row,
            pl.BlockSpec((states + 1, chunk), block),
        ],
        scratch=[lanes] + [pltpu.VMEM((tokens, depth), BF16)] * 2,
        name="mixer_back",
    )
    end = entering(grid, back_pair, rate, True)
    grad_out_proj = call(
        out_grad_kernel,
        shape(width, depth),
        (scan, act, row(skip_gain), joined, grad_resid),
        grid=(chunks,),
        in_specs=[tok, tok, one_row, gate_half, full(tokens, depth)],
        out_specs=out_rows,
        scratch=[pltpu.VMEM((tokens, depth), BF16)] * 2,
        name="out_grad",
    )
    grad_in_gate, grad_gate_normed = call(
        gate_grad_kernel,
        [shape(depth, width), shape(tokens, depth)],
        (block_input, row(mixer_gain), grad_gate, in_proj),
        grid=(chunks,),
        in_specs=[
            full(tokens, depth), full(1, depth), tok,
            pl.BlockSpec((depth, chunk), lambda c: (0, chunks + c)),
        ],
        out_specs=[pl.BlockSpec((depth, chunk), block), full(tokens, depth)],
        scratch=[pltpu.VMEM((tokens, depth), BF16)] * 2,
        name="gate_grad",
    )
    grad_out_proj = sum_everywhere(grid, grad_out_proj)
    grad_in_gate = sum_everywhere(grid, grad_in_gate)
    grad_act, grad_pre, grad_decay, grad_proj = call(
        functools.partial(scan_back_kernel, rank_n, states),
        [
            shape(tokens, width), shape(tokens, width), shape(states, width), shape(rank_n + 2 * states, tokens),
        ],
        (
            masked, steps, drive, act, pre, grad_scan, row(skip_gain), history, start, end, rate, proj, step_proj,
        ),
        grid=(chunks,),
        in_specs=[
            tok, tok, tok, tok, tok, tok, one_row, history_block, state_rows, state_rows, state_rows, proj_full,
            pl.BlockSpec((rank_n, chunk), block),
        ],
        out_specs=[tok, tok, state_rows, proj_full],
        scratch=[lanes, lanes] + [pltpu.VMEM((tokens, chunk), F32)] * 2,
        name="scan_back",
    )
    used = depth + 2 * states + 2 * rank_n + states + taps + 4
    unit = 16 * grid.size["inner"] * grid.size["y"]
    packed = -(-(used + 8) // unit) * unit
    grads, input_grad, edge, gain_row = call(
        functools.partial(input_back_kernel, rank_n, states),
        [shape(packed, width), shape(tokens, depth), shape(HALO, depth), shape(1, depth)],
        (
            grad_proj, proj, state_proj_t, act, grad_act, grad_pre, conv, joined, conv_weight, since, in_proj,
            block_input, halo, row(mixer_gain), grad_gate_normed, grad_resid, grad_decay, grad_skip,
        ),
        grid=(chunks,),
        in_specs=[
            proj_full, proj_full, pl.BlockSpec((rank_n + 2 * states, chunk), block), tok, tok, tok, tok,
            pl.BlockSpec((ext, chunk), block), pl.BlockSpec((taps, chunk), block), full(tokens, 1),
            pl.BlockSpec((depth, chunk), block), full(tokens, depth), full(HALO, depth), full(1, depth),
            full(tokens, depth), full(tokens, depth), state_rows, one_row,
        ],
        out_specs=[
            pl.BlockSpec((packed, chunk), block), full(tokens, depth), full(HALO, depth), full(1, depth),
        ],
        scratch=[pltpu.VMEM((ext, depth), BF16)] * 2
        + [pltpu.VMEM((ext, chunk), F32), pltpu.VMEM((ext, depth), F32)],
        name="input_back",
    )
    from_next = grid.along(edge, -1)
    input_grad = jnp.concatenate([input_grad[: tokens - HALO], input_grad[tokens - HALO :] + from_next], axis=0)
    small = jnp.concatenate([small[:9], gain_row, loads[0:1], small[11:]], axis=0).reshape(8, width)
    grads = lax.dynamic_update_slice(grads, small, (used, 0))
    grads = sum_everywhere(grid, grads)

    combined = jnp.dot(table.T, result.astype(F32), precision=lax.Precision.HIGHEST, preferred_element_type=F32)
    block_output = resid + gate * combined

    at = depth
    grad_state_proj = grads[at : at + 2 * states + rank_n].T
    at += 2 * states + rank_n
    grad_step_proj = grads[at : at + rank_n]
    at += rank_n
    grad_decay_log = grads[at : at + states].T
    at += states
    grad_conv_weight = grads[at : at + taps]
    at += taps
    grad_conv_bias, grad_step_bias, grad_skip_gain = grads[at], grads[at + 1], grads[at + 2]
    small = grads[used : used + 8].reshape(16, depth)
    return (
        block_output,
        input_grad,
        small[9],
        jnp.concatenate([grads[:depth], grad_in_gate], axis=1),
        grad_conv_weight,
        grad_conv_bias,
        grad_state_proj,
        grad_step_proj,
        grad_step_bias,
        grad_decay_log,
        grad_skip_gain,
        grad_out_proj,
        small[8],
        small[:experts].T,
        grad_up[None],
        grad_down[None],
        small[10, :experts].astype(jnp.int32),
        small[10, 128 : 128 + experts].astype(jnp.int32),
    )


def solution(mesh):
    rows, copied = P(("seq", "exp"), None), P()
    up, down = P("exp", None, "seq"), P("exp", "seq", None)
    in_specs = (rows, copied, rows, rows) + (copied,) * 12 + (up, down)
    out_specs = (rows, rows) + (copied,) * 12 + (up, down, copied, copied)
    return jax.shard_map(per_device, mesh=mesh, in_specs=in_specs, out_specs=out_specs, check_vma=False)
```

```python
import functools

import jax
import jax.numpy as jnp
from jax import lax
from jax.experimental import pallas as pl
from jax.experimental.pallas import tpu as pltpu
from jax.sharding import PartitionSpec as P

F32 = jnp.float32
BF16 = jnp.bfloat16
EPS = 1e-05
LOG2E = 1.4426950408889634
HALO = 16
RESET = 1e9
AXES = ("seq", "exp")
NN, NT, TN = ((1,), (0,)), ((1,), (1,)), ((0,), (0,))
VMEM_BYTES = 52 << 20


class Grid:
    def __init__(self):
        self.seq, self.exp = lax.axis_size("seq"), lax.axis_size("exp")
        self.outer = 4
        self.size = {
            "core": 2,
            "y": self.exp // 2,
            "inner": self.seq // self.outer,
            "outer": self.outer,
        }
        self.total = self.seq * self.exp
        index, step, self.step, self.at = lax.axis_index(AXES), 1, {}, {}
        for name in ("core", "y", "inner", "outer"):
            self.step[name] = step
            self.at[name] = (index // step) % self.size[name]
            step *= self.size[name]
        self.index = index

    def swap(self, block, name, mask):
        return self.swap_bits(block, mask * self.step[name])

    def swap_bits(self, block, bits):
        return lax.ppermute(block, AXES, [(i, i ^ bits) for i in range(self.total)])

    def along(self, block, distance):
        route = [(i - distance, i) for i in range(self.total) if 0 <= i - distance < self.total]
        return lax.ppermute(block, AXES, route)


def tie(*values):
    return lax.optimization_barrier(values)


def outer_reduce(grid, parts):
    through = grid.swap(parts[3], "outer", 1)
    return outer_reduce_rest(grid, parts, through)


def outer_reduce_rest(grid, parts, through):
    through, near = tie(through, parts[1])
    near = grid.swap(near, "outer", 1)
    far = grid.swap(parts[2] + through, "outer", 2)
    return parts[0] + near + far


def in_order(parts, place):
    bit = 1
    while bit < len(parts):
        turned = ((place // bit) % 2) == 1
        parts = [jnp.where(turned, parts[i ^ bit], parts[i]) for i in range(len(parts))]
        bit *= 2
    return parts


def scatter_rows(grid, block, name):
    count, place = grid.size[name], grid.at[name]
    if count == 1:
        return block
    rows = block.shape[0] // count
    piece = lambda s: lax.dynamic_slice_in_dim(block, (place ^ s) * rows, rows, 0)
    got = [grid.swap(piece(s), name, s) for s in range(1, count)]
    total = piece(0)
    for part in got:
        total = total + part
    return total


def gather_rows(grid, block, name):
    count = grid.size[name]
    if count == 1:
        return block
    parts = [block] + [grid.swap(block, name, s) for s in range(1, count)]
    return jnp.concatenate(in_order(parts, grid.at[name]), axis=0)


def sum_first(grid, half):
    rows = half.shape[0] // 2
    return scatter_rows(grid, half[:rows], "inner"), scatter_rows(grid, half[rows:], "y")


def sum_second(grid, first, second):
    return jnp.concatenate([scatter_rows(grid, first, "y"), scatter_rows(grid, second, "inner")], axis=0)


def sum_outer(grid, both):
    count, place = grid.size["outer"], grid.at["outer"]
    columns = both.shape[1] // count
    piece = lambda s: lax.dynamic_slice_in_dim(both, (place ^ s) * columns, columns, 1)
    got = [grid.swap(piece(s), "outer", s) for s in range(1, count)]
    total = piece(0)
    for part in got:
        total = total + part
    return total


def spread_outer(grid, total):
    count = grid.size["outer"]
    parts = [total] + [grid.swap(total, "outer", s) for s in range(1, count)]
    return jnp.concatenate(in_order(parts, grid.at["outer"]), axis=1)


def spread_second(grid, both):
    own = both.shape[0] // 2
    return gather_rows(grid, both[:own], "y"), gather_rows(grid, both[own:], "inner")


def spread_first(grid, first, second):
    return jnp.concatenate([gather_rows(grid, first, "inner"), gather_rows(grid, second, "y")], axis=0)


def join_states_kernel(last, later_ref, total_ref, got_ref, ahead_ref, rate_ref, *outs):
    states = rate_ref.shape[0]
    rows, sums = slice(0, states), slice(states, states + 1)

    def follow(early, late, out):
        out[rows, :] = jnp.exp2(rate_ref[...] * late[sums, :]) * early[rows, :] + late[rows, :]
        out[sums, :] = early[sums, :] + late[sums, :]

    @pl.when(later_ref[0] == 1)
    def _():
        follow(got_ref, ahead_ref, outs[0])
        if not last:
            follow(got_ref, total_ref, outs[1])

    @pl.when(later_ref[0] == 0)
    def _():
        outs[0][...] = ahead_ref[...]
        if not last:
            follow(total_ref, got_ref, outs[1])


def entering(grid, pair, rate, backward, between=None):
    states = rate.shape[0]
    total, ahead, extra = pair, jnp.zeros_like(pair), None
    bits = 1
    while bits < grid.total:
        got = grid.swap_bits(total, bits)
        later = ((grid.index // bits) % 2).astype(jnp.int32)
        later = (1 - later if backward else later).reshape(1)
        last = 2 * bits >= grid.total
        whole = pl.BlockSpec(memory_space=pltpu.VMEM)
        ahead, *rest = call(
            functools.partial(join_states_kernel, last),
            [shape(*pair.shape)] * (1 if last else 2),
            (later, total, got, ahead, rate),
            in_specs=[SMEM] + [whole] * 4,
            name="join_states",
        )
        total = rest[0] if rest else None
        if bits == 4 and between:
            total, *extra = between(total)
        bits *= 2
    return ahead[:states], extra


def pad_rows(block, rows):
    return jnp.pad(block, ((0, rows - block.shape[0]), (0, 0)))


def send_y(grid, block, cap, tail):
    width, slots = 2 * cap, grid.exp * cap
    held, tails = [block[:width]], [block[slots:]]
    for s in range(1, grid.size["y"]):
        part = block[s * width : (s + 1) * width]
        got = grid.swap(jnp.concatenate([part, block[slots:]], axis=0) if tail else part, "y", s)
        held.append(got[:width])
        tails.append(got[width:])
    return held, tails


def send_core(grid, held, tails, cap, tail):
    ny = grid.size["y"]
    mine, others = [h[:cap] for h in held], [h[cap:] for h in held]
    if tail:
        others.append(pad_rows(jnp.concatenate([t[2 * s + 1 : 2 * s + 2] for s, t in enumerate(tails)], axis=0), 8))
    got = grid.swap(jnp.concatenate(others, axis=0), "core", 1)
    out = mine + [got[: ny * cap]]
    if tail:
        ends = [t[2 * s : 2 * s + 1] for s, t in enumerate(tails)] + [got[ny * cap : ny * cap + ny]]
        out.append(pad_rows(jnp.concatenate(ends, axis=0), 8))
    return jnp.concatenate(out, axis=0)


def from_experts(grid, block, cap, tail):
    ny = grid.size["y"]
    half, slots = ny * cap, 2 * ny * cap
    send = block[half:slots]
    if tail:
        send = jnp.concatenate([send, pad_rows(block[slots + ny : slots + 2 * ny], 8)], axis=0)
    got = grid.swap(send, "core", 1)
    rows, ends = [], []
    for s in range(ny):
        pair = [block[s * cap : (s + 1) * cap], got[s * cap : (s + 1) * cap]]
        both = [block[slots + s : slots + s + 1], got[half + s : half + s + 1]] if tail else []
        if s:
            if tail:
                pair.append(pad_rows(jnp.concatenate(both, axis=0), 8))
            back = grid.swap(jnp.concatenate(pair, axis=0), "y", s)
            pair, both = [back[: 2 * cap]], [back[2 * cap : 2 * cap + 2]]
        rows += pair
        ends += both
    if tail:
        rows.append(pad_rows(jnp.concatenate(ends, axis=0), 8))
    return jnp.concatenate(rows, axis=0)


def split(value):
    high = value.astype(BF16)
    return high, (value - high.astype(F32)).astype(BF16)


def dot(left, right, dims):
    return lax.dot_general(left, right, (dims, ((), ())), preferred_element_type=F32)


def product(left, right, dims):
    return dot(left[0], right[0], dims) + (dot(left[0], right[1], dims) + dot(left[1], right[0], dims))


def pick(exact, value, dims):
    high, low = split(value)
    return dot(exact, high, dims) + dot(exact, low, dims)


def sigmoid(value):
    return 1.0 / (1.0 + jnp.exp(-value))


def softplus(value):
    small = jnp.exp(-jnp.abs(value))
    series = small * (1.0 - small * (0.5 - small * (1.0 / 3.0 - small * (0.25 - small * 0.2))))
    return jnp.maximum(value, 0.0) + jnp.where(small < 0.03, series, jnp.log(1.0 + small))


def iota(shape, dim):
    return lax.broadcasted_iota(jnp.int32, shape, dim)


def scale_of(value):
    return lax.rsqrt(jnp.mean(value * value, axis=1, keepdims=True) + EPS)


def over_lanes(ref, columns):
    rows = columns.shape[0]
    for t in range(columns.shape[1]):
        ref[t] = jnp.broadcast_to(columns[:, t : t + 1], (rows, 128))


def widen(value, width):
    return jnp.concatenate([value] * (width // 128), axis=1)


def call(kernel, outs, ins, grid=None, in_specs=None, out_specs=None, scratch=(), name=None):
    whole = pl.BlockSpec(memory_space=pltpu.VMEM)
    return pl.pallas_call(
        kernel,
        out_shape=outs,
        grid=grid or (),
        in_specs=in_specs or [whole] * len(ins),
        out_specs=out_specs or jax.tree.map(lambda _: whole, outs),
        scratch_shapes=scratch,
        name=name,
        cost_estimate=pl.CostEstimate(flops=1000, transcendentals=0, bytes_accessed=1000),
        compiler_params=pltpu.CompilerParams(vmem_limit_bytes=VMEM_BYTES),
    )(*ins)


def shape(*dims, dtype=F32):
    return jax.ShapeDtypeStruct(dims, dtype)


SMEM = pl.BlockSpec(memory_space=pltpu.SMEM)


def full(*dims):
    return pl.BlockSpec(dims, lambda c: (0,) * len(dims))


def route_kernel(experts, cap, me_ref, ids_ref, grad_ref, sent_ref, table_ref, rank_ref, load_ref):
    ids = ids_ref[...]
    tokens = ids.shape[0]
    chosen = (ids == iota((tokens, 128), 1)).astype(F32)
    before = (iota((tokens, tokens), 0) > iota((tokens, tokens), 1)).astype(BF16)
    rank = jnp.sum(dot(before, chosen.astype(BF16), NN) * chosen, axis=1, keepdims=True)
    kept = (rank < cap).astype(F32)
    place = jnp.where(rank < cap, ((ids ^ me_ref[0]) * cap).astype(F32) + rank, -1.0)
    row = jnp.broadcast_to(place, (tokens, tokens)).T
    slots = experts * cap
    table = (iota((slots, tokens), 0).astype(F32) == jnp.broadcast_to(row[0:1], (slots, tokens))).astype(F32)
    table = table.astype(BF16)
    table_ref[...] = table
    rank_ref[...] = rank
    sent_ref[...] = pick(table, grad_ref[...], NN)
    load_ref[...] = jnp.zeros_like(load_ref)
    load_ref[0:1, 0:128] = jnp.sum(chosen, axis=0, keepdims=True)
    load_ref[0:1, 128:256] = jnp.sum(chosen * (1.0 - kept), axis=0, keepdims=True)


def join_kernel(x_ref, halo_ref, gain_ref, weight_ref, joined_ref, high, low):
    @pl.when(pl.program_id(0) == 0)
    def _():
        x = jnp.concatenate([halo_ref[...], x_ref[...]], axis=0)
        high[...], low[...] = split(x * scale_of(x) * gain_ref[...])

    joined_ref[...] = product((high[...], low[...]), split(weight_ref[...]), NN)


def features_kernel(
    rank_n,
    states,
    inner_ref,
    since_ref,
    conv_w_ref,
    conv_b_ref,
    state_proj_ref,
    step_proj_ref,
    step_bias_ref,
    rate_ref,
    conv_ref,
    act_ref,
    pre_ref,
    steps_ref,
    masked_ref,
    drive_ref,
    proj_ref,
    pair_ref,
    in_lanes,
):
    tokens, width = act_ref.shape
    taps = conv_w_ref.shape[0]
    since = since_ref[...]
    conv = jnp.broadcast_to(conv_b_ref[...], (tokens, width))
    for k in range(taps):
        valid = (since >= taps - 1 - k).astype(F32)
        first = HALO - taps + 1 + k
        conv = conv + inner_ref[first : first + tokens, :] * valid * conv_w_ref[k : k + 1, :]
    act = conv * sigmoid(conv)
    conv_ref[...] = conv
    act_ref[...] = act
    proj = product(split(state_proj_ref[...]), split(act), NT)
    proj_ref[...] = proj
    pre = product(split(proj[:rank_n]), split(step_proj_ref[...]), TN) + step_bias_ref[...]
    pre_ref[...] = pre
    steps = softplus(pre)
    steps_ref[...] = steps
    masked = jnp.where(since == 0, RESET, steps)
    masked_ref[...] = masked
    drive_ref[...] = steps * act
    pair_ref[states : states + 1, :] = jnp.sum(masked, axis=0, keepdims=True)
    over_lanes(in_lanes, proj[rank_n : rank_n + states])
    chunk = 512
    for c in range(width // chunk):
        part = slice(c * chunk, (c + 1) * chunk)
        rate = rate_ref[:, part]

        def eight(group, state):
            for i in range(8):
                t = group * 8 + i
                decay = jnp.exp2(masked_ref[pl.ds(t, 1), part] * rate)
                state = decay * state + drive_ref[pl.ds(t, 1), part] * widen(in_lanes[t], chunk)
            return state

        pair_ref[0:states, part] = lax.fori_loop(0, tokens // 8, eight, jnp.zeros((states, chunk), F32))


def slot_tables(slots, cap, experts):
    slot = iota((slots, 8), 0)
    first = sum((slot >= cap * e).astype(jnp.int32) for e in range(1, experts))
    block = (first == iota((slots, 8), 1)).astype(F32)
    slot = iota((slots, 128), 0)
    first = sum(((slot >= cap * e).astype(jnp.int32) for e in range(1, experts)))
    within = (slot - first * cap == iota((slots, 128), 1)).astype(F32)
    return block, within


def scan_kernel(
    rank_n,
    states,
    experts,
    cap,
    me_ref,
    masked_ref,
    drive_ref,
    act_ref,
    gate_z_ref,
    start_ref,
    rate_ref,
    skip_ref,
    proj_ref,
    out_proj_ref,
    x_ref,
    gain_ref,
    router_ref,
    ids_ref,
    rank_ref,
    table_ref,
    scan_ref,
    history_ref,
    resid_ref,
    sent_ref,
    probs_ref,
    gate_ref,
    in_lanes,
    out_lanes,
    total,
):
    tokens, chunk = masked_ref.shape
    step = pl.program_id(0)

    @pl.when(step == 0)
    def _():
        over_lanes(in_lanes, proj_ref[rank_n : rank_n + states, :])
        over_lanes(out_lanes, proj_ref[rank_n + states : rank_n + 2 * states, :])
        total[...] = x_ref[...]

    rate = rate_ref[...]

    def eight(group, state):
        for i in range(8):
            t = group * 8 + i
            decay = jnp.exp2(masked_ref[pl.ds(t, 1), :] * rate)
            state = decay * state + drive_ref[pl.ds(t, 1), :] * widen(in_lanes[t], chunk)
            history_ref[t] = state
            scan_ref[pl.ds(t, 1), :] = jnp.sum(state * widen(out_lanes[t], chunk), axis=0, keepdims=True)
        return state

    lax.fori_loop(0, tokens // 8, eight, start_ref[...])
    gate_z = gate_z_ref[HALO:, :]
    mixed = (scan_ref[...] + skip_ref[...] * act_ref[...]) * (gate_z * sigmoid(gate_z))
    total[...] += product(split(mixed), split(out_proj_ref[...]), NN)

    @pl.when(step == pl.num_programs(0) - 1)
    def _():
        resid = total[...]
        resid_ref[...] = resid
        normed = resid * scale_of(resid) * gain_ref[...]
        logits = product(split(normed), split(router_ref[...]), NT)
        known = iota((tokens, 8), 1) < experts
        logits = jnp.where(known, logits, -1e30)
        raised = jnp.exp(logits - jnp.max(logits, axis=1, keepdims=True))
        raised = jnp.where(known, raised, 0.0)
        probs = raised / jnp.sum(raised, axis=1, keepdims=True)
        probs_ref[...] = probs
        ids = ids_ref[...]
        gate = jnp.sum(jnp.where(ids == iota((tokens, 8), 1), probs, 0.0), axis=1, keepdims=True)
        gate_ref[...] = gate
        slots = experts * cap
        sent_ref[0:slots, :] = pick(table_ref[...], normed, NN)
        sent_ref[slots:, :] = jnp.zeros((8, sent_ref.shape[1]), F32)
        rank = rank_ref[...].astype(jnp.int32)
        to_block = jnp.where(((ids ^ me_ref[0]) == iota((tokens, 8), 1)) & (rank < cap), gate, 0.0)
        at_rank = (rank == iota((tokens, 128), 1)).astype(BF16)
        high, low = split(to_block)
        rest = (to_block - high.astype(F32) - low.astype(F32)).astype(BF16)
        rows = dot(high, at_rank, TN) + (dot(low, at_rank, TN) + dot(rest, at_rank, TN))
        sent_ref[slots:, 0:128] = rows


def early_kernel(pieces, slices, *refs):
    grads, downs, outs = refs[:pieces], refs[pieces : pieces + slices], refs[pieces + slices :]
    downs = [split(d[...]) for d in downs]
    for p in range(pieces):
        grad = split(grads[p][...])
        for i in range(slices):
            outs[p][i] = product(grad, downs[i], NT)


def gelu_parts(value):
    inner = 0.7978845608 * (value + 0.044715 * value * value * value)
    tanh = jnp.tanh(inner)
    slope = 0.5 * (1.0 + tanh) + 0.5 * value * (1.0 - tanh * tanh) * 0.7978845608 * (
        1.0 + 3.0 * 0.044715 * value * value
    )
    return 0.5 * value * (1.0 + tanh), slope


def expert_kernel(slices, experts, cap, *refs):
    tokens_ref, ups, pulled_ref = refs[0], refs[1 : slices + 1], refs[slices + 1]
    back_ref, hidden_ref, grad_ref = refs[slices + 2 :]
    slots = experts * cap
    block, within = slot_tables(slots, cap, experts)
    within = within.astype(BF16)
    rows = split(tokens_ref[0:slots, :])
    back = jnp.zeros((slots, tokens_ref.shape[1]), F32)
    to_gate = jnp.zeros((slots, 1), F32)
    for i in range(slices):
        up = split(ups[i][...])
        hidden, slope = gelu_parts(product(rows, up, NN))
        pull = pulled_ref[i]
        grad = pull * slope
        hidden_ref[i] = hidden
        grad_ref[i] = grad
        to_gate += jnp.sum(hidden * pull, axis=1, keepdims=True)
        back += product(split(grad), up, NT)
    back_ref[0:slots, :] = back
    back_ref[slots:, :] = jnp.zeros((8, tokens_ref.shape[1]), F32)
    high, low = split(block * to_gate)
    rest = (block * to_gate - high.astype(F32) - low.astype(F32)).astype(BF16)
    back_ref[slots:, 0:128] = dot(high, within, TN) + (dot(low, within, TN) + dot(rest, within, TN))


def expert_grads_kernel(pieces, slices, experts, cap, *refs):
    tokens, grads, hiddens, pulls = (refs[i * pieces : (i + 1) * pieces] for i in range(4))
    downs, outs = refs[4 * pieces : 4 * pieces + slices], refs[4 * pieces + slices :]
    results, up_outs, down_outs = outs[:pieces], outs[pieces : pieces + slices], outs[pieces + slices :]
    slots = experts * cap
    downs = [split(d[...]) for d in downs]
    block, within = slot_tables(slots, cap, experts)
    within = within.astype(BF16)
    for p in range(pieces):
        ends = tokens[p][slots:, 0:128]
        high, low = split(ends)
        rest = (ends - high.astype(F32) - low.astype(F32)).astype(BF16)
        spread = dot(within, high, NT) + (dot(within, low, NT) + dot(within, rest, NT))
        gate = jnp.sum(spread * block, axis=1, keepdims=True)
        rows = split(tokens[p][0:slots, :] * gate)
        gated = split(grads[p][...] * gate)
        total = None
        for i in range(slices):
            hidden = split(hiddens[p][i])
            part = product(hidden, downs[i], NN)
            total = part if total is None else total + part
            up = product(rows, split(pulls[p][i]), TN)
            down = product(hidden, gated, TN)
            if p == 0:
                up_outs[i][...] = up
                down_outs[i][...] = down
            else:
                up_outs[i][...] += up
                down_outs[i][...] += down
        results[p][...] = total


def silu_parts(value):
    sig = sigmoid(value)
    return value * sig, sig * (1.0 + value * (1.0 - sig))


def mixer_back_kernel(
    rank_n,
    states,
    experts,
    cap,
    me_ref,
    back_ref,
    table_ref,
    gate_ref,
    probs_ref,
    ids_ref,
    rank_ref,
    resid_ref,
    grad_ref,
    gain_ref,
    router_ref,
    out_proj_ref,
    gate_z_ref,
    scan_ref,
    act_ref,
    skip_ref,
    masked_ref,
    rate_ref,
    proj_ref,
    steps_row_ref,
    grad_resid_ref,
    small_ref,
    grad_scan_ref,
    grad_gate_ref,
    grad_skip_ref,
    pair_ref,
    out_lanes,
    high,
    low,
):
    tokens, chunk = masked_ref.shape

    @pl.when(pl.program_id(0) == 0)
    def _():
        over_lanes(out_lanes, proj_ref[rank_n + states : rank_n + 2 * states, :])
        slots = experts * cap
        ids, rank = ids_ref[...], rank_ref[...].astype(jnp.int32)
        back = pick(table_ref[...], back_ref[0:slots, :], TN)
        at_rank = (rank == iota((tokens, 128), 1)).astype(BF16)
        ends = back_ref[slots:, 0:128]
        first, second = split(ends)
        third = (ends - first.astype(F32) - second.astype(F32)).astype(BF16)
        spread = dot(at_rank, first, NT) + (dot(at_rank, second, NT) + dot(at_rank, third, NT))
        mine = ((ids ^ me_ref[0]) == iota((tokens, 8), 1)) & (rank < cap)
        grad_gate = jnp.sum(jnp.where(mine, spread, 0.0), axis=1, keepdims=True)
        probs = probs_ref[...]
        grad_probs = jnp.where(ids == iota((tokens, 8), 1), grad_gate, 0.0)
        grad_logits = probs * (grad_probs - jnp.sum(probs * grad_probs, axis=1, keepdims=True))
        resid, gain = resid_ref[...], gain_ref[...]
        scale = scale_of(resid)
        normed = resid * scale * gain
        logits_two = split(grad_logits)
        grad_normed = gate_ref[...] * back + product(logits_two, split(router_ref[...]), NN)
        small_ref[...] = jnp.zeros_like(small_ref)
        small_ref[0:8, :] = product(logits_two, split(normed), TN)
        small_ref[8:9, :] = jnp.sum(grad_normed * resid * scale, axis=0, keepdims=True)
        pulled = gain * grad_normed
        grad_resid = (
            grad_ref[...]
            + scale * pulled
            - resid * (scale * scale * scale) * jnp.mean(pulled * resid, axis=1, keepdims=True)
        )
        grad_resid_ref[...] = grad_resid
        high[...], low[...] = split(grad_resid)

    grad_mixed = product((high[...], low[...]), split(out_proj_ref[...]), NT)
    silu, slope = silu_parts(gate_z_ref[HALO:, :])
    act = act_ref[...]
    grad_scan = grad_mixed * silu
    grad_scan_ref[...] = grad_scan
    grad_gate_ref[...] = grad_mixed * (scan_ref[...] + skip_ref[...] * act) * slope
    grad_skip_ref[...] = jnp.sum(grad_scan * act, axis=0, keepdims=True)
    rate = rate_ref[...]

    def eight(group, state):
        for i in range(8):
            t = tokens - 1 - (group * 8 + i)
            decay = jnp.exp2(masked_ref[pl.ds(t, 1), :] * rate)
            state = decay * (state + grad_scan_ref[pl.ds(t, 1), :] * widen(out_lanes[t], chunk))
        return state

    pair_ref[0:states, :] = lax.fori_loop(0, tokens // 8, eight, jnp.zeros((states, chunk), F32))
    pair_ref[states : states + 1, :] = steps_row_ref[...]


def late_grads_kernel(
    scan_ref, act_ref, skip_ref, gate_z_ref, grad_resid_ref, x_ref, gain_ref, grad_gate_ref, weight_ref,
    out_ref, normed_ref, high, low, high_x, low_x,
):
    depth = x_ref.shape[1]

    @pl.when(pl.program_id(0) == 0)
    def _():
        x = x_ref[...]
        high_x[...], low_x[...] = split(x * scale_of(x) * gain_ref[...])
        high[...], low[...] = split(grad_resid_ref[...])
        normed_ref[...] = jnp.zeros_like(normed_ref)

    grad = split(grad_gate_ref[...])
    out_ref[0:depth, :] = product((high_x[...], low_x[...]), grad, TN)
    normed_ref[...] += product(grad, split(weight_ref[...]), NT)
    gate_z = gate_z_ref[HALO:, :]
    mixed = (scan_ref[...] + skip_ref[...] * act_ref[...]) * (gate_z * sigmoid(gate_z))
    out_ref[depth:, :] = product(split(mixed), (high[...], low[...]), TN)


def scan_back_kernel(
    rank_n,
    states,
    masked_ref,
    steps_ref,
    drive_ref,
    act_ref,
    pre_ref,
    grad_scan_ref,
    skip_ref,
    history_ref,
    start_ref,
    end_ref,
    rate_ref,
    proj_ref,
    step_proj_ref,
    grad_act_ref,
    grad_pre_ref,
    grad_decay_ref,
    grad_proj_ref,
    in_lanes,
    out_lanes,
    grad_drive,
    grad_steps,
):
    tokens, chunk = masked_ref.shape
    step = pl.program_id(0)

    @pl.when(step == 0)
    def _():
        over_lanes(in_lanes, proj_ref[rank_n : rank_n + states, :])
        over_lanes(out_lanes, proj_ref[rank_n + states : rank_n + 2 * states, :])
        grad_proj_ref[...] = jnp.zeros_like(grad_proj_ref)

    rate = rate_ref[...]
    lane = iota((states, tokens), 1)

    def one(t, before, carried):
        state, decays, grad_in, grad_out = carried
        masked = masked_ref[pl.ds(t, 1), :]
        grad = grad_scan_ref[pl.ds(t, 1), :]
        decay = jnp.exp2(masked * rate)
        state = state + grad * widen(out_lanes[t], chunk)
        at_out = jnp.sum(history_ref[t] * grad, axis=1, keepdims=True)
        at_in = jnp.sum(state * drive_ref[pl.ds(t, 1), :], axis=1, keepdims=True)
        grad_out = jnp.where(lane == t, at_out, grad_out)
        grad_in = jnp.where(lane == t, at_in, grad_in)
        grad_drive[pl.ds(t, 1), :] = jnp.sum(state * widen(in_lanes[t], chunk), axis=0, keepdims=True)
        state = decay * state
        pulled = state * before
        grad_steps[pl.ds(t, 1), :] = jnp.sum(pulled * rate, axis=0, keepdims=True)
        return state, decays + pulled * masked, grad_in, grad_out

    def four(group, carried):
        for i in range(4):
            t = tokens - 1 - (group * 4 + i)
            carried = one(t, history_ref[t - 1], carried)
        return carried

    nothing = jnp.zeros((states, tokens), F32)
    carried = lax.fori_loop(
        0, tokens // 4 - 1, four, (end_ref[...], jnp.zeros((states, chunk), F32), nothing, nothing)
    )
    for t in (3, 2, 1):
        carried = one(t, history_ref[t - 1], carried)
    _, decays, grad_in, grad_out = one(0, start_ref[...], carried)
    grad_decay_ref[...] = decays * (rate * (1.0 / LOG2E))
    steps, act = steps_ref[...], act_ref[...]
    grad_act_ref[...] = skip_ref[...] * grad_scan_ref[...] + grad_drive[...] * steps
    grad_pre = (grad_steps[...] * (1.0 / LOG2E) + grad_drive[...] * act) * sigmoid(pre_ref[...])
    grad_pre_ref[...] = grad_pre
    grad_proj_ref[0:rank_n, :] += product(split(step_proj_ref[...]), split(grad_pre), NT)
    grad_proj_ref[rank_n : rank_n + states, :] += grad_in
    grad_proj_ref[rank_n + states : rank_n + 2 * states, :] += grad_out


def input_back_kernel(
    rank_n,
    states,
    grad_proj_ref,
    proj_ref,
    state_proj_ref,
    act_ref,
    grad_act_ref,
    grad_pre_ref,
    conv_ref,
    inner_ref,
    conv_w_ref,
    since_ref,
    weight_ref,
    x_ref,
    halo_ref,
    gain_ref,
    grad_gate_normed_ref,
    grad_resid_ref,
    grad_decay_ref,
    grad_skip_ref,
    out_ref,
    input_ref,
    edge_ref,
    gain_row_ref,
    high,
    low,
    grad_inner,
    total,
):
    tokens, chunk = act_ref.shape
    depth = x_ref.shape[1]
    taps = conv_w_ref.shape[0]
    step = pl.program_id(0)

    @pl.when(step == 0)
    def _():
        x = jnp.concatenate([halo_ref[...], x_ref[...]], axis=0)
        high[...], low[...] = split(x * scale_of(x) * gain_ref[...])
        total[...] = jnp.zeros_like(total)

    act, grad_pre = split(act_ref[...]), grad_pre_ref[...]
    grad_pre_two = split(grad_pre)
    grad_proj = split(grad_proj_ref[...])
    grad_act = grad_act_ref[...] + product(grad_proj, split(state_proj_ref[...]), TN)
    _, slope = silu_parts(conv_ref[...])
    grad_conv = grad_act * slope
    since = since_ref[...]
    grad_inner[...] = jnp.zeros_like(grad_inner)
    base = depth
    out_ref[base : base + 2 * states + rank_n, :] = product(grad_proj, act, NN)
    base += 2 * states + rank_n
    out_ref[base : base + rank_n, :] = product(split(proj_ref[0:rank_n, :]), grad_pre_two, NN)
    base += rank_n
    out_ref[base : base + states, :] = grad_decay_ref[...]
    base += states
    rows = []
    for k in range(taps):
        valid = (since >= taps - 1 - k).astype(F32)
        first = HALO - taps + 1 + k
        held = grad_conv * valid
        rows.append(jnp.sum(held * inner_ref[first : first + tokens, :], axis=0, keepdims=True))
        grad_inner[first : first + tokens, :] += held * conv_w_ref[k : k + 1, :]
    rows.append(jnp.sum(grad_conv, axis=0, keepdims=True))
    rows.append(jnp.sum(grad_pre, axis=0, keepdims=True))
    rows.append(grad_skip_ref[...])
    out_ref[base:, :] = jnp.zeros((out_ref.shape[0] - base, chunk), F32)
    for i, row in enumerate(rows):
        out_ref[base + i : base + i + 1, :] = row
    grads = split(grad_inner[...])
    out_ref[0:depth, :] = product((high[...], low[...]), grads, TN)
    total[...] += product(grads, split(weight_ref[...]), NT)

    @pl.when(step == pl.num_programs(0) - 1)
    def _():
        gain = gain_ref[...]

        def rows_back(x, grad):
            scale = scale_of(x)
            pulled = gain * grad
            back = scale * pulled - x * (scale * scale * scale) * jnp.mean(pulled * x, axis=1, keepdims=True)
            return back, jnp.sum(grad * x * scale, axis=0, keepdims=True)

        edge, edge_gain = rows_back(halo_ref[...], total[0:HALO, :])
        own, own_gain = rows_back(x_ref[...], total[HALO:, :] + grad_gate_normed_ref[...])
        edge_ref[...] = edge
        input_ref[...] = grad_resid_ref[...] + own
        gain_row_ref[...] = edge_gain + own_gain


def per_device(
    block_input,
    seq_lengths,
    expert_ids,
    output_grad,
    mixer_gain,
    in_proj,
    conv_weight,
    conv_bias,
    state_proj,
    step_proj,
    step_bias,
    decay_log,
    skip_gain,
    out_proj,
    router_gain,
    router,
    expert_up,
    expert_down,
):
    grid = Grid()
    tokens, depth = block_input.shape
    taps, width = conv_weight.shape
    rank_n, states, experts = step_proj.shape[0], decay_log.shape[1], router.shape[1]
    cap = (5 * tokens + 4 * experts - 1) // (4 * experts)
    slots, hidden = experts * cap, expert_up.shape[2]
    chunk = 512
    chunks = width // chunk
    pieces, slices = grid.size["outer"], grid.size["inner"]
    me = lax.axis_index("exp").astype(jnp.int32).reshape(1)
    ext = HALO + tokens

    halo = grid.along(block_input[tokens - HALO :], 1)

    count = seq_lengths.shape[0]
    earlier = jnp.arange(count)[:, None] > jnp.arange(count)[None, :]
    starts = jnp.sum(jnp.where(earlier, seq_lengths[None, :], 0), axis=1)
    position = grid.index * tokens + jnp.arange(tokens, dtype=jnp.int32)
    own_start = jnp.max(jnp.where(starts[None, :] <= position[:, None], starts[None, :], 0), axis=1)
    since = (position - own_start)[:, None]
    rate = -jnp.exp(decay_log.T) * LOG2E
    state_proj_t = state_proj.T
    router_t = pad_rows(router.T, 8)
    row = lambda vector: vector.reshape(1, -1)

    sent_grads, table, rank, loads = call(
        functools.partial(route_kernel, experts, cap),
        [shape(slots, depth), shape(slots, tokens, dtype=BF16), shape(tokens, 1), shape(8, depth)],
        (me, expert_ids, output_grad),
        in_specs=[SMEM] + [pl.BlockSpec(memory_space=pltpu.VMEM)] * 2,
        name="route",
    )
    halo, sent_grads = tie(halo, sent_grads)
    held_grads, _ = send_y(grid, sent_grads, cap, False)
    up, down = expert_up[0], expert_down[0]
    ups = [up] + [grid.swap(up, "inner", s) for s in range(1, slices)]
    downs = [down] + [grid.swap(down, "inner", s) for s in range(1, slices)]

    block = lambda c: (0, c)
    joined = call(
        join_kernel,
        shape(ext, 2 * width),
        (block_input, halo, row(mixer_gain), in_proj),
        grid=(2 * chunks,),
        in_specs=[full(tokens, depth), full(HALO, depth), full(1, depth), pl.BlockSpec((depth, chunk), block)],
        out_specs=pl.BlockSpec((ext, chunk), block),
        scratch=[pltpu.VMEM((ext, depth), BF16)] * 2,
        name="join",
    )
    joined, *held_grads = tie(joined, *held_grads)
    conv, act, pre, steps, masked, drive, proj, pair = call(
        functools.partial(features_kernel, rank_n, states),
        [shape(tokens, width)] * 6 + [shape(rank_n + 2 * states, tokens), shape(states + 1, width)],
        (joined, since, conv_weight, row(conv_bias), state_proj_t, step_proj, row(step_bias), rate),
        grid=(1,),
        in_specs=[
            full(ext, width),
            full(tokens, 1),
            full(taps, width),
            full(1, width),
            full(rank_n + 2 * states, width),
            full(rank_n, width),
            full(1, width),
            full(states, width),
        ],
        out_specs=[full(tokens, width)] * 6 + [full(rank_n + 2 * states, tokens), full(states + 1, width)],
        scratch=[pltpu.VMEM((tokens, states, 128), F32)],
        name="features",
    )
    own_grads = send_core(grid, held_grads, None, cap, False)
    pair, own_grads, *downs = tie(pair, own_grads, *downs)
    near_grads, far_grads = grid.swap(own_grads, "outer", 1), grid.swap(own_grads, "outer", 2)
    start, (near_grads, far_grads) = entering(
        grid, pair, rate, False, lambda total: tie(total, near_grads, far_grads)
    )
    last_grads = grid.swap(far_grads, "outer", 1)
    start, last_grads = tie(start, last_grads)
    tok = pl.BlockSpec((tokens, chunk), block)
    gate_half = pl.BlockSpec((ext, chunk), lambda c: (0, chunks + c))
    one_row = pl.BlockSpec((1, chunk), block)
    state_rows = pl.BlockSpec((states, chunk), block)
    history_block = pl.BlockSpec((tokens, states, chunk), lambda c: (0, 0, c))
    out_rows = pl.BlockSpec((chunk, depth), lambda c: (c, 0))
    proj_full = full(rank_n + 2 * states, tokens)
    lanes = pltpu.VMEM((tokens, states, 128), F32)
    scan, history, resid, sent, probs, gate = call(
        functools.partial(scan_kernel, rank_n, states, experts, cap),
        [
            shape(tokens, width),
            shape(tokens, states, width),
            shape(tokens, depth),
            shape(slots + 8, depth),
            shape(tokens, 8),
            shape(tokens, 1),
        ],
        (
            me, masked, drive, act, joined, start, rate, row(skip_gain), proj, out_proj, block_input,
            row(router_gain), router_t, expert_ids, rank, table,
        ),
        grid=(chunks,),
        in_specs=[
            SMEM, tok, tok, tok, gate_half, state_rows, state_rows, one_row, proj_full, out_rows,
            full(tokens, depth), full(1, depth), full(8, depth), full(tokens, 1), full(tokens, 1),
            full(slots, tokens),
        ],
        out_specs=[
            tok, history_block, full(tokens, depth), full(slots + 8, depth), full(tokens, 8), full(tokens, 1),
        ],
        scratch=[lanes, lanes, pltpu.VMEM((tokens, depth), F32)],
        name="scan",
    )

    grad_pieces = [own_grads, near_grads, far_grads, last_grads]
    pulled = call(
        functools.partial(early_kernel, pieces, slices),
        [shape(slices, slots, hidden)] * pieces,
        (*grad_pieces, *downs),
        name="early",
    )
    own_tokens = send_core(grid, *send_y(grid, sent, cap, True), cap, True)
    own_tokens, *pulled = tie(own_tokens, *pulled)
    near_tokens, far_tokens = grid.swap(own_tokens, "outer", 1), grid.swap(own_tokens, "outer", 2)

    def expert(rows, pulled_rows):
        return call(
            functools.partial(expert_kernel, slices, experts, cap),
            [shape(slots + 8, depth)] + [shape(slices, slots, hidden)] * 2,
            (rows, *ups, pulled_rows),
            name="expert",
        )

    own_outs = expert(own_tokens, pulled[0])
    near_tokens, far_tokens, *own_outs = tie(near_tokens, far_tokens, *own_outs)
    last_tokens = grid.swap(far_tokens, "outer", 1)
    near_outs, far_outs = expert(near_tokens, pulled[1]), expert(far_tokens, pulled[2])
    last_tokens, near_outs, far_outs = tie(last_tokens, near_outs, far_outs)
    last_outs = expert(last_tokens, pulled[3])
    token_pieces = [own_tokens, near_tokens, far_tokens, last_tokens]
    backs, hiddens, pulls = zip(own_outs, near_outs, far_outs, last_outs)
    back = from_experts(grid, outer_reduce(grid, backs), cap, True)
    outs = call(
        functools.partial(expert_grads_kernel, pieces, slices, experts, cap),
        [shape(slots, depth)] * pieces + [shape(depth, hidden)] * slices + [shape(hidden, depth)] * slices,
        (*token_pieces, *grad_pieces, *hiddens, *pulls, *downs),
        name="expert_grads",
    )
    results, up_grads, down_grads = outs[:pieces], outs[pieces : pieces + slices], outs[pieces + slices :]
    others_up = [grid.swap(up_grads[s], "inner", s) for s in range(1, slices)]
    back, *others_up = tie(back, *others_up)
    grad_up = functools.reduce(jnp.add, others_up, up_grads[0])
    others_down = [grid.swap(down_grads[s], "inner", s) for s in range(1, slices)]

    grad_resid, small, grad_scan, grad_gate, grad_skip, back_pair = call(
        functools.partial(mixer_back_kernel, rank_n, states, experts, cap),
        [
            shape(tokens, depth),
            shape(16, depth),
            shape(tokens, width),
            shape(tokens, width),
            shape(1, width),
            shape(states + 1, width),
        ],
        (
            me, back, table, gate, probs, expert_ids, rank, resid, output_grad, row(router_gain), router_t,
            out_proj, joined, scan, act, row(skip_gain), masked, rate, proj, pair[states:],
        ),
        grid=(chunks,),
        in_specs=[
            SMEM, full(slots + 8, depth), full(slots, tokens), full(tokens, 1), full(tokens, 8),
            full(tokens, 1), full(tokens, 1), full(tokens, depth), full(tokens, depth), full(1, depth),
            full(8, depth), out_rows, gate_half, tok, tok, one_row, tok, state_rows, proj_full, one_row,
        ],
        out_specs=[
            full(tokens, depth), full(16, depth), tok, tok, one_row,
            pl.BlockSpec((states + 1, chunk), block),
        ],
        scratch=[lanes] + [pltpu.VMEM((tokens, depth), BF16)] * 2,
        name="mixer_back",
    )
    back_pair, *results = tie(back_pair, *results)
    wide = pl.BlockSpec((tokens, depth), block)
    late, grad_gate_normed = call(
        late_grads_kernel,
        [shape(2 * depth, width), shape(tokens, depth)],
        (scan, act, row(skip_gain), joined, grad_resid, block_input, row(mixer_gain), grad_gate, in_proj),
        grid=(2,),
        in_specs=[
            wide, wide, pl.BlockSpec((1, depth), block), pl.BlockSpec((ext, depth), lambda c: (0, 2 + c)),
            full(tokens, depth), full(tokens, depth), full(1, depth), wide,
            pl.BlockSpec((depth, depth), lambda c: (0, 2 + c)),
        ],
        out_specs=[pl.BlockSpec((2 * depth, depth), block), full(tokens, depth)],
        scratch=[pltpu.VMEM((tokens, depth), BF16)] * 4,
        name="late_grads",
    )
    end, _ = entering(grid, back_pair, rate, True)
    late = scatter_rows(grid, late, "core")
    end, late = tie(end, late)
    late = sum_first(grid, late)
    through = grid.swap(results[3], "outer", 1)
    grad_act, grad_pre, grad_decay, grad_proj = call(
        functools.partial(scan_back_kernel, rank_n, states),
        [
            shape(tokens, width), shape(tokens, width), shape(states, width), shape(rank_n + 2 * states, tokens),
        ],
        (
            masked, steps, drive, act, pre, grad_scan, row(skip_gain), history, start, end, rate, proj, step_proj,
        ),
        grid=(chunks,),
        in_specs=[
            tok, tok, tok, tok, tok, tok, one_row, history_block, state_rows, state_rows, state_rows, proj_full,
            pl.BlockSpec((rank_n, chunk), block),
        ],
        out_specs=[tok, tok, state_rows, proj_full],
        scratch=[lanes, lanes] + [pltpu.VMEM((tokens, chunk), F32)] * 2,
        name="scan_back",
    )
    grad_proj, through, first, second, *others_down = tie(grad_proj, through, *late, *others_down)
    grad_down = functools.reduce(jnp.add, others_down, down_grads[0])
    late = sum_second(grid, first, second)
    result = outer_reduce_rest(grid, results, through)
    used = depth + 2 * states + 2 * rank_n + states + taps + 4
    unit = 16 * grid.size["inner"] * grid.size["y"]
    packed = -(-(used + 8) // unit) * unit
    grads, input_grad, edge, gain_row = call(
        functools.partial(input_back_kernel, rank_n, states),
        [shape(packed, width), shape(tokens, depth), shape(HALO, depth), shape(1, depth)],
        (
            grad_proj, proj, state_proj_t, act, grad_act, grad_pre, conv, joined, conv_weight, since, in_proj,
            block_input, halo, row(mixer_gain), grad_gate_normed, grad_resid, grad_decay, grad_skip,
        ),
        grid=(chunks,),
        in_specs=[
            proj_full, proj_full, pl.BlockSpec((rank_n + 2 * states, chunk), block), tok, tok, tok, tok,
            pl.BlockSpec((ext, chunk), block), pl.BlockSpec((taps, chunk), block), full(tokens, 1),
            pl.BlockSpec((depth, chunk), block), full(tokens, depth), full(HALO, depth), full(1, depth),
            full(tokens, depth), full(tokens, depth), state_rows, one_row,
        ],
        out_specs=[
            pl.BlockSpec((packed, chunk), block), full(tokens, depth), full(HALO, depth), full(1, depth),
        ],
        scratch=[pltpu.VMEM((ext, depth), BF16)] * 2
        + [pltpu.VMEM((ext, chunk), F32), pltpu.VMEM((ext, depth), F32)],
        name="input_back",
    )
    from_next = grid.along(edge, -1)
    input_grad = jnp.concatenate([input_grad[: tokens - HALO], input_grad[tokens - HALO :] + from_next], axis=0)
    small = jnp.concatenate([small[:9], gain_row, loads[0:1], small[11:]], axis=0).reshape(8, width)
    grads = lax.dynamic_update_slice(grads, small, (used, 0))
    grads, late, result = tie(grads, late, result)
    result = from_experts(grid, result, cap, False)
    late = sum_outer(grid, late)
    grads = sum_second(grid, *sum_first(grid, scatter_rows(grid, grads, "core")))
    late, grads, result = tie(late, grads, result)
    late = spread_outer(grid, late)
    late, grads = tie(late, grads)
    first, second = spread_second(grid, late)
    grads = sum_outer(grid, grads)
    first, second, grads = tie(first, second, grads)
    late = spread_first(grid, first, second)
    grads = spread_outer(grid, grads)
    late, grads = tie(late, grads)
    late = gather_rows(grid, late, "core")
    first, second = spread_second(grid, grads)
    late, first, second = tie(late, first, second)
    grads = gather_rows(grid, spread_first(grid, first, second), "core")

    combined = jnp.dot(table.T, result.astype(F32), precision=lax.Precision.HIGHEST, preferred_element_type=F32)
    block_output = resid + gate * combined

    at = depth
    grad_state_proj = grads[at : at + 2 * states + rank_n].T
    at += 2 * states + rank_n
    grad_step_proj = grads[at : at + rank_n]
    at += rank_n
    grad_decay_log = grads[at : at + states].T
    at += states
    grad_conv_weight = grads[at : at + taps]
    at += taps
    grad_conv_bias, grad_step_bias, grad_skip_gain = grads[at], grads[at + 1], grads[at + 2]
    small = grads[used : used + 8].reshape(16, depth)
    return (
        block_output,
        input_grad,
        small[9],
        jnp.concatenate([grads[:depth], late[:depth]], axis=1),
        grad_conv_weight,
        grad_conv_bias,
        grad_state_proj,
        grad_step_proj,
        grad_step_bias,
        grad_decay_log,
        grad_skip_gain,
        jnp.concatenate([late[depth:, :depth], late[depth:, depth:]], axis=0),
        small[8],
        small[:experts].T,
        grad_up[None],
        grad_down[None],
        small[10, :experts].astype(jnp.int32),
        small[10, 128 : 128 + experts].astype(jnp.int32),
    )


def solution(mesh):
    rows, copied = P(("seq", "exp"), None), P()
    up, down = P("exp", None, "seq"), P("exp", "seq", None)
    in_specs = (rows, copied, rows, rows) + (copied,) * 12 + (up, down)
    out_specs = (rows, rows) + (copied,) * 12 + (up, down, copied, copied)
    return jax.shard_map(per_device, mesh=mesh, in_specs=in_specs, out_specs=out_specs, check_vma=False)
```

```python
import functools

import jax
import jax.numpy as jnp
from jax import lax
from jax.experimental import pallas as pl
from jax.experimental.pallas import tpu as pltpu
from jax.sharding import PartitionSpec as P

F32 = jnp.float32
BF16 = jnp.bfloat16
EPS = 1e-05
LOG2E = 1.4426950408889634
HALO = 16
RESET = 1e9
AXES = ("seq", "exp")
NN, NT, TN = ((1,), (0,)), ((1,), (1,)), ((0,), (0,))
VMEM_BYTES = 52 << 20
MICROSECONDS = {
    "route": 1, "join": 8, "features": 8, "join_states": 1, "scan": 14, "early": 7, "expert": 4.4,
    "expert_grads": 17, "mixer_back": 9.6, "late": 6, "scan_back": 10, "input_back": 11, "finish_late": 8, "finish": 6,
}


class Grid:
    def __init__(self):
        self.seq, self.exp = lax.axis_size("seq"), lax.axis_size("exp")
        self.outer = 4
        self.size = {
            "core": 2,
            "y": self.exp // 2,
            "inner": self.seq // self.outer,
            "outer": self.outer,
        }
        self.total = self.seq * self.exp
        index, step, self.step, self.at = lax.axis_index(AXES), 1, {}, {}
        for name in ("core", "y", "inner", "outer"):
            self.step[name] = step
            self.at[name] = (index // step) % self.size[name]
            step *= self.size[name]
        self.index = index

    def swap(self, block, name, mask):
        return self.swap_bits(block, mask * self.step[name])

    def swap_bits(self, block, bits):
        return lax.ppermute(block, AXES, [(i, i ^ bits) for i in range(self.total)])

    def along(self, block, distance):
        route = [(i - distance, i) for i in range(self.total) if 0 <= i - distance < self.total]
        return lax.ppermute(block, AXES, route)


def tie(*values):
    return lax.optimization_barrier(values)


def outer_reduce_rest(grid, parts, through):
    through, near = tie(through, parts[1])
    near = grid.swap(near, "outer", 1)
    far = grid.swap(parts[2] + through, "outer", 2)
    return parts[0] + near + far


def in_order(parts, place):
    bit = 1
    while bit < len(parts):
        turned = ((place // bit) % 2) == 1
        parts = [jnp.where(turned, parts[i ^ bit], parts[i]) for i in range(len(parts))]
        bit *= 2
    return parts


def scatter_rows(grid, block, name):
    count, place = grid.size[name], grid.at[name]
    if count == 1:
        return block
    rows = block.shape[0] // count
    piece = lambda s: lax.dynamic_slice_in_dim(block, (place ^ s) * rows, rows, 0)
    got = [grid.swap(piece(s), name, s) for s in range(1, count)]
    total = piece(0)
    for part in got:
        total = total + part
    return total


def gather_rows(grid, block, name):
    count = grid.size[name]
    if count == 1:
        return block
    parts = [block] + [grid.swap(block, name, s) for s in range(1, count)]
    return jnp.concatenate(in_order(parts, grid.at[name]), axis=0)


def sum_first(grid, half):
    rows = half.shape[0] // 2
    return scatter_rows(grid, half[:rows], "inner"), scatter_rows(grid, half[rows:], "y")


def sum_second(grid, first, second):
    return jnp.concatenate([scatter_rows(grid, first, "y"), scatter_rows(grid, second, "inner")], axis=0)


def sum_outer(grid, both):
    count, place = grid.size["outer"], grid.at["outer"]
    columns = both.shape[1] // count
    piece = lambda s: lax.dynamic_slice_in_dim(both, (place ^ s) * columns, columns, 1)
    got = [grid.swap(piece(s), "outer", s) for s in range(1, count)]
    total = piece(0)
    for part in got:
        total = total + part
    return total


def spread_outer(grid, total):
    count = grid.size["outer"]
    parts = [total] + [grid.swap(total, "outer", s) for s in range(1, count)]
    return jnp.concatenate(in_order(parts, grid.at["outer"]), axis=1)


def cut_outer(grid, both):
    columns = both.shape[1] // 4
    return [
        lax.dynamic_slice_in_dim(both, (grid.at["outer"] ^ s) * columns, columns, 1) for s in range(4)
    ]


def join_outer(grid, own, near, far, last):
    return jnp.concatenate(in_order([own, near, far, last], grid.at["outer"]), axis=1)


def spread_second(grid, both):
    own = both.shape[0] // 2
    return gather_rows(grid, both[:own], "y"), gather_rows(grid, both[own:], "inner")


def spread_first(grid, first, second):
    return jnp.concatenate([gather_rows(grid, first, "inner"), gather_rows(grid, second, "y")], axis=0)


def join_states_kernel(last, later_ref, total_ref, got_ref, ahead_ref, rate_ref, *outs):
    states = rate_ref.shape[0]
    rows, sums = slice(0, states), slice(states, states + 1)

    def follow(early, late, out):
        out[rows, :] = jnp.exp2(rate_ref[...] * late[sums, :]) * early[rows, :] + late[rows, :]
        out[sums, :] = early[sums, :] + late[sums, :]

    @pl.when(later_ref[0] == 1)
    def _():
        follow(got_ref, ahead_ref, outs[0])
        if not last:
            follow(got_ref, total_ref, outs[1])

    @pl.when(later_ref[0] == 0)
    def _():
        outs[0][...] = ahead_ref[...]
        if not last:
            follow(total_ref, got_ref, outs[1])


def entering(grid, pair, rate, backward, after):
    states = rate.shape[0]
    total, ahead, hop = pair, jnp.zeros_like(pair), 1
    bits = 1
    while bits < grid.total:
        got = grid.swap_bits(total, bits)
        later = ((grid.index // bits) % 2).astype(jnp.int32)
        later = (1 - later if backward else later).reshape(1)
        last = 2 * bits >= grid.total
        whole = pl.BlockSpec(memory_space=pltpu.VMEM)
        ahead, *rest = call(
            functools.partial(join_states_kernel, last),
            [shape(*pair.shape)] * (1 if last else 2),
            (later, total, got, ahead, rate),
            in_specs=[SMEM] + [whole] * 4,
            name="join_states",
        )
        total = rest[0] if rest else None
        if hop in after:
            total = after[hop](total)
        bits, hop = 2 * bits, hop + 1
    return ahead[:states]


def pad_rows(block, rows):
    return jnp.pad(block, ((0, rows - block.shape[0]), (0, 0)))


def send_y(grid, block, cap, tail):
    width, slots = 2 * cap, grid.exp * cap
    held, tails = [block[:width]], [block[slots:]]
    for s in range(1, grid.size["y"]):
        part = block[s * width : (s + 1) * width]
        got = grid.swap(jnp.concatenate([part, block[slots:]], axis=0) if tail else part, "y", s)
        held.append(got[:width])
        tails.append(got[width:])
    return held, tails


def send_core(grid, held, tails, cap, tail):
    ny = grid.size["y"]
    mine, others = [h[:cap] for h in held], [h[cap:] for h in held]
    if tail:
        others.append(pad_rows(jnp.concatenate([t[2 * s + 1 : 2 * s + 2] for s, t in enumerate(tails)], axis=0), 8))
    got = grid.swap(jnp.concatenate(others, axis=0), "core", 1)
    out = mine + [got[: ny * cap]]
    if tail:
        ends = [t[2 * s : 2 * s + 1] for s, t in enumerate(tails)] + [got[ny * cap : ny * cap + ny]]
        out.append(pad_rows(jnp.concatenate(ends, axis=0), 8))
    return jnp.concatenate(out, axis=0)


def back_core(grid, block, cap, tail):
    ny = grid.size["y"]
    half, slots = ny * cap, 2 * ny * cap
    send = block[half:slots]
    if tail:
        send = jnp.concatenate([send, pad_rows(block[slots + ny : slots + 2 * ny], 8)], axis=0)
    return grid.swap(send, "core", 1)


def back_y(grid, block, got, cap, tail):
    ny = grid.size["y"]
    half, slots = ny * cap, 2 * ny * cap
    rows, ends = [], []
    for s in range(ny):
        pair = [block[s * cap : (s + 1) * cap], got[s * cap : (s + 1) * cap]]
        both = [block[slots + s : slots + s + 1], got[half + s : half + s + 1]] if tail else []
        if s:
            if tail:
                pair.append(pad_rows(jnp.concatenate(both, axis=0), 8))
            back = grid.swap(jnp.concatenate(pair, axis=0), "y", s)
            pair, both = [back[: 2 * cap]], [back[2 * cap : 2 * cap + 2]]
        rows += pair
        ends += both
    if tail:
        rows.append(pad_rows(jnp.concatenate(ends, axis=0), 8))
    return jnp.concatenate(rows, axis=0)


def split(value):
    high = value.astype(BF16)
    return high, (value - high.astype(F32)).astype(BF16)


def dot(left, right, dims):
    return lax.dot_general(left, right, (dims, ((), ())), preferred_element_type=F32)


def product(left, right, dims):
    return dot(left[0], right[0], dims) + (dot(left[0], right[1], dims) + dot(left[1], right[0], dims))


def pick(exact, value, dims):
    high, low = split(value)
    return dot(exact, high, dims) + dot(exact, low, dims)


def sigmoid(value):
    return 1.0 / (1.0 + jnp.exp(-value))


def softplus(value):
    small = jnp.exp(-jnp.abs(value))
    series = small * (1.0 - small * (0.5 - small * (1.0 / 3.0 - small * (0.25 - small * 0.2))))
    return jnp.maximum(value, 0.0) + jnp.where(small < 0.03, series, jnp.log(1.0 + small))


def iota(shape, dim):
    return lax.broadcasted_iota(jnp.int32, shape, dim)


def scale_of(value):
    return lax.rsqrt(jnp.mean(value * value, axis=1, keepdims=True) + EPS)


def over_lanes(ref, columns):
    rows = columns.shape[0]
    for t in range(columns.shape[1]):
        ref[t] = jnp.broadcast_to(columns[:, t : t + 1], (rows, 128))


def widen(value, width):
    return jnp.concatenate([value] * (width // 128), axis=1)


def call(kernel, outs, ins, grid=None, in_specs=None, out_specs=None, scratch=(), name=None, aliases=None):
    whole = pl.BlockSpec(memory_space=pltpu.VMEM)
    return pl.pallas_call(
        kernel,
        out_shape=outs,
        grid=grid or (),
        in_specs=in_specs or [whole] * len(ins),
        out_specs=out_specs or jax.tree.map(lambda _: whole, outs),
        scratch_shapes=scratch,
        name=name,
        cost_estimate=pl.CostEstimate(
            flops=int(MICROSECONDS[name] * 1.1e9), transcendentals=0, bytes_accessed=int(MICROSECONDS[name] * 1e6)
        ),
        input_output_aliases=aliases or {},
        compiler_params=pltpu.CompilerParams(vmem_limit_bytes=VMEM_BYTES),
    )(*ins)


def shape(*dims, dtype=F32):
    return jax.ShapeDtypeStruct(dims, dtype)


SMEM = pl.BlockSpec(memory_space=pltpu.SMEM)


def full(*dims):
    return pl.BlockSpec(dims, lambda c: (0,) * len(dims))


def route_kernel(experts, cap, me_ref, ids_ref, grad_ref, sent_ref, table_ref, rank_ref, load_ref):
    ids = ids_ref[...]
    tokens = ids.shape[0]
    chosen = (ids == iota((tokens, 128), 1)).astype(F32)
    before = (iota((tokens, tokens), 0) > iota((tokens, tokens), 1)).astype(BF16)
    rank = jnp.sum(dot(before, chosen.astype(BF16), NN) * chosen, axis=1, keepdims=True)
    kept = (rank < cap).astype(F32)
    place = jnp.where(rank < cap, ((ids ^ me_ref[0]) * cap).astype(F32) + rank, -1.0)
    row = jnp.broadcast_to(place, (tokens, tokens)).T
    slots = experts * cap
    table = (iota((slots, tokens), 0).astype(F32) == jnp.broadcast_to(row[0:1], (slots, tokens))).astype(F32)
    table = table.astype(BF16)
    table_ref[...] = table
    rank_ref[...] = rank
    sent_ref[...] = pick(table, grad_ref[...], NN)
    load_ref[...] = jnp.zeros_like(load_ref)
    load_ref[0:1, 0:128] = jnp.sum(chosen, axis=0, keepdims=True)
    load_ref[0:1, 128:256] = jnp.sum(chosen * (1.0 - kept), axis=0, keepdims=True)


def join_kernel(x_ref, halo_ref, gain_ref, weight_ref, joined_ref, high, low):
    @pl.when(pl.program_id(0) == 0)
    def _():
        x = jnp.concatenate([halo_ref[...], x_ref[...]], axis=0)
        high[...], low[...] = split(x * scale_of(x) * gain_ref[...])

    joined_ref[...] = product((high[...], low[...]), split(weight_ref[...]), NN)


def features_kernel(
    rank_n,
    states,
    inner_ref,
    since_ref,
    conv_w_ref,
    conv_b_ref,
    state_proj_ref,
    step_proj_ref,
    step_bias_ref,
    rate_ref,
    conv_ref,
    act_ref,
    pre_ref,
    steps_ref,
    masked_ref,
    drive_ref,
    proj_ref,
    pair_ref,
    in_lanes,
):
    tokens, width = act_ref.shape
    taps = conv_w_ref.shape[0]
    since = since_ref[...]
    conv = jnp.broadcast_to(conv_b_ref[...], (tokens, width))
    for k in range(taps):
        valid = (since >= taps - 1 - k).astype(F32)
        first = HALO - taps + 1 + k
        conv = conv + inner_ref[first : first + tokens, :] * valid * conv_w_ref[k : k + 1, :]
    act = conv * sigmoid(conv)
    conv_ref[...] = conv
    act_ref[...] = act
    proj = product(split(state_proj_ref[...]), split(act), NT)
    proj_ref[...] = proj
    pre = product(split(proj[:rank_n]), split(step_proj_ref[...]), TN) + step_bias_ref[...]
    pre_ref[...] = pre
    steps = softplus(pre)
    steps_ref[...] = steps
    masked = jnp.where(since == 0, RESET, steps)
    masked_ref[...] = masked
    drive_ref[...] = steps * act
    pair_ref[states : states + 1, :] = jnp.sum(masked, axis=0, keepdims=True)
    over_lanes(in_lanes, proj[rank_n : rank_n + states])
    chunk = 512
    for c in range(width // chunk):
        part = slice(c * chunk, (c + 1) * chunk)
        rate = rate_ref[:, part]

        def eight(group, state):
            for i in range(8):
                t = group * 8 + i
                decay = jnp.exp2(masked_ref[pl.ds(t, 1), part] * rate)
                state = decay * state + drive_ref[pl.ds(t, 1), part] * widen(in_lanes[t], chunk)
            return state

        pair_ref[0:states, part] = lax.fori_loop(0, tokens // 8, eight, jnp.zeros((states, chunk), F32))


def slot_tables(slots, cap, experts):
    slot = iota((slots, 8), 0)
    first = sum((slot >= cap * e).astype(jnp.int32) for e in range(1, experts))
    block = (first == iota((slots, 8), 1)).astype(F32)
    slot = iota((slots, 128), 0)
    first = sum(((slot >= cap * e).astype(jnp.int32) for e in range(1, experts)))
    within = (slot - first * cap == iota((slots, 128), 1)).astype(F32)
    return block, within


def scan_kernel(
    rank_n,
    states,
    experts,
    cap,
    me_ref,
    masked_ref,
    drive_ref,
    act_ref,
    gate_z_ref,
    start_ref,
    rate_ref,
    skip_ref,
    proj_ref,
    out_proj_ref,
    x_ref,
    gain_ref,
    router_ref,
    ids_ref,
    rank_ref,
    table_ref,
    scan_ref,
    history_ref,
    resid_ref,
    sent_ref,
    probs_ref,
    gate_ref,
    in_lanes,
    out_lanes,
    total,
):
    tokens, chunk = masked_ref.shape
    step = pl.program_id(0)

    @pl.when(step == 0)
    def _():
        over_lanes(in_lanes, proj_ref[rank_n : rank_n + states, :])
        over_lanes(out_lanes, proj_ref[rank_n + states : rank_n + 2 * states, :])
        total[...] = x_ref[...]

    rate = rate_ref[...]

    def eight(group, state):
        for i in range(8):
            t = group * 8 + i
            decay = jnp.exp2(masked_ref[pl.ds(t, 1), :] * rate)
            state = decay * state + drive_ref[pl.ds(t, 1), :] * widen(in_lanes[t], chunk)
            history_ref[t] = state
            scan_ref[pl.ds(t, 1), :] = jnp.sum(state * widen(out_lanes[t], chunk), axis=0, keepdims=True)
        return state

    lax.fori_loop(0, tokens // 8, eight, start_ref[...])
    gate_z = gate_z_ref[HALO:, :]
    mixed = (scan_ref[...] + skip_ref[...] * act_ref[...]) * (gate_z * sigmoid(gate_z))
    total[...] += product(split(mixed), split(out_proj_ref[...]), NN)

    @pl.when(step == pl.num_programs(0) - 1)
    def _():
        resid = total[...]
        resid_ref[...] = resid
        normed = resid * scale_of(resid) * gain_ref[...]
        logits = product(split(normed), split(router_ref[...]), NT)
        known = iota((tokens, 8), 1) < experts
        logits = jnp.where(known, logits, -1e30)
        raised = jnp.exp(logits - jnp.max(logits, axis=1, keepdims=True))
        raised = jnp.where(known, raised, 0.0)
        probs = raised / jnp.sum(raised, axis=1, keepdims=True)
        probs_ref[...] = probs
        ids = ids_ref[...]
        gate = jnp.sum(jnp.where(ids == iota((tokens, 8), 1), probs, 0.0), axis=1, keepdims=True)
        gate_ref[...] = gate
        slots = experts * cap
        sent_ref[0:slots, :] = pick(table_ref[...], normed, NN)
        sent_ref[slots:, :] = jnp.zeros((8, sent_ref.shape[1]), F32)
        rank = rank_ref[...].astype(jnp.int32)
        to_block = jnp.where(((ids ^ me_ref[0]) == iota((tokens, 8), 1)) & (rank < cap), gate, 0.0)
        at_rank = (rank == iota((tokens, 128), 1)).astype(BF16)
        high, low = split(to_block)
        rest = (to_block - high.astype(F32) - low.astype(F32)).astype(BF16)
        rows = dot(high, at_rank, TN) + (dot(low, at_rank, TN) + dot(rest, at_rank, TN))
        sent_ref[slots:, 0:128] = rows


def early_kernel(pieces, slices, *refs):
    grads, downs, outs = refs[:pieces], refs[pieces : pieces + slices], refs[pieces + slices :]
    downs = [split(d[...]) for d in downs]
    for p in range(pieces):
        grad = split(grads[p][...])
        for i in range(slices):
            outs[p][i] = product(grad, downs[i], NT)


def gelu_parts(value):
    inner = 0.7978845608 * (value + 0.044715 * value * value * value)
    tanh = jnp.tanh(inner)
    slope = 0.5 * (1.0 + tanh) + 0.5 * value * (1.0 - tanh * tanh) * 0.7978845608 * (
        1.0 + 3.0 * 0.044715 * value * value
    )
    return 0.5 * value * (1.0 + tanh), slope


def expert_kernel(slices, experts, cap, *refs):
    tokens_ref, ups, pulled_ref = refs[0], refs[1 : slices + 1], refs[slices + 1]
    back_ref, hidden_ref, grad_ref = refs[slices + 2 :]
    slots = experts * cap
    block, within = slot_tables(slots, cap, experts)
    within = within.astype(BF16)
    rows = split(tokens_ref[0:slots, :])
    back = jnp.zeros((slots, tokens_ref.shape[1]), F32)
    to_gate = jnp.zeros((slots, 1), F32)
    for i in range(slices):
        up = split(ups[i][...])
        hidden, slope = gelu_parts(product(rows, up, NN))
        pull = pulled_ref[i]
        grad = pull * slope
        hidden_ref[i] = hidden
        grad_ref[i] = grad
        to_gate += jnp.sum(hidden * pull, axis=1, keepdims=True)
        back += product(split(grad), up, NT)
    back_ref[0:slots, :] = back
    back_ref[slots:, :] = jnp.zeros((8, tokens_ref.shape[1]), F32)
    high, low = split(block * to_gate)
    rest = (block * to_gate - high.astype(F32) - low.astype(F32)).astype(BF16)
    back_ref[slots:, 0:128] = dot(high, within, TN) + (dot(low, within, TN) + dot(rest, within, TN))


def expert_grads_kernel(pieces, slices, experts, cap, *refs):
    tokens, grads, hiddens, pulls = (refs[i * pieces : (i + 1) * pieces] for i in range(4))
    downs, outs = refs[4 * pieces : 4 * pieces + slices], refs[4 * pieces + slices :]
    results, up_outs, down_outs = outs[:pieces], outs[pieces : pieces + slices], outs[pieces + slices :]
    slots = experts * cap
    downs = [split(d[...]) for d in downs]
    block, within = slot_tables(slots, cap, experts)
    within = within.astype(BF16)
    for p in range(pieces):
        ends = tokens[p][slots:, 0:128]
        high, low = split(ends)
        rest = (ends - high.astype(F32) - low.astype(F32)).astype(BF16)
        spread = dot(within, high, NT) + (dot(within, low, NT) + dot(within, rest, NT))
        gate = jnp.sum(spread * block, axis=1, keepdims=True)
        rows = split(tokens[p][0:slots, :] * gate)
        gated = split(grads[p][...] * gate)
        total = None
        for i in range(slices):
            hidden = split(hiddens[p][i])
            part = product(hidden, downs[i], NN)
            total = part if total is None else total + part
            up = product(rows, split(pulls[p][i]), TN)
            down = product(hidden, gated, TN)
            if p == 0:
                up_outs[i][...] = up
                down_outs[i][...] = down
            else:
                up_outs[i][...] += up
                down_outs[i][...] += down
        results[p][...] = total


def silu_parts(value):
    sig = sigmoid(value)
    return value * sig, sig * (1.0 + value * (1.0 - sig))


def mixer_back_kernel(
    rank_n,
    states,
    experts,
    cap,
    me_ref,
    back_ref,
    table_ref,
    gate_ref,
    probs_ref,
    ids_ref,
    rank_ref,
    resid_ref,
    grad_ref,
    gain_ref,
    router_ref,
    out_proj_ref,
    gate_z_ref,
    scan_ref,
    act_ref,
    skip_ref,
    masked_ref,
    rate_ref,
    proj_ref,
    steps_row_ref,
    grad_resid_ref,
    small_ref,
    grad_scan_ref,
    grad_gate_ref,
    grad_skip_ref,
    pair_ref,
    out_lanes,
    high,
    low,
):
    tokens, chunk = masked_ref.shape

    @pl.when(pl.program_id(0) == 0)
    def _():
        over_lanes(out_lanes, proj_ref[rank_n + states : rank_n + 2 * states, :])
        slots = experts * cap
        ids, rank = ids_ref[...], rank_ref[...].astype(jnp.int32)
        back = pick(table_ref[...], back_ref[0:slots, :], TN)
        at_rank = (rank == iota((tokens, 128), 1)).astype(BF16)
        ends = back_ref[slots:, 0:128]
        first, second = split(ends)
        third = (ends - first.astype(F32) - second.astype(F32)).astype(BF16)
        spread = dot(at_rank, first, NT) + (dot(at_rank, second, NT) + dot(at_rank, third, NT))
        mine = ((ids ^ me_ref[0]) == iota((tokens, 8), 1)) & (rank < cap)
        grad_gate = jnp.sum(jnp.where(mine, spread, 0.0), axis=1, keepdims=True)
        probs = probs_ref[...]
        grad_probs = jnp.where(ids == iota((tokens, 8), 1), grad_gate, 0.0)
        grad_logits = probs * (grad_probs - jnp.sum(probs * grad_probs, axis=1, keepdims=True))
        resid, gain = resid_ref[...], gain_ref[...]
        scale = scale_of(resid)
        normed = resid * scale * gain
        logits_two = split(grad_logits)
        grad_normed = gate_ref[...] * back + product(logits_two, split(router_ref[...]), NN)
        small_ref[...] = jnp.zeros_like(small_ref)
        small_ref[0:8, :] = product(logits_two, split(normed), TN)
        small_ref[8:9, :] = jnp.sum(grad_normed * resid * scale, axis=0, keepdims=True)
        pulled = gain * grad_normed
        grad_resid = (
            grad_ref[...]
            + scale * pulled
            - resid * (scale * scale * scale) * jnp.mean(pulled * resid, axis=1, keepdims=True)
        )
        grad_resid_ref[...] = grad_resid
        high[...], low[...] = split(grad_resid)

    grad_mixed = product((high[...], low[...]), split(out_proj_ref[...]), NT)
    silu, slope = silu_parts(gate_z_ref[HALO:, :])
    act = act_ref[...]
    grad_scan = grad_mixed * silu
    grad_scan_ref[...] = grad_scan
    grad_gate_ref[...] = grad_mixed * (scan_ref[...] + skip_ref[...] * act) * slope
    grad_skip_ref[...] = jnp.sum(grad_scan * act, axis=0, keepdims=True)
    rate = rate_ref[...]

    def eight(group, state):
        for i in range(8):
            t = tokens - 1 - (group * 8 + i)
            decay = jnp.exp2(masked_ref[pl.ds(t, 1), :] * rate)
            state = decay * (state + grad_scan_ref[pl.ds(t, 1), :] * widen(out_lanes[t], chunk))
        return state

    pair_ref[0:states, :] = lax.fori_loop(0, tokens // 8, eight, jnp.zeros((states, chunk), F32))
    pair_ref[states : states + 1, :] = steps_row_ref[...]


def late_kernel(
    which_ref, scan_ref, act_ref, skip_ref, gate_z_ref, grad_resid_ref, x_ref, gain_ref, grad_gate_ref, *refs
):
    high, low = refs[-2:]
    if len(refs) == 5:
        weight_ref, out_ref, normed_ref = refs[:3]
    else:
        weight_ref, out_ref, normed_ref = None, refs[0], None

    @pl.when(pl.program_id(0) == 0)
    def _():
        @pl.when(which_ref[0] == 0)
        def _():
            high[...], low[...] = split(grad_resid_ref[...])

        @pl.when(which_ref[0] == 1)
        def _():
            x = x_ref[...]
            high[...], low[...] = split(x * scale_of(x) * gain_ref[...])

        if normed_ref is not None:
            normed_ref[...] = jnp.zeros_like(normed_ref)

    @pl.when(which_ref[0] == 0)
    def _():
        gate_z = gate_z_ref[HALO:, :]
        mixed = (scan_ref[...] + skip_ref[...] * act_ref[...]) * (gate_z * sigmoid(gate_z))
        out_ref[...] = product(split(mixed), (high[...], low[...]), TN)

    @pl.when(which_ref[0] == 1)
    def _():
        out_ref[...] = product((high[...], low[...]), split(grad_gate_ref[...]), TN)

    if normed_ref is not None:
        normed_ref[...] += product(split(grad_gate_ref[...]), split(weight_ref[...]), NT)


def scan_back_kernel(
    rank_n,
    states,
    masked_ref,
    steps_ref,
    drive_ref,
    act_ref,
    pre_ref,
    grad_scan_ref,
    skip_ref,
    history_ref,
    start_ref,
    end_ref,
    rate_ref,
    proj_ref,
    step_proj_ref,
    *refs,
):
    grad_act_ref, grad_pre_ref, grad_decay_ref, grad_proj_ref, in_lanes, out_lanes, grad_drive, grad_steps = refs[-8:]
    tokens, chunk = masked_ref.shape
    over_lanes(in_lanes, proj_ref[rank_n : rank_n + states, :])
    over_lanes(out_lanes, proj_ref[rank_n + states : rank_n + 2 * states, :])

    rate = rate_ref[...]
    lane = iota((states, tokens), 1)

    def one(t, before, carried):
        state, decays, grad_in, grad_out = carried
        masked = masked_ref[pl.ds(t, 1), :]
        grad = grad_scan_ref[pl.ds(t, 1), :]
        decay = jnp.exp2(masked * rate)
        state = state + grad * widen(out_lanes[t], chunk)
        at_out = jnp.sum(history_ref[t] * grad, axis=1, keepdims=True)
        at_in = jnp.sum(state * drive_ref[pl.ds(t, 1), :], axis=1, keepdims=True)
        grad_out = jnp.where(lane == t, at_out, grad_out)
        grad_in = jnp.where(lane == t, at_in, grad_in)
        grad_drive[pl.ds(t, 1), :] = jnp.sum(state * widen(in_lanes[t], chunk), axis=0, keepdims=True)
        state = decay * state
        pulled = state * before
        grad_steps[pl.ds(t, 1), :] = jnp.sum(pulled * rate, axis=0, keepdims=True)
        return state, decays + pulled * masked, grad_in, grad_out

    def four(group, carried):
        for i in range(4):
            t = tokens - 1 - (group * 4 + i)
            carried = one(t, history_ref[t - 1], carried)
        return carried

    nothing = jnp.zeros((states, tokens), F32)
    carried = lax.fori_loop(
        0, tokens // 4 - 1, four, (end_ref[...], jnp.zeros((states, chunk), F32), nothing, nothing)
    )
    for t in (3, 2, 1):
        carried = one(t, history_ref[t - 1], carried)
    _, decays, grad_in, grad_out = one(0, start_ref[...], carried)
    grad_decay_ref[...] = decays * (rate * (1.0 / LOG2E))
    steps, act = steps_ref[...], act_ref[...]
    grad_act_ref[...] = skip_ref[...] * grad_scan_ref[...] + grad_drive[...] * steps
    grad_pre = (grad_steps[...] * (1.0 / LOG2E) + grad_drive[...] * act) * sigmoid(pre_ref[...])
    grad_pre_ref[...] = grad_pre
    grad_proj_ref[0:rank_n, :] = product(split(step_proj_ref[...]), split(grad_pre), NT)
    grad_proj_ref[rank_n : rank_n + states, :] = grad_in
    grad_proj_ref[rank_n + states : rank_n + 2 * states, :] = grad_out


def input_back_kernel(
    rank_n,
    states,
    core_ref,
    proj_a_ref,
    proj_b_ref,
    proj_c_ref,
    proj_ref,
    state_proj_ref,
    act_ref,
    grad_act_ref,
    grad_pre_ref,
    conv_ref,
    inner_ref,
    conv_w_ref,
    since_ref,
    weight_ref,
    x_ref,
    halo_ref,
    gain_ref,
    grad_gate_normed_ref,
    grad_resid_ref,
    grad_decay_ref,
    grad_skip_ref,
    small_ref,
    keep_ref,
    send_ref,
    input_ref,
    edge_ref,
    high,
    low,
    grad_inner,
    total,
):
    tokens, chunk = act_ref.shape
    depth = x_ref.shape[1]
    half = depth // 2
    taps = conv_w_ref.shape[0]
    step = pl.program_id(0)

    @pl.when(step == 0)
    def _():
        x = jnp.concatenate([halo_ref[...], x_ref[...]], axis=0)
        high[...], low[...] = split(x * scale_of(x) * gain_ref[...])
        total[...] = jnp.zeros_like(total)

    act, grad_pre = split(act_ref[...]), grad_pre_ref[...]
    grad_proj = split(proj_a_ref[...] + proj_b_ref[...] + proj_c_ref[...])
    grad_act = grad_act_ref[...] + product(grad_proj, split(state_proj_ref[...]), TN)
    _, slope = silu_parts(conv_ref[...])
    grad_conv = grad_act * slope
    since = since_ref[...]
    grad_inner[...] = jnp.zeros_like(grad_inner)
    rows = []
    for k in range(taps):
        valid = (since >= taps - 1 - k).astype(F32)
        first = HALO - taps + 1 + k
        held = grad_conv * valid
        rows.append(jnp.sum(held * inner_ref[first : first + tokens, :], axis=0, keepdims=True))
        grad_inner[first : first + tokens, :] += held * conv_w_ref[k : k + 1, :]
    rows.append(jnp.sum(grad_conv, axis=0, keepdims=True))
    rows.append(jnp.sum(grad_pre, axis=0, keepdims=True))
    rows.append(grad_skip_ref[...])
    grads = split(grad_inner[...])
    total[...] += product(grads, split(weight_ref[...]), NT)
    of_state_proj = product(grad_proj, act, NN)
    of_step_proj = product(split(proj_ref[0:rank_n, :]), split(grad_pre), NN)

    def first_half(out_ref):
        out_ref[0:half, :] = product((high[:, 0:half], low[:, 0:half]), grads, TN)
        at = half + 2 * states + rank_n
        out_ref[half:at, :] = of_state_proj
        out_ref[at : at + states, :] = grad_decay_ref[...]
        if at + states < out_ref.shape[0]:
            out_ref[at + states :, :] = jnp.zeros((out_ref.shape[0] - at - states, chunk), F32)

    def second_half(out_ref):
        out_ref[0:half, :] = product((high[:, half:], low[:, half:]), grads, TN)
        out_ref[half : half + rank_n, :] = of_step_proj
        at = half + rank_n
        out_ref[at:, :] = jnp.zeros((out_ref.shape[0] - at, chunk), F32)
        for i, row in enumerate(rows):
            out_ref[at + i : at + i + 1, :] = row

    @pl.when(core_ref[0] == 0)
    def _():
        first_half(keep_ref)
        second_half(send_ref)

    @pl.when(core_ref[0] == 1)
    def _():
        second_half(keep_ref)
        first_half(send_ref)

    @pl.when(step == pl.num_programs(0) - 1)
    def _():
        gain = gain_ref[...]

        def rows_back(x, grad):
            scale = scale_of(x)
            pulled = gain * grad
            back = scale * pulled - x * (scale * scale * scale) * jnp.mean(pulled * x, axis=1, keepdims=True)
            return back, jnp.sum(grad * x * scale, axis=0, keepdims=True)

        edge, edge_gain = rows_back(halo_ref[...], total[0:HALO, :])
        own, own_gain = rows_back(x_ref[...], total[HALO:, :] + grad_gate_normed_ref[...])
        edge_ref[...] = edge
        input_ref[...] = grad_resid_ref[...] + own
        small = jnp.concatenate([small_ref[0:10, :], edge_gain + own_gain], axis=0)

        def place_small(out_ref):
            at = half + rank_n + 8
            out_ref[at : at + 11, :] = small[:, 0:chunk]
            out_ref[at + 16 : at + 27, 0 : depth - chunk] = small[:, chunk:]

        @pl.when(core_ref[0] == 0)
        def _():
            place_small(send_ref)

        @pl.when(core_ref[0] == 1)
        def _():
            place_small(keep_ref)


def finish_late_kernel(core_ref, first_ref, second_ref, got_first_ref, got_second_ref, in_ref, out_ref):
    depth = out_ref.shape[2]
    step = pl.program_id(0)

    def write(gate, out):
        in_ref[...] = gate
        out_ref[0] = out[:, 0:depth]
        out_ref[1] = out[:, depth:]

    for i, (own, got) in enumerate(((first_ref, got_first_ref), (second_ref, got_second_ref))):

        @pl.when((core_ref[0] == 0) & (step == i))
        def _():
            write(own[...], got[...])

        @pl.when((core_ref[0] == 1) & (step == i))
        def _():
            write(got[...], own[...])


def finish_kernel(
    rank_n, states, taps, core_ref, first_ref, second_ref, got_first_ref, got_second_ref, _,
    in_ref, state_proj_ref, step_proj_ref, decay_ref, conv_w_ref, rows_ref, small_ref,
):
    depth = in_ref.shape[0]
    half, quarter = depth // 2, first_ref.shape[0]
    rest = half - quarter

    def first_half(one, two):
        in_ref[0:quarter, :] = one[...]
        in_ref[quarter:half, :] = two[0:rest, :]
        at = rest + 2 * states + rank_n
        state_proj_ref[...] = two[rest:at, :].T
        decay_ref[...] = two[at : at + states, :].T

    def second_half(one, two):
        in_ref[half : half + quarter, :] = one[...]
        in_ref[half + quarter :, :] = two[0:rest, :]
        step_proj_ref[...] = two[rest : rest + rank_n, :]
        at = rest + rank_n
        conv_w_ref[...] = two[at : at + taps, :]
        rows_ref[...] = two[at : at + 8, :]
        small_ref[...] = two[at + 8 : at + 40, :]

    @pl.when(core_ref[0] == 0)
    def _():
        first_half(first_ref, second_ref)
        second_half(got_first_ref, got_second_ref)

    @pl.when(core_ref[0] == 1)
    def _():
        first_half(got_first_ref, got_second_ref)
        second_half(first_ref, second_ref)


def per_device(
    block_input,
    seq_lengths,
    expert_ids,
    output_grad,
    mixer_gain,
    in_proj,
    conv_weight,
    conv_bias,
    state_proj,
    step_proj,
    step_bias,
    decay_log,
    skip_gain,
    out_proj,
    router_gain,
    router,
    expert_up,
    expert_down,
):
    grid = Grid()
    tokens, depth = block_input.shape
    taps, width = conv_weight.shape
    rank_n, states, experts = step_proj.shape[0], decay_log.shape[1], router.shape[1]
    cap = (5 * tokens + 4 * experts - 1) // (4 * experts)
    slots, hidden = experts * cap, expert_up.shape[2]
    chunk = 512
    chunks = width // chunk
    pieces, slices = grid.size["outer"], grid.size["inner"]
    me = lax.axis_index("exp").astype(jnp.int32).reshape(1)
    ext = HALO + tokens

    halo = grid.along(block_input[tokens - HALO :], 1)

    count = seq_lengths.shape[0]
    earlier = jnp.arange(count)[:, None] > jnp.arange(count)[None, :]
    starts = jnp.sum(jnp.where(earlier, seq_lengths[None, :], 0), axis=1)
    position = grid.index * tokens + jnp.arange(tokens, dtype=jnp.int32)
    own_start = jnp.max(jnp.where(starts[None, :] <= position[:, None], starts[None, :], 0), axis=1)
    since = (position - own_start)[:, None]
    rate = -jnp.exp(decay_log.T) * LOG2E
    state_proj_t = state_proj.T
    router_t = pad_rows(router.T, 8)
    row = lambda vector: vector.reshape(1, -1)

    sent_grads, table, rank, loads = call(
        functools.partial(route_kernel, experts, cap),
        [shape(slots, depth), shape(slots, tokens, dtype=BF16), shape(tokens, 1), shape(8, depth)],
        (me, expert_ids, output_grad),
        in_specs=[SMEM] + [pl.BlockSpec(memory_space=pltpu.VMEM)] * 2,
        name="route",
    )
    halo, sent_grads = tie(halo, sent_grads)
    held_grads, _ = send_y(grid, sent_grads, cap, False)
    up, down = expert_up[0], expert_down[0]
    ups = [up] + [grid.swap(up, "inner", s) for s in range(1, slices)]
    downs = [down] + [grid.swap(down, "inner", s) for s in range(1, slices)]

    block = lambda c: (0, c)
    joined = call(
        join_kernel,
        shape(ext, 2 * width),
        (block_input, halo, row(mixer_gain), in_proj),
        grid=(2 * chunks,),
        in_specs=[full(tokens, depth), full(HALO, depth), full(1, depth), pl.BlockSpec((depth, chunk), block)],
        out_specs=pl.BlockSpec((ext, chunk), block),
        scratch=[pltpu.VMEM((ext, depth), BF16)] * 2,
        name="join",
    )
    joined, *held_grads = tie(joined, *held_grads)
    conv, act, pre, steps, masked, drive, proj, pair = call(
        functools.partial(features_kernel, rank_n, states),
        [shape(tokens, width)] * 6 + [shape(rank_n + 2 * states, tokens), shape(states + 1, width)],
        (joined, since, conv_weight, row(conv_bias), state_proj_t, step_proj, row(step_bias), rate),
        grid=(1,),
        in_specs=[
            full(ext, width),
            full(tokens, 1),
            full(taps, width),
            full(1, width),
            full(rank_n + 2 * states, width),
            full(rank_n, width),
            full(1, width),
            full(states, width),
        ],
        out_specs=[full(tokens, width)] * 6 + [full(rank_n + 2 * states, tokens), full(states + 1, width)],
        scratch=[pltpu.VMEM((tokens, states, 128), F32)],
        name="features",
    )
    own_grads = send_core(grid, held_grads, None, cap, False)
    pair, own_grads, *downs = tie(pair, own_grads, *downs)
    near_grads, far_grads = grid.swap(own_grads, "outer", 1), grid.swap(own_grads, "outer", 2)
    held = {}

    def third(total):
        total, held["near"], held["far"] = tie(total, near_grads, far_grads)
        return total

    start = entering(grid, pair, rate, False, {3: third})
    near_grads = held["near"]
    start, far_grads = tie(start, held["far"])
    last_grads = grid.swap(far_grads, "outer", 1)
    tok = pl.BlockSpec((tokens, chunk), block)
    gate_half = pl.BlockSpec((ext, chunk), lambda c: (0, chunks + c))
    one_row = pl.BlockSpec((1, chunk), block)
    state_rows = pl.BlockSpec((states, chunk), block)
    history_block = pl.BlockSpec((tokens, states, chunk), lambda c: (0, 0, c))
    out_rows = pl.BlockSpec((chunk, depth), lambda c: (c, 0))
    proj_full = full(rank_n + 2 * states, tokens)
    lanes = pltpu.VMEM((tokens, states, 128), F32)
    scan, history, resid, sent, probs, gate = call(
        functools.partial(scan_kernel, rank_n, states, experts, cap),
        [
            shape(tokens, width),
            shape(tokens, states, width),
            shape(tokens, depth),
            shape(slots + 8, depth),
            shape(tokens, 8),
            shape(tokens, 1),
        ],
        (
            me, masked, drive, act, joined, start, rate, row(skip_gain), proj, out_proj, block_input,
            row(router_gain), router_t, expert_ids, rank, table,
        ),
        grid=(chunks,),
        in_specs=[
            SMEM, tok, tok, tok, gate_half, state_rows, state_rows, one_row, proj_full, out_rows,
            full(tokens, depth), full(1, depth), full(8, depth), full(tokens, 1), full(tokens, 1),
            full(slots, tokens),
        ],
        out_specs=[
            tok, history_block, full(tokens, depth), full(slots + 8, depth), full(tokens, 8), full(tokens, 1),
        ],
        scratch=[lanes, lanes, pltpu.VMEM((tokens, depth), F32)],
        name="scan",
    )

    sent, last_grads = tie(sent, last_grads)
    grad_pieces = [own_grads, near_grads, far_grads, last_grads]
    pulled = call(
        functools.partial(early_kernel, pieces, slices),
        [shape(slices, slots, hidden)] * pieces,
        (*grad_pieces, *downs),
        name="early",
    )
    own_tokens = send_core(grid, *send_y(grid, sent, cap, True), cap, True)
    own_tokens, *pulled = tie(own_tokens, *pulled)
    near_tokens, far_tokens = grid.swap(own_tokens, "outer", 1), grid.swap(own_tokens, "outer", 2)

    def expert(rows, pulled_rows):
        return call(
            functools.partial(expert_kernel, slices, experts, cap),
            [shape(slots + 8, depth)] + [shape(slices, slots, hidden)] * 2,
            (rows, *ups, pulled_rows),
            name="expert",
        )

    own_outs = expert(own_tokens, pulled[0])
    near_tokens, far_tokens, *own_outs = tie(near_tokens, far_tokens, *own_outs)
    last_tokens = grid.swap(far_tokens, "outer", 1)
    near_outs, far_outs = expert(near_tokens, pulled[1]), expert(far_tokens, pulled[2])
    last_tokens, near_outs, far_outs = tie(last_tokens, near_outs, far_outs)
    last_outs = expert(last_tokens, pulled[3])
    token_pieces = [own_tokens, near_tokens, far_tokens, last_tokens]
    backs, hiddens, pulls = zip(own_outs, near_outs, far_outs, last_outs)
    back_through = grid.swap(backs[3], "outer", 1)
    outs = call(
        functools.partial(expert_grads_kernel, pieces, slices, experts, cap),
        [shape(slots, depth)] * pieces + [shape(depth, hidden)] * slices + [shape(hidden, depth)] * slices,
        (*token_pieces, *grad_pieces, *hiddens, *pulls, *downs),
        name="expert_grads",
    )
    back, *outs = tie(outer_reduce_rest(grid, backs, back_through), *outs)
    back = back_y(grid, back, back_core(grid, back, cap, True), cap, True)
    results, up_grads, down_grads = outs[:pieces], outs[pieces : pieces + slices], outs[pieces + slices :]
    halves = lambda array: [array[: array.shape[0] // 2], array[array.shape[0] // 2 :]]
    ups_sent, downs_sent = ([halves(g) for g in grads[1:]] for grads in (up_grads, down_grads))

    def inner_swaps(sent, half):
        return [grid.swap(pair[half], "inner", s) for s, pair in enumerate(sent, 1)]

    up_first = inner_swaps(ups_sent, 0)
    back, last_result, ups_sent, *up_first = tie(back, results[3], ups_sent, *up_first)
    through = grid.swap(last_result, "outer", 1)
    up_second = inner_swaps(ups_sent, 1)

    grad_resid, small, grad_scan, grad_gate, grad_skip, back_pair = call(
        functools.partial(mixer_back_kernel, rank_n, states, experts, cap),
        [
            shape(tokens, depth),
            shape(16, depth),
            shape(tokens, width),
            shape(tokens, width),
            shape(1, width),
            shape(states + 1, width),
        ],
        (
            me, back, table, gate, probs, expert_ids, rank, resid, output_grad, row(router_gain), router_t,
            out_proj, joined, scan, act, row(skip_gain), masked, rate, proj, pair[states:],
        ),
        grid=(chunks,),
        in_specs=[
            SMEM, full(slots + 8, depth), full(slots, tokens), full(tokens, 1), full(tokens, 8),
            full(tokens, 1), full(tokens, 1), full(tokens, depth), full(tokens, depth), full(1, depth),
            full(8, depth), out_rows, gate_half, tok, tok, one_row, tok, state_rows, proj_full, one_row,
        ],
        out_specs=[
            full(tokens, depth), full(16, depth), tok, tok, one_row,
            pl.BlockSpec((states + 1, chunk), block),
        ],
        scratch=[lanes] + [pltpu.VMEM((tokens, depth), BF16)] * 2,
        name="mixer_back",
    )
    back_pair, through, downs_sent, *up_second = tie(back_pair, through, downs_sent, *up_second)
    core = grid.at["core"].astype(jnp.int32).reshape(1)
    wide = pl.BlockSpec((tokens, depth), block)

    def late(which, weight):
        return call(
            late_kernel,
            [shape(depth, width)] + [shape(tokens, depth)] * len(weight),
            (
                which, scan, act, row(skip_gain), joined, grad_resid, block_input, row(mixer_gain), grad_gate,
                *weight,
            ),
            grid=(2,),
            in_specs=[
                SMEM, wide, wide, pl.BlockSpec((1, depth), block), pl.BlockSpec((ext, depth), lambda c: (0, 2 + c)),
                full(tokens, depth), full(tokens, depth), full(1, depth), wide,
            ]
            + [pl.BlockSpec((depth, depth), lambda c: (0, 2 + c))] * len(weight),
            out_specs=[pl.BlockSpec((depth, depth), block)] + [full(tokens, depth)] * len(weight),
            scratch=[pltpu.VMEM((tokens, depth), BF16)] * 2,
            name="late",
        )

    (late_sent,) = late(core, ())
    late_kept, grad_gate_normed = late(1 - core, (in_proj,))
    late_got = grid.swap(late_sent, "core", 1)
    near = grid.swap(results[1], "outer", 1)
    far = grid.swap(results[2] + through, "outer", 2)
    down_first = inner_swaps(downs_sent, 0)

    def second(total):
        total, held["second"], *held["down_first"] = tie(total, downs_sent, *down_first)
        held["down_second"] = inner_swaps(held["second"], 1)
        return total

    def third(total):
        total, held["late_got"], held["late_kept"], held["normed"], held["near"], held["far"] = tie(
            total, late_got, late_kept, grad_gate_normed, near, far
        )
        held["late"] = sum_first(grid, held["late_kept"] + held["late_got"])
        return total

    def fourth(total):
        total, *held["down_second"] = tie(total, *held["down_second"])
        return total

    end = entering(grid, back_pair, rate, True, {2: second, 3: third, 4: fourth})
    grad_gate_normed = held["normed"]
    late_first, late_second = held["late"]

    def with_others(own, firsts, seconds):
        for pair in zip(firsts, seconds):
            own = own + jnp.concatenate(pair, axis=0)
        return own

    grad_up = with_others(up_grads[0], up_first, up_second)
    grad_down = with_others(down_grads[0], held["down_first"], held["down_second"])
    result = results[0] + held["near"] + held["far"]
    result_got = back_core(grid, result, cap, False)

    def scan_back(c, before):
        at = lambda _: (0, c)
        tok, one_row = pl.BlockSpec((tokens, chunk), at), pl.BlockSpec((1, chunk), at)
        state_rows = pl.BlockSpec((states, chunk), at)
        return call(
            functools.partial(scan_back_kernel, rank_n, states),
            [
                shape(tokens, width), shape(tokens, width), shape(states, width),
                shape(rank_n + 2 * states, tokens),
            ],
            (
                masked, steps, drive, act, pre, grad_scan, row(skip_gain), history, start, end, rate, proj,
                step_proj, *before,
            ),
            grid=(1,),
            in_specs=[
                tok, tok, tok, tok, tok, tok, one_row,
                pl.BlockSpec((tokens, states, chunk), lambda _: (0, 0, c)), state_rows, state_rows, state_rows,
                proj_full, pl.BlockSpec((rank_n, chunk), at),
            ]
            + [pl.BlockSpec(memory_space=pl.ANY)] * len(before),
            out_specs=[tok, tok, state_rows, proj_full],
            scratch=[lanes, lanes] + [pltpu.VMEM((tokens, chunk), F32)] * 2,
            name="scan_back",
            aliases={13 + i: i for i in range(len(before))},
        )

    *filled, grad_proj_a = scan_back(0, ())
    *filled, late_first, late_second, result_got = tie(*filled, late_first, late_second, result_got)
    late_both = sum_second(grid, late_first, late_second)
    result = back_y(grid, result, result_got, cap, False)
    *filled, grad_proj_b = scan_back(1, filled)
    *filled, late_both = tie(*filled, late_both)
    late_cut = cut_outer(grid, late_both)
    late_through = grid.swap(late_cut[3], "outer", 1)
    grad_act, grad_pre, grad_decay, grad_proj_c = scan_back(2, filled)
    grad_act, late_through, result = tie(grad_act, late_through, result)
    late_total = outer_reduce_rest(grid, late_cut, late_through)
    unit = 2 * grid.size["inner"] * grid.size["y"]
    half = -(-max(depth // 2 + 3 * states + rank_n, depth // 2 + rank_n + 40) // unit) * unit
    small = jnp.concatenate([small[:9], loads[0:1]], axis=0)
    kept, sent_half, input_grad, edge = call(
        functools.partial(input_back_kernel, rank_n, states),
        [shape(half, width), shape(half, width), shape(tokens, depth), shape(HALO, depth)],
        (
            core, grad_proj_a, grad_proj_b, grad_proj_c, proj, state_proj_t, act, grad_act, grad_pre, conv, joined,
            conv_weight, since, in_proj, block_input, halo, row(mixer_gain), grad_gate_normed, grad_resid,
            grad_decay, grad_skip, small,
        ),
        grid=(chunks,),
        in_specs=[
            SMEM, proj_full, proj_full, proj_full, proj_full, pl.BlockSpec((rank_n + 2 * states, chunk), block),
            tok, tok, tok, tok, pl.BlockSpec((ext, chunk), block), pl.BlockSpec((taps, chunk), block),
            full(tokens, 1), pl.BlockSpec((depth, chunk), block), full(tokens, depth), full(HALO, depth),
            full(1, depth), full(tokens, depth), full(tokens, depth), state_rows, one_row, full(10, depth),
        ],
        out_specs=[
            pl.BlockSpec((half, chunk), block), pl.BlockSpec((half, chunk), block), full(tokens, depth),
            full(HALO, depth),
        ],
        scratch=[pltpu.VMEM((ext, depth), BF16)] * 2
        + [pltpu.VMEM((ext, chunk), F32), pltpu.VMEM((ext, depth), F32)],
        name="input_back",
    )
    kept, sent_half, late_total = tie(kept, sent_half, late_total)
    late_near, late_far = grid.swap(late_total, "outer", 1), grid.swap(late_total, "outer", 2)
    from_next = grid.along(edge, -1)
    input_grad = jnp.concatenate([input_grad[: tokens - HALO], input_grad[tokens - HALO :] + from_next], axis=0)
    combined = jnp.dot(table.T, result.astype(F32), precision=lax.Precision.HIGHEST, preferred_element_type=F32)
    block_output = resid + gate * combined
    grads_first, grads_second = sum_first(grid, kept + grid.swap(sent_half, "core", 1))
    late_near, late_far, grads_first, grads_second, input_grad, block_output, grad_up, grad_down = tie(
        late_near, late_far, grads_first, grads_second, input_grad, block_output, grad_up, grad_down
    )
    late_last = grid.swap(late_far, "outer", 1)
    grads = sum_second(grid, grads_first, grads_second)
    late_last, grads = tie(late_last, grads)
    late_first, late_second = spread_second(grid, join_outer(grid, late_total, late_near, late_far, late_last))
    grads = sum_outer(grid, grads)
    late_first, late_second, grads = tie(late_first, late_second, grads)
    late_first, late_second = gather_rows(grid, late_first, "inner"), gather_rows(grid, late_second, "y")
    grads = spread_outer(grid, grads)
    late_first, late_second, grads = tie(late_first, late_second, grads)
    late_other = [grid.swap(late_first, "core", 1), grid.swap(late_second, "core", 1)]
    grads_first, grads_second = spread_second(grid, grads)
    grads_first, grads_second, *late_other = tie(grads_first, grads_second, *late_other)
    grads_first, grads_second = gather_rows(grid, grads_first, "inner"), gather_rows(grid, grads_second, "y")
    quarter = pl.BlockSpec((half // 2, chunk), block)
    late_rows = full(depth // 2, width)
    grad_in_proj, grad_out_proj = call(
        finish_late_kernel,
        [shape(depth, 2 * width), shape(2, depth, depth)],
        (core, late_first, late_second, *late_other),
        grid=(2,),
        in_specs=[SMEM] + [late_rows] * 4,
        out_specs=[
            pl.BlockSpec((depth // 2, width), lambda r: (r, 1)),
            pl.BlockSpec((2, depth // 2, depth), lambda r: (0, r, 0)),
        ],
        name="finish_late",
    )
    grads_first, grads_second, grad_in_proj = tie(grads_first, grads_second, grad_in_proj)
    grads_other = [grid.swap(grads_first, "core", 1), grid.swap(grads_second, "core", 1)]
    tall = lambda columns: pl.BlockSpec((chunk, columns), lambda c: (c, 0))
    (
        grad_in_proj, grad_state_proj, grad_step_proj, grad_decay_log, grad_conv_weight, rows, small,
    ) = call(
        functools.partial(finish_kernel, rank_n, states, taps),
        [
            shape(depth, 2 * width), shape(width, rank_n + 2 * states), shape(rank_n, width),
            shape(width, states), shape(taps, width), shape(8, width), shape(32, chunk),
        ],
        (core, grads_first, grads_second, *grads_other, grad_in_proj),
        grid=(chunks,),
        in_specs=[SMEM] + [quarter] * 4 + [pl.BlockSpec(memory_space=pl.ANY)],
        out_specs=[
            pl.BlockSpec((depth, chunk), block), tall(rank_n + 2 * states), pl.BlockSpec((rank_n, chunk), block),
            tall(states), pl.BlockSpec((taps, chunk), block), pl.BlockSpec((8, chunk), block), full(32, chunk),
        ],
        name="finish",
        aliases={5: 0},
    )
    small = jnp.concatenate([small[:16], small[16:, : depth - chunk]], axis=1)
    return (
        block_output,
        input_grad,
        small[10],
        grad_in_proj,
        grad_conv_weight,
        rows[taps],
        grad_state_proj,
        grad_step_proj,
        rows[taps + 1],
        grad_decay_log,
        rows[taps + 2],
        grad_out_proj.reshape(width, depth),
        small[8],
        small[:experts].T,
        grad_up[None],
        grad_down[None],
        small[9, :experts].astype(jnp.int32),
        small[9, 128 : 128 + experts].astype(jnp.int32),
    )


def solution(mesh):
    rows, copied = P(("seq", "exp"), None), P()
    up, down = P("exp", None, "seq"), P("exp", "seq", None)
    in_specs = (rows, copied, rows, rows) + (copied,) * 12 + (up, down)
    out_specs = (rows, rows) + (copied,) * 12 + (up, down, copied, copied)
    return jax.shard_map(per_device, mesh=mesh, in_specs=in_specs, out_specs=out_specs, check_vma=False)
```

```python
import functools

import jax
import jax.numpy as jnp
from jax import lax
from jax.experimental import pallas as pl
from jax.experimental.pallas import tpu as pltpu
from jax.sharding import PartitionSpec as P

F32 = jnp.float32
BF16 = jnp.bfloat16
EPS = 1e-05
LOG2E = 1.4426950408889634
HALO = 16
RESET = 1e9
AXES = ("seq", "exp")
NN, NT, TN = ((1,), (0,)), ((1,), (1,)), ((0,), (0,))
VMEM_BYTES = 52 << 20
MICROSECONDS = {
    "route": 1, "join": 8, "features": 250, "join_states": 1, "scan": 14, "early": 7, "expert": 4.4,
    "expert_grads": 17, "mixer_back": 300, "late": 200, "scan_back": 10, "input_back": 11, "finish_late": 8, "finish": 6,
}


class Grid:
    def __init__(self):
        self.seq, self.exp = lax.axis_size("seq"), lax.axis_size("exp")
        self.outer = 4
        self.size = {
            "core": 2,
            "y": self.exp // 2,
            "inner": self.seq // self.outer,
            "outer": self.outer,
        }
        self.total = self.seq * self.exp
        index, step, self.step, self.at = lax.axis_index(AXES), 1, {}, {}
        for name in ("core", "y", "inner", "outer"):
            self.step[name] = step
            self.at[name] = (index // step) % self.size[name]
            step *= self.size[name]
        self.index = index

    def swap(self, block, name, mask):
        return self.swap_bits(block, mask * self.step[name])

    def swap_bits(self, block, bits):
        return lax.ppermute(block, AXES, [(i, i ^ bits) for i in range(self.total)])

    def along(self, block, distance):
        route = [(i - distance, i) for i in range(self.total) if 0 <= i - distance < self.total]
        return lax.ppermute(block, AXES, route)


def tie(*values):
    return lax.optimization_barrier(values)


def outer_reduce_rest(grid, parts, through):
    through, near = tie(through, parts[1])
    near = grid.swap(near, "outer", 1)
    far = grid.swap(parts[2] + through, "outer", 2)
    return parts[0] + near + far


def in_order(parts, place):
    bit = 1
    while bit < len(parts):
        turned = ((place // bit) % 2) == 1
        parts = [jnp.where(turned, parts[i ^ bit], parts[i]) for i in range(len(parts))]
        bit *= 2
    return parts


def rows_of(parts, first, rows):
    return functools.reduce(jnp.add, [lax.dynamic_slice_in_dim(part, first, rows, 0) for part in parts])


def scatter_rows(grid, parts, name, rows, start=0):
    count, place = grid.size[name], grid.at[name]
    rows = rows // count
    piece = lambda s: rows_of(parts, start + (place ^ s) * rows, rows)
    got = [grid.swap(piece(s), name, s) for s in range(1, count)]
    return [piece(0)] + got


def gather_rows(grid, block, name):
    count = grid.size[name]
    if count == 1:
        return block
    parts = [block] + [grid.swap(block, name, s) for s in range(1, count)]
    return jnp.concatenate(in_order(parts, grid.at[name]), axis=0)


def sum_first(grid, parts):
    rows = parts[0].shape[0] // 2
    return scatter_rows(grid, parts, "inner", rows), scatter_rows(grid, parts, "y", rows, rows)


def sum_second(grid, first, second):
    rows = first[0].shape[0]
    first, second = scatter_rows(grid, first, "y", rows), scatter_rows(grid, second, "inner", rows)
    return [jnp.concatenate(pair, axis=0) for pair in zip(first, second)]


def cut_outer(grid, parts):
    columns = parts[0].shape[1] // grid.outer
    return [
        functools.reduce(
            jnp.add,
            [lax.dynamic_slice_in_dim(p, (grid.at["outer"] ^ s) * columns, columns, 1) for p in parts],
        )
        for s in range(grid.outer)
    ]


def sum_outer(grid, parts):
    own, *others = cut_outer(grid, parts)
    return functools.reduce(jnp.add, [grid.swap(part, "outer", s) for s, part in enumerate(others, 1)], own)


def spread_outer(grid, total):
    count = grid.size["outer"]
    parts = [total] + [grid.swap(total, "outer", s) for s in range(1, count)]
    return jnp.concatenate(in_order(parts, grid.at["outer"]), axis=1)


def join_outer(grid, own, near, far, last):
    return jnp.concatenate(in_order([own, near, far, last], grid.at["outer"]), axis=1)


def spread_second(grid, both):
    own = both.shape[0] // 2
    return gather_rows(grid, both[:own], "y"), gather_rows(grid, both[own:], "inner")


def spread_first(grid, first, second):
    return jnp.concatenate([gather_rows(grid, first, "inner"), gather_rows(grid, second, "y")], axis=0)


def join_states_kernel(last, later_ref, total_ref, got_ref, ahead_ref, rate_ref, *outs):
    states = rate_ref.shape[0]
    rows, sums = slice(0, states), slice(states, states + 1)

    def follow(early, late, out):
        out[rows, :] = jnp.exp2(rate_ref[...] * late[sums, :]) * early[rows, :] + late[rows, :]
        out[sums, :] = early[sums, :] + late[sums, :]

    @pl.when(later_ref[0] == 1)
    def _():
        follow(got_ref, ahead_ref, outs[0])
        if not last:
            follow(got_ref, total_ref, outs[1])

    @pl.when(later_ref[0] == 0)
    def _():
        outs[0][...] = ahead_ref[...]
        if not last:
            follow(total_ref, got_ref, outs[1])


def entering(grid, pair, rate, backward, after):
    states = rate.shape[0]
    total, ahead, hop = pair, jnp.zeros_like(pair), 1
    bits = 1
    while bits < grid.total:
        got = grid.swap_bits(total, bits)
        later = ((grid.index // bits) % 2).astype(jnp.int32)
        later = (1 - later if backward else later).reshape(1)
        last = 2 * bits >= grid.total
        whole = pl.BlockSpec(memory_space=pltpu.VMEM)
        ahead, *rest = call(
            functools.partial(join_states_kernel, last),
            [shape(*pair.shape)] * (1 if last else 2),
            (later, total, got, ahead, rate),
            in_specs=[SMEM] + [whole] * 4,
            name="join_states",
        )
        total = rest[0] if rest else None
        if hop in after:
            total = after[hop](total)
        bits, hop = 2 * bits, hop + 1
    return ahead[:states]


def pad_rows(block, rows):
    return jnp.pad(block, ((0, rows - block.shape[0]), (0, 0)))


def send_y(grid, block, cap, tail):
    width, slots = 2 * cap, grid.exp * cap
    held, tails = [block[:width]], [block[slots:]]
    for s in range(1, grid.size["y"]):
        part = block[s * width : (s + 1) * width]
        got = grid.swap(jnp.concatenate([part, block[slots:]], axis=0) if tail else part, "y", s)
        held.append(got[:width])
        tails.append(got[width:])
    return held, tails


def send_core(grid, held, tails, cap, tail):
    ny = grid.size["y"]
    mine, others = [h[:cap] for h in held], [h[cap:] for h in held]
    if tail:
        others.append(pad_rows(jnp.concatenate([t[2 * s + 1 : 2 * s + 2] for s, t in enumerate(tails)], axis=0), 8))
    got = grid.swap(jnp.concatenate(others, axis=0), "core", 1)
    out = mine + [got[: ny * cap]]
    if tail:
        ends = [t[2 * s : 2 * s + 1] for s, t in enumerate(tails)] + [got[ny * cap : ny * cap + ny]]
        out.append(pad_rows(jnp.concatenate(ends, axis=0), 8))
    return jnp.concatenate(out, axis=0)


def back_core(grid, block, cap, tail):
    ny = grid.size["y"]
    half, slots = ny * cap, 2 * ny * cap
    send = block[half:slots]
    if tail:
        send = jnp.concatenate([send, pad_rows(block[slots + ny : slots + 2 * ny], 8)], axis=0)
    return grid.swap(send, "core", 1)


def back_y(grid, block, got, cap, tail):
    ny = grid.size["y"]
    half, slots = ny * cap, 2 * ny * cap
    rows, ends = [], []
    for s in range(ny):
        pair = [block[s * cap : (s + 1) * cap], got[s * cap : (s + 1) * cap]]
        both = [block[slots + s : slots + s + 1], got[half + s : half + s + 1]] if tail else []
        if s:
            if tail:
                pair.append(pad_rows(jnp.concatenate(both, axis=0), 8))
            back = grid.swap(jnp.concatenate(pair, axis=0), "y", s)
            pair, both = [back[: 2 * cap]], [back[2 * cap : 2 * cap + 2]]
        rows += pair
        ends += both
    if tail:
        rows.append(pad_rows(jnp.concatenate(ends, axis=0), 8))
    return jnp.concatenate(rows, axis=0)


def split(value):
    high = value.astype(BF16)
    return high, (value - high.astype(F32)).astype(BF16)


def dot(left, right, dims):
    return lax.dot_general(left, right, (dims, ((), ())), preferred_element_type=F32)


def product(left, right, dims):
    return dot(left[0], right[0], dims) + (dot(left[0], right[1], dims) + dot(left[1], right[0], dims))


def pick(exact, value, dims):
    high, low = split(value)
    return dot(exact, high, dims) + dot(exact, low, dims)


def sigmoid(value):
    return 1.0 / (1.0 + jnp.exp(-value))


def softplus(value):
    small = jnp.exp(-jnp.abs(value))
    series = small * (1.0 - small * (0.5 - small * (1.0 / 3.0 - small * (0.25 - small * 0.2))))
    return jnp.maximum(value, 0.0) + jnp.where(small < 0.03, series, jnp.log(1.0 + small))


def iota(shape, dim):
    return lax.broadcasted_iota(jnp.int32, shape, dim)


def scale_of(value):
    return lax.rsqrt(jnp.mean(value * value, axis=1, keepdims=True) + EPS)


def over_lanes(ref, columns):
    rows = columns.shape[0]
    for t in range(columns.shape[1]):
        ref[t] = jnp.broadcast_to(columns[:, t : t + 1], (rows, 128))


def widen(value, width):
    return jnp.concatenate([value] * (width // 128), axis=1)


def call(kernel, outs, ins, grid=None, in_specs=None, out_specs=None, scratch=(), name=None, aliases=None):
    whole = pl.BlockSpec(memory_space=pltpu.VMEM)
    return pl.pallas_call(
        kernel,
        out_shape=outs,
        grid=grid or (),
        in_specs=in_specs or [whole] * len(ins),
        out_specs=out_specs or jax.tree.map(lambda _: whole, outs),
        scratch_shapes=scratch,
        name=name,
        cost_estimate=pl.CostEstimate(
            flops=int(MICROSECONDS[name] * 1.1e9), transcendentals=0, bytes_accessed=int(MICROSECONDS[name] * 1e6)
        ),
        input_output_aliases=aliases or {},
        compiler_params=pltpu.CompilerParams(vmem_limit_bytes=VMEM_BYTES),
    )(*ins)


def shape(*dims, dtype=F32):
    return jax.ShapeDtypeStruct(dims, dtype)


SMEM = pl.BlockSpec(memory_space=pltpu.SMEM)


def full(*dims):
    return pl.BlockSpec(dims, lambda *_: (0,) * len(dims))


def route_kernel(experts, cap, me_ref, ids_ref, grad_ref, sent_ref, table_ref, rank_ref, load_ref):
    ids = ids_ref[...]
    tokens = ids.shape[0]
    chosen = (ids == iota((tokens, 128), 1)).astype(F32)
    before = (iota((tokens, tokens), 0) > iota((tokens, tokens), 1)).astype(BF16)
    rank = jnp.sum(dot(before, chosen.astype(BF16), NN) * chosen, axis=1, keepdims=True)
    kept = (rank < cap).astype(F32)
    place = jnp.where(rank < cap, ((ids ^ me_ref[0]) * cap).astype(F32) + rank, -1.0)
    row = jnp.broadcast_to(place, (tokens, tokens)).T
    slots = experts * cap
    table = (iota((slots, tokens), 0).astype(F32) == jnp.broadcast_to(row[0:1], (slots, tokens))).astype(F32)
    table = table.astype(BF16)
    table_ref[...] = table
    rank_ref[...] = rank
    sent_ref[...] = pick(table, grad_ref[...], NN)
    load_ref[...] = jnp.zeros_like(load_ref)
    load_ref[0:1, 0:128] = jnp.sum(chosen, axis=0, keepdims=True)
    load_ref[0:1, 128:256] = jnp.sum(chosen * (1.0 - kept), axis=0, keepdims=True)


def join_kernel(x_ref, halo_ref, gain_ref, weight_ref, joined_ref, high, low):
    @pl.when(pl.program_id(0) == 0)
    def _():
        x = jnp.concatenate([halo_ref[...], x_ref[...]], axis=0)
        high[...], low[...] = split(x * scale_of(x) * gain_ref[...])

    joined_ref[...] = product((high[...], low[...]), split(weight_ref[...]), NN)


def features_kernel(
    rank_n,
    states,
    inner_ref,
    since_ref,
    conv_w_ref,
    conv_b_ref,
    state_proj_ref,
    step_proj_ref,
    step_bias_ref,
    rate_ref,
    conv_ref,
    act_ref,
    pre_ref,
    steps_ref,
    masked_ref,
    drive_ref,
    proj_ref,
    pair_ref,
    in_lanes,
):
    tokens, width = act_ref.shape
    taps = conv_w_ref.shape[0]
    since = since_ref[...]
    conv = jnp.broadcast_to(conv_b_ref[...], (tokens, width))
    for k in range(taps):
        valid = (since >= taps - 1 - k).astype(F32)
        first = HALO - taps + 1 + k
        conv = conv + inner_ref[first : first + tokens, :] * valid * conv_w_ref[k : k + 1, :]
    act = conv * sigmoid(conv)
    conv_ref[...] = conv
    act_ref[...] = act
    proj = product(split(state_proj_ref[...]), split(act), NT)
    proj_ref[...] = proj
    pre = product(split(proj[:rank_n]), split(step_proj_ref[...]), TN) + step_bias_ref[...]
    pre_ref[...] = pre
    steps = softplus(pre)
    steps_ref[...] = steps
    masked = jnp.where(since == 0, RESET, steps)
    masked_ref[...] = masked
    drive_ref[...] = steps * act
    pair_ref[states : states + 1, :] = jnp.sum(masked, axis=0, keepdims=True)
    over_lanes(in_lanes, proj[rank_n : rank_n + states])
    chunk = 512
    for c in range(width // chunk):
        part = slice(c * chunk, (c + 1) * chunk)
        rate = rate_ref[:, part]

        def eight(group, state):
            for i in range(8):
                t = group * 8 + i
                decay = jnp.exp2(masked_ref[pl.ds(t, 1), part] * rate)
                state = decay * state + drive_ref[pl.ds(t, 1), part] * widen(in_lanes[t], chunk)
            return state

        pair_ref[0:states, part] = lax.fori_loop(0, tokens // 8, eight, jnp.zeros((states, chunk), F32))


def slot_tables(slots, cap, experts):
    slot = iota((slots, 8), 0)
    first = sum((slot >= cap * e).astype(jnp.int32) for e in range(1, experts))
    block = (first == iota((slots, 8), 1)).astype(F32)
    slot = iota((slots, 128), 0)
    first = sum(((slot >= cap * e).astype(jnp.int32) for e in range(1, experts)))
    within = (slot - first * cap == iota((slots, 128), 1)).astype(F32)
    return block, within


def scan_kernel(
    rank_n,
    states,
    experts,
    cap,
    me_ref,
    masked_ref,
    drive_ref,
    act_ref,
    gate_z_ref,
    start_ref,
    rate_ref,
    skip_ref,
    proj_ref,
    out_proj_ref,
    x_ref,
    gain_ref,
    router_ref,
    ids_ref,
    rank_ref,
    table_ref,
    scan_ref,
    history_ref,
    resid_ref,
    sent_ref,
    probs_ref,
    gate_ref,
    in_lanes,
    out_lanes,
    total,
):
    tokens, chunk = masked_ref.shape
    step = pl.program_id(0)

    @pl.when(step == 0)
    def _():
        over_lanes(in_lanes, proj_ref[rank_n : rank_n + states, :])
        over_lanes(out_lanes, proj_ref[rank_n + states : rank_n + 2 * states, :])
        total[...] = x_ref[...]

    rate = rate_ref[...]

    def eight(group, state):
        for i in range(8):
            t = group * 8 + i
            decay = jnp.exp2(masked_ref[pl.ds(t, 1), :] * rate)
            state = decay * state + drive_ref[pl.ds(t, 1), :] * widen(in_lanes[t], chunk)
            history_ref[t] = state
            scan_ref[pl.ds(t, 1), :] = jnp.sum(state * widen(out_lanes[t], chunk), axis=0, keepdims=True)
        return state

    lax.fori_loop(0, tokens // 8, eight, start_ref[...])
    gate_z = gate_z_ref[HALO:, :]
    mixed = (scan_ref[...] + skip_ref[...] * act_ref[...]) * (gate_z * sigmoid(gate_z))
    total[...] += product(split(mixed), split(out_proj_ref[...]), NN)

    @pl.when(step == pl.num_programs(0) - 1)
    def _():
        resid = total[...]
        resid_ref[...] = resid
        normed = resid * scale_of(resid) * gain_ref[...]
        logits = product(split(normed), split(router_ref[...]), NT)
        known = iota((tokens, 8), 1) < experts
        logits = jnp.where(known, logits, -1e30)
        raised = jnp.exp(logits - jnp.max(logits, axis=1, keepdims=True))
        raised = jnp.where(known, raised, 0.0)
        probs = raised / jnp.sum(raised, axis=1, keepdims=True)
        probs_ref[...] = probs
        ids = ids_ref[...]
        gate = jnp.sum(jnp.where(ids == iota((tokens, 8), 1), probs, 0.0), axis=1, keepdims=True)
        gate_ref[...] = gate
        slots = experts * cap
        sent_ref[0:slots, :] = pick(table_ref[...], normed, NN)
        sent_ref[slots:, :] = jnp.zeros((8, sent_ref.shape[1]), F32)
        rank = rank_ref[...].astype(jnp.int32)
        to_block = jnp.where(((ids ^ me_ref[0]) == iota((tokens, 8), 1)) & (rank < cap), gate, 0.0)
        at_rank = (rank == iota((tokens, 128), 1)).astype(BF16)
        high, low = split(to_block)
        rest = (to_block - high.astype(F32) - low.astype(F32)).astype(BF16)
        rows = dot(high, at_rank, TN) + (dot(low, at_rank, TN) + dot(rest, at_rank, TN))
        sent_ref[slots:, 0:128] = rows


def early_kernel(pieces, slices, *refs):
    grads, downs, outs = refs[:pieces], refs[pieces : pieces + slices], refs[pieces + slices :]
    downs = [split(d[...]) for d in downs]
    for p in range(pieces):
        grad = split(grads[p][...])
        for i in range(slices):
            outs[p][i] = product(grad, downs[i], NT)


def gelu_parts(value):
    inner = 0.7978845608 * (value + 0.044715 * value * value * value)
    tanh = jnp.tanh(inner)
    slope = 0.5 * (1.0 + tanh) + 0.5 * value * (1.0 - tanh * tanh) * 0.7978845608 * (
        1.0 + 3.0 * 0.044715 * value * value
    )
    return 0.5 * value * (1.0 + tanh), slope


def expert_kernel(slices, experts, cap, *refs):
    tokens_ref, ups, pulled_ref = refs[0], refs[1 : slices + 1], refs[slices + 1]
    back_ref, hidden_ref, grad_ref = refs[slices + 2 :]
    slots = experts * cap
    block, within = slot_tables(slots, cap, experts)
    within = within.astype(BF16)
    rows = split(tokens_ref[0:slots, :])
    back = jnp.zeros((slots, tokens_ref.shape[1]), F32)
    to_gate = jnp.zeros((slots, 1), F32)
    for i in range(slices):
        up = split(ups[i][...])
        hidden, slope = gelu_parts(product(rows, up, NN))
        pull = pulled_ref[i]
        grad = pull * slope
        hidden_ref[i] = hidden
        grad_ref[i] = grad
        to_gate += jnp.sum(hidden * pull, axis=1, keepdims=True)
        back += product(split(grad), up, NT)
    back_ref[0:slots, :] = back
    back_ref[slots:, :] = jnp.zeros((8, tokens_ref.shape[1]), F32)
    high, low = split(block * to_gate)
    rest = (block * to_gate - high.astype(F32) - low.astype(F32)).astype(BF16)
    back_ref[slots:, 0:128] = dot(high, within, TN) + (dot(low, within, TN) + dot(rest, within, TN))


def expert_grads_kernel(pieces, slices, experts, cap, *refs):
    tokens, grads, hiddens, pulls = (refs[i * pieces : (i + 1) * pieces] for i in range(4))
    downs, outs = refs[4 * pieces : 4 * pieces + slices], refs[4 * pieces + slices :]
    results, up_outs, down_outs = outs[:pieces], outs[pieces : pieces + slices], outs[pieces + slices :]
    slots = experts * cap
    downs = [split(d[...]) for d in downs]
    block, within = slot_tables(slots, cap, experts)
    within = within.astype(BF16)
    for p in range(pieces):
        ends = tokens[p][slots:, 0:128]
        high, low = split(ends)
        rest = (ends - high.astype(F32) - low.astype(F32)).astype(BF16)
        spread = dot(within, high, NT) + (dot(within, low, NT) + dot(within, rest, NT))
        gate = jnp.sum(spread * block, axis=1, keepdims=True)
        rows = split(tokens[p][0:slots, :] * gate)
        gated = split(grads[p][...] * gate)
        total = None
        for i in range(slices):
            hidden = split(hiddens[p][i])
            part = product(hidden, downs[i], NN)
            total = part if total is None else total + part
            up = product(rows, split(pulls[p][i]), TN)
            down = product(hidden, gated, TN)
            if p == 0:
                up_outs[i][...] = up
                down_outs[i][...] = down
            else:
                up_outs[i][...] += up
                down_outs[i][...] += down
        results[p][...] = total


def silu_parts(value):
    sig = sigmoid(value)
    return value * sig, sig * (1.0 + value * (1.0 - sig))


def mixer_back_kernel(
    rank_n,
    states,
    experts,
    cap,
    me_ref,
    back_ref,
    table_ref,
    gate_ref,
    probs_ref,
    ids_ref,
    rank_ref,
    resid_ref,
    grad_ref,
    gain_ref,
    router_ref,
    out_proj_ref,
    gate_z_ref,
    scan_ref,
    act_ref,
    skip_ref,
    masked_ref,
    rate_ref,
    proj_ref,
    steps_row_ref,
    grad_resid_ref,
    small_ref,
    grad_scan_ref,
    grad_gate_ref,
    grad_skip_ref,
    pair_ref,
    out_lanes,
    high,
    low,
):
    tokens, chunk = masked_ref.shape

    @pl.when(pl.program_id(0) == 0)
    def _():
        over_lanes(out_lanes, proj_ref[rank_n + states : rank_n + 2 * states, :])
        slots = experts * cap
        ids, rank = ids_ref[...], rank_ref[...].astype(jnp.int32)
        back = pick(table_ref[...], back_ref[0:slots, :], TN)
        at_rank = (rank == iota((tokens, 128), 1)).astype(BF16)
        ends = back_ref[slots:, 0:128]
        first, second = split(ends)
        third = (ends - first.astype(F32) - second.astype(F32)).astype(BF16)
        spread = dot(at_rank, first, NT) + (dot(at_rank, second, NT) + dot(at_rank, third, NT))
        mine = ((ids ^ me_ref[0]) == iota((tokens, 8), 1)) & (rank < cap)
        grad_gate = jnp.sum(jnp.where(mine, spread, 0.0), axis=1, keepdims=True)
        probs = probs_ref[...]
        grad_probs = jnp.where(ids == iota((tokens, 8), 1), grad_gate, 0.0)
        grad_logits = probs * (grad_probs - jnp.sum(probs * grad_probs, axis=1, keepdims=True))
        resid, gain = resid_ref[...], gain_ref[...]
        scale = scale_of(resid)
        normed = resid * scale * gain
        logits_two = split(grad_logits)
        grad_normed = gate_ref[...] * back + product(logits_two, split(router_ref[...]), NN)
        small_ref[...] = jnp.zeros_like(small_ref)
        small_ref[0:8, :] = product(logits_two, split(normed), TN)
        small_ref[8:9, :] = jnp.sum(grad_normed * resid * scale, axis=0, keepdims=True)
        pulled = gain * grad_normed
        grad_resid = (
            grad_ref[...]
            + scale * pulled
            - resid * (scale * scale * scale) * jnp.mean(pulled * resid, axis=1, keepdims=True)
        )
        grad_resid_ref[...] = grad_resid
        high[...], low[...] = split(grad_resid)

    grad_mixed = product((high[...], low[...]), split(out_proj_ref[...]), NT)
    silu, slope = silu_parts(gate_z_ref[HALO:, :])
    act = act_ref[...]
    grad_scan = grad_mixed * silu
    grad_scan_ref[...] = grad_scan
    grad_gate_ref[...] = grad_mixed * (scan_ref[...] + skip_ref[...] * act) * slope
    grad_skip_ref[...] = jnp.sum(grad_scan * act, axis=0, keepdims=True)
    rate = rate_ref[...]

    def eight(group, state):
        for i in range(8):
            t = tokens - 1 - (group * 8 + i)
            decay = jnp.exp2(masked_ref[pl.ds(t, 1), :] * rate)
            state = decay * (state + grad_scan_ref[pl.ds(t, 1), :] * widen(out_lanes[t], chunk))
        return state

    pair_ref[0:states, :] = lax.fori_loop(0, tokens // 8, eight, jnp.zeros((states, chunk), F32))
    pair_ref[states : states + 1, :] = steps_row_ref[...]


def late_kernel(
    which_ref, scan_ref, act_ref, skip_ref, gate_z_ref, grad_resid_ref, x_ref, gain_ref, grad_gate_ref, *refs
):
    high, low = refs[-2:]
    if len(refs) == 5:
        weight_ref, out_ref, normed_ref = refs[:3]
    else:
        weight_ref, out_ref, normed_ref = None, refs[0], None

    @pl.when(pl.program_id(0) == 0)
    def _():
        @pl.when(which_ref[0] == 0)
        def _():
            high[...], low[...] = split(grad_resid_ref[...])

        @pl.when(which_ref[0] == 1)
        def _():
            x = x_ref[...]
            high[...], low[...] = split(x * scale_of(x) * gain_ref[...])

        if normed_ref is not None:
            normed_ref[...] = jnp.zeros_like(normed_ref)

    @pl.when(which_ref[0] == 0)
    def _():
        gate_z = gate_z_ref[HALO:, :]
        mixed = (scan_ref[...] + skip_ref[...] * act_ref[...]) * (gate_z * sigmoid(gate_z))
        out_ref[...] = product(split(mixed), (high[...], low[...]), TN)

    @pl.when(which_ref[0] == 1)
    def _():
        out_ref[...] = product((high[...], low[...]), split(grad_gate_ref[...]), TN)

    if normed_ref is not None:
        normed_ref[...] += product(split(grad_gate_ref[...]), split(weight_ref[...]), NT)


def scan_back_kernel(
    rank_n,
    states,
    masked_ref,
    steps_ref,
    drive_ref,
    act_ref,
    pre_ref,
    grad_scan_ref,
    skip_ref,
    history_ref,
    before_ref,
    start_ref,
    end_ref,
    rate_ref,
    proj_ref,
    step_proj_ref,
    *refs,
):
    (
        grad_act_ref, grad_pre_ref, grad_decay_ref, grad_proj_ref,
        in_lanes, out_lanes, grad_drive, grad_steps, at_in, at_out, carried_ref, decays_ref, sums_ref,
    ) = refs[-13:]
    tokens, chunk = masked_ref.shape
    block = history_ref.shape[0]
    step, blocks = pl.program_id(0), pl.num_programs(0)
    first = (blocks - 1 - step) * block

    @pl.when(step == 0)
    def _():
        over_lanes(in_lanes, proj_ref[rank_n : rank_n + states, :])
        over_lanes(out_lanes, proj_ref[rank_n + states : rank_n + 2 * states, :])
        carried_ref[...] = end_ref[...]
        decays_ref[...] = jnp.zeros_like(decays_ref)
        sums_ref[...] = jnp.zeros_like(sums_ref)

    rate = rate_ref[...]
    entering_state = jnp.where(first == 0, start_ref[...], before_ref[7])

    def narrow(value):
        return functools.reduce(jnp.add, [value[:, c : c + 128] for c in range(0, chunk, 128)])

    def one(local, before, carried):
        state, decays = carried
        t = first + local
        masked = masked_ref[pl.ds(t, 1), :]
        grad = grad_scan_ref[pl.ds(t, 1), :]
        decay = jnp.exp2(masked * rate)
        state = state + grad * widen(out_lanes[t], chunk)
        at_out[local] = narrow(history_ref[local] * grad)
        at_in[local] = narrow(state * drive_ref[pl.ds(t, 1), :])
        grad_drive[pl.ds(t, 1), :] = jnp.sum(state * widen(in_lanes[t], chunk), axis=0, keepdims=True)
        state = decay * state
        pulled = state * before
        grad_steps[pl.ds(t, 1), :] = jnp.sum(pulled * rate, axis=0, keepdims=True)
        return state, decays + pulled * masked

    def eight(group, carried):
        for i in range(8):
            local = block - 1 - (group * 8 + i)
            carried = one(local, history_ref[local - 1], carried)
        return carried

    carried = lax.fori_loop(0, block // 8 - 1, eight, (carried_ref[...], decays_ref[...]))
    for local in range(7, 0, -1):
        carried = one(local, history_ref[local - 1], carried)
    carried_ref[...], decays_ref[...] = one(0, entering_state, carried)

    ones = jnp.ones((128, 128), BF16)
    lane = iota((states, 128), 1)
    for i, held in enumerate((at_in, at_out)):
        high, low = split(held[...].reshape(block * states, 128))
        spread = (dot(high, ones, NN) + dot(low, ones, NN)).reshape(block, states, 128)
        total = sums_ref[i]
        for local in range(block):
            total = jnp.where(lane == first + local, spread[local], total)
        sums_ref[i] = total

    @pl.when(step == blocks - 1)
    def _():
        grad_decay_ref[...] = decays_ref[...] * (rate * (1.0 / LOG2E))
        steps, act = steps_ref[...], act_ref[...]
        grad_act_ref[...] = skip_ref[...] * grad_scan_ref[...] + grad_drive[...] * steps
        grad_pre = (grad_steps[...] * (1.0 / LOG2E) + grad_drive[...] * act) * sigmoid(pre_ref[...])
        grad_pre_ref[...] = grad_pre
        grad_proj_ref[0:rank_n, :] = product(split(step_proj_ref[...]), split(grad_pre), NT)
        grad_proj_ref[rank_n : rank_n + states, :] = sums_ref[0]
        grad_proj_ref[rank_n + states : rank_n + 2 * states, :] = sums_ref[1]


def input_back_kernel(
    rank_n,
    states,
    core_ref,
    proj_a_ref,
    proj_b_ref,
    proj_c_ref,
    proj_ref,
    state_proj_ref,
    act_ref,
    grad_act_ref,
    grad_pre_ref,
    conv_ref,
    inner_ref,
    conv_w_ref,
    since_ref,
    weight_ref,
    x_ref,
    halo_ref,
    gain_ref,
    grad_gate_normed_ref,
    grad_resid_ref,
    grad_decay_ref,
    grad_skip_ref,
    small_ref,
    keep_ref,
    send_ref,
    input_ref,
    edge_ref,
    high,
    low,
    grad_inner,
    total,
):
    tokens, chunk = act_ref.shape
    depth = x_ref.shape[1]
    half = depth // 2
    taps = conv_w_ref.shape[0]
    step = pl.program_id(0)

    @pl.when(step == 0)
    def _():
        x = jnp.concatenate([halo_ref[...], x_ref[...]], axis=0)
        high[...], low[...] = split(x * scale_of(x) * gain_ref[...])
        total[...] = jnp.zeros_like(total)

    act, grad_pre = split(act_ref[...]), grad_pre_ref[...]
    grad_proj = split(proj_a_ref[...] + proj_b_ref[...] + proj_c_ref[...])
    grad_act = grad_act_ref[...] + product(grad_proj, split(state_proj_ref[...]), TN)
    _, slope = silu_parts(conv_ref[...])
    grad_conv = grad_act * slope
    since = since_ref[...]
    grad_inner[...] = jnp.zeros_like(grad_inner)
    rows = []
    for k in range(taps):
        valid = (since >= taps - 1 - k).astype(F32)
        first = HALO - taps + 1 + k
        held = grad_conv * valid
        rows.append(jnp.sum(held * inner_ref[first : first + tokens, :], axis=0, keepdims=True))
        grad_inner[first : first + tokens, :] += held * conv_w_ref[k : k + 1, :]
    rows.append(jnp.sum(grad_conv, axis=0, keepdims=True))
    rows.append(jnp.sum(grad_pre, axis=0, keepdims=True))
    rows.append(grad_skip_ref[...])
    grads = split(grad_inner[...])
    total[...] += product(grads, split(weight_ref[...]), NT)
    of_state_proj = product(grad_proj, act, NN)
    of_step_proj = product(split(proj_ref[0:rank_n, :]), split(grad_pre), NN)

    def first_half(out_ref):
        out_ref[0:half, :] = product((high[:, 0:half], low[:, 0:half]), grads, TN)
        at = half + 2 * states + rank_n
        out_ref[half:at, :] = of_state_proj
        out_ref[at : at + states, :] = grad_decay_ref[...]
        if at + states < out_ref.shape[0]:
            out_ref[at + states :, :] = jnp.zeros((out_ref.shape[0] - at - states, chunk), F32)

    def second_half(out_ref):
        out_ref[0:half, :] = product((high[:, half:], low[:, half:]), grads, TN)
        out_ref[half : half + rank_n, :] = of_step_proj
        at = half + rank_n
        out_ref[at:, :] = jnp.zeros((out_ref.shape[0] - at, chunk), F32)
        for i, row in enumerate(rows):
            out_ref[at + i : at + i + 1, :] = row

    @pl.when(core_ref[0] == 0)
    def _():
        first_half(keep_ref)
        second_half(send_ref)

    @pl.when(core_ref[0] == 1)
    def _():
        second_half(keep_ref)
        first_half(send_ref)

    @pl.when(step == pl.num_programs(0) - 1)
    def _():
        gain = gain_ref[...]

        def rows_back(x, grad):
            scale = scale_of(x)
            pulled = gain * grad
            back = scale * pulled - x * (scale * scale * scale) * jnp.mean(pulled * x, axis=1, keepdims=True)
            return back, jnp.sum(grad * x * scale, axis=0, keepdims=True)

        edge, edge_gain = rows_back(halo_ref[...], total[0:HALO, :])
        own, own_gain = rows_back(x_ref[...], total[HALO:, :] + grad_gate_normed_ref[...])
        edge_ref[...] = edge
        input_ref[...] = grad_resid_ref[...] + own
        small = jnp.concatenate([small_ref[0:10, :], edge_gain + own_gain], axis=0)

        def place_small(out_ref):
            at = half + rank_n + 8
            out_ref[at : at + 11, :] = small[:, 0:chunk]
            out_ref[at + 16 : at + 27, 0 : depth - chunk] = small[:, chunk:]

        @pl.when(core_ref[0] == 0)
        def _():
            place_small(send_ref)

        @pl.when(core_ref[0] == 1)
        def _():
            place_small(keep_ref)


def finish_late_kernel(core_ref, first_ref, second_ref, got_first_ref, got_second_ref, in_ref, out_ref):
    depth = out_ref.shape[2]
    step = pl.program_id(0)

    def write(gate, out):
        in_ref[...] = gate
        out_ref[0] = out[:, 0:depth]
        out_ref[1] = out[:, depth:]

    for i, (own, got) in enumerate(((first_ref, got_first_ref), (second_ref, got_second_ref))):

        @pl.when((core_ref[0] == 0) & (step == i))
        def _():
            write(own[...], got[...])

        @pl.when((core_ref[0] == 1) & (step == i))
        def _():
            write(got[...], own[...])


def finish_kernel(
    rank_n, states, taps, core_ref, first_ref, second_ref, got_first_ref, got_second_ref, _,
    in_ref, state_proj_ref, step_proj_ref, decay_ref, conv_w_ref, rows_ref, small_ref,
):
    depth = in_ref.shape[0]
    half, quarter = depth // 2, first_ref.shape[0]
    rest = half - quarter

    def first_half(one, two):
        in_ref[0:quarter, :] = one[...]
        in_ref[quarter:half, :] = two[0:rest, :]
        at = rest + 2 * states + rank_n
        state_proj_ref[...] = two[rest:at, :].T
        decay_ref[...] = two[at : at + states, :].T

    def second_half(one, two):
        in_ref[half : half + quarter, :] = one[...]
        in_ref[half + quarter :, :] = two[0:rest, :]
        step_proj_ref[...] = two[rest : rest + rank_n, :]
        at = rest + rank_n
        conv_w_ref[...] = two[at : at + taps, :]
        rows_ref[...] = two[at : at + 8, :]
        small_ref[...] = two[at + 8 : at + 40, :]

    @pl.when(core_ref[0] == 0)
    def _():
        first_half(first_ref, second_ref)
        second_half(got_first_ref, got_second_ref)

    @pl.when(core_ref[0] == 1)
    def _():
        first_half(got_first_ref, got_second_ref)
        second_half(first_ref, second_ref)


def per_device(
    block_input,
    seq_lengths,
    expert_ids,
    output_grad,
    mixer_gain,
    in_proj,
    conv_weight,
    conv_bias,
    state_proj,
    step_proj,
    step_bias,
    decay_log,
    skip_gain,
    out_proj,
    router_gain,
    router,
    expert_up,
    expert_down,
):
    grid = Grid()
    tokens, depth = block_input.shape
    taps, width = conv_weight.shape
    rank_n, states, experts = step_proj.shape[0], decay_log.shape[1], router.shape[1]
    cap = (5 * tokens + 4 * experts - 1) // (4 * experts)
    slots, hidden = experts * cap, expert_up.shape[2]
    chunk = 512
    chunks = width // chunk
    pieces, slices = grid.size["outer"], grid.size["inner"]
    token_block = 64
    blocks = tokens // token_block
    me = lax.axis_index("exp").astype(jnp.int32).reshape(1)
    ext = HALO + tokens

    halo = grid.along(block_input[tokens - HALO :], 1)

    count = seq_lengths.shape[0]
    earlier = jnp.arange(count)[:, None] > jnp.arange(count)[None, :]
    starts = jnp.sum(jnp.where(earlier, seq_lengths[None, :], 0), axis=1)
    position = grid.index * tokens + jnp.arange(tokens, dtype=jnp.int32)
    own_start = jnp.max(jnp.where(starts[None, :] <= position[:, None], starts[None, :], 0), axis=1)
    since = (position - own_start)[:, None]
    rate = -jnp.exp(decay_log.T) * LOG2E
    state_proj_t = state_proj.T
    router_t = pad_rows(router.T, 8)
    row = lambda vector: vector.reshape(1, -1)

    sent_grads, table, rank, loads = call(
        functools.partial(route_kernel, experts, cap),
        [shape(slots, depth), shape(slots, tokens, dtype=BF16), shape(tokens, 1), shape(8, depth)],
        (me, expert_ids, output_grad),
        in_specs=[SMEM] + [pl.BlockSpec(memory_space=pltpu.VMEM)] * 2,
        name="route",
    )
    halo, sent_grads = tie(halo, sent_grads)
    held_grads, _ = send_y(grid, sent_grads, cap, False)
    up, down = expert_up[0], expert_down[0]
    ups = [up] + [grid.swap(up, "inner", s) for s in range(1, slices)]
    downs = [down] + [grid.swap(down, "inner", s) for s in range(1, slices)]

    block = lambda c, *_: (0, c)
    joined = call(
        join_kernel,
        shape(ext, 2 * width),
        (block_input, halo, row(mixer_gain), in_proj),
        grid=(2 * chunks,),
        in_specs=[full(tokens, depth), full(HALO, depth), full(1, depth), pl.BlockSpec((depth, chunk), block)],
        out_specs=pl.BlockSpec((ext, chunk), block),
        scratch=[pltpu.VMEM((ext, depth), BF16)] * 2,
        name="join",
    )
    joined, *held_grads = tie(joined, *held_grads)
    own_grads = send_core(grid, held_grads, None, cap, False)
    joined, own_grads = tie(joined, own_grads)
    near_grads, far_grads = grid.swap(own_grads, "outer", 1), grid.swap(own_grads, "outer", 2)
    conv, act, pre, steps, masked, drive, proj, pair = call(
        functools.partial(features_kernel, rank_n, states),
        [shape(tokens, width)] * 6 + [shape(rank_n + 2 * states, tokens), shape(states + 1, width)],
        (joined, since, conv_weight, row(conv_bias), state_proj_t, step_proj, row(step_bias), rate),
        grid=(1,),
        in_specs=[
            full(ext, width),
            full(tokens, 1),
            full(taps, width),
            full(1, width),
            full(rank_n + 2 * states, width),
            full(rank_n, width),
            full(1, width),
            full(states, width),
        ],
        out_specs=[full(tokens, width)] * 6 + [full(rank_n + 2 * states, tokens), full(states + 1, width)],
        scratch=[pltpu.VMEM((tokens, states, 128), F32)],
        name="features",
    )
    pair, *downs = tie(pair, *downs)
    held = {}

    def third(total):
        total, held["near"], held["far"] = tie(total, near_grads, far_grads)
        return total

    start = entering(grid, pair, rate, False, {2: third})
    start, near_grads, far_grads = tie(start, held["near"], held["far"])
    last_grads = grid.swap(far_grads, "outer", 1)
    tok = pl.BlockSpec((tokens, chunk), block)
    gate_half = pl.BlockSpec((ext, chunk), lambda c, *_: (0, chunks + c))
    one_row = pl.BlockSpec((1, chunk), block)
    state_rows = pl.BlockSpec((states, chunk), block)
    history_block = pl.BlockSpec((tokens, states, chunk), lambda c: (0, 0, c))
    out_rows = pl.BlockSpec((chunk, depth), lambda c, *_: (c, 0))
    proj_full = full(rank_n + 2 * states, tokens)
    lanes = pltpu.VMEM((tokens, states, 128), F32)
    scan, history, resid, sent, probs, gate = call(
        functools.partial(scan_kernel, rank_n, states, experts, cap),
        [
            shape(tokens, width),
            shape(tokens, states, width),
            shape(tokens, depth),
            shape(slots + 8, depth),
            shape(tokens, 8),
            shape(tokens, 1),
        ],
        (
            me, masked, drive, act, joined, start, rate, row(skip_gain), proj, out_proj, block_input,
            row(router_gain), router_t, expert_ids, rank, table,
        ),
        grid=(chunks,),
        in_specs=[
            SMEM, tok, tok, tok, gate_half, state_rows, state_rows, one_row, proj_full, out_rows,
            full(tokens, depth), full(1, depth), full(8, depth), full(tokens, 1), full(tokens, 1),
            full(slots, tokens),
        ],
        out_specs=[
            tok, history_block, full(tokens, depth), full(slots + 8, depth), full(tokens, 8), full(tokens, 1),
        ],
        scratch=[lanes, lanes, pltpu.VMEM((tokens, depth), F32)],
        name="scan",
    )

    sent, last_grads = tie(sent, last_grads)
    grad_pieces = [own_grads, near_grads, far_grads, last_grads]
    pulled = call(
        functools.partial(early_kernel, pieces, slices),
        [shape(slices, slots, hidden)] * pieces,
        (*grad_pieces, *downs),
        name="early",
    )
    own_tokens = send_core(grid, *send_y(grid, sent, cap, True), cap, True)
    own_tokens, *pulled = tie(own_tokens, *pulled)
    near_tokens, far_tokens = grid.swap(own_tokens, "outer", 1), grid.swap(own_tokens, "outer", 2)

    def expert(rows, pulled_rows):
        return call(
            functools.partial(expert_kernel, slices, experts, cap),
            [shape(slots + 8, depth)] + [shape(slices, slots, hidden)] * 2,
            (rows, *ups, pulled_rows),
            name="expert",
        )

    own_outs = expert(own_tokens, pulled[0])
    near_tokens, far_tokens, *own_outs = tie(near_tokens, far_tokens, *own_outs)
    last_tokens = grid.swap(far_tokens, "outer", 1)
    near_outs, far_outs = expert(near_tokens, pulled[1]), expert(far_tokens, pulled[2])
    last_tokens, near_outs, far_outs = tie(last_tokens, near_outs, far_outs)
    last_outs = expert(last_tokens, pulled[3])
    token_pieces = [own_tokens, near_tokens, far_tokens, last_tokens]
    backs, hiddens, pulls = zip(own_outs, near_outs, far_outs, last_outs)
    back_through = grid.swap(backs[3], "outer", 1)
    outs = call(
        functools.partial(expert_grads_kernel, pieces, slices, experts, cap),
        [shape(slots, depth)] * pieces + [shape(depth, hidden)] * slices + [shape(hidden, depth)] * slices,
        (*token_pieces, *grad_pieces, *hiddens, *pulls, *downs),
        name="expert_grads",
    )
    back, *outs = tie(outer_reduce_rest(grid, backs, back_through), *outs)
    back = back_y(grid, back, back_core(grid, back, cap, True), cap, True)
    results, up_grads, down_grads = outs[:pieces], outs[pieces : pieces + slices], outs[pieces + slices :]
    halves = lambda array: [array[: array.shape[0] // 2], array[array.shape[0] // 2 :]]
    ups_sent, downs_sent = ([halves(g) for g in grads[1:]] for grads in (up_grads, down_grads))

    def inner_swaps(sent, half):
        return [grid.swap(pair[half], "inner", s) for s, pair in enumerate(sent, 1)]

    up_first = inner_swaps(ups_sent, 0)
    back, last_result, ups_sent, *up_first = tie(back, results[3], ups_sent, *up_first)
    through = grid.swap(last_result, "outer", 1)
    up_second = inner_swaps(ups_sent, 1)

    grad_resid, small, grad_scan, grad_gate, grad_skip, back_pair = call(
        functools.partial(mixer_back_kernel, rank_n, states, experts, cap),
        [
            shape(tokens, depth),
            shape(16, depth),
            shape(tokens, width),
            shape(tokens, width),
            shape(1, width),
            shape(states + 1, width),
        ],
        (
            me, back, table, gate, probs, expert_ids, rank, resid, output_grad, row(router_gain), router_t,
            out_proj, joined, scan, act, row(skip_gain), masked, rate, proj, pair[states:],
        ),
        grid=(chunks,),
        in_specs=[
            SMEM, full(slots + 8, depth), full(slots, tokens), full(tokens, 1), full(tokens, 8),
            full(tokens, 1), full(tokens, 1), full(tokens, depth), full(tokens, depth), full(1, depth),
            full(8, depth), out_rows, gate_half, tok, tok, one_row, tok, state_rows, proj_full, one_row,
        ],
        out_specs=[
            full(tokens, depth), full(16, depth), tok, tok, one_row,
            pl.BlockSpec((states + 1, chunk), block),
        ],
        scratch=[lanes] + [pltpu.VMEM((tokens, depth), BF16)] * 2,
        name="mixer_back",
    )
    back_pair, downs_sent = tie(back_pair, downs_sent)
    core = grid.at["core"].astype(jnp.int32).reshape(1)
    wide = pl.BlockSpec((tokens, depth), block)

    def late(which, weight):
        return call(
            late_kernel,
            [shape(depth, width)] + [shape(tokens, depth)] * len(weight),
            (
                which, scan, act, row(skip_gain), joined, grad_resid, block_input, row(mixer_gain), grad_gate,
                *weight,
            ),
            grid=(2,),
            in_specs=[
                SMEM, wide, wide, pl.BlockSpec((1, depth), block), pl.BlockSpec((ext, depth), lambda c: (0, 2 + c)),
                full(tokens, depth), full(tokens, depth), full(1, depth), wide,
            ]
            + [pl.BlockSpec((depth, depth), lambda c: (0, 2 + c))] * len(weight),
            out_specs=[pl.BlockSpec((depth, depth), block)] + [full(tokens, depth)] * len(weight),
            scratch=[pltpu.VMEM((tokens, depth), BF16)] * 2,
            name="late",
        )

    (late_sent,) = late(core, ())
    late_kept, grad_gate_normed = late(1 - core, (in_proj,))
    late_got = grid.swap(late_sent, "core", 1)
    down_first = inner_swaps(downs_sent, 0)

    def first(total):
        total, held["through"], held["downs"], *held["up_second"] = tie(total, through, downs_sent, *up_second)
        return total

    def second(total):
        total, got, kept, held["normed"], *held["down_first"] = tie(
            total, late_got, late_kept, grad_gate_normed, *down_first
        )
        held["late"] = sum_first(grid, [kept, got])
        return total

    end = entering(grid, back_pair, rate, True, {1: first, 2: second})
    up_second = held["up_second"]
    end, near, far = tie(end, results[1], results[2] + held["through"])
    near, far = grid.swap(near, "outer", 1), grid.swap(far, "outer", 2)
    grad_gate_normed = held["normed"]
    late_first, late_second = held["late"]

    def with_others(own, firsts, seconds):
        for pair in zip(firsts, seconds):
            own = own + jnp.concatenate(pair, axis=0)
        return own

    def scan_back(c, before):
        at = lambda _: (0, c)
        tok, one_row = pl.BlockSpec((tokens, chunk), at), pl.BlockSpec((1, chunk), at)
        state_rows = pl.BlockSpec((states, chunk), at)
        return call(
            functools.partial(scan_back_kernel, rank_n, states),
            [
                shape(tokens, width), shape(tokens, width), shape(states, width),
                shape(rank_n + 2 * states, tokens),
            ],
            (
                masked, steps, drive, act, pre, grad_scan, row(skip_gain), history, history, start, end, rate, proj,
                step_proj, *before,
            ),
            grid=(blocks,),
            in_specs=[
                tok, tok, tok, tok, tok, tok, one_row,
                pl.BlockSpec((token_block, states, chunk), lambda i: (blocks - 1 - i, 0, c)),
                pl.BlockSpec(
                    (8, states, chunk),
                    lambda i: (jnp.maximum((blocks - 1 - i) * (token_block // 8) - 1, 0), 0, c),
                ),
                state_rows, state_rows, state_rows, proj_full, pl.BlockSpec((rank_n, chunk), at),
            ]
            + [pl.BlockSpec(memory_space=pl.ANY)] * len(before),
            out_specs=[tok, tok, state_rows, proj_full],
            scratch=[lanes, lanes]
            + [pltpu.VMEM((tokens, chunk), F32)] * 2
            + [pltpu.VMEM((token_block, states, 128), F32)] * 2
            + [pltpu.VMEM((states, chunk), F32)] * 2
            + [pltpu.VMEM((2, states, 128), F32)],
            name="scan_back",
            aliases={14 + i: i for i in range(len(before))},
        )

    *filled, grad_proj_a = scan_back(0, ())
    filled, late_first, late_second = tie(filled, late_first, late_second)
    late_both = sum_second(grid, late_first, late_second)
    *filled, grad_proj_b = scan_back(1, filled)
    filled, late_both, near, far, downs_sent = tie(filled, late_both, near, far, held["downs"])
    down_second = inner_swaps(downs_sent, 1)
    result = results[0] + near + far
    result_got = back_core(grid, result, cap, False)
    late_cut = cut_outer(grid, late_both)
    late_through = grid.swap(late_cut[3], "outer", 1)
    grad_act, grad_pre, grad_decay, grad_proj_c = scan_back(2, filled)
    grad_act, late_through, result_got, down_second = tie(grad_act, late_through, result_got, down_second)
    late_total = outer_reduce_rest(grid, late_cut, late_through)
    unit = 2 * grid.size["inner"] * grid.size["y"]
    half = -(-max(depth // 2 + 3 * states + rank_n, depth // 2 + rank_n + 40) // unit) * unit
    small = jnp.concatenate([small[:9], loads[0:1]], axis=0)
    kept, sent_half, input_grad, edge = call(
        functools.partial(input_back_kernel, rank_n, states),
        [shape(half, width), shape(half, width), shape(tokens, depth), shape(HALO, depth)],
        (
            core, grad_proj_a, grad_proj_b, grad_proj_c, proj, state_proj_t, act, grad_act, grad_pre, conv, joined,
            conv_weight, since, in_proj, block_input, halo, row(mixer_gain), grad_gate_normed, grad_resid,
            grad_decay, grad_skip, small,
        ),
        grid=(chunks,),
        in_specs=[
            SMEM, proj_full, proj_full, proj_full, proj_full, pl.BlockSpec((rank_n + 2 * states, chunk), block),
            tok, tok, tok, tok, pl.BlockSpec((ext, chunk), block), pl.BlockSpec((taps, chunk), block),
            full(tokens, 1), pl.BlockSpec((depth, chunk), block), full(tokens, depth), full(HALO, depth),
            full(1, depth), full(tokens, depth), full(tokens, depth), state_rows, one_row, full(10, depth),
        ],
        out_specs=[
            pl.BlockSpec((half, chunk), block), pl.BlockSpec((half, chunk), block), full(tokens, depth),
            full(HALO, depth),
        ],
        scratch=[pltpu.VMEM((ext, depth), BF16)] * 2
        + [pltpu.VMEM((ext, chunk), F32), pltpu.VMEM((ext, depth), F32)],
        name="input_back",
    )
    kept, sent_half, late_total = tie(kept, sent_half, late_total)
    late_near, late_far = grid.swap(late_total, "outer", 1), grid.swap(late_total, "outer", 2)
    sent_got = grid.swap(sent_half, "core", 1)
    kept, sent_got = tie(kept, sent_got)
    grads_first, grads_second = sum_first(grid, [kept, sent_got])
    late_near, late_far, grads_first, grads_second, edge, result, result_got, up_parts, down_parts = tie(
        late_near, late_far, grads_first, grads_second, edge, result, result_got,
        [up_grads[0], up_first, up_second], [down_grads[0], held["down_first"], down_second],
    )
    from_next = grid.along(edge, -1)
    input_grad = jnp.concatenate([input_grad[: tokens - HALO], input_grad[tokens - HALO :] + from_next], axis=0)
    grad_up, grad_down = with_others(*up_parts), with_others(*down_parts)
    late_last = grid.swap(late_far, "outer", 1)
    grads = sum_second(grid, grads_first, grads_second)
    late_last, grads, input_grad = tie(late_last, grads, input_grad)
    result = back_y(grid, result, result_got, cap, False)
    late_first, late_second = spread_second(grid, join_outer(grid, late_total, late_near, late_far, late_last))
    grads = sum_outer(grid, grads)
    late_first, late_second, grads, result, grad_up = tie(late_first, late_second, grads, result, grad_up)
    combined = jnp.dot(table.T, result.astype(F32), precision=lax.Precision.HIGHEST, preferred_element_type=F32)
    block_output = resid + gate * combined
    late_first, late_second = gather_rows(grid, late_first, "inner"), gather_rows(grid, late_second, "y")
    grads = spread_outer(grid, grads)
    late_first, late_second, grads, block_output, grad_down = tie(
        late_first, late_second, grads, block_output, grad_down
    )
    late_other = [grid.swap(late_first, "core", 1), grid.swap(late_second, "core", 1)]
    grads_first, grads_second = spread_second(grid, grads)
    grads_first, grads_second, *late_other = tie(grads_first, grads_second, *late_other)
    grads_first, grads_second = gather_rows(grid, grads_first, "inner"), gather_rows(grid, grads_second, "y")
    quarter = pl.BlockSpec((half // 2, chunk), block)
    late_rows = full(depth // 2, width)
    grad_in_proj, grad_out_proj = call(
        finish_late_kernel,
        [shape(depth, 2 * width), shape(2, depth, depth)],
        (core, late_first, late_second, *late_other),
        grid=(2,),
        in_specs=[SMEM] + [late_rows] * 4,
        out_specs=[
            pl.BlockSpec((depth // 2, width), lambda r: (r, 1)),
            pl.BlockSpec((2, depth // 2, depth), lambda r: (0, r, 0)),
        ],
        name="finish_late",
    )
    grads_first, grads_second, grad_in_proj = tie(grads_first, grads_second, grad_in_proj)
    grads_other = [grid.swap(grads_first, "core", 1), grid.swap(grads_second, "core", 1)]
    tall = lambda columns: pl.BlockSpec((chunk, columns), lambda c: (c, 0))
    (
        grad_in_proj, grad_state_proj, grad_step_proj, grad_decay_log, grad_conv_weight, rows, small,
    ) = call(
        functools.partial(finish_kernel, rank_n, states, taps),
        [
            shape(depth, 2 * width), shape(width, rank_n + 2 * states), shape(rank_n, width),
            shape(width, states), shape(taps, width), shape(8, width), shape(32, chunk),
        ],
        (core, grads_first, grads_second, *grads_other, grad_in_proj),
        grid=(chunks,),
        in_specs=[SMEM] + [quarter] * 4 + [pl.BlockSpec(memory_space=pl.ANY)],
        out_specs=[
            pl.BlockSpec((depth, chunk), block), tall(rank_n + 2 * states), pl.BlockSpec((rank_n, chunk), block),
            tall(states), pl.BlockSpec((taps, chunk), block), pl.BlockSpec((8, chunk), block), full(32, chunk),
        ],
        name="finish",
        aliases={5: 0},
    )
    small = jnp.concatenate([small[:16], small[16:, : depth - chunk]], axis=1)
    return (
        block_output,
        input_grad,
        small[10],
        grad_in_proj,
        grad_conv_weight,
        rows[taps],
        grad_state_proj,
        grad_step_proj,
        rows[taps + 1],
        grad_decay_log,
        rows[taps + 2],
        grad_out_proj.reshape(width, depth),
        small[8],
        small[:experts].T,
        grad_up[None],
        grad_down[None],
        small[9, :experts].astype(jnp.int32),
        small[9, 128 : 128 + experts].astype(jnp.int32),
    )


def solution(mesh):
    rows, copied = P(("seq", "exp"), None), P()
    up, down = P("exp", None, "seq"), P("exp", "seq", None)
    in_specs = (rows, copied, rows, rows) + (copied,) * 12 + (up, down)
    out_specs = (rows, rows) + (copied,) * 12 + (up, down, copied, copied)
    return jax.shard_map(per_device, mesh=mesh, in_specs=in_specs, out_specs=out_specs, check_vma=False)
```

```python
import functools

import jax
import jax.numpy as jnp
from jax import lax
from jax.experimental import pallas as pl
from jax.experimental.pallas import tpu as pltpu
from jax.sharding import PartitionSpec as P

F32 = jnp.float32
BF16 = jnp.bfloat16
EPS = 1e-05
LOG2E = 1.4426950408889634
HALO = 16
RESET = 1e9
AXES = ("seq", "exp")
NN, NT, TN = ((1,), (0,)), ((1,), (1,)), ((0,), (0,))
VMEM_BYTES = 52 << 20
MICROSECONDS = {
    "route": 1, "join": 8, "features": 250, "join_states": 1, "scan": 200, "early": 200, "expert": 60,
    "expert_grads": 300, "mixer_back": 300, "late": 200, "scan_back": 10, "input_back": 11, "finish_late": 8, "finish": 6,
}


class Grid:
    def __init__(self):
        self.seq, self.exp = lax.axis_size("seq"), lax.axis_size("exp")
        self.outer = 4
        self.size = {
            "core": 2,
            "y": self.exp // 2,
            "inner": self.seq // self.outer,
            "outer": self.outer,
        }
        self.total = self.seq * self.exp
        index, step, self.step, self.at = lax.axis_index(AXES), 1, {}, {}
        for name in ("core", "y", "inner", "outer"):
            self.step[name] = step
            self.at[name] = (index // step) % self.size[name]
            step *= self.size[name]
        self.index = index

    def swap(self, block, name, mask):
        return self.swap_bits(block, mask * self.step[name])

    def swap_bits(self, block, bits):
        return lax.ppermute(block, AXES, [(i, i ^ bits) for i in range(self.total)])

    def along(self, block, distance):
        route = [(i - distance, i) for i in range(self.total) if 0 <= i - distance < self.total]
        return lax.ppermute(block, AXES, route)


def tie(*values):
    return lax.optimization_barrier(values)


def outer_reduce_rest(grid, parts, through):
    through, near = tie(through, parts[1])
    near = grid.swap(near, "outer", 1)
    far = grid.swap(parts[2] + through, "outer", 2)
    return parts[0] + near + far


def in_order(parts, place):
    bit = 1
    while bit < len(parts):
        turned = ((place // bit) % 2) == 1
        parts = [jnp.where(turned, parts[i ^ bit], parts[i]) for i in range(len(parts))]
        bit *= 2
    return parts


def rows_of(parts, first, rows):
    return functools.reduce(jnp.add, [lax.dynamic_slice_in_dim(part, first, rows, 0) for part in parts])


def scatter_rows(grid, parts, name, rows, start=0):
    count, place = grid.size[name], grid.at[name]
    rows = rows // count
    piece = lambda s: rows_of(parts, start + (place ^ s) * rows, rows)
    got = [grid.swap(piece(s), name, s) for s in range(1, count)]
    return [piece(0)] + got


def gather_rows(grid, block, name):
    count = grid.size[name]
    if count == 1:
        return block
    parts = [block] + [grid.swap(block, name, s) for s in range(1, count)]
    return jnp.concatenate(in_order(parts, grid.at[name]), axis=0)


def sum_first(grid, parts):
    rows = parts[0].shape[0] // 2
    return scatter_rows(grid, parts, "inner", rows), scatter_rows(grid, parts, "y", rows, rows)


def sum_second(grid, first, second):
    rows = first[0].shape[0]
    first, second = scatter_rows(grid, first, "y", rows), scatter_rows(grid, second, "inner", rows)
    return [jnp.concatenate(pair, axis=0) for pair in zip(first, second)]


def cut_outer(grid, parts):
    columns = parts[0].shape[1] // grid.outer
    return [
        functools.reduce(
            jnp.add,
            [lax.dynamic_slice_in_dim(p, (grid.at["outer"] ^ s) * columns, columns, 1) for p in parts],
        )
        for s in range(grid.outer)
    ]


def sum_outer(grid, parts):
    own, *others = cut_outer(grid, parts)
    return functools.reduce(jnp.add, [grid.swap(part, "outer", s) for s, part in enumerate(others, 1)], own)


def spread_outer(grid, total):
    count = grid.size["outer"]
    parts = [total] + [grid.swap(total, "outer", s) for s in range(1, count)]
    return jnp.concatenate(in_order(parts, grid.at["outer"]), axis=1)


def join_outer(grid, own, near, far, last):
    return jnp.concatenate(in_order([own, near, far, last], grid.at["outer"]), axis=1)


def spread_second(grid, both):
    own = both.shape[0] // 2
    return gather_rows(grid, both[:own], "y"), gather_rows(grid, both[own:], "inner")


def spread_first(grid, first, second):
    return jnp.concatenate([gather_rows(grid, first, "inner"), gather_rows(grid, second, "y")], axis=0)


def join_states_kernel(last, later_ref, total_ref, got_ref, ahead_ref, rate_ref, *outs):
    states = rate_ref.shape[0]
    rows, sums = slice(0, states), slice(states, states + 1)

    def follow(early, late, out):
        out[rows, :] = jnp.exp2(rate_ref[...] * late[sums, :]) * early[rows, :] + late[rows, :]
        out[sums, :] = early[sums, :] + late[sums, :]

    @pl.when(later_ref[0] == 1)
    def _():
        follow(got_ref, ahead_ref, outs[0])
        if not last:
            follow(got_ref, total_ref, outs[1])

    @pl.when(later_ref[0] == 0)
    def _():
        outs[0][...] = ahead_ref[...]
        if not last:
            follow(total_ref, got_ref, outs[1])


def entering(grid, pair, rate, backward, after):
    states = rate.shape[0]
    total, ahead, hop = pair, jnp.zeros_like(pair), 1
    bits = 1
    while bits < grid.total:
        got = grid.swap_bits(total, bits)
        later = ((grid.index // bits) % 2).astype(jnp.int32)
        later = (1 - later if backward else later).reshape(1)
        last = 2 * bits >= grid.total
        whole = pl.BlockSpec(memory_space=pltpu.VMEM)
        ahead, *rest = call(
            functools.partial(join_states_kernel, last),
            [shape(*pair.shape)] * (1 if last else 2),
            (later, total, got, ahead, rate),
            in_specs=[SMEM] + [whole] * 4,
            name="join_states",
        )
        total = rest[0] if rest else None
        if hop in after:
            total = after[hop](total)
        bits, hop = 2 * bits, hop + 1
    return ahead[:states]


def pad_rows(block, rows):
    return jnp.pad(block, ((0, rows - block.shape[0]), (0, 0)))


def core_first(grid, block, cap, tail):
    ny, width = grid.size["y"], 2 * cap
    slots = ny * width
    send = [block[s * width + cap : (s + 1) * width] for s in range(ny)] + ([block[slots:]] if tail else [])
    got = grid.swap(jnp.concatenate(send, axis=0), "core", 1)
    parts = []
    for s in range(ny):
        rows = [block[s * width : s * width + cap], got[s * cap : (s + 1) * cap]]
        if tail:
            ends = [block[slots + 2 * s : slots + 2 * s + 1], got[ny * cap + 2 * s + 1 : ny * cap + 2 * s + 2]]
            rows.append(pad_rows(jnp.concatenate(ends, axis=0), 8))
        parts.append(jnp.concatenate(rows, axis=0))
    return parts


def swap_y(grid, parts):
    return [parts[0]] + [grid.swap(part, "y", s) for s, part in enumerate(parts[1:], 1)]


def core_last(grid, parts, cap, tail):
    ny = grid.size["y"]
    send = [p[cap : 2 * cap] for p in parts]
    if tail:
        send.append(pad_rows(jnp.concatenate([p[2 * cap + 1 : 2 * cap + 2] for p in parts], axis=0), 8))
    got = grid.swap(jnp.concatenate(send, axis=0), "core", 1)
    rows, ends = [], []
    for s, p in enumerate(parts):
        rows += [p[:cap], got[s * cap : (s + 1) * cap]]
        if tail:
            ends += [p[2 * cap : 2 * cap + 1], got[ny * cap + s : ny * cap + s + 1]]
    if tail:
        rows.append(pad_rows(jnp.concatenate(ends, axis=0), 8))
    return jnp.concatenate(rows, axis=0)


def split(value):
    high = value.astype(BF16)
    return high, (value - high.astype(F32)).astype(BF16)


def dot(left, right, dims):
    return lax.dot_general(left, right, (dims, ((), ())), preferred_element_type=F32)


def product(left, right, dims):
    return dot(left[0], right[0], dims) + (dot(left[0], right[1], dims) + dot(left[1], right[0], dims))


def pick(exact, value, dims):
    high, low = split(value)
    return dot(exact, high, dims) + dot(exact, low, dims)


def sigmoid(value):
    return 1.0 / (1.0 + jnp.exp(-value))


def softplus(value):
    small = jnp.exp(-jnp.abs(value))
    series = small * (1.0 - small * (0.5 - small * (1.0 / 3.0 - small * (0.25 - small * 0.2))))
    return jnp.maximum(value, 0.0) + jnp.where(small < 0.03, series, jnp.log(1.0 + small))


def iota(shape, dim):
    return lax.broadcasted_iota(jnp.int32, shape, dim)


def scale_of(value):
    return lax.rsqrt(jnp.mean(value * value, axis=1, keepdims=True) + EPS)


def over_lanes(ref, columns):
    rows = columns.shape[0]
    for t in range(columns.shape[1]):
        ref[t] = jnp.broadcast_to(columns[:, t : t + 1], (rows, 128))


def widen(value, width):
    return jnp.concatenate([value] * (width // 128), axis=1)


def call(kernel, outs, ins, grid=None, in_specs=None, out_specs=None, scratch=(), name=None, aliases=None):
    whole = pl.BlockSpec(memory_space=pltpu.VMEM)
    return pl.pallas_call(
        kernel,
        out_shape=outs,
        grid=grid or (),
        in_specs=in_specs or [whole] * len(ins),
        out_specs=out_specs or jax.tree.map(lambda _: whole, outs),
        scratch_shapes=scratch,
        name=name,
        cost_estimate=pl.CostEstimate(
            flops=int(MICROSECONDS[name] * 1.1e9), transcendentals=0, bytes_accessed=int(MICROSECONDS[name] * 1e6)
        ),
        input_output_aliases=aliases or {},
        compiler_params=pltpu.CompilerParams(vmem_limit_bytes=VMEM_BYTES),
    )(*ins)


def shape(*dims, dtype=F32):
    return jax.ShapeDtypeStruct(dims, dtype)


SMEM = pl.BlockSpec(memory_space=pltpu.SMEM)


def full(*dims):
    return pl.BlockSpec(dims, lambda *_: (0,) * len(dims))


def route_kernel(experts, cap, me_ref, ids_ref, grad_ref, sent_ref, table_ref, rank_ref, load_ref):
    ids = ids_ref[...]
    tokens = ids.shape[0]
    chosen = (ids == iota((tokens, 128), 1)).astype(F32)
    before = (iota((tokens, tokens), 0) > iota((tokens, tokens), 1)).astype(BF16)
    rank = jnp.sum(dot(before, chosen.astype(BF16), NN) * chosen, axis=1, keepdims=True)
    kept = (rank < cap).astype(F32)
    place = jnp.where(rank < cap, ((ids ^ me_ref[0]) * cap).astype(F32) + rank, -1.0)
    row = jnp.broadcast_to(place, (tokens, tokens)).T
    slots = experts * cap
    table = (iota((slots, tokens), 0).astype(F32) == jnp.broadcast_to(row[0:1], (slots, tokens))).astype(F32)
    table = table.astype(BF16)
    table_ref[...] = table
    rank_ref[...] = rank
    sent_ref[...] = pick(table, grad_ref[...], NN)
    load_ref[...] = jnp.zeros_like(load_ref)
    load_ref[0:1, 0:128] = jnp.sum(chosen, axis=0, keepdims=True)
    load_ref[0:1, 128:256] = jnp.sum(chosen * (1.0 - kept), axis=0, keepdims=True)


def join_kernel(x_ref, halo_ref, gain_ref, weight_ref, joined_ref, high, low):
    @pl.when(pl.program_id(0) == 0)
    def _():
        x = jnp.concatenate([halo_ref[...], x_ref[...]], axis=0)
        high[...], low[...] = split(x * scale_of(x) * gain_ref[...])

    joined_ref[...] = product((high[...], low[...]), split(weight_ref[...]), NN)


def features_kernel(
    rank_n,
    states,
    inner_ref,
    since_ref,
    conv_w_ref,
    conv_b_ref,
    state_proj_ref,
    step_proj_ref,
    step_bias_ref,
    rate_ref,
    conv_ref,
    act_ref,
    pre_ref,
    steps_ref,
    masked_ref,
    drive_ref,
    proj_ref,
    pair_ref,
    in_lanes,
):
    tokens, width = act_ref.shape
    taps = conv_w_ref.shape[0]
    since = since_ref[...]
    conv = jnp.broadcast_to(conv_b_ref[...], (tokens, width))
    for k in range(taps):
        valid = (since >= taps - 1 - k).astype(F32)
        first = HALO - taps + 1 + k
        conv = conv + inner_ref[first : first + tokens, :] * valid * conv_w_ref[k : k + 1, :]
    act = conv * sigmoid(conv)
    conv_ref[...] = conv
    act_ref[...] = act
    proj = product(split(state_proj_ref[...]), split(act), NT)
    proj_ref[...] = proj
    pre = product(split(proj[:rank_n]), split(step_proj_ref[...]), TN) + step_bias_ref[...]
    pre_ref[...] = pre
    steps = softplus(pre)
    steps_ref[...] = steps
    masked = jnp.where(since == 0, RESET, steps)
    masked_ref[...] = masked
    drive_ref[...] = steps * act
    pair_ref[states : states + 1, :] = jnp.sum(masked, axis=0, keepdims=True)
    over_lanes(in_lanes, proj[rank_n : rank_n + states])
    chunk = 512
    for c in range(width // chunk):
        part = slice(c * chunk, (c + 1) * chunk)
        rate = rate_ref[:, part]

        def eight(group, state):
            for i in range(8):
                t = group * 8 + i
                decay = jnp.exp2(masked_ref[pl.ds(t, 1), part] * rate)
                state = decay * state + drive_ref[pl.ds(t, 1), part] * widen(in_lanes[t], chunk)
            return state

        pair_ref[0:states, part] = lax.fori_loop(0, tokens // 8, eight, jnp.zeros((states, chunk), F32))


def slot_tables(slots, cap, experts):
    slot = iota((slots, 8), 0)
    first = sum((slot >= cap * e).astype(jnp.int32) for e in range(1, experts))
    block = (first == iota((slots, 8), 1)).astype(F32)
    slot = iota((slots, 128), 0)
    first = sum(((slot >= cap * e).astype(jnp.int32) for e in range(1, experts)))
    within = (slot - first * cap == iota((slots, 128), 1)).astype(F32)
    return block, within


def scan_kernel(
    rank_n,
    states,
    experts,
    cap,
    me_ref,
    masked_ref,
    drive_ref,
    act_ref,
    gate_z_ref,
    start_ref,
    rate_ref,
    skip_ref,
    proj_ref,
    out_proj_ref,
    x_ref,
    gain_ref,
    router_ref,
    ids_ref,
    rank_ref,
    table_ref,
    scan_ref,
    history_ref,
    resid_ref,
    sent_ref,
    probs_ref,
    gate_ref,
    in_lanes,
    out_lanes,
    total,
):
    tokens, chunk = masked_ref.shape
    step = pl.program_id(0)

    @pl.when(step == 0)
    def _():
        over_lanes(in_lanes, proj_ref[rank_n : rank_n + states, :])
        over_lanes(out_lanes, proj_ref[rank_n + states : rank_n + 2 * states, :])
        total[...] = x_ref[...]

    rate = rate_ref[...]

    def eight(group, state):
        for i in range(8):
            t = group * 8 + i
            decay = jnp.exp2(masked_ref[pl.ds(t, 1), :] * rate)
            state = decay * state + drive_ref[pl.ds(t, 1), :] * widen(in_lanes[t], chunk)
            history_ref[t] = state
            scan_ref[pl.ds(t, 1), :] = jnp.sum(state * widen(out_lanes[t], chunk), axis=0, keepdims=True)
        return state

    lax.fori_loop(0, tokens // 8, eight, start_ref[...])
    gate_z = gate_z_ref[HALO:, :]
    mixed = (scan_ref[...] + skip_ref[...] * act_ref[...]) * (gate_z * sigmoid(gate_z))
    total[...] += product(split(mixed), split(out_proj_ref[...]), NN)

    @pl.when(step == pl.num_programs(0) - 1)
    def _():
        resid = total[...]
        resid_ref[...] = resid
        normed = resid * scale_of(resid) * gain_ref[...]
        logits = product(split(normed), split(router_ref[...]), NT)
        known = iota((tokens, 8), 1) < experts
        logits = jnp.where(known, logits, -1e30)
        raised = jnp.exp(logits - jnp.max(logits, axis=1, keepdims=True))
        raised = jnp.where(known, raised, 0.0)
        probs = raised / jnp.sum(raised, axis=1, keepdims=True)
        probs_ref[...] = probs
        ids = ids_ref[...]
        gate = jnp.sum(jnp.where(ids == iota((tokens, 8), 1), probs, 0.0), axis=1, keepdims=True)
        gate_ref[...] = gate
        slots = experts * cap
        sent_ref[0:slots, :] = pick(table_ref[...], normed, NN)
        sent_ref[slots:, :] = jnp.zeros((8, sent_ref.shape[1]), F32)
        rank = rank_ref[...].astype(jnp.int32)
        to_block = jnp.where(((ids ^ me_ref[0]) == iota((tokens, 8), 1)) & (rank < cap), gate, 0.0)
        at_rank = (rank == iota((tokens, 128), 1)).astype(BF16)
        high, low = split(to_block)
        rest = (to_block - high.astype(F32) - low.astype(F32)).astype(BF16)
        rows = dot(high, at_rank, TN) + (dot(low, at_rank, TN) + dot(rest, at_rank, TN))
        sent_ref[slots:, 0:128] = rows


def early_kernel(pieces, slices, *refs):
    grads, downs, outs = refs[:pieces], refs[pieces : pieces + slices], refs[pieces + slices :]
    downs = [split(d[...]) for d in downs]
    for p in range(pieces):
        grad = split(grads[p][...])
        for i in range(slices):
            outs[p][i] = product(grad, downs[i], NT)


def gelu_parts(value):
    inner = 0.7978845608 * (value + 0.044715 * value * value * value)
    tanh = jnp.tanh(inner)
    slope = 0.5 * (1.0 + tanh) + 0.5 * value * (1.0 - tanh * tanh) * 0.7978845608 * (
        1.0 + 3.0 * 0.044715 * value * value
    )
    return 0.5 * value * (1.0 + tanh), slope


def expert_kernel(parts, slices, cap, *refs):
    tokens, ups, pulled_ref = refs[:parts], refs[parts : parts + slices], refs[parts + slices]
    backs, hidden_ref, grad_ref = refs[parts + slices + 1 : -2], refs[-2], refs[-1]
    width = 2 * cap
    slots, depth = parts * width, tokens[0].shape[1]
    block, within = slot_tables(width, cap, 2)
    within = within.astype(BF16)
    rows = split(jnp.concatenate([t[0:width, :] for t in tokens], axis=0))
    back = jnp.zeros((slots, depth), F32)
    to_gate = jnp.zeros((slots, 1), F32)
    for i in range(slices):
        up = split(ups[i][...])
        hidden, slope = gelu_parts(product(rows, up, NN))
        pull = pulled_ref[i]
        grad = pull * slope
        hidden_ref[i] = hidden
        grad_ref[i] = grad
        to_gate += jnp.sum(hidden * pull, axis=1, keepdims=True)
        back += product(split(grad), up, NT)
    for p in range(parts):
        part = slice(p * width, (p + 1) * width)
        backs[p][0:width, :] = back[part]
        backs[p][width:, :] = jnp.zeros((8, depth), F32)
        mine = block * to_gate[part]
        high, low = split(mine)
        rest = (mine - high.astype(F32) - low.astype(F32)).astype(BF16)
        backs[p][width:, 0:128] = dot(high, within, TN) + (dot(low, within, TN) + dot(rest, within, TN))


def expert_grads_kernel(pieces, parts, slices, cap, *refs):
    tokens, refs = refs[: pieces * parts], refs[pieces * parts :]
    grads, hiddens, pulls = (refs[i * pieces : (i + 1) * pieces] for i in range(3))
    downs, outs = refs[3 * pieces : 3 * pieces + slices], refs[3 * pieces + slices :]
    results, up_outs, down_outs = outs[:pieces], outs[pieces : pieces + slices], outs[pieces + slices :]
    width = 2 * cap
    downs = [split(d[...]) for d in downs]
    block, within = slot_tables(width, cap, 2)
    within = within.astype(BF16)
    for p in range(pieces):
        rows, gates = [], []
        for token in tokens[p * parts : (p + 1) * parts]:
            ends = token[width:, 0:128]
            high, low = split(ends)
            rest = (ends - high.astype(F32) - low.astype(F32)).astype(BF16)
            spread = dot(within, high, NT) + (dot(within, low, NT) + dot(within, rest, NT))
            gates.append(jnp.sum(spread * block, axis=1, keepdims=True))
            rows.append(token[0:width, :] * gates[-1])
        rows = split(jnp.concatenate(rows, axis=0))
        gated = split(grads[p][...] * jnp.concatenate(gates, axis=0))
        total = None
        for i in range(slices):
            hidden = split(hiddens[p][i])
            part = product(hidden, downs[i], NN)
            total = part if total is None else total + part
            up = product(rows, split(pulls[p][i]), TN)
            down = product(hidden, gated, TN)
            if p == 0:
                up_outs[i][...] = up
                down_outs[i][...] = down
            else:
                up_outs[i][...] += up
                down_outs[i][...] += down
        results[p][...] = total


def silu_parts(value):
    sig = sigmoid(value)
    return value * sig, sig * (1.0 + value * (1.0 - sig))


def mixer_back_kernel(
    rank_n,
    states,
    experts,
    cap,
    me_ref,
    back_ref,
    table_ref,
    gate_ref,
    probs_ref,
    ids_ref,
    rank_ref,
    resid_ref,
    grad_ref,
    gain_ref,
    router_ref,
    out_proj_ref,
    gate_z_ref,
    scan_ref,
    act_ref,
    skip_ref,
    masked_ref,
    rate_ref,
    proj_ref,
    steps_row_ref,
    grad_resid_ref,
    small_ref,
    grad_scan_ref,
    grad_gate_ref,
    grad_skip_ref,
    pair_ref,
    out_lanes,
    high,
    low,
):
    tokens, chunk = masked_ref.shape

    @pl.when(pl.program_id(0) == 0)
    def _():
        over_lanes(out_lanes, proj_ref[rank_n + states : rank_n + 2 * states, :])
        slots = experts * cap
        ids, rank = ids_ref[...], rank_ref[...].astype(jnp.int32)
        back = pick(table_ref[...], back_ref[0:slots, :], TN)
        at_rank = (rank == iota((tokens, 128), 1)).astype(BF16)
        ends = back_ref[slots:, 0:128]
        first, second = split(ends)
        third = (ends - first.astype(F32) - second.astype(F32)).astype(BF16)
        spread = dot(at_rank, first, NT) + (dot(at_rank, second, NT) + dot(at_rank, third, NT))
        mine = ((ids ^ me_ref[0]) == iota((tokens, 8), 1)) & (rank < cap)
        grad_gate = jnp.sum(jnp.where(mine, spread, 0.0), axis=1, keepdims=True)
        probs = probs_ref[...]
        grad_probs = jnp.where(ids == iota((tokens, 8), 1), grad_gate, 0.0)
        grad_logits = probs * (grad_probs - jnp.sum(probs * grad_probs, axis=1, keepdims=True))
        resid, gain = resid_ref[...], gain_ref[...]
        scale = scale_of(resid)
        normed = resid * scale * gain
        logits_two = split(grad_logits)
        grad_normed = gate_ref[...] * back + product(logits_two, split(router_ref[...]), NN)
        small_ref[...] = jnp.zeros_like(small_ref)
        small_ref[0:8, :] = product(logits_two, split(normed), TN)
        small_ref[8:9, :] = jnp.sum(grad_normed * resid * scale, axis=0, keepdims=True)
        pulled = gain * grad_normed
        grad_resid = (
            grad_ref[...]
            + scale * pulled
            - resid * (scale * scale * scale) * jnp.mean(pulled * resid, axis=1, keepdims=True)
        )
        grad_resid_ref[...] = grad_resid
        high[...], low[...] = split(grad_resid)

    grad_mixed = product((high[...], low[...]), split(out_proj_ref[...]), NT)
    silu, slope = silu_parts(gate_z_ref[HALO:, :])
    act = act_ref[...]
    grad_scan = grad_mixed * silu
    grad_scan_ref[...] = grad_scan
    grad_gate_ref[...] = grad_mixed * (scan_ref[...] + skip_ref[...] * act) * slope
    grad_skip_ref[...] = jnp.sum(grad_scan * act, axis=0, keepdims=True)
    rate = rate_ref[...]

    def eight(group, state):
        for i in range(8):
            t = tokens - 1 - (group * 8 + i)
            decay = jnp.exp2(masked_ref[pl.ds(t, 1), :] * rate)
            state = decay * (state + grad_scan_ref[pl.ds(t, 1), :] * widen(out_lanes[t], chunk))
        return state

    pair_ref[0:states, :] = lax.fori_loop(0, tokens // 8, eight, jnp.zeros((states, chunk), F32))
    pair_ref[states : states + 1, :] = steps_row_ref[...]


def late_kernel(
    which_ref, scan_ref, act_ref, skip_ref, gate_z_ref, grad_resid_ref, x_ref, gain_ref, grad_gate_ref, *refs
):
    high, low = refs[-2:]
    if len(refs) == 5:
        weight_ref, out_ref, normed_ref = refs[:3]
    else:
        weight_ref, out_ref, normed_ref = None, refs[0], None

    @pl.when(pl.program_id(0) == 0)
    def _():
        @pl.when(which_ref[0] == 0)
        def _():
            high[...], low[...] = split(grad_resid_ref[...])

        @pl.when(which_ref[0] == 1)
        def _():
            x = x_ref[...]
            high[...], low[...] = split(x * scale_of(x) * gain_ref[...])

        if normed_ref is not None:
            normed_ref[...] = jnp.zeros_like(normed_ref)

    @pl.when(which_ref[0] == 0)
    def _():
        gate_z = gate_z_ref[HALO:, :]
        mixed = (scan_ref[...] + skip_ref[...] * act_ref[...]) * (gate_z * sigmoid(gate_z))
        out_ref[...] = product(split(mixed), (high[...], low[...]), TN)

    @pl.when(which_ref[0] == 1)
    def _():
        out_ref[...] = product((high[...], low[...]), split(grad_gate_ref[...]), TN)

    if normed_ref is not None:
        normed_ref[...] += product(split(grad_gate_ref[...]), split(weight_ref[...]), NT)


def scan_back_kernel(
    rank_n,
    states,
    masked_ref,
    steps_ref,
    drive_ref,
    act_ref,
    pre_ref,
    grad_scan_ref,
    skip_ref,
    history_ref,
    before_ref,
    start_ref,
    end_ref,
    rate_ref,
    proj_ref,
    step_proj_ref,
    *refs,
):
    (
        grad_act_ref, grad_pre_ref, grad_decay_ref, grad_proj_ref,
        in_lanes, out_lanes, grad_drive, grad_steps, at_in, at_out, carried_ref, decays_ref, sums_ref,
    ) = refs[-13:]
    tokens, chunk = masked_ref.shape
    block = history_ref.shape[0]
    step, blocks = pl.program_id(0), pl.num_programs(0)
    first = (blocks - 1 - step) * block

    @pl.when(step == 0)
    def _():
        over_lanes(in_lanes, proj_ref[rank_n : rank_n + states, :])
        over_lanes(out_lanes, proj_ref[rank_n + states : rank_n + 2 * states, :])
        carried_ref[...] = end_ref[...]
        decays_ref[...] = jnp.zeros_like(decays_ref)
        sums_ref[...] = jnp.zeros_like(sums_ref)

    rate = rate_ref[...]
    entering_state = jnp.where(first == 0, start_ref[...], before_ref[7])

    def narrow(value):
        return functools.reduce(jnp.add, [value[:, c : c + 128] for c in range(0, chunk, 128)])

    def one(local, before, carried):
        state, decays = carried
        t = first + local
        masked = masked_ref[pl.ds(t, 1), :]
        grad = grad_scan_ref[pl.ds(t, 1), :]
        decay = jnp.exp2(masked * rate)
        state = state + grad * widen(out_lanes[t], chunk)
        at_out[local] = narrow(history_ref[local] * grad)
        at_in[local] = narrow(state * drive_ref[pl.ds(t, 1), :])
        grad_drive[pl.ds(t, 1), :] = jnp.sum(state * widen(in_lanes[t], chunk), axis=0, keepdims=True)
        state = decay * state
        pulled = state * before
        grad_steps[pl.ds(t, 1), :] = jnp.sum(pulled * rate, axis=0, keepdims=True)
        return state, decays + pulled * masked

    def eight(group, carried):
        for i in range(8):
            local = block - 1 - (group * 8 + i)
            carried = one(local, history_ref[local - 1], carried)
        return carried

    carried = lax.fori_loop(0, block // 8 - 1, eight, (carried_ref[...], decays_ref[...]))
    for local in range(7, 0, -1):
        carried = one(local, history_ref[local - 1], carried)
    carried_ref[...], decays_ref[...] = one(0, entering_state, carried)

    ones = jnp.ones((128, 128), BF16)
    lane = iota((states, 128), 1)
    for i, held in enumerate((at_in, at_out)):
        high, low = split(held[...].reshape(block * states, 128))
        spread = (dot(high, ones, NN) + dot(low, ones, NN)).reshape(block, states, 128)
        total = sums_ref[i]
        for local in range(block):
            total = jnp.where(lane == first + local, spread[local], total)
        sums_ref[i] = total

    @pl.when(step == blocks - 1)
    def _():
        grad_decay_ref[...] = decays_ref[...] * (rate * (1.0 / LOG2E))
        steps, act = steps_ref[...], act_ref[...]
        grad_act_ref[...] = skip_ref[...] * grad_scan_ref[...] + grad_drive[...] * steps
        grad_pre = (grad_steps[...] * (1.0 / LOG2E) + grad_drive[...] * act) * sigmoid(pre_ref[...])
        grad_pre_ref[...] = grad_pre
        grad_proj_ref[0:rank_n, :] = product(split(step_proj_ref[...]), split(grad_pre), NT)
        grad_proj_ref[rank_n : rank_n + states, :] = sums_ref[0]
        grad_proj_ref[rank_n + states : rank_n + 2 * states, :] = sums_ref[1]


def input_back_kernel(
    rank_n,
    states,
    core_ref,
    proj_a_ref,
    proj_b_ref,
    proj_c_ref,
    proj_ref,
    state_proj_ref,
    act_ref,
    grad_act_ref,
    grad_pre_ref,
    conv_ref,
    inner_ref,
    conv_w_ref,
    since_ref,
    weight_ref,
    x_ref,
    halo_ref,
    gain_ref,
    grad_gate_normed_ref,
    grad_resid_ref,
    grad_decay_ref,
    grad_skip_ref,
    small_ref,
    keep_ref,
    send_ref,
    input_ref,
    edge_ref,
    high,
    low,
    grad_inner,
    total,
):
    tokens, chunk = act_ref.shape
    depth = x_ref.shape[1]
    half = depth // 2
    taps = conv_w_ref.shape[0]
    step = pl.program_id(0)

    @pl.when(step == 0)
    def _():
        x = jnp.concatenate([halo_ref[...], x_ref[...]], axis=0)
        high[...], low[...] = split(x * scale_of(x) * gain_ref[...])
        total[...] = jnp.zeros_like(total)

    act, grad_pre = split(act_ref[...]), grad_pre_ref[...]
    grad_proj = split(proj_a_ref[...] + proj_b_ref[...] + proj_c_ref[...])
    grad_act = grad_act_ref[...] + product(grad_proj, split(state_proj_ref[...]), TN)
    _, slope = silu_parts(conv_ref[...])
    grad_conv = grad_act * slope
    since = since_ref[...]
    grad_inner[...] = jnp.zeros_like(grad_inner)
    rows = []
    for k in range(taps):
        valid = (since >= taps - 1 - k).astype(F32)
        first = HALO - taps + 1 + k
        held = grad_conv * valid
        rows.append(jnp.sum(held * inner_ref[first : first + tokens, :], axis=0, keepdims=True))
        grad_inner[first : first + tokens, :] += held * conv_w_ref[k : k + 1, :]
    rows.append(jnp.sum(grad_conv, axis=0, keepdims=True))
    rows.append(jnp.sum(grad_pre, axis=0, keepdims=True))
    rows.append(grad_skip_ref[...])
    grads = split(grad_inner[...])
    total[...] += product(grads, split(weight_ref[...]), NT)
    of_state_proj = product(grad_proj, act, NN)
    of_step_proj = product(split(proj_ref[0:rank_n, :]), split(grad_pre), NN)

    def first_half(out_ref):
        out_ref[0:half, :] = product((high[:, 0:half], low[:, 0:half]), grads, TN)
        at = half + 2 * states + rank_n
        out_ref[half:at, :] = of_state_proj
        out_ref[at : at + states, :] = grad_decay_ref[...]
        if at + states < out_ref.shape[0]:
            out_ref[at + states :, :] = jnp.zeros((out_ref.shape[0] - at - states, chunk), F32)

    def second_half(out_ref):
        out_ref[0:half, :] = product((high[:, half:], low[:, half:]), grads, TN)
        out_ref[half : half + rank_n, :] = of_step_proj
        at = half + rank_n
        out_ref[at:, :] = jnp.zeros((out_ref.shape[0] - at, chunk), F32)
        for i, row in enumerate(rows):
            out_ref[at + i : at + i + 1, :] = row

    @pl.when(core_ref[0] == 0)
    def _():
        first_half(keep_ref)
        second_half(send_ref)

    @pl.when(core_ref[0] == 1)
    def _():
        second_half(keep_ref)
        first_half(send_ref)

    @pl.when(step == pl.num_programs(0) - 1)
    def _():
        gain = gain_ref[...]

        def rows_back(x, grad):
            scale = scale_of(x)
            pulled = gain * grad
            back = scale * pulled - x * (scale * scale * scale) * jnp.mean(pulled * x, axis=1, keepdims=True)
            return back, jnp.sum(grad * x * scale, axis=0, keepdims=True)

        edge, edge_gain = rows_back(halo_ref[...], total[0:HALO, :])
        own, own_gain = rows_back(x_ref[...], total[HALO:, :] + grad_gate_normed_ref[...])
        edge_ref[...] = edge
        input_ref[...] = grad_resid_ref[...] + own
        small = jnp.concatenate([small_ref[0:10, :], edge_gain + own_gain], axis=0)

        def place_small(out_ref):
            at = half + rank_n + 8
            out_ref[at : at + 11, :] = small[:, 0:chunk]
            out_ref[at + 16 : at + 27, 0 : depth - chunk] = small[:, chunk:]

        @pl.when(core_ref[0] == 0)
        def _():
            place_small(send_ref)

        @pl.when(core_ref[0] == 1)
        def _():
            place_small(keep_ref)


def finish_late_kernel(core_ref, first_ref, second_ref, got_first_ref, got_second_ref, in_ref, out_ref):
    depth = out_ref.shape[2]
    step = pl.program_id(0)

    def write(gate, out):
        in_ref[...] = gate
        out_ref[0] = out[:, 0:depth]
        out_ref[1] = out[:, depth:]

    for i, (own, got) in enumerate(((first_ref, got_first_ref), (second_ref, got_second_ref))):

        @pl.when((core_ref[0] == 0) & (step == i))
        def _():
            write(own[...], got[...])

        @pl.when((core_ref[0] == 1) & (step == i))
        def _():
            write(got[...], own[...])


def finish_kernel(
    rank_n, states, taps, core_ref, first_ref, second_ref, got_first_ref, got_second_ref, _,
    in_ref, state_proj_ref, step_proj_ref, decay_ref, conv_w_ref, rows_ref, small_ref,
):
    depth = in_ref.shape[0]
    half, quarter = depth // 2, first_ref.shape[0]
    rest = half - quarter

    def first_half(one, two):
        in_ref[0:quarter, :] = one[...]
        in_ref[quarter:half, :] = two[0:rest, :]
        at = rest + 2 * states + rank_n
        state_proj_ref[...] = two[rest:at, :].T
        decay_ref[...] = two[at : at + states, :].T

    def second_half(one, two):
        in_ref[half : half + quarter, :] = one[...]
        in_ref[half + quarter :, :] = two[0:rest, :]
        step_proj_ref[...] = two[rest : rest + rank_n, :]
        at = rest + rank_n
        conv_w_ref[...] = two[at : at + taps, :]
        rows_ref[...] = two[at : at + 8, :]
        small_ref[...] = two[at + 8 : at + 40, :]

    @pl.when(core_ref[0] == 0)
    def _():
        first_half(first_ref, second_ref)
        second_half(got_first_ref, got_second_ref)

    @pl.when(core_ref[0] == 1)
    def _():
        first_half(got_first_ref, got_second_ref)
        second_half(first_ref, second_ref)


def per_device(
    block_input,
    seq_lengths,
    expert_ids,
    output_grad,
    mixer_gain,
    in_proj,
    conv_weight,
    conv_bias,
    state_proj,
    step_proj,
    step_bias,
    decay_log,
    skip_gain,
    out_proj,
    router_gain,
    router,
    expert_up,
    expert_down,
):
    grid = Grid()
    tokens, depth = block_input.shape
    taps, width = conv_weight.shape
    rank_n, states, experts = step_proj.shape[0], decay_log.shape[1], router.shape[1]
    cap = (5 * tokens + 4 * experts - 1) // (4 * experts)
    slots, hidden = experts * cap, expert_up.shape[2]
    chunk = 512
    chunks = width // chunk
    pieces, slices = grid.size["outer"], grid.size["inner"]
    token_block = 64
    blocks = tokens // token_block
    me = lax.axis_index("exp").astype(jnp.int32).reshape(1)
    ext = HALO + tokens

    halo = grid.along(block_input[tokens - HALO :], 1)

    count = seq_lengths.shape[0]
    earlier = jnp.arange(count)[:, None] > jnp.arange(count)[None, :]
    starts = jnp.sum(jnp.where(earlier, seq_lengths[None, :], 0), axis=1)
    position = grid.index * tokens + jnp.arange(tokens, dtype=jnp.int32)
    own_start = jnp.max(jnp.where(starts[None, :] <= position[:, None], starts[None, :], 0), axis=1)
    since = (position - own_start)[:, None]
    rate = -jnp.exp(decay_log.T) * LOG2E
    state_proj_t = state_proj.T
    router_t = pad_rows(router.T, 8)
    row = lambda vector: vector.reshape(1, -1)

    sent_grads, table, rank, loads = call(
        functools.partial(route_kernel, experts, cap),
        [shape(slots, depth), shape(slots, tokens, dtype=BF16), shape(tokens, 1), shape(8, depth)],
        (me, expert_ids, output_grad),
        in_specs=[SMEM] + [pl.BlockSpec(memory_space=pltpu.VMEM)] * 2,
        name="route",
    )
    halo, sent_grads = tie(halo, sent_grads)
    held_grads = core_first(grid, sent_grads, cap, False)
    up, down = expert_up[0], expert_down[0]
    up_rows = depth // 2
    downs = [down] + [grid.swap(down, "inner", s) for s in range(1, slices)]

    block = lambda c, *_: (0, c)
    joined = call(
        join_kernel,
        shape(ext, 2 * width),
        (block_input, halo, row(mixer_gain), in_proj),
        grid=(2 * chunks,),
        in_specs=[full(tokens, depth), full(HALO, depth), full(1, depth), pl.BlockSpec((depth, chunk), block)],
        out_specs=pl.BlockSpec((ext, chunk), block),
        scratch=[pltpu.VMEM((ext, depth), BF16)] * 2,
        name="join",
    )
    joined, *held_grads = tie(joined, *swap_y(grid, held_grads))
    own_grads = jnp.concatenate(held_grads, axis=0)
    joined, own_grads = tie(joined, own_grads)
    near_grads, far_grads = grid.swap(own_grads, "outer", 1), grid.swap(own_grads, "outer", 2)
    conv, act, pre, steps, masked, drive, proj, pair = call(
        functools.partial(features_kernel, rank_n, states),
        [shape(tokens, width)] * 6 + [shape(rank_n + 2 * states, tokens), shape(states + 1, width)],
        (joined, since, conv_weight, row(conv_bias), state_proj_t, step_proj, row(step_bias), rate),
        grid=(1,),
        in_specs=[
            full(ext, width),
            full(tokens, 1),
            full(taps, width),
            full(1, width),
            full(rank_n + 2 * states, width),
            full(rank_n, width),
            full(1, width),
            full(states, width),
        ],
        out_specs=[full(tokens, width)] * 6 + [full(rank_n + 2 * states, tokens), full(states + 1, width)],
        scratch=[pltpu.VMEM((tokens, states, 128), F32)],
        name="features",
    )
    pair, *downs = tie(pair, *downs)
    held = {}

    def third(total):
        total, held["near"], held["far"] = tie(total, near_grads, far_grads)
        return total

    start = entering(grid, pair, rate, False, {2: third})
    start, near_grads, far_grads = tie(start, held["near"], held["far"])
    up_top = [grid.swap(up[:up_rows], "inner", s) for s in range(1, slices)]
    last_grads = grid.swap(far_grads, "outer", 1)
    tok = pl.BlockSpec((tokens, chunk), block)
    gate_half = pl.BlockSpec((ext, chunk), lambda c, *_: (0, chunks + c))
    one_row = pl.BlockSpec((1, chunk), block)
    state_rows = pl.BlockSpec((states, chunk), block)
    history_block = pl.BlockSpec((tokens, states, chunk), lambda c: (0, 0, c))
    out_rows = pl.BlockSpec((chunk, depth), lambda c, *_: (c, 0))
    proj_full = full(rank_n + 2 * states, tokens)
    lanes = pltpu.VMEM((tokens, states, 128), F32)
    scan, history, resid, sent, probs, gate = call(
        functools.partial(scan_kernel, rank_n, states, experts, cap),
        [
            shape(tokens, width),
            shape(tokens, states, width),
            shape(tokens, depth),
            shape(slots + 8, depth),
            shape(tokens, 8),
            shape(tokens, 1),
        ],
        (
            me, masked, drive, act, joined, start, rate, row(skip_gain), proj, out_proj, block_input,
            row(router_gain), router_t, expert_ids, rank, table,
        ),
        grid=(chunks,),
        in_specs=[
            SMEM, tok, tok, tok, gate_half, state_rows, state_rows, one_row, proj_full, out_rows,
            full(tokens, depth), full(1, depth), full(8, depth), full(tokens, 1), full(tokens, 1),
            full(slots, tokens),
        ],
        out_specs=[
            tok, history_block, full(tokens, depth), full(slots + 8, depth), full(tokens, 8), full(tokens, 1),
        ],
        scratch=[lanes, lanes, pltpu.VMEM((tokens, depth), F32)],
        name="scan",
    )

    sent, last_grads, up_top, up_bottom = tie(sent, last_grads, up_top, up[up_rows:])
    up_bottom = [grid.swap(up_bottom, "inner", s) for s in range(1, slices)]
    own_tokens, last_grads = tie(core_first(grid, sent, cap, True), last_grads)
    grad_pieces = [own_grads, near_grads, far_grads, last_grads]
    pulled = call(
        functools.partial(early_kernel, pieces, slices),
        [shape(slices, slots, hidden)] * pieces,
        (*grad_pieces, *downs),
        name="early",
    )
    parts = grid.size["y"]
    outer_swap = lambda blocks, mask: [grid.swap(block, "outer", mask) for block in blocks]
    near_first, far_first = outer_swap(own_tokens[:1], 1), outer_swap(own_tokens[:1], 2)
    own_tokens, pulled, up_bottom = tie(swap_y(grid, own_tokens), pulled, up_bottom)
    ups = [up] + [jnp.concatenate(pair, axis=0) for pair in zip(up_top, up_bottom)]
    near_second, far_second = outer_swap(own_tokens[1:], 1), outer_swap(own_tokens[1:], 2)

    def expert(rows, pulled_rows):
        *outs, hidden_rows, pull_rows = call(
            functools.partial(expert_kernel, parts, slices, cap),
            [shape(2 * cap + 8, depth)] * parts + [shape(slices, slots, hidden)] * 2,
            (*rows, *ups, pulled_rows),
            name="expert",
        )
        return outs, hidden_rows, pull_rows

    own_outs = expert(own_tokens, pulled[0])
    near_first, far_first, own_outs = tie(near_first, far_first, own_outs)
    last_first = outer_swap(far_first, 1)
    near_second, far_second = tie(near_second, far_second)
    last_second = outer_swap(far_second, 1)
    near_tokens, far_tokens = near_first + near_second, far_first + far_second
    near_outs, far_outs = expert(near_tokens, pulled[1]), expert(far_tokens, pulled[2])
    last_first, last_second, near_outs, far_outs = tie(last_first, last_second, near_outs, far_outs)
    last_tokens = last_first + last_second
    last_outs = expert(last_tokens, pulled[3])
    token_pieces = [own_tokens, near_tokens, far_tokens, last_tokens]
    backs, hiddens, pulls = zip(own_outs, near_outs, far_outs, last_outs)
    back_through = outer_swap(backs[3][1:], 1)
    back_through, last_zero = tie(back_through, backs[3][0])
    zero_through = grid.swap(last_zero, "outer", 1)
    back_parts = [
        outer_reduce_rest(grid, [b[part] for b in backs], back_through[part - 1]) for part in range(1, parts)
    ]
    outs = call(
        functools.partial(expert_grads_kernel, pieces, parts, slices, cap),
        [shape(slots, depth)] * pieces + [shape(depth, hidden)] * slices + [shape(hidden, depth)] * slices,
        (*sum(token_pieces, []), *grad_pieces, *hiddens, *pulls, *downs),
        name="expert_grads",
    )
    back_parts, zero_through, zero, outs = tie(back_parts, zero_through, [b[0] for b in backs], outs)
    first_part = outer_reduce_rest(grid, zero, zero_through)
    back_parts = swap_y(grid, [None] + back_parts)[1:]
    first_part, back_parts = tie(first_part, back_parts)
    back = core_last(grid, [first_part] + back_parts, cap, True)
    results, up_grads, down_grads = outs[:pieces], outs[pieces : pieces + slices], outs[pieces + slices :]
    halves = lambda array: [array[: array.shape[0] // 2], array[array.shape[0] // 2 :]]
    ups_sent, downs_sent = ([halves(g) for g in grads[1:]] for grads in (up_grads, down_grads))

    def inner_swaps(sent, half):
        return [grid.swap(pair[half], "inner", s) for s, pair in enumerate(sent, 1)]

    up_first = inner_swaps(ups_sent, 0)
    back, last_result, ups_sent = tie(back, results[3], ups_sent)
    through = grid.swap(last_result, "outer", 1)
    up_second = inner_swaps(ups_sent, 1)

    grad_resid, small, grad_scan, grad_gate, grad_skip, back_pair = call(
        functools.partial(mixer_back_kernel, rank_n, states, experts, cap),
        [
            shape(tokens, depth),
            shape(16, depth),
            shape(tokens, width),
            shape(tokens, width),
            shape(1, width),
            shape(states + 1, width),
        ],
        (
            me, back, table, gate, probs, expert_ids, rank, resid, output_grad, row(router_gain), router_t,
            out_proj, joined, scan, act, row(skip_gain), masked, rate, proj, pair[states:],
        ),
        grid=(chunks,),
        in_specs=[
            SMEM, full(slots + 8, depth), full(slots, tokens), full(tokens, 1), full(tokens, 8),
            full(tokens, 1), full(tokens, 1), full(tokens, depth), full(tokens, depth), full(1, depth),
            full(8, depth), out_rows, gate_half, tok, tok, one_row, tok, state_rows, proj_full, one_row,
        ],
        out_specs=[
            full(tokens, depth), full(16, depth), tok, tok, one_row,
            pl.BlockSpec((states + 1, chunk), block),
        ],
        scratch=[lanes] + [pltpu.VMEM((tokens, depth), BF16)] * 2,
        name="mixer_back",
    )
    back_pair, downs_sent, *up_first = tie(back_pair, downs_sent, *up_first)
    core = grid.at["core"].astype(jnp.int32).reshape(1)
    wide = pl.BlockSpec((tokens, depth), block)

    def late(which, weight):
        return call(
            late_kernel,
            [shape(depth, width)] + [shape(tokens, depth)] * len(weight),
            (
                which, scan, act, row(skip_gain), joined, grad_resid, block_input, row(mixer_gain), grad_gate,
                *weight,
            ),
            grid=(2,),
            in_specs=[
                SMEM, wide, wide, pl.BlockSpec((1, depth), block), pl.BlockSpec((ext, depth), lambda c: (0, 2 + c)),
                full(tokens, depth), full(tokens, depth), full(1, depth), wide,
            ]
            + [pl.BlockSpec((depth, depth), lambda c: (0, 2 + c))] * len(weight),
            out_specs=[pl.BlockSpec((depth, depth), block)] + [full(tokens, depth)] * len(weight),
            scratch=[pltpu.VMEM((tokens, depth), BF16)] * 2,
            name="late",
        )

    (late_sent,) = late(core, ())
    late_kept, grad_gate_normed = late(1 - core, (in_proj,))
    late_got = grid.swap(late_sent, "core", 1)
    down_first = inner_swaps(downs_sent, 0)

    def first(total):
        total, held["through"], held["downs"], *held["up_second"] = tie(total, through, downs_sent, *up_second)
        return total

    def second(total):
        total, got, kept, held["normed"], *held["down_first"] = tie(
            total, late_got, late_kept, grad_gate_normed, *down_first
        )
        held["late"] = sum_first(grid, [kept, got])
        return total

    end = entering(grid, back_pair, rate, True, {1: first, 2: second})
    up_second = held["up_second"]
    end, near, far = tie(end, results[1], results[2] + held["through"])
    near, far = grid.swap(near, "outer", 1), grid.swap(far, "outer", 2)
    grad_gate_normed = held["normed"]
    late_first, late_second = held["late"]

    def with_others(own, firsts, seconds):
        for pair in zip(firsts, seconds):
            own = own + jnp.concatenate(pair, axis=0)
        return own

    def scan_back(c, before):
        at = lambda _: (0, c)
        tok, one_row = pl.BlockSpec((tokens, chunk), at), pl.BlockSpec((1, chunk), at)
        state_rows = pl.BlockSpec((states, chunk), at)
        return call(
            functools.partial(scan_back_kernel, rank_n, states),
            [
                shape(tokens, width), shape(tokens, width), shape(states, width),
                shape(rank_n + 2 * states, tokens),
            ],
            (
                masked, steps, drive, act, pre, grad_scan, row(skip_gain), history, history, start, end, rate, proj,
                step_proj, *before,
            ),
            grid=(blocks,),
            in_specs=[
                tok, tok, tok, tok, tok, tok, one_row,
                pl.BlockSpec((token_block, states, chunk), lambda i: (blocks - 1 - i, 0, c)),
                pl.BlockSpec(
                    (8, states, chunk),
                    lambda i: (jnp.maximum((blocks - 1 - i) * (token_block // 8) - 1, 0), 0, c),
                ),
                state_rows, state_rows, state_rows, proj_full, pl.BlockSpec((rank_n, chunk), at),
            ]
            + [pl.BlockSpec(memory_space=pl.ANY)] * len(before),
            out_specs=[tok, tok, state_rows, proj_full],
            scratch=[lanes, lanes]
            + [pltpu.VMEM((tokens, chunk), F32)] * 2
            + [pltpu.VMEM((token_block, states, 128), F32)] * 2
            + [pltpu.VMEM((states, chunk), F32)] * 2
            + [pltpu.VMEM((2, states, 128), F32)],
            name="scan_back",
            aliases={14 + i: i for i in range(len(before))},
        )

    *filled, grad_proj_a = scan_back(0, ())
    filled, late_first, late_second = tie(filled, late_first, late_second)
    late_both = sum_second(grid, late_first, late_second)
    *filled, grad_proj_b = scan_back(1, filled)
    filled, late_both, near, far, downs_sent = tie(filled, late_both, near, far, held["downs"])
    down_second = inner_swaps(downs_sent, 1)
    result = results[0] + near + far
    result_parts = swap_y(grid, [result[p * 2 * cap : (p + 1) * 2 * cap] for p in range(parts)])
    late_cut = cut_outer(grid, late_both)
    late_through = grid.swap(late_cut[3], "outer", 1)
    grad_act, grad_pre, grad_decay, grad_proj_c = scan_back(2, filled)
    grad_act, late_through, result_parts, down_second = tie(grad_act, late_through, result_parts, down_second)
    late_total = outer_reduce_rest(grid, late_cut, late_through)
    unit = 2 * grid.size["inner"] * grid.size["y"]
    half = -(-max(depth // 2 + 3 * states + rank_n, depth // 2 + rank_n + 40) // unit) * unit
    small = jnp.concatenate([small[:9], loads[0:1]], axis=0)
    kept, sent_half, input_grad, edge = call(
        functools.partial(input_back_kernel, rank_n, states),
        [shape(half, width), shape(half, width), shape(tokens, depth), shape(HALO, depth)],
        (
            core, grad_proj_a, grad_proj_b, grad_proj_c, proj, state_proj_t, act, grad_act, grad_pre, conv, joined,
            conv_weight, since, in_proj, block_input, halo, row(mixer_gain), grad_gate_normed, grad_resid,
            grad_decay, grad_skip, small,
        ),
        grid=(chunks,),
        in_specs=[
            SMEM, proj_full, proj_full, proj_full, proj_full, pl.BlockSpec((rank_n + 2 * states, chunk), block),
            tok, tok, tok, tok, pl.BlockSpec((ext, chunk), block), pl.BlockSpec((taps, chunk), block),
            full(tokens, 1), pl.BlockSpec((depth, chunk), block), full(tokens, depth), full(HALO, depth),
            full(1, depth), full(tokens, depth), full(tokens, depth), state_rows, one_row, full(10, depth),
        ],
        out_specs=[
            pl.BlockSpec((half, chunk), block), pl.BlockSpec((half, chunk), block), full(tokens, depth),
            full(HALO, depth),
        ],
        scratch=[pltpu.VMEM((ext, depth), BF16)] * 2
        + [pltpu.VMEM((ext, chunk), F32), pltpu.VMEM((ext, depth), F32)],
        name="input_back",
    )
    kept, sent_half, late_total = tie(kept, sent_half, late_total)
    late_near, late_far = grid.swap(late_total, "outer", 1), grid.swap(late_total, "outer", 2)
    sent_got = grid.swap(sent_half, "core", 1)
    kept, sent_got = tie(kept, sent_got)
    grads_first, grads_second = sum_first(grid, [kept, sent_got])
    late_near, late_far, grads_first, grads_second = tie(late_near, late_far, grads_first, grads_second)
    late_last = grid.swap(late_far, "outer", 1)
    grads = sum_second(grid, grads_first, grads_second)
    late_last, grads, edge, result_parts, up_parts, down_parts = tie(
        late_last, grads, edge, result_parts,
        [up_grads[0], up_first, up_second], [down_grads[0], held["down_first"], down_second],
    )
    from_next = grid.along(edge, -1)
    input_grad = jnp.concatenate([input_grad[: tokens - HALO], input_grad[tokens - HALO :] + from_next], axis=0)
    grad_up, grad_down = with_others(*up_parts), with_others(*down_parts)
    result = core_last(grid, result_parts, cap, False)
    late_first, late_second = spread_second(grid, join_outer(grid, late_total, late_near, late_far, late_last))
    grads = sum_outer(grid, grads)
    late_first, late_second, grads, result, grad_up, input_grad = tie(
        late_first, late_second, grads, result, grad_up, input_grad
    )
    combined = jnp.dot(table.T, result.astype(F32), precision=lax.Precision.HIGHEST, preferred_element_type=F32)
    block_output = resid + gate * combined
    late_first, late_second = gather_rows(grid, late_first, "inner"), gather_rows(grid, late_second, "y")
    grads = spread_outer(grid, grads)
    late_first, late_second, grads, block_output, grad_down = tie(
        late_first, late_second, grads, block_output, grad_down
    )
    late_other = [grid.swap(late_first, "core", 1), grid.swap(late_second, "core", 1)]
    grads_first, grads_second = spread_second(grid, grads)
    grads_first, grads_second, *late_other = tie(grads_first, grads_second, *late_other)
    grads_first, grads_second = gather_rows(grid, grads_first, "inner"), gather_rows(grid, grads_second, "y")
    quarter = pl.BlockSpec((half // 2, chunk), block)
    late_rows = full(depth // 2, width)
    grad_in_proj, grad_out_proj = call(
        finish_late_kernel,
        [shape(depth, 2 * width), shape(2, depth, depth)],
        (core, late_first, late_second, *late_other),
        grid=(2,),
        in_specs=[SMEM] + [late_rows] * 4,
        out_specs=[
            pl.BlockSpec((depth // 2, width), lambda r: (r, 1)),
            pl.BlockSpec((2, depth // 2, depth), lambda r: (0, r, 0)),
        ],
        name="finish_late",
    )
    grads_first, grads_second, grad_in_proj = tie(grads_first, grads_second, grad_in_proj)
    grads_other = [grid.swap(grads_first, "core", 1), grid.swap(grads_second, "core", 1)]
    tall = lambda columns: pl.BlockSpec((chunk, columns), lambda c: (c, 0))
    (
        grad_in_proj, grad_state_proj, grad_step_proj, grad_decay_log, grad_conv_weight, rows, small,
    ) = call(
        functools.partial(finish_kernel, rank_n, states, taps),
        [
            shape(depth, 2 * width), shape(width, rank_n + 2 * states), shape(rank_n, width),
            shape(width, states), shape(taps, width), shape(8, width), shape(32, chunk),
        ],
        (core, grads_first, grads_second, *grads_other, grad_in_proj),
        grid=(chunks,),
        in_specs=[SMEM] + [quarter] * 4 + [pl.BlockSpec(memory_space=pl.ANY)],
        out_specs=[
            pl.BlockSpec((depth, chunk), block), tall(rank_n + 2 * states), pl.BlockSpec((rank_n, chunk), block),
            tall(states), pl.BlockSpec((taps, chunk), block), pl.BlockSpec((8, chunk), block), full(32, chunk),
        ],
        name="finish",
        aliases={5: 0},
    )
    small = jnp.concatenate([small[:16], small[16:, : depth - chunk]], axis=1)
    return (
        block_output,
        input_grad,
        small[10],
        grad_in_proj,
        grad_conv_weight,
        rows[taps],
        grad_state_proj,
        grad_step_proj,
        rows[taps + 1],
        grad_decay_log,
        rows[taps + 2],
        grad_out_proj.reshape(width, depth),
        small[8],
        small[:experts].T,
        grad_up[None],
        grad_down[None],
        small[9, :experts].astype(jnp.int32),
        small[9, 128 : 128 + experts].astype(jnp.int32),
    )


def solution(mesh):
    rows, copied = P(("seq", "exp"), None), P()
    up, down = P("exp", None, "seq"), P("exp", "seq", None)
    in_specs = (rows, copied, rows, rows) + (copied,) * 12 + (up, down)
    out_specs = (rows, rows) + (copied,) * 12 + (up, down, copied, copied)
    return jax.shard_map(per_device, mesh=mesh, in_specs=in_specs, out_specs=out_specs, check_vma=False)
```

```python
import functools

import jax
import jax.numpy as jnp
from jax import lax
from jax.experimental import pallas as pl
from jax.experimental.pallas import tpu as pltpu
from jax.sharding import PartitionSpec as P

F32 = jnp.float32
BF16 = jnp.bfloat16
EPS = 1e-05
LOG2E = 1.4426950408889634
HALO = 16
RESET = 1e9
AXES = ("seq", "exp")
NN, NT, TN = ((1,), (0,)), ((1,), (1,)), ((0,), (0,))
VMEM_BYTES = 52 << 20
MICROSECONDS = {
    "route": 1, "join": 8, "features": 250, "join_states": 1, "scan": 200, "early": 200, "expert": 60,
    "expert_grads": 300, "mixer_back": 300, "late": 200, "scan_back": 10, "input_back": 11, "finish_late": 8, "finish": 6,
}


class Grid:
    def __init__(self):
        self.seq, self.exp = lax.axis_size("seq"), lax.axis_size("exp")
        self.outer = 4
        self.size = {
            "core": 2,
            "y": self.exp // 2,
            "inner": self.seq // self.outer,
            "outer": self.outer,
        }
        self.total = self.seq * self.exp
        index, step, self.step, self.at = lax.axis_index(AXES), 1, {}, {}
        for name in ("core", "y", "inner", "outer"):
            self.step[name] = step
            self.at[name] = (index // step) % self.size[name]
            step *= self.size[name]
        self.index = index

    def swap(self, block, name, mask):
        return self.swap_bits(block, mask * self.step[name])

    def swap_bits(self, block, bits):
        return lax.ppermute(block, AXES, [(i, i ^ bits) for i in range(self.total)])

    def along(self, block, distance):
        route = [(i - distance, i) for i in range(self.total) if 0 <= i - distance < self.total]
        return lax.ppermute(block, AXES, route)


def tie(*values):
    return lax.optimization_barrier(values)


def outer_reduce_rest(grid, parts, through):
    through, near = tie(through, parts[1])
    near = grid.swap(near, "outer", 1)
    far = grid.swap(parts[2] + through, "outer", 2)
    return parts[0] + near + far


def in_order(parts, place):
    bit = 1
    while bit < len(parts):
        turned = ((place // bit) % 2) == 1
        parts = [jnp.where(turned, parts[i ^ bit], parts[i]) for i in range(len(parts))]
        bit *= 2
    return parts


def rows_of(parts, first, rows):
    return functools.reduce(jnp.add, [lax.dynamic_slice_in_dim(part, first, rows, 0) for part in parts])


def scatter_rows(grid, parts, name, rows, start=0):
    count, place = grid.size[name], grid.at[name]
    rows = rows // count
    piece = lambda s: rows_of(parts, start + (place ^ s) * rows, rows)
    got = [grid.swap(piece(s), name, s) for s in range(1, count)]
    return [piece(0)] + got


def gather_rows(grid, block, name):
    count = grid.size[name]
    if count == 1:
        return block
    parts = [block] + [grid.swap(block, name, s) for s in range(1, count)]
    return jnp.concatenate(in_order(parts, grid.at[name]), axis=0)


def sum_first(grid, parts):
    rows = parts[0].shape[0] // 2
    return scatter_rows(grid, parts, "inner", rows), scatter_rows(grid, parts, "y", rows, rows)


def sum_second(grid, first, second):
    rows = first[0].shape[0]
    first, second = scatter_rows(grid, first, "y", rows), scatter_rows(grid, second, "inner", rows)
    return [jnp.concatenate(pair, axis=0) for pair in zip(first, second)]


def cut_outer(grid, parts):
    columns = parts[0].shape[1] // grid.outer
    return [
        functools.reduce(
            jnp.add,
            [lax.dynamic_slice_in_dim(p, (grid.at["outer"] ^ s) * columns, columns, 1) for p in parts],
        )
        for s in range(grid.outer)
    ]


def sum_outer(grid, parts):
    own, *others = cut_outer(grid, parts)
    return functools.reduce(jnp.add, [grid.swap(part, "outer", s) for s, part in enumerate(others, 1)], own)


def spread_outer(grid, total):
    count = grid.size["outer"]
    parts = [total] + [grid.swap(total, "outer", s) for s in range(1, count)]
    return jnp.concatenate(in_order(parts, grid.at["outer"]), axis=1)


def join_outer(grid, own, near, far, last):
    return jnp.concatenate(in_order([own, near, far, last], grid.at["outer"]), axis=1)


def spread_second(grid, both):
    own = both.shape[0] // 2
    return gather_rows(grid, both[:own], "y"), gather_rows(grid, both[own:], "inner")


def spread_first(grid, first, second):
    return jnp.concatenate([gather_rows(grid, first, "inner"), gather_rows(grid, second, "y")], axis=0)


def join_states_kernel(last, later_ref, total_ref, got_ref, ahead_ref, rate_ref, *outs):
    states = rate_ref.shape[0]
    rows, sums = slice(0, states), slice(states, states + 1)

    def follow(early, late, out):
        out[rows, :] = jnp.exp2(rate_ref[...] * late[sums, :]) * early[rows, :] + late[rows, :]
        out[sums, :] = early[sums, :] + late[sums, :]

    @pl.when(later_ref[0] == 1)
    def _():
        follow(got_ref, ahead_ref, outs[0])
        if not last:
            follow(got_ref, total_ref, outs[1])

    @pl.when(later_ref[0] == 0)
    def _():
        outs[0][...] = ahead_ref[...]
        if not last:
            follow(total_ref, got_ref, outs[1])


def entering(grid, pair, rate, backward, after):
    states = rate.shape[0]
    total, ahead, hop = pair, jnp.zeros_like(pair), 1
    bits = 1
    while bits < grid.total:
        got = grid.swap_bits(total, bits)
        later = ((grid.index // bits) % 2).astype(jnp.int32)
        later = (1 - later if backward else later).reshape(1)
        last = 2 * bits >= grid.total
        whole = pl.BlockSpec(memory_space=pltpu.VMEM)
        ahead, *rest = call(
            functools.partial(join_states_kernel, last),
            [shape(*pair.shape)] * (1 if last else 2),
            (later, total, got, ahead, rate),
            in_specs=[SMEM] + [whole] * 4,
            name="join_states",
        )
        total = rest[0] if rest else None
        if hop in after:
            total = after[hop](total)
        bits, hop = 2 * bits, hop + 1
    return ahead[:states]


def pad_rows(block, rows):
    return jnp.pad(block, ((0, rows - block.shape[0]), (0, 0)))


def core_first(grid, block, cap, tail):
    ny, width = grid.size["y"], 2 * cap
    slots = ny * width
    send = [block[s * width + cap : (s + 1) * width] for s in range(ny)] + ([block[slots:]] if tail else [])
    got = grid.swap(jnp.concatenate(send, axis=0), "core", 1)
    parts = []
    for s in range(ny):
        rows = [block[s * width : s * width + cap], got[s * cap : (s + 1) * cap]]
        if tail:
            ends = [block[slots + 2 * s : slots + 2 * s + 1], got[ny * cap + 2 * s + 1 : ny * cap + 2 * s + 2]]
            rows.append(pad_rows(jnp.concatenate(ends, axis=0), 8))
        parts.append(jnp.concatenate(rows, axis=0))
    return parts


def swap_y(grid, parts):
    return [parts[0]] + [grid.swap(part, "y", s) for s, part in enumerate(parts[1:], 1)]


def core_last(grid, parts, cap, tail):
    ny = grid.size["y"]
    send = [p[cap : 2 * cap] for p in parts]
    if tail:
        send.append(pad_rows(jnp.concatenate([p[2 * cap + 1 : 2 * cap + 2] for p in parts], axis=0), 8))
    got = grid.swap(jnp.concatenate(send, axis=0), "core", 1)
    rows, ends = [], []
    for s, p in enumerate(parts):
        rows += [p[:cap], got[s * cap : (s + 1) * cap]]
        if tail:
            ends += [p[2 * cap : 2 * cap + 1], got[ny * cap + s : ny * cap + s + 1]]
    if tail:
        rows.append(pad_rows(jnp.concatenate(ends, axis=0), 8))
    return jnp.concatenate(rows, axis=0)


def split(value):
    high = value.astype(BF16)
    return high, (value - high.astype(F32)).astype(BF16)


def dot(left, right, dims):
    return lax.dot_general(left, right, (dims, ((), ())), preferred_element_type=F32)


def product(left, right, dims):
    return dot(left[0], right[0], dims) + (dot(left[0], right[1], dims) + dot(left[1], right[0], dims))


def pick(exact, value, dims):
    high, low = split(value)
    return dot(exact, high, dims) + dot(exact, low, dims)


def sigmoid(value):
    return 1.0 / (1.0 + jnp.exp(-value))


def softplus(value):
    small = jnp.exp(-jnp.abs(value))
    series = small * (1.0 - small * (0.5 - small * (1.0 / 3.0 - small * (0.25 - small * 0.2))))
    return jnp.maximum(value, 0.0) + jnp.where(small < 0.03, series, jnp.log(1.0 + small))


def iota(shape, dim):
    return lax.broadcasted_iota(jnp.int32, shape, dim)


def scale_of(value):
    return lax.rsqrt(jnp.mean(value * value, axis=1, keepdims=True) + EPS)


def over_lanes(ref, columns):
    rows = columns.shape[0]
    for t in range(columns.shape[1]):
        ref[t] = jnp.broadcast_to(columns[:, t : t + 1], (rows, 128))


def widen(value, width):
    return jnp.concatenate([value] * (width // 128), axis=1)


def call(kernel, outs, ins, grid=None, in_specs=None, out_specs=None, scratch=(), name=None, aliases=None):
    whole = pl.BlockSpec(memory_space=pltpu.VMEM)
    return pl.pallas_call(
        kernel,
        out_shape=outs,
        grid=grid or (),
        in_specs=in_specs or [whole] * len(ins),
        out_specs=out_specs or jax.tree.map(lambda _: whole, outs),
        scratch_shapes=scratch,
        name=name,
        cost_estimate=pl.CostEstimate(
            flops=int(MICROSECONDS[name] * 1.1e9), transcendentals=0, bytes_accessed=int(MICROSECONDS[name] * 1e6)
        ),
        input_output_aliases=aliases or {},
        compiler_params=pltpu.CompilerParams(vmem_limit_bytes=VMEM_BYTES),
    )(*ins)


def shape(*dims, dtype=F32):
    return jax.ShapeDtypeStruct(dims, dtype)


SMEM = pl.BlockSpec(memory_space=pltpu.SMEM)


def full(*dims):
    return pl.BlockSpec(dims, lambda *_: (0,) * len(dims))


def route_kernel(experts, cap, me_ref, ids_ref, grad_ref, sent_ref, table_ref, rank_ref, load_ref):
    ids = ids_ref[...]
    tokens = ids.shape[0]
    chosen = (ids == iota((tokens, 128), 1)).astype(F32)
    before = (iota((tokens, tokens), 0) > iota((tokens, tokens), 1)).astype(BF16)
    rank = jnp.sum(dot(before, chosen.astype(BF16), NN) * chosen, axis=1, keepdims=True)
    kept = (rank < cap).astype(F32)
    place = jnp.where(rank < cap, ((ids ^ me_ref[0]) * cap).astype(F32) + rank, -1.0)
    row = jnp.broadcast_to(place, (tokens, tokens)).T
    slots = experts * cap
    table = (iota((slots, tokens), 0).astype(F32) == jnp.broadcast_to(row[0:1], (slots, tokens))).astype(F32)
    table = table.astype(BF16)
    table_ref[...] = table
    rank_ref[...] = rank
    sent_ref[...] = pick(table, grad_ref[...], NN)
    load_ref[...] = jnp.zeros_like(load_ref)
    load_ref[0:1, 0:128] = jnp.sum(chosen, axis=0, keepdims=True)
    load_ref[0:1, 128:256] = jnp.sum(chosen * (1.0 - kept), axis=0, keepdims=True)


def join_kernel(x_ref, halo_ref, gain_ref, weight_ref, joined_ref, high, low):
    @pl.when(pl.program_id(0) == 0)
    def _():
        x = jnp.concatenate([halo_ref[...], x_ref[...]], axis=0)
        high[...], low[...] = split(x * scale_of(x) * gain_ref[...])

    joined_ref[...] = product((high[...], low[...]), split(weight_ref[...]), NN)


def features_kernel(
    rank_n,
    states,
    inner_ref,
    since_ref,
    conv_w_ref,
    conv_b_ref,
    state_proj_ref,
    step_proj_ref,
    step_bias_ref,
    rate_ref,
    conv_ref,
    act_ref,
    pre_ref,
    steps_ref,
    masked_ref,
    drive_ref,
    proj_ref,
    pair_ref,
    in_lanes,
):
    tokens, width = act_ref.shape
    taps = conv_w_ref.shape[0]
    since = since_ref[...]
    conv = jnp.broadcast_to(conv_b_ref[...], (tokens, width))
    for k in range(taps):
        valid = (since >= taps - 1 - k).astype(F32)
        first = HALO - taps + 1 + k
        conv = conv + inner_ref[first : first + tokens, :] * valid * conv_w_ref[k : k + 1, :]
    act = conv * sigmoid(conv)
    conv_ref[...] = conv
    act_ref[...] = act
    proj = product(split(state_proj_ref[...]), split(act), NT)
    proj_ref[...] = proj
    pre = product(split(proj[:rank_n]), split(step_proj_ref[...]), TN) + step_bias_ref[...]
    pre_ref[...] = pre
    steps = softplus(pre)
    steps_ref[...] = steps
    masked = jnp.where(since == 0, RESET, steps)
    masked_ref[...] = masked
    drive_ref[...] = steps * act
    pair_ref[states : states + 1, :] = jnp.sum(masked, axis=0, keepdims=True)
    over_lanes(in_lanes, proj[rank_n : rank_n + states])
    chunk = 512
    for c in range(width // chunk):
        part = slice(c * chunk, (c + 1) * chunk)
        rate = rate_ref[:, part]

        def eight(group, state):
            for i in range(8):
                t = group * 8 + i
                decay = jnp.exp2(masked_ref[pl.ds(t, 1), part] * rate)
                state = decay * state + drive_ref[pl.ds(t, 1), part] * widen(in_lanes[t], chunk)
            return state

        pair_ref[0:states, part] = lax.fori_loop(0, tokens // 8, eight, jnp.zeros((states, chunk), F32))


def slot_tables(slots, cap, experts):
    slot = iota((slots, 8), 0)
    first = sum((slot >= cap * e).astype(jnp.int32) for e in range(1, experts))
    block = (first == iota((slots, 8), 1)).astype(F32)
    slot = iota((slots, 128), 0)
    first = sum(((slot >= cap * e).astype(jnp.int32) for e in range(1, experts)))
    within = (slot - first * cap == iota((slots, 128), 1)).astype(F32)
    return block, within


def scan_kernel(
    rank_n,
    states,
    experts,
    cap,
    me_ref,
    masked_ref,
    drive_ref,
    act_ref,
    gate_z_ref,
    start_ref,
    rate_ref,
    skip_ref,
    proj_ref,
    out_proj_ref,
    x_ref,
    gain_ref,
    router_ref,
    ids_ref,
    rank_ref,
    table_ref,
    scan_ref,
    history_ref,
    resid_ref,
    sent_ref,
    probs_ref,
    gate_ref,
    in_lanes,
    out_lanes,
    total,
):
    tokens, chunk = masked_ref.shape
    step = pl.program_id(0)

    @pl.when(step == 0)
    def _():
        over_lanes(in_lanes, proj_ref[rank_n : rank_n + states, :])
        over_lanes(out_lanes, proj_ref[rank_n + states : rank_n + 2 * states, :])
        total[...] = x_ref[...]

    rate = rate_ref[...]

    def eight(group, state):
        for i in range(8):
            t = group * 8 + i
            decay = jnp.exp2(masked_ref[pl.ds(t, 1), :] * rate)
            state = decay * state + drive_ref[pl.ds(t, 1), :] * widen(in_lanes[t], chunk)
            history_ref[t] = state
            scan_ref[pl.ds(t, 1), :] = jnp.sum(state * widen(out_lanes[t], chunk), axis=0, keepdims=True)
        return state

    lax.fori_loop(0, tokens // 8, eight, start_ref[...])
    gate_z = gate_z_ref[HALO:, :]
    mixed = (scan_ref[...] + skip_ref[...] * act_ref[...]) * (gate_z * sigmoid(gate_z))
    total[...] += product(split(mixed), split(out_proj_ref[...]), NN)

    @pl.when(step == pl.num_programs(0) - 1)
    def _():
        resid = total[...]
        resid_ref[...] = resid
        normed = resid * scale_of(resid) * gain_ref[...]
        logits = product(split(normed), split(router_ref[...]), NT)
        known = iota((tokens, 8), 1) < experts
        logits = jnp.where(known, logits, -1e30)
        raised = jnp.exp(logits - jnp.max(logits, axis=1, keepdims=True))
        raised = jnp.where(known, raised, 0.0)
        probs = raised / jnp.sum(raised, axis=1, keepdims=True)
        probs_ref[...] = probs
        ids = ids_ref[...]
        gate = jnp.sum(jnp.where(ids == iota((tokens, 8), 1), probs, 0.0), axis=1, keepdims=True)
        gate_ref[...] = gate
        slots = experts * cap
        sent_ref[0:slots, :] = pick(table_ref[...], normed, NN)
        sent_ref[slots:, :] = jnp.zeros((8, sent_ref.shape[1]), F32)
        rank = rank_ref[...].astype(jnp.int32)
        to_block = jnp.where(((ids ^ me_ref[0]) == iota((tokens, 8), 1)) & (rank < cap), gate, 0.0)
        at_rank = (rank == iota((tokens, 128), 1)).astype(BF16)
        high, low = split(to_block)
        rest = (to_block - high.astype(F32) - low.astype(F32)).astype(BF16)
        rows = dot(high, at_rank, TN) + (dot(low, at_rank, TN) + dot(rest, at_rank, TN))
        sent_ref[slots:, 0:128] = rows


def early_kernel(pieces, slices, *refs):
    grads, downs, outs = refs[:pieces], refs[pieces : pieces + slices], refs[pieces + slices :]
    downs = [split(d[...]) for d in downs]
    for p in range(pieces):
        grad = split(grads[p][...])
        for i in range(slices):
            outs[p][i] = product(grad, downs[i], NT)


def gelu_parts(value):
    inner = 0.7978845608 * (value + 0.044715 * value * value * value)
    tanh = jnp.tanh(inner)
    slope = 0.5 * (1.0 + tanh) + 0.5 * value * (1.0 - tanh * tanh) * 0.7978845608 * (
        1.0 + 3.0 * 0.044715 * value * value
    )
    return 0.5 * value * (1.0 + tanh), slope


def expert_kernel(parts, slices, cap, *refs):
    tokens, ups, pulled_ref = refs[:parts], refs[parts : parts + slices], refs[parts + slices]
    backs, hidden_ref, grad_ref = refs[parts + slices + 1 : -2], refs[-2], refs[-1]
    width = 2 * cap
    slots, depth = parts * width, tokens[0].shape[1]
    block, within = slot_tables(width, cap, 2)
    within = within.astype(BF16)
    rows = split(jnp.concatenate([t[0:width, :] for t in tokens], axis=0))
    back = jnp.zeros((slots, depth), F32)
    to_gate = jnp.zeros((slots, 1), F32)
    for i in range(slices):
        up = split(ups[i][...])
        hidden, slope = gelu_parts(product(rows, up, NN))
        pull = pulled_ref[i]
        grad = pull * slope
        hidden_ref[i] = hidden
        grad_ref[i] = grad
        to_gate += jnp.sum(hidden * pull, axis=1, keepdims=True)
        back += product(split(grad), up, NT)
    for p in range(parts):
        part = slice(p * width, (p + 1) * width)
        backs[p][0:width, :] = back[part]
        backs[p][width:, :] = jnp.zeros((8, depth), F32)
        mine = block * to_gate[part]
        high, low = split(mine)
        rest = (mine - high.astype(F32) - low.astype(F32)).astype(BF16)
        backs[p][width:, 0:128] = dot(high, within, TN) + (dot(low, within, TN) + dot(rest, within, TN))


def expert_grads_kernel(pieces, parts, slices, cap, *refs):
    tokens, refs = refs[: pieces * parts], refs[pieces * parts :]
    grads, hiddens, pulls = (refs[i * pieces : (i + 1) * pieces] for i in range(3))
    downs, outs = refs[3 * pieces : 3 * pieces + slices], refs[3 * pieces + slices :]
    results, up_outs, down_outs = outs[:pieces], outs[pieces : pieces + slices], outs[pieces + slices :]
    width = 2 * cap
    downs = [split(d[...]) for d in downs]
    block, within = slot_tables(width, cap, 2)
    within = within.astype(BF16)
    for p in range(pieces):
        rows, gates = [], []
        for token in tokens[p * parts : (p + 1) * parts]:
            ends = token[width:, 0:128]
            high, low = split(ends)
            rest = (ends - high.astype(F32) - low.astype(F32)).astype(BF16)
            spread = dot(within, high, NT) + (dot(within, low, NT) + dot(within, rest, NT))
            gates.append(jnp.sum(spread * block, axis=1, keepdims=True))
            rows.append(token[0:width, :] * gates[-1])
        rows = split(jnp.concatenate(rows, axis=0))
        gated = split(grads[p][...] * jnp.concatenate(gates, axis=0))
        total = None
        for i in range(slices):
            hidden = split(hiddens[p][i])
            part = product(hidden, downs[i], NN)
            total = part if total is None else total + part
            up = product(rows, split(pulls[p][i]), TN)
            down = product(hidden, gated, TN)
            if p == 0:
                up_outs[i][...] = up
                down_outs[i][...] = down
            else:
                up_outs[i][...] += up
                down_outs[i][...] += down
        results[p][...] = total


def silu_parts(value):
    sig = sigmoid(value)
    return value * sig, sig * (1.0 + value * (1.0 - sig))


def mixer_back_kernel(
    rank_n,
    states,
    experts,
    cap,
    me_ref,
    back_ref,
    table_ref,
    gate_ref,
    probs_ref,
    ids_ref,
    rank_ref,
    resid_ref,
    grad_ref,
    gain_ref,
    router_ref,
    out_proj_ref,
    gate_z_ref,
    scan_ref,
    act_ref,
    skip_ref,
    masked_ref,
    rate_ref,
    proj_ref,
    steps_row_ref,
    grad_resid_ref,
    small_ref,
    grad_scan_ref,
    grad_gate_ref,
    grad_skip_ref,
    pair_ref,
    out_lanes,
    high,
    low,
):
    tokens, chunk = masked_ref.shape

    @pl.when(pl.program_id(0) == 0)
    def _():
        over_lanes(out_lanes, proj_ref[rank_n + states : rank_n + 2 * states, :])
        slots = experts * cap
        ids, rank = ids_ref[...], rank_ref[...].astype(jnp.int32)
        back = pick(table_ref[...], back_ref[0:slots, :], TN)
        at_rank = (rank == iota((tokens, 128), 1)).astype(BF16)
        ends = back_ref[slots:, 0:128]
        first, second = split(ends)
        third = (ends - first.astype(F32) - second.astype(F32)).astype(BF16)
        spread = dot(at_rank, first, NT) + (dot(at_rank, second, NT) + dot(at_rank, third, NT))
        mine = ((ids ^ me_ref[0]) == iota((tokens, 8), 1)) & (rank < cap)
        grad_gate = jnp.sum(jnp.where(mine, spread, 0.0), axis=1, keepdims=True)
        probs = probs_ref[...]
        grad_probs = jnp.where(ids == iota((tokens, 8), 1), grad_gate, 0.0)
        grad_logits = probs * (grad_probs - jnp.sum(probs * grad_probs, axis=1, keepdims=True))
        resid, gain = resid_ref[...], gain_ref[...]
        scale = scale_of(resid)
        normed = resid * scale * gain
        logits_two = split(grad_logits)
        grad_normed = gate_ref[...] * back + product(logits_two, split(router_ref[...]), NN)
        small_ref[...] = jnp.zeros_like(small_ref)
        small_ref[0:8, :] = product(logits_two, split(normed), TN)
        small_ref[8:9, :] = jnp.sum(grad_normed * resid * scale, axis=0, keepdims=True)
        pulled = gain * grad_normed
        grad_resid = (
            grad_ref[...]
            + scale * pulled
            - resid * (scale * scale * scale) * jnp.mean(pulled * resid, axis=1, keepdims=True)
        )
        grad_resid_ref[...] = grad_resid
        high[...], low[...] = split(grad_resid)

    grad_mixed = product((high[...], low[...]), split(out_proj_ref[...]), NT)
    silu, slope = silu_parts(gate_z_ref[HALO:, :])
    act = act_ref[...]
    grad_scan = grad_mixed * silu
    grad_scan_ref[...] = grad_scan
    grad_gate_ref[...] = grad_mixed * (scan_ref[...] + skip_ref[...] * act) * slope
    grad_skip_ref[...] = jnp.sum(grad_scan * act, axis=0, keepdims=True)
    rate = rate_ref[...]

    def eight(group, state):
        for i in range(8):
            t = tokens - 1 - (group * 8 + i)
            decay = jnp.exp2(masked_ref[pl.ds(t, 1), :] * rate)
            state = decay * (state + grad_scan_ref[pl.ds(t, 1), :] * widen(out_lanes[t], chunk))
        return state

    pair_ref[0:states, :] = lax.fori_loop(0, tokens // 8, eight, jnp.zeros((states, chunk), F32))
    pair_ref[states : states + 1, :] = steps_row_ref[...]


def late_kernel(
    which_ref, scan_ref, act_ref, skip_ref, gate_z_ref, grad_resid_ref, x_ref, gain_ref, grad_gate_ref, *refs
):
    high, low = refs[-2:]
    if len(refs) == 5:
        weight_ref, out_ref, normed_ref = refs[:3]
    else:
        weight_ref, out_ref, normed_ref = None, refs[0], None

    @pl.when(pl.program_id(0) == 0)
    def _():
        @pl.when(which_ref[0] == 0)
        def _():
            high[...], low[...] = split(grad_resid_ref[...])

        @pl.when(which_ref[0] == 1)
        def _():
            x = x_ref[...]
            high[...], low[...] = split(x * scale_of(x) * gain_ref[...])

        if normed_ref is not None:
            normed_ref[...] = jnp.zeros_like(normed_ref)

    @pl.when(which_ref[0] == 0)
    def _():
        gate_z = gate_z_ref[HALO:, :]
        mixed = (scan_ref[...] + skip_ref[...] * act_ref[...]) * (gate_z * sigmoid(gate_z))
        out_ref[...] = product(split(mixed), (high[...], low[...]), TN)

    @pl.when(which_ref[0] == 1)
    def _():
        out_ref[...] = product((high[...], low[...]), split(grad_gate_ref[...]), TN)

    if normed_ref is not None:
        normed_ref[...] += product(split(grad_gate_ref[...]), split(weight_ref[...]), NT)


def scan_back_kernel(
    rank_n,
    states,
    masked_ref,
    steps_ref,
    drive_ref,
    act_ref,
    pre_ref,
    grad_scan_ref,
    skip_ref,
    history_ref,
    before_ref,
    start_ref,
    end_ref,
    rate_ref,
    proj_ref,
    step_proj_ref,
    *refs,
):
    (
        grad_act_ref, grad_pre_ref, grad_decay_ref, grad_proj_ref,
        in_lanes, out_lanes, grad_drive, grad_steps, at_in, at_out, carried_ref, decays_ref, sums_ref,
    ) = refs[-13:]
    tokens, chunk = masked_ref.shape
    block = history_ref.shape[0]
    step, blocks = pl.program_id(0), pl.num_programs(0)
    first = (blocks - 1 - step) * block

    @pl.when(step == 0)
    def _():
        over_lanes(in_lanes, proj_ref[rank_n : rank_n + states, :])
        over_lanes(out_lanes, proj_ref[rank_n + states : rank_n + 2 * states, :])
        carried_ref[...] = end_ref[...]
        decays_ref[...] = jnp.zeros_like(decays_ref)
        sums_ref[...] = jnp.zeros_like(sums_ref)

    rate = rate_ref[...]
    entering_state = jnp.where(first == 0, start_ref[...], before_ref[7])

    def narrow(value):
        return functools.reduce(jnp.add, [value[:, c : c + 128] for c in range(0, chunk, 128)])

    def one(local, before, carried):
        state, decays = carried
        t = first + local
        masked = masked_ref[pl.ds(t, 1), :]
        grad = grad_scan_ref[pl.ds(t, 1), :]
        decay = jnp.exp2(masked * rate)
        state = state + grad * widen(out_lanes[t], chunk)
        at_out[local] = narrow(history_ref[local] * grad)
        at_in[local] = narrow(state * drive_ref[pl.ds(t, 1), :])
        grad_drive[pl.ds(t, 1), :] = jnp.sum(state * widen(in_lanes[t], chunk), axis=0, keepdims=True)
        state = decay * state
        pulled = state * before
        grad_steps[pl.ds(t, 1), :] = jnp.sum(pulled * rate, axis=0, keepdims=True)
        return state, decays + pulled * masked

    def eight(group, carried):
        for i in range(8):
            local = block - 1 - (group * 8 + i)
            carried = one(local, history_ref[local - 1], carried)
        return carried

    carried = lax.fori_loop(0, block // 8 - 1, eight, (carried_ref[...], decays_ref[...]))
    for local in range(7, 0, -1):
        carried = one(local, history_ref[local - 1], carried)
    carried_ref[...], decays_ref[...] = one(0, entering_state, carried)

    ones = jnp.ones((128, 128), BF16)
    lane = iota((states, 128), 1)
    for i, held in enumerate((at_in, at_out)):
        high, low = split(held[...].reshape(block * states, 128))
        spread = (dot(high, ones, NN) + dot(low, ones, NN)).reshape(block, states, 128)
        total = sums_ref[i]
        for local in range(block):
            total = jnp.where(lane == first + local, spread[local], total)
        sums_ref[i] = total

    @pl.when(step == blocks - 1)
    def _():
        grad_decay_ref[...] = decays_ref[...] * (rate * (1.0 / LOG2E))
        steps, act = steps_ref[...], act_ref[...]
        grad_act_ref[...] = skip_ref[...] * grad_scan_ref[...] + grad_drive[...] * steps
        grad_pre = (grad_steps[...] * (1.0 / LOG2E) + grad_drive[...] * act) * sigmoid(pre_ref[...])
        grad_pre_ref[...] = grad_pre
        grad_proj_ref[0:rank_n, :] = product(split(step_proj_ref[...]), split(grad_pre), NT)
        grad_proj_ref[rank_n : rank_n + states, :] = sums_ref[0]
        grad_proj_ref[rank_n + states : rank_n + 2 * states, :] = sums_ref[1]


def input_back_kernel(
    rank_n,
    states,
    core_ref,
    proj_a_ref,
    proj_b_ref,
    proj_c_ref,
    proj_ref,
    state_proj_ref,
    act_ref,
    grad_act_ref,
    grad_pre_ref,
    conv_ref,
    inner_ref,
    conv_w_ref,
    since_ref,
    weight_ref,
    x_ref,
    halo_ref,
    gain_ref,
    grad_gate_normed_ref,
    grad_resid_ref,
    grad_decay_ref,
    grad_skip_ref,
    small_ref,
    keep_ref,
    send_ref,
    input_ref,
    edge_ref,
    high,
    low,
    grad_inner,
    total,
):
    tokens, chunk = act_ref.shape
    depth = x_ref.shape[1]
    half = depth // 2
    taps = conv_w_ref.shape[0]
    step = pl.program_id(0)

    @pl.when(step == 0)
    def _():
        x = jnp.concatenate([halo_ref[...], x_ref[...]], axis=0)
        high[...], low[...] = split(x * scale_of(x) * gain_ref[...])
        total[...] = jnp.zeros_like(total)

    act, grad_pre = split(act_ref[...]), grad_pre_ref[...]
    grad_proj = split(proj_a_ref[...] + proj_b_ref[...] + proj_c_ref[...])
    grad_act = grad_act_ref[...] + product(grad_proj, split(state_proj_ref[...]), TN)
    _, slope = silu_parts(conv_ref[...])
    grad_conv = grad_act * slope
    since = since_ref[...]
    grad_inner[...] = jnp.zeros_like(grad_inner)
    rows = []
    for k in range(taps):
        valid = (since >= taps - 1 - k).astype(F32)
        first = HALO - taps + 1 + k
        held = grad_conv * valid
        rows.append(jnp.sum(held * inner_ref[first : first + tokens, :], axis=0, keepdims=True))
        grad_inner[first : first + tokens, :] += held * conv_w_ref[k : k + 1, :]
    rows.append(jnp.sum(grad_conv, axis=0, keepdims=True))
    rows.append(jnp.sum(grad_pre, axis=0, keepdims=True))
    rows.append(grad_skip_ref[...])
    grads = split(grad_inner[...])
    total[...] += product(grads, split(weight_ref[...]), NT)
    of_state_proj = product(grad_proj, act, NN)
    of_step_proj = product(split(proj_ref[0:rank_n, :]), split(grad_pre), NN)

    def first_half(out_ref):
        out_ref[0:half, :] = product((high[:, 0:half], low[:, 0:half]), grads, TN)
        at = half + 2 * states + rank_n
        out_ref[half:at, :] = of_state_proj
        out_ref[at : at + states, :] = grad_decay_ref[...]
        if at + states < out_ref.shape[0]:
            out_ref[at + states :, :] = jnp.zeros((out_ref.shape[0] - at - states, chunk), F32)

    def second_half(out_ref):
        out_ref[0:half, :] = product((high[:, half:], low[:, half:]), grads, TN)
        out_ref[half : half + rank_n, :] = of_step_proj
        at = half + rank_n
        out_ref[at:, :] = jnp.zeros((out_ref.shape[0] - at, chunk), F32)
        for i, row in enumerate(rows):
            out_ref[at + i : at + i + 1, :] = row

    @pl.when(core_ref[0] == 0)
    def _():
        first_half(keep_ref)
        second_half(send_ref)

    @pl.when(core_ref[0] == 1)
    def _():
        second_half(keep_ref)
        first_half(send_ref)

    @pl.when(step == pl.num_programs(0) - 1)
    def _():
        gain = gain_ref[...]

        def rows_back(x, grad):
            scale = scale_of(x)
            pulled = gain * grad
            back = scale * pulled - x * (scale * scale * scale) * jnp.mean(pulled * x, axis=1, keepdims=True)
            return back, jnp.sum(grad * x * scale, axis=0, keepdims=True)

        edge, edge_gain = rows_back(halo_ref[...], total[0:HALO, :])
        own, own_gain = rows_back(x_ref[...], total[HALO:, :] + grad_gate_normed_ref[...])
        edge_ref[...] = edge
        input_ref[...] = grad_resid_ref[...] + own
        small = jnp.concatenate([small_ref[0:10, :], edge_gain + own_gain], axis=0)

        def place_small(out_ref):
            at = half + rank_n + 8
            out_ref[at : at + 11, :] = small[:, 0:chunk]
            out_ref[at + 16 : at + 27, 0 : depth - chunk] = small[:, chunk:]

        @pl.when(core_ref[0] == 0)
        def _():
            place_small(send_ref)

        @pl.when(core_ref[0] == 1)
        def _():
            place_small(keep_ref)


def finish_late_kernel(core_ref, first_ref, second_ref, got_first_ref, got_second_ref, in_ref, out_ref):
    depth = out_ref.shape[2]
    step = pl.program_id(0)

    def write(gate, out):
        in_ref[...] = gate
        out_ref[0] = out[:, 0:depth]
        out_ref[1] = out[:, depth:]

    for i, (own, got) in enumerate(((first_ref, got_first_ref), (second_ref, got_second_ref))):

        @pl.when((core_ref[0] == 0) & (step == i))
        def _():
            write(own[...], got[...])

        @pl.when((core_ref[0] == 1) & (step == i))
        def _():
            write(got[...], own[...])


def finish_kernel(
    rank_n, states, taps, core_ref, first_ref, second_ref, got_first_ref, got_second_ref, _,
    in_ref, state_proj_ref, step_proj_ref, decay_ref, conv_w_ref, rows_ref, small_ref,
):
    depth = in_ref.shape[0]
    half, quarter = depth // 2, first_ref.shape[0]
    rest = half - quarter

    def first_half(one, two):
        in_ref[0:quarter, :] = one[...]
        in_ref[quarter:half, :] = two[0:rest, :]
        at = rest + 2 * states + rank_n
        state_proj_ref[...] = two[rest:at, :].T
        decay_ref[...] = two[at : at + states, :].T

    def second_half(one, two):
        in_ref[half : half + quarter, :] = one[...]
        in_ref[half + quarter :, :] = two[0:rest, :]
        step_proj_ref[...] = two[rest : rest + rank_n, :]
        at = rest + rank_n
        conv_w_ref[...] = two[at : at + taps, :]
        rows_ref[...] = two[at : at + 8, :]
        small_ref[...] = two[at + 8 : at + 40, :]

    @pl.when(core_ref[0] == 0)
    def _():
        first_half(first_ref, second_ref)
        second_half(got_first_ref, got_second_ref)

    @pl.when(core_ref[0] == 1)
    def _():
        first_half(got_first_ref, got_second_ref)
        second_half(first_ref, second_ref)


def per_device(
    block_input,
    seq_lengths,
    expert_ids,
    output_grad,
    mixer_gain,
    in_proj,
    conv_weight,
    conv_bias,
    state_proj,
    step_proj,
    step_bias,
    decay_log,
    skip_gain,
    out_proj,
    router_gain,
    router,
    expert_up,
    expert_down,
):
    grid = Grid()
    tokens, depth = block_input.shape
    taps, width = conv_weight.shape
    rank_n, states, experts = step_proj.shape[0], decay_log.shape[1], router.shape[1]
    cap = (5 * tokens + 4 * experts - 1) // (4 * experts)
    slots, hidden = experts * cap, expert_up.shape[2]
    chunk = 512
    chunks = width // chunk
    pieces, slices = grid.size["outer"], grid.size["inner"]
    token_block = 64
    blocks = tokens // token_block
    me = lax.axis_index("exp").astype(jnp.int32).reshape(1)
    ext = HALO + tokens

    halo = grid.along(block_input[tokens - HALO :], 1)

    count = seq_lengths.shape[0]
    earlier = jnp.arange(count)[:, None] > jnp.arange(count)[None, :]
    starts = jnp.sum(jnp.where(earlier, seq_lengths[None, :], 0), axis=1)
    position = grid.index * tokens + jnp.arange(tokens, dtype=jnp.int32)
    own_start = jnp.max(jnp.where(starts[None, :] <= position[:, None], starts[None, :], 0), axis=1)
    since = (position - own_start)[:, None]
    rate = -jnp.exp(decay_log.T) * LOG2E
    state_proj_t = state_proj.T
    router_t = pad_rows(router.T, 8)
    row = lambda vector: vector.reshape(1, -1)

    sent_grads, table, rank, loads = call(
        functools.partial(route_kernel, experts, cap),
        [shape(slots, depth), shape(slots, tokens, dtype=BF16), shape(tokens, 1), shape(8, depth)],
        (me, expert_ids, output_grad),
        in_specs=[SMEM] + [pl.BlockSpec(memory_space=pltpu.VMEM)] * 2,
        name="route",
    )
    halo, sent_grads = tie(halo, sent_grads)
    held_grads = core_first(grid, sent_grads, cap, False)
    up, down = expert_up[0], expert_down[0]
    up_rows = depth // 2
    downs = [down] + [grid.swap(down, "inner", s) for s in range(1, slices)]

    block = lambda c, *_: (0, c)
    joined = call(
        join_kernel,
        shape(ext, 2 * width),
        (block_input, halo, row(mixer_gain), in_proj),
        grid=(2 * chunks,),
        in_specs=[full(tokens, depth), full(HALO, depth), full(1, depth), pl.BlockSpec((depth, chunk), block)],
        out_specs=pl.BlockSpec((ext, chunk), block),
        scratch=[pltpu.VMEM((ext, depth), BF16)] * 2,
        name="join",
    )
    joined, *held_grads = tie(joined, *swap_y(grid, held_grads))
    own_grads = jnp.concatenate(held_grads, axis=0)
    joined, own_grads = tie(joined, own_grads)
    near_grads, far_grads = grid.swap(own_grads, "outer", 1), grid.swap(own_grads, "outer", 2)
    conv, act, pre, steps, masked, drive, proj, pair = call(
        functools.partial(features_kernel, rank_n, states),
        [shape(tokens, width)] * 6 + [shape(rank_n + 2 * states, tokens), shape(states + 1, width)],
        (joined, since, conv_weight, row(conv_bias), state_proj_t, step_proj, row(step_bias), rate),
        grid=(1,),
        in_specs=[
            full(ext, width),
            full(tokens, 1),
            full(taps, width),
            full(1, width),
            full(rank_n + 2 * states, width),
            full(rank_n, width),
            full(1, width),
            full(states, width),
        ],
        out_specs=[full(tokens, width)] * 6 + [full(rank_n + 2 * states, tokens), full(states + 1, width)],
        scratch=[pltpu.VMEM((tokens, states, 128), F32)],
        name="features",
    )
    pair, *downs = tie(pair, *downs)
    held = {}

    def third(total):
        total, held["near"], held["far"] = tie(total, near_grads, far_grads)
        return total

    start = entering(grid, pair, rate, False, {2: third})
    start, near_grads, far_grads = tie(start, held["near"], held["far"])
    up_top = [grid.swap(up[:up_rows], "inner", s) for s in range(1, slices)]
    last_grads = grid.swap(far_grads, "outer", 1)
    tok = pl.BlockSpec((tokens, chunk), block)
    gate_half = pl.BlockSpec((ext, chunk), lambda c, *_: (0, chunks + c))
    one_row = pl.BlockSpec((1, chunk), block)
    state_rows = pl.BlockSpec((states, chunk), block)
    history_block = pl.BlockSpec((tokens, states, chunk), lambda c: (0, 0, c))
    out_rows = pl.BlockSpec((chunk, depth), lambda c, *_: (c, 0))
    proj_full = full(rank_n + 2 * states, tokens)
    lanes = pltpu.VMEM((tokens, states, 128), F32)
    scan, history, resid, sent, probs, gate = call(
        functools.partial(scan_kernel, rank_n, states, experts, cap),
        [
            shape(tokens, width),
            shape(tokens, states, width),
            shape(tokens, depth),
            shape(slots + 8, depth),
            shape(tokens, 8),
            shape(tokens, 1),
        ],
        (
            me, masked, drive, act, joined, start, rate, row(skip_gain), proj, out_proj, block_input,
            row(router_gain), router_t, expert_ids, rank, table,
        ),
        grid=(chunks,),
        in_specs=[
            SMEM, tok, tok, tok, gate_half, state_rows, state_rows, one_row, proj_full, out_rows,
            full(tokens, depth), full(1, depth), full(8, depth), full(tokens, 1), full(tokens, 1),
            full(slots, tokens),
        ],
        out_specs=[
            tok, history_block, full(tokens, depth), full(slots + 8, depth), full(tokens, 8), full(tokens, 1),
        ],
        scratch=[lanes, lanes, pltpu.VMEM((tokens, depth), F32)],
        name="scan",
    )

    sent, last_grads, up_top, up_bottom = tie(sent, last_grads, up_top, up[up_rows:])
    up_bottom = [grid.swap(up_bottom, "inner", s) for s in range(1, slices)]
    own_tokens, last_grads = tie(core_first(grid, sent, cap, True), last_grads)
    grad_pieces = [own_grads, near_grads, far_grads, last_grads]
    pulled = call(
        functools.partial(early_kernel, pieces, slices),
        [shape(slices, slots, hidden)] * pieces,
        (*grad_pieces, *downs),
        name="early",
    )
    parts = grid.size["y"]
    outer_swap = lambda blocks, mask: [grid.swap(block, "outer", mask) for block in blocks]
    near_first, far_first = outer_swap(own_tokens[:1], 1), outer_swap(own_tokens[:1], 2)
    own_tokens, pulled, up_bottom = tie(swap_y(grid, own_tokens), pulled, up_bottom)
    ups = [up] + [jnp.concatenate(pair, axis=0) for pair in zip(up_top, up_bottom)]
    near_second, far_second = outer_swap(own_tokens[1:], 1), outer_swap(own_tokens[1:], 2)

    def expert(rows, pulled_rows):
        *outs, hidden_rows, pull_rows = call(
            functools.partial(expert_kernel, parts, slices, cap),
            [shape(2 * cap + 8, depth)] * parts + [shape(slices, slots, hidden)] * 2,
            (*rows, *ups, pulled_rows),
            name="expert",
        )
        return outs, hidden_rows, pull_rows

    own_outs = expert(own_tokens, pulled[0])
    near_first, far_first, own_outs = tie(near_first, far_first, own_outs)
    last_first = outer_swap(far_first, 1)
    near_second, far_second = tie(near_second, far_second)
    last_second = outer_swap(far_second, 1)
    near_tokens, far_tokens = near_first + near_second, far_first + far_second
    near_outs, far_outs = expert(near_tokens, pulled[1]), expert(far_tokens, pulled[2])
    last_first, last_second, near_outs, far_outs = tie(last_first, last_second, near_outs, far_outs)
    last_tokens = last_first + last_second
    last_outs = expert(last_tokens, pulled[3])
    token_pieces = [own_tokens, near_tokens, far_tokens, last_tokens]
    backs, hiddens, pulls = zip(own_outs, near_outs, far_outs, last_outs)
    back_through = outer_swap(backs[3][1:], 1)
    back_through, last_zero = tie(back_through, backs[3][0])
    zero_through = grid.swap(last_zero, "outer", 1)
    back_parts = [
        outer_reduce_rest(grid, [b[part] for b in backs], back_through[part - 1]) for part in range(1, parts)
    ]
    outs = call(
        functools.partial(expert_grads_kernel, pieces, parts, slices, cap),
        [shape(slots, depth)] * pieces + [shape(depth, hidden)] * slices + [shape(hidden, depth)] * slices,
        (*sum(token_pieces, []), *grad_pieces, *hiddens, *pulls, *downs),
        name="expert_grads",
    )
    back_parts, zero_through, zero, outs = tie(back_parts, zero_through, [b[0] for b in backs], outs)
    first_part = outer_reduce_rest(grid, zero, zero_through)
    back_parts = swap_y(grid, [None] + back_parts)[1:]
    first_part, back_parts = tie(first_part, back_parts)
    back = core_last(grid, [first_part] + back_parts, cap, True)
    results, up_grads, down_grads = outs[:pieces], outs[pieces : pieces + slices], outs[pieces + slices :]
    halves = lambda array: [array[: array.shape[0] // 2], array[array.shape[0] // 2 :]]
    ups_sent, downs_sent = ([halves(g) for g in grads[1:]] for grads in (up_grads, down_grads))

    def inner_swaps(sent, half):
        return [grid.swap(pair[half], "inner", s) for s, pair in enumerate(sent, 1)]

    up_first = inner_swaps(ups_sent, 0)
    back, last_result, ups_sent = tie(back, results[3], ups_sent)
    through = grid.swap(last_result, "outer", 1)
    up_second = inner_swaps(ups_sent, 1)

    grad_resid, small, grad_scan, grad_gate, grad_skip, back_pair = call(
        functools.partial(mixer_back_kernel, rank_n, states, experts, cap),
        [
            shape(tokens, depth),
            shape(16, depth),
            shape(tokens, width),
            shape(tokens, width),
            shape(1, width),
            shape(states + 1, width),
        ],
        (
            me, back, table, gate, probs, expert_ids, rank, resid, output_grad, row(router_gain), router_t,
            out_proj, joined, scan, act, row(skip_gain), masked, rate, proj, pair[states:],
        ),
        grid=(chunks,),
        in_specs=[
            SMEM, full(slots + 8, depth), full(slots, tokens), full(tokens, 1), full(tokens, 8),
            full(tokens, 1), full(tokens, 1), full(tokens, depth), full(tokens, depth), full(1, depth),
            full(8, depth), out_rows, gate_half, tok, tok, one_row, tok, state_rows, proj_full, one_row,
        ],
        out_specs=[
            full(tokens, depth), full(16, depth), tok, tok, one_row,
            pl.BlockSpec((states + 1, chunk), block),
        ],
        scratch=[lanes] + [pltpu.VMEM((tokens, depth), BF16)] * 2,
        name="mixer_back",
    )
    back_pair, downs_sent, *up_first = tie(back_pair, downs_sent, *up_first)
    core = grid.at["core"].astype(jnp.int32).reshape(1)
    wide = pl.BlockSpec((tokens, depth), block)

    def late(which, weight):
        return call(
            late_kernel,
            [shape(depth, width)] + [shape(tokens, depth)] * len(weight),
            (
                which, scan, act, row(skip_gain), joined, grad_resid, block_input, row(mixer_gain), grad_gate,
                *weight,
            ),
            grid=(2,),
            in_specs=[
                SMEM, wide, wide, pl.BlockSpec((1, depth), block), pl.BlockSpec((ext, depth), lambda c: (0, 2 + c)),
                full(tokens, depth), full(tokens, depth), full(1, depth), wide,
            ]
            + [pl.BlockSpec((depth, depth), lambda c: (0, 2 + c))] * len(weight),
            out_specs=[pl.BlockSpec((depth, depth), block)] + [full(tokens, depth)] * len(weight),
            scratch=[pltpu.VMEM((tokens, depth), BF16)] * 2,
            name="late",
        )

    (late_sent,) = late(core, ())
    late_kept, grad_gate_normed = late(1 - core, (in_proj,))
    late_got = grid.swap(late_sent, "core", 1)
    down_first = inner_swaps(downs_sent, 0)

    def first(total):
        total, held["through"], held["downs"], *held["up_second"] = tie(total, through, downs_sent, *up_second)
        return total

    def second(total):
        total, got, kept, held["normed"], *held["down_first"] = tie(
            total, late_got, late_kept, grad_gate_normed, *down_first
        )
        held["late"] = sum_first(grid, [kept, got])
        return total

    end = entering(grid, back_pair, rate, True, {1: first, 2: second})
    up_second = held["up_second"]
    end, near, far = tie(end, results[1], results[2] + held["through"])
    near, far = grid.swap(near, "outer", 1), grid.swap(far, "outer", 2)
    grad_gate_normed = held["normed"]
    late_first, late_second = held["late"]

    def with_others(own, firsts, seconds):
        for pair in zip(firsts, seconds):
            own = own + jnp.concatenate(pair, axis=0)
        return own

    def scan_back(c, before):
        at = lambda _: (0, c)
        tok, one_row = pl.BlockSpec((tokens, chunk), at), pl.BlockSpec((1, chunk), at)
        state_rows = pl.BlockSpec((states, chunk), at)
        return call(
            functools.partial(scan_back_kernel, rank_n, states),
            [
                shape(tokens, width), shape(tokens, width), shape(states, width),
                shape(rank_n + 2 * states, tokens),
            ],
            (
                masked, steps, drive, act, pre, grad_scan, row(skip_gain), history, history, start, end, rate, proj,
                step_proj, *before,
            ),
            grid=(blocks,),
            in_specs=[
                tok, tok, tok, tok, tok, tok, one_row,
                pl.BlockSpec((token_block, states, chunk), lambda i: (blocks - 1 - i, 0, c)),
                pl.BlockSpec(
                    (8, states, chunk),
                    lambda i: (jnp.maximum((blocks - 1 - i) * (token_block // 8) - 1, 0), 0, c),
                ),
                state_rows, state_rows, state_rows, proj_full, pl.BlockSpec((rank_n, chunk), at),
            ]
            + [pl.BlockSpec(memory_space=pl.ANY)] * len(before),
            out_specs=[tok, tok, state_rows, proj_full],
            scratch=[lanes, lanes]
            + [pltpu.VMEM((tokens, chunk), F32)] * 2
            + [pltpu.VMEM((token_block, states, 128), F32)] * 2
            + [pltpu.VMEM((states, chunk), F32)] * 2
            + [pltpu.VMEM((2, states, 128), F32)],
            name="scan_back",
            aliases={14 + i: i for i in range(len(before))},
        )

    *filled, grad_proj_a = scan_back(0, ())
    filled, late_first, late_second = tie(filled, late_first, late_second)
    late_both = sum_second(grid, late_first, late_second)
    *filled, grad_proj_b = scan_back(1, filled)
    filled, late_both, near, far, downs_sent = tie(filled, late_both, near, far, held["downs"])
    down_second = inner_swaps(downs_sent, 1)
    result = results[0] + near + far
    result_parts = swap_y(grid, [result[p * 2 * cap : (p + 1) * 2 * cap] for p in range(parts)])
    late_cut = cut_outer(grid, late_both)
    late_through = grid.swap(late_cut[3], "outer", 1)
    grad_act, grad_pre, grad_decay, grad_proj_c = scan_back(2, filled)
    grad_act, late_through, result_parts, down_second = tie(grad_act, late_through, result_parts, down_second)
    late_total = outer_reduce_rest(grid, late_cut, late_through)
    unit = 2 * grid.size["inner"] * grid.size["y"]
    half = -(-max(depth // 2 + 3 * states + rank_n, depth // 2 + rank_n + 40) // unit) * unit
    small = jnp.concatenate([small[:9], loads[0:1]], axis=0)
    kept, sent_half, input_grad, edge = call(
        functools.partial(input_back_kernel, rank_n, states),
        [shape(half, width), shape(half, width), shape(tokens, depth), shape(HALO, depth)],
        (
            core, grad_proj_a, grad_proj_b, grad_proj_c, proj, state_proj_t, act, grad_act, grad_pre, conv, joined,
            conv_weight, since, in_proj, block_input, halo, row(mixer_gain), grad_gate_normed, grad_resid,
            grad_decay, grad_skip, small,
        ),
        grid=(chunks,),
        in_specs=[
            SMEM, proj_full, proj_full, proj_full, proj_full, pl.BlockSpec((rank_n + 2 * states, chunk), block),
            tok, tok, tok, tok, pl.BlockSpec((ext, chunk), block), pl.BlockSpec((taps, chunk), block),
            full(tokens, 1), pl.BlockSpec((depth, chunk), block), full(tokens, depth), full(HALO, depth),
            full(1, depth), full(tokens, depth), full(tokens, depth), state_rows, one_row, full(10, depth),
        ],
        out_specs=[
            pl.BlockSpec((half, chunk), block), pl.BlockSpec((half, chunk), block), full(tokens, depth),
            full(HALO, depth),
        ],
        scratch=[pltpu.VMEM((ext, depth), BF16)] * 2
        + [pltpu.VMEM((ext, chunk), F32), pltpu.VMEM((ext, depth), F32)],
        name="input_back",
    )
    kept, sent_half, late_total = tie(kept, sent_half, late_total)
    late_near, late_far = grid.swap(late_total, "outer", 1), grid.swap(late_total, "outer", 2)
    sent_got = grid.swap(sent_half, "core", 1)
    kept, sent_got = tie(kept, sent_got)
    grads_first, grads_second = sum_first(grid, [kept, sent_got])
    late_near, late_far, grads_first, grads_second = tie(late_near, late_far, grads_first, grads_second)
    late_last = grid.swap(late_far, "outer", 1)
    grads = sum_second(grid, grads_first, grads_second)
    late_last, grads, edge, result_parts, up_parts, down_parts = tie(
        late_last, grads, edge, result_parts,
        [up_grads[0], up_first, up_second], [down_grads[0], held["down_first"], down_second],
    )
    from_next = grid.along(edge, -1)
    input_grad = jnp.concatenate([input_grad[: tokens - HALO], input_grad[tokens - HALO :] + from_next], axis=0)
    grad_up = with_others(*up_parts)
    result = core_last(grid, result_parts, cap, False)
    late_first, late_second = spread_second(grid, join_outer(grid, late_total, late_near, late_far, late_last))
    grads = sum_outer(grid, grads)
    late_first, late_second, grads, grad_up = tie(late_first, late_second, grads, grad_up)
    late_first, late_second = gather_rows(grid, late_first, "inner"), gather_rows(grid, late_second, "y")
    grads = spread_outer(grid, grads)
    late_first, late_second, grads, result, input_grad = tie(late_first, late_second, grads, result, input_grad)
    combined = jnp.dot(table.T, result.astype(F32), precision=lax.Precision.HIGHEST, preferred_element_type=F32)
    block_output = resid + gate * combined
    late_other = [grid.swap(late_first, "core", 1), grid.swap(late_second, "core", 1)]
    grads_first, grads_second = spread_second(grid, grads)
    grads_first, grads_second, down_parts, block_output, *late_other = tie(
        grads_first, grads_second, down_parts, block_output, *late_other
    )
    grad_down = with_others(*down_parts)
    grads_first, grads_second = gather_rows(grid, grads_first, "inner"), gather_rows(grid, grads_second, "y")
    quarter = pl.BlockSpec((half // 2, chunk), block)
    late_rows = full(depth // 2, width)
    grad_in_proj, grad_out_proj = call(
        finish_late_kernel,
        [shape(depth, 2 * width), shape(2, depth, depth)],
        (core, late_first, late_second, *late_other),
        grid=(2,),
        in_specs=[SMEM] + [late_rows] * 4,
        out_specs=[
            pl.BlockSpec((depth // 2, width), lambda r: (r, 1)),
            pl.BlockSpec((2, depth // 2, depth), lambda r: (0, r, 0)),
        ],
        name="finish_late",
    )
    grads_first, grads_second, grad_in_proj, grad_down = tie(grads_first, grads_second, grad_in_proj, grad_down)
    grads_other = [grid.swap(grads_first, "core", 1), grid.swap(grads_second, "core", 1)]
    tall = lambda columns: pl.BlockSpec((chunk, columns), lambda c: (c, 0))
    (
        grad_in_proj, grad_state_proj, grad_step_proj, grad_decay_log, grad_conv_weight, rows, small,
    ) = call(
        functools.partial(finish_kernel, rank_n, states, taps),
        [
            shape(depth, 2 * width), shape(width, rank_n + 2 * states), shape(rank_n, width),
            shape(width, states), shape(taps, width), shape(8, width), shape(32, chunk),
        ],
        (core, grads_first, grads_second, *grads_other, grad_in_proj),
        grid=(chunks,),
        in_specs=[SMEM] + [quarter] * 4 + [pl.BlockSpec(memory_space=pl.ANY)],
        out_specs=[
            pl.BlockSpec((depth, chunk), block), tall(rank_n + 2 * states), pl.BlockSpec((rank_n, chunk), block),
            tall(states), pl.BlockSpec((taps, chunk), block), pl.BlockSpec((8, chunk), block), full(32, chunk),
        ],
        name="finish",
        aliases={5: 0},
    )
    small = jnp.concatenate([small[:16], small[16:, : depth - chunk]], axis=1)
    return (
        block_output,
        input_grad,
        small[10],
        grad_in_proj,
        grad_conv_weight,
        rows[taps],
        grad_state_proj,
        grad_step_proj,
        rows[taps + 1],
        grad_decay_log,
        rows[taps + 2],
        grad_out_proj.reshape(width, depth),
        small[8],
        small[:experts].T,
        grad_up[None],
        grad_down[None],
        small[9, :experts].astype(jnp.int32),
        small[9, 128 : 128 + experts].astype(jnp.int32),
    )


def solution(mesh):
    rows, copied = P(("seq", "exp"), None), P()
    up, down = P("exp", None, "seq"), P("exp", "seq", None)
    in_specs = (rows, copied, rows, rows) + (copied,) * 12 + (up, down)
    out_specs = (rows, rows) + (copied,) * 12 + (up, down, copied, copied)
    return jax.shard_map(per_device, mesh=mesh, in_specs=in_specs, out_specs=out_specs, check_vma=False)
```

```python
import functools

import jax
import jax.numpy as jnp
from jax import lax
from jax.experimental import pallas as pl
from jax.experimental.pallas import tpu as pltpu
from jax.sharding import PartitionSpec as P

F32 = jnp.float32
BF16 = jnp.bfloat16
EPS = 1e-05
LOG2E = 1.4426950408889634
HALO = 16
RESET = 1e9
AXES = ("seq", "exp")
NN, NT, TN = ((1,), (0,)), ((1,), (1,)), ((0,), (0,))
VMEM_BYTES = 52 << 20
MICROSECONDS = {
    "route": 1, "join": 8, "features": 250, "join_states": 1, "scan": 200, "early": 200, "expert": 60,
    "expert_grads": 300, "mixer_back": 300, "late": 200, "scan_back": 10, "input_back": 11, "finish_late": 8, "finish": 6,
}


class Grid:
    def __init__(self):
        self.seq, self.exp = lax.axis_size("seq"), lax.axis_size("exp")
        self.outer = 4
        self.size = {
            "core": 2,
            "y": self.exp // 2,
            "inner": self.seq // self.outer,
            "outer": self.outer,
        }
        self.total = self.seq * self.exp
        index, step, self.step, self.at = lax.axis_index(AXES), 1, {}, {}
        for name in ("core", "y", "inner", "outer"):
            self.step[name] = step
            self.at[name] = (index // step) % self.size[name]
            step *= self.size[name]
        self.index = index

    def swap(self, block, name, mask):
        return self.swap_bits(block, mask * self.step[name])

    def swap_bits(self, block, bits):
        return lax.ppermute(block, AXES, [(i, i ^ bits) for i in range(self.total)])

    def along(self, block, distance):
        route = [(i - distance, i) for i in range(self.total) if 0 <= i - distance < self.total]
        return lax.ppermute(block, AXES, route)


def tie(*values):
    return lax.optimization_barrier(values)


def outer_reduce_rest(grid, parts, through):
    through, near = tie(through, parts[1])
    near = grid.swap(near, "outer", 1)
    far = grid.swap(parts[2] + through, "outer", 2)
    return parts[0] + near + far


def in_order(parts, place):
    bit = 1
    while bit < len(parts):
        turned = ((place // bit) % 2) == 1
        parts = [jnp.where(turned, parts[i ^ bit], parts[i]) for i in range(len(parts))]
        bit *= 2
    return parts


def rows_of(parts, first, rows):
    return functools.reduce(jnp.add, [lax.dynamic_slice_in_dim(part, first, rows, 0) for part in parts])


def scatter_rows(grid, parts, name, rows, start=0):
    count, place = grid.size[name], grid.at[name]
    rows = rows // count
    sent = [rows_of(parts, start + (place ^ s) * rows, rows) for s in range(1, count)]
    got = [grid.swap(block, name, s) for s, block in enumerate(sent, 1)]
    parts, _ = tie(list(parts), sent)
    return [rows_of(parts, start + place * rows, rows)] + got


def gather_rows(grid, block, name):
    count = grid.size[name]
    if count == 1:
        return block
    parts = [block] + [grid.swap(block, name, s) for s in range(1, count)]
    return jnp.concatenate(in_order(parts, grid.at[name]), axis=0)


def sum_first(grid, parts):
    rows = parts[0].shape[0] // 2
    return scatter_rows(grid, parts, "inner", rows), scatter_rows(grid, parts, "y", rows, rows)


def sum_second(grid, first, second):
    rows = first[0].shape[0]
    first, second = scatter_rows(grid, first, "y", rows), scatter_rows(grid, second, "inner", rows)
    return [jnp.concatenate(pair, axis=0) for pair in zip(first, second)]


def cut_outer(grid, parts):
    columns = parts[0].shape[1] // grid.outer
    return [
        functools.reduce(
            jnp.add,
            [lax.dynamic_slice_in_dim(p, (grid.at["outer"] ^ s) * columns, columns, 1) for p in parts],
        )
        for s in range(grid.outer)
    ]


def sum_outer(grid, parts):
    own, *others = cut_outer(grid, parts)
    return functools.reduce(jnp.add, [grid.swap(part, "outer", s) for s, part in enumerate(others, 1)], own)


def spread_outer(grid, total):
    count = grid.size["outer"]
    parts = [total] + [grid.swap(total, "outer", s) for s in range(1, count)]
    return jnp.concatenate(in_order(parts, grid.at["outer"]), axis=1)


def join_outer(grid, own, near, far, last):
    return jnp.concatenate(in_order([own, near, far, last], grid.at["outer"]), axis=1)


def spread_second(grid, both):
    own = both.shape[0] // 2
    return gather_rows(grid, both[:own], "y"), gather_rows(grid, both[own:], "inner")


def spread_first(grid, first, second):
    return jnp.concatenate([gather_rows(grid, first, "inner"), gather_rows(grid, second, "y")], axis=0)


def join_states_kernel(last, later_ref, total_ref, got_ref, ahead_ref, rate_ref, *outs):
    states = rate_ref.shape[0]
    rows, sums = slice(0, states), slice(states, states + 1)

    def follow(early, late, out):
        out[rows, :] = jnp.exp2(rate_ref[...] * late[sums, :]) * early[rows, :] + late[rows, :]
        out[sums, :] = early[sums, :] + late[sums, :]

    @pl.when(later_ref[0] == 1)
    def _():
        follow(got_ref, ahead_ref, outs[0])
        if not last:
            follow(got_ref, total_ref, outs[1])

    @pl.when(later_ref[0] == 0)
    def _():
        outs[0][...] = ahead_ref[...]
        if not last:
            follow(total_ref, got_ref, outs[1])


def entering(grid, pair, rate, backward, after):
    states = rate.shape[0]
    total, ahead, hop = pair, jnp.zeros_like(pair), 1
    bits = 1
    while bits < grid.total:
        got = grid.swap_bits(total, bits)
        later = ((grid.index // bits) % 2).astype(jnp.int32)
        later = (1 - later if backward else later).reshape(1)
        last = 2 * bits >= grid.total
        whole = pl.BlockSpec(memory_space=pltpu.VMEM)
        ahead, *rest = call(
            functools.partial(join_states_kernel, last),
            [shape(*pair.shape)] * (1 if last else 2),
            (later, total, got, ahead, rate),
            in_specs=[SMEM] + [whole] * 4,
            name="join_states",
        )
        total = rest[0] if rest else None
        if hop in after:
            total = after[hop](total)
        bits, hop = 2 * bits, hop + 1
    return ahead[:states]


def pad_rows(block, rows):
    return jnp.pad(block, ((0, rows - block.shape[0]), (0, 0)))


def core_first(grid, block, cap, tail):
    ny, width = grid.size["y"], 2 * cap
    slots = ny * width
    send = [block[s * width + cap : (s + 1) * width] for s in range(ny)] + ([block[slots:]] if tail else [])
    got = grid.swap(jnp.concatenate(send, axis=0), "core", 1)
    parts = []
    for s in range(ny):
        rows = [block[s * width : s * width + cap], got[s * cap : (s + 1) * cap]]
        if tail:
            ends = [block[slots + 2 * s : slots + 2 * s + 1], got[ny * cap + 2 * s + 1 : ny * cap + 2 * s + 2]]
            rows.append(pad_rows(jnp.concatenate(ends, axis=0), 8))
        parts.append(jnp.concatenate(rows, axis=0))
    return parts


def swap_y(grid, parts):
    return [parts[0]] + [grid.swap(part, "y", s) for s, part in enumerate(parts[1:], 1)]


def core_last(grid, parts, cap, tail):
    ny = grid.size["y"]
    send = [p[cap : 2 * cap] for p in parts]
    if tail:
        send.append(pad_rows(jnp.concatenate([p[2 * cap + 1 : 2 * cap + 2] for p in parts], axis=0), 8))
    got = grid.swap(jnp.concatenate(send, axis=0), "core", 1)
    rows, ends = [], []
    for s, p in enumerate(parts):
        rows += [p[:cap], got[s * cap : (s + 1) * cap]]
        if tail:
            ends += [p[2 * cap : 2 * cap + 1], got[ny * cap + s : ny * cap + s + 1]]
    if tail:
        rows.append(pad_rows(jnp.concatenate(ends, axis=0), 8))
    return jnp.concatenate(rows, axis=0)


def split(value):
    high = value.astype(BF16)
    return high, (value - high.astype(F32)).astype(BF16)


def dot(left, right, dims):
    return lax.dot_general(left, right, (dims, ((), ())), preferred_element_type=F32)


def product(left, right, dims):
    return dot(left[0], right[0], dims) + (dot(left[0], right[1], dims) + dot(left[1], right[0], dims))


def pick(exact, value, dims):
    high, low = split(value)
    return dot(exact, high, dims) + dot(exact, low, dims)


def sigmoid(value):
    return 1.0 / (1.0 + jnp.exp(-value))


def softplus(value):
    small = jnp.exp(-jnp.abs(value))
    series = small * (1.0 - small * (0.5 - small * (1.0 / 3.0 - small * (0.25 - small * 0.2))))
    return jnp.maximum(value, 0.0) + jnp.where(small < 0.03, series, jnp.log(1.0 + small))


def iota(shape, dim):
    return lax.broadcasted_iota(jnp.int32, shape, dim)


def scale_of(value):
    return lax.rsqrt(jnp.mean(value * value, axis=1, keepdims=True) + EPS)


def over_lanes(ref, columns):
    rows = columns.shape[0]
    for t in range(columns.shape[1]):
        ref[t] = jnp.broadcast_to(columns[:, t : t + 1], (rows, 128))


def widen(value, width):
    return jnp.concatenate([value] * (width // 128), axis=1)


def call(kernel, outs, ins, grid=None, in_specs=None, out_specs=None, scratch=(), name=None, aliases=None):
    whole = pl.BlockSpec(memory_space=pltpu.VMEM)
    return pl.pallas_call(
        kernel,
        out_shape=outs,
        grid=grid or (),
        in_specs=in_specs or [whole] * len(ins),
        out_specs=out_specs or jax.tree.map(lambda _: whole, outs),
        scratch_shapes=scratch,
        name=name,
        cost_estimate=pl.CostEstimate(
            flops=int(MICROSECONDS[name] * 1.1e9), transcendentals=0, bytes_accessed=int(MICROSECONDS[name] * 1e6)
        ),
        input_output_aliases=aliases or {},
        compiler_params=pltpu.CompilerParams(vmem_limit_bytes=VMEM_BYTES),
    )(*ins)


def shape(*dims, dtype=F32):
    return jax.ShapeDtypeStruct(dims, dtype)


SMEM = pl.BlockSpec(memory_space=pltpu.SMEM)


def full(*dims):
    return pl.BlockSpec(dims, lambda *_: (0,) * len(dims))


def route_kernel(experts, cap, me_ref, ids_ref, grad_ref, sent_ref, table_ref, rank_ref, load_ref):
    ids = ids_ref[...]
    tokens = ids.shape[0]
    chosen = (ids == iota((tokens, 128), 1)).astype(F32)
    before = (iota((tokens, tokens), 0) > iota((tokens, tokens), 1)).astype(BF16)
    rank = jnp.sum(dot(before, chosen.astype(BF16), NN) * chosen, axis=1, keepdims=True)
    kept = (rank < cap).astype(F32)
    place = jnp.where(rank < cap, ((ids ^ me_ref[0]) * cap).astype(F32) + rank, -1.0)
    row = jnp.broadcast_to(place, (tokens, tokens)).T
    slots = experts * cap
    table = (iota((slots, tokens), 0).astype(F32) == jnp.broadcast_to(row[0:1], (slots, tokens))).astype(F32)
    table = table.astype(BF16)
    table_ref[...] = table
    rank_ref[...] = rank
    sent_ref[...] = pick(table, grad_ref[...], NN)
    load_ref[...] = jnp.zeros_like(load_ref)
    load_ref[0:1, 0:128] = jnp.sum(chosen, axis=0, keepdims=True)
    load_ref[0:1, 128:256] = jnp.sum(chosen * (1.0 - kept), axis=0, keepdims=True)


def join_kernel(x_ref, halo_ref, gain_ref, weight_ref, joined_ref, high, low):
    @pl.when(pl.program_id(0) == 0)
    def _():
        x = jnp.concatenate([halo_ref[...], x_ref[...]], axis=0)
        high[...], low[...] = split(x * scale_of(x) * gain_ref[...])

    joined_ref[...] = product((high[...], low[...]), split(weight_ref[...]), NN)


def features_kernel(
    rank_n,
    states,
    inner_ref,
    since_ref,
    conv_w_ref,
    conv_b_ref,
    state_proj_ref,
    step_proj_ref,
    step_bias_ref,
    rate_ref,
    conv_ref,
    act_ref,
    pre_ref,
    steps_ref,
    masked_ref,
    drive_ref,
    proj_ref,
    pair_ref,
    in_lanes,
):
    tokens, width = act_ref.shape
    taps = conv_w_ref.shape[0]
    since = since_ref[...]
    conv = jnp.broadcast_to(conv_b_ref[...], (tokens, width))
    for k in range(taps):
        valid = (since >= taps - 1 - k).astype(F32)
        first = HALO - taps + 1 + k
        conv = conv + inner_ref[first : first + tokens, :] * valid * conv_w_ref[k : k + 1, :]
    act = conv * sigmoid(conv)
    conv_ref[...] = conv
    act_ref[...] = act
    proj = product(split(state_proj_ref[...]), split(act), NT)
    proj_ref[...] = proj
    pre = product(split(proj[:rank_n]), split(step_proj_ref[...]), TN) + step_bias_ref[...]
    pre_ref[...] = pre
    steps = softplus(pre)
    steps_ref[...] = steps
    masked = jnp.where(since == 0, RESET, steps)
    masked_ref[...] = masked
    drive_ref[...] = steps * act
    pair_ref[states : states + 1, :] = jnp.sum(masked, axis=0, keepdims=True)
    over_lanes(in_lanes, proj[rank_n : rank_n + states])
    chunk = 512
    for c in range(width // chunk):
        part = slice(c * chunk, (c + 1) * chunk)
        rate = rate_ref[:, part]

        def eight(group, state):
            for i in range(8):
                t = group * 8 + i
                decay = jnp.exp2(masked_ref[pl.ds(t, 1), part] * rate)
                state = decay * state + drive_ref[pl.ds(t, 1), part] * widen(in_lanes[t], chunk)
            return state

        pair_ref[0:states, part] = lax.fori_loop(0, tokens // 8, eight, jnp.zeros((states, chunk), F32))


def slot_tables(slots, cap, experts):
    slot = iota((slots, 8), 0)
    first = sum((slot >= cap * e).astype(jnp.int32) for e in range(1, experts))
    block = (first == iota((slots, 8), 1)).astype(F32)
    slot = iota((slots, 128), 0)
    first = sum(((slot >= cap * e).astype(jnp.int32) for e in range(1, experts)))
    within = (slot - first * cap == iota((slots, 128), 1)).astype(F32)
    return block, within


def scan_kernel(
    rank_n,
    states,
    experts,
    cap,
    me_ref,
    masked_ref,
    drive_ref,
    act_ref,
    gate_z_ref,
    start_ref,
    rate_ref,
    skip_ref,
    proj_ref,
    out_proj_ref,
    x_ref,
    gain_ref,
    router_ref,
    ids_ref,
    rank_ref,
    table_ref,
    scan_ref,
    history_ref,
    resid_ref,
    sent_ref,
    probs_ref,
    gate_ref,
    in_lanes,
    out_lanes,
    total,
):
    tokens, chunk = masked_ref.shape
    step = pl.program_id(0)

    @pl.when(step == 0)
    def _():
        over_lanes(in_lanes, proj_ref[rank_n : rank_n + states, :])
        over_lanes(out_lanes, proj_ref[rank_n + states : rank_n + 2 * states, :])
        total[...] = x_ref[...]

    rate = rate_ref[...]

    def eight(group, state):
        for i in range(8):
            t = group * 8 + i
            decay = jnp.exp2(masked_ref[pl.ds(t, 1), :] * rate)
            state = decay * state + drive_ref[pl.ds(t, 1), :] * widen(in_lanes[t], chunk)
            history_ref[t] = state
            scan_ref[pl.ds(t, 1), :] = jnp.sum(state * widen(out_lanes[t], chunk), axis=0, keepdims=True)
        return state

    lax.fori_loop(0, tokens // 8, eight, start_ref[...])
    gate_z = gate_z_ref[HALO:, :]
    mixed = (scan_ref[...] + skip_ref[...] * act_ref[...]) * (gate_z * sigmoid(gate_z))
    total[...] += product(split(mixed), split(out_proj_ref[...]), NN)

    @pl.when(step == pl.num_programs(0) - 1)
    def _():
        resid = total[...]
        resid_ref[...] = resid
        normed = resid * scale_of(resid) * gain_ref[...]
        logits = product(split(normed), split(router_ref[...]), NT)
        known = iota((tokens, 8), 1) < experts
        logits = jnp.where(known, logits, -1e30)
        raised = jnp.exp(logits - jnp.max(logits, axis=1, keepdims=True))
        raised = jnp.where(known, raised, 0.0)
        probs = raised / jnp.sum(raised, axis=1, keepdims=True)
        probs_ref[...] = probs
        ids = ids_ref[...]
        gate = jnp.sum(jnp.where(ids == iota((tokens, 8), 1), probs, 0.0), axis=1, keepdims=True)
        gate_ref[...] = gate
        slots = experts * cap
        sent_ref[0:slots, :] = pick(table_ref[...], normed, NN)
        sent_ref[slots:, :] = jnp.zeros((8, sent_ref.shape[1]), F32)
        rank = rank_ref[...].astype(jnp.int32)
        to_block = jnp.where(((ids ^ me_ref[0]) == iota((tokens, 8), 1)) & (rank < cap), gate, 0.0)
        at_rank = (rank == iota((tokens, 128), 1)).astype(BF16)
        high, low = split(to_block)
        rest = (to_block - high.astype(F32) - low.astype(F32)).astype(BF16)
        rows = dot(high, at_rank, TN) + (dot(low, at_rank, TN) + dot(rest, at_rank, TN))
        sent_ref[slots:, 0:128] = rows


def early_kernel(pieces, slices, *refs):
    grads, downs, outs = refs[:pieces], refs[pieces : pieces + slices], refs[pieces + slices :]
    downs = [split(d[...]) for d in downs]
    for p in range(pieces):
        grad = split(grads[p][...])
        for i in range(slices):
            outs[p][i] = product(grad, downs[i], NT)


def gelu_parts(value):
    inner = 0.7978845608 * (value + 0.044715 * value * value * value)
    tanh = jnp.tanh(inner)
    slope = 0.5 * (1.0 + tanh) + 0.5 * value * (1.0 - tanh * tanh) * 0.7978845608 * (
        1.0 + 3.0 * 0.044715 * value * value
    )
    return 0.5 * value * (1.0 + tanh), slope


def expert_kernel(parts, slices, cap, *refs):
    tokens, ups, pulled_ref = refs[:parts], refs[parts : parts + slices], refs[parts + slices]
    backs, hidden_ref, grad_ref = refs[parts + slices + 1 : -2], refs[-2], refs[-1]
    width = 2 * cap
    slots, depth = parts * width, tokens[0].shape[1]
    block, within = slot_tables(width, cap, 2)
    within = within.astype(BF16)
    rows = split(jnp.concatenate([t[0:width, :] for t in tokens], axis=0))
    back = jnp.zeros((slots, depth), F32)
    to_gate = jnp.zeros((slots, 1), F32)
    for i in range(slices):
        up = split(ups[i][...])
        hidden, slope = gelu_parts(product(rows, up, NN))
        pull = pulled_ref[i]
        grad = pull * slope
        hidden_ref[i] = hidden
        grad_ref[i] = grad
        to_gate += jnp.sum(hidden * pull, axis=1, keepdims=True)
        back += product(split(grad), up, NT)
    for p in range(parts):
        part = slice(p * width, (p + 1) * width)
        backs[p][0:width, :] = back[part]
        backs[p][width:, :] = jnp.zeros((8, depth), F32)
        mine = block * to_gate[part]
        high, low = split(mine)
        rest = (mine - high.astype(F32) - low.astype(F32)).astype(BF16)
        backs[p][width:, 0:128] = dot(high, within, TN) + (dot(low, within, TN) + dot(rest, within, TN))


def expert_grads_kernel(pieces, parts, slices, cap, *refs):
    tokens, refs = refs[: pieces * parts], refs[pieces * parts :]
    grads, hiddens, pulls = (refs[i * pieces : (i + 1) * pieces] for i in range(3))
    downs, outs = refs[3 * pieces : 3 * pieces + slices], refs[3 * pieces + slices :]
    results, up_outs, down_outs = outs[:pieces], outs[pieces : pieces + slices], outs[pieces + slices :]
    width = 2 * cap
    downs = [split(d[...]) for d in downs]
    block, within = slot_tables(width, cap, 2)
    within = within.astype(BF16)
    for p in range(pieces):
        rows, gates = [], []
        for token in tokens[p * parts : (p + 1) * parts]:
            ends = token[width:, 0:128]
            high, low = split(ends)
            rest = (ends - high.astype(F32) - low.astype(F32)).astype(BF16)
            spread = dot(within, high, NT) + (dot(within, low, NT) + dot(within, rest, NT))
            gates.append(jnp.sum(spread * block, axis=1, keepdims=True))
            rows.append(token[0:width, :] * gates[-1])
        rows = split(jnp.concatenate(rows, axis=0))
        gated = split(grads[p][...] * jnp.concatenate(gates, axis=0))
        total = None
        for i in range(slices):
            hidden = split(hiddens[p][i])
            part = product(hidden, downs[i], NN)
            total = part if total is None else total + part
            up = product(rows, split(pulls[p][i]), TN)
            down = product(hidden, gated, TN)
            if p == 0:
                up_outs[i][...] = up
                down_outs[i][...] = down
            else:
                up_outs[i][...] += up
                down_outs[i][...] += down
        results[p][...] = total


def silu_parts(value):
    sig = sigmoid(value)
    return value * sig, sig * (1.0 + value * (1.0 - sig))


def mixer_back_kernel(
    rank_n,
    states,
    experts,
    cap,
    me_ref,
    back_ref,
    table_ref,
    gate_ref,
    probs_ref,
    ids_ref,
    rank_ref,
    resid_ref,
    grad_ref,
    gain_ref,
    router_ref,
    out_proj_ref,
    gate_z_ref,
    scan_ref,
    act_ref,
    skip_ref,
    masked_ref,
    rate_ref,
    proj_ref,
    steps_row_ref,
    grad_resid_ref,
    small_ref,
    grad_scan_ref,
    grad_gate_ref,
    grad_skip_ref,
    pair_ref,
    out_lanes,
    high,
    low,
):
    tokens, chunk = masked_ref.shape

    @pl.when(pl.program_id(0) == 0)
    def _():
        over_lanes(out_lanes, proj_ref[rank_n + states : rank_n + 2 * states, :])
        slots = experts * cap
        ids, rank = ids_ref[...], rank_ref[...].astype(jnp.int32)
        back = pick(table_ref[...], back_ref[0:slots, :], TN)
        at_rank = (rank == iota((tokens, 128), 1)).astype(BF16)
        ends = back_ref[slots:, 0:128]
        first, second = split(ends)
        third = (ends - first.astype(F32) - second.astype(F32)).astype(BF16)
        spread = dot(at_rank, first, NT) + (dot(at_rank, second, NT) + dot(at_rank, third, NT))
        mine = ((ids ^ me_ref[0]) == iota((tokens, 8), 1)) & (rank < cap)
        grad_gate = jnp.sum(jnp.where(mine, spread, 0.0), axis=1, keepdims=True)
        probs = probs_ref[...]
        grad_probs = jnp.where(ids == iota((tokens, 8), 1), grad_gate, 0.0)
        grad_logits = probs * (grad_probs - jnp.sum(probs * grad_probs, axis=1, keepdims=True))
        resid, gain = resid_ref[...], gain_ref[...]
        scale = scale_of(resid)
        normed = resid * scale * gain
        logits_two = split(grad_logits)
        grad_normed = gate_ref[...] * back + product(logits_two, split(router_ref[...]), NN)
        small_ref[...] = jnp.zeros_like(small_ref)
        small_ref[0:8, :] = product(logits_two, split(normed), TN)
        small_ref[8:9, :] = jnp.sum(grad_normed * resid * scale, axis=0, keepdims=True)
        pulled = gain * grad_normed
        grad_resid = (
            grad_ref[...]
            + scale * pulled
            - resid * (scale * scale * scale) * jnp.mean(pulled * resid, axis=1, keepdims=True)
        )
        grad_resid_ref[...] = grad_resid
        high[...], low[...] = split(grad_resid)

    grad_mixed = product((high[...], low[...]), split(out_proj_ref[...]), NT)
    silu, slope = silu_parts(gate_z_ref[HALO:, :])
    act = act_ref[...]
    grad_scan = grad_mixed * silu
    grad_scan_ref[...] = grad_scan
    grad_gate_ref[...] = grad_mixed * (scan_ref[...] + skip_ref[...] * act) * slope
    grad_skip_ref[...] = jnp.sum(grad_scan * act, axis=0, keepdims=True)
    rate = rate_ref[...]

    def eight(group, state):
        for i in range(8):
            t = tokens - 1 - (group * 8 + i)
            decay = jnp.exp2(masked_ref[pl.ds(t, 1), :] * rate)
            state = decay * (state + grad_scan_ref[pl.ds(t, 1), :] * widen(out_lanes[t], chunk))
        return state

    pair_ref[0:states, :] = lax.fori_loop(0, tokens // 8, eight, jnp.zeros((states, chunk), F32))
    pair_ref[states : states + 1, :] = steps_row_ref[...]


def late_kernel(
    which_ref, scan_ref, act_ref, skip_ref, gate_z_ref, grad_resid_ref, x_ref, gain_ref, grad_gate_ref, *refs
):
    high, low = refs[-2:]
    if len(refs) == 5:
        weight_ref, out_ref, normed_ref = refs[:3]
    else:
        weight_ref, out_ref, normed_ref = None, refs[0], None

    @pl.when(pl.program_id(0) == 0)
    def _():
        @pl.when(which_ref[0] == 0)
        def _():
            high[...], low[...] = split(grad_resid_ref[...])

        @pl.when(which_ref[0] == 1)
        def _():
            x = x_ref[...]
            high[...], low[...] = split(x * scale_of(x) * gain_ref[...])

        if normed_ref is not None:
            normed_ref[...] = jnp.zeros_like(normed_ref)

    @pl.when(which_ref[0] == 0)
    def _():
        gate_z = gate_z_ref[HALO:, :]
        mixed = (scan_ref[...] + skip_ref[...] * act_ref[...]) * (gate_z * sigmoid(gate_z))
        out_ref[...] = product(split(mixed), (high[...], low[...]), TN)

    @pl.when(which_ref[0] == 1)
    def _():
        out_ref[...] = product((high[...], low[...]), split(grad_gate_ref[...]), TN)

    if normed_ref is not None:
        normed_ref[...] += product(split(grad_gate_ref[...]), split(weight_ref[...]), NT)


def scan_back_kernel(
    rank_n,
    states,
    masked_ref,
    steps_ref,
    drive_ref,
    act_ref,
    pre_ref,
    grad_scan_ref,
    skip_ref,
    history_ref,
    before_ref,
    start_ref,
    end_ref,
    rate_ref,
    proj_ref,
    step_proj_ref,
    *refs,
):
    (
        grad_act_ref, grad_pre_ref, grad_decay_ref, grad_proj_ref,
        in_lanes, out_lanes, grad_drive, grad_steps, at_in, at_out, carried_ref, decays_ref, sums_ref,
    ) = refs[-13:]
    tokens, chunk = masked_ref.shape
    block = history_ref.shape[0]
    step, blocks = pl.program_id(0), pl.num_programs(0)
    first = (blocks - 1 - step) * block

    @pl.when(step == 0)
    def _():
        over_lanes(in_lanes, proj_ref[rank_n : rank_n + states, :])
        over_lanes(out_lanes, proj_ref[rank_n + states : rank_n + 2 * states, :])
        carried_ref[...] = end_ref[...]
        decays_ref[...] = jnp.zeros_like(decays_ref)
        sums_ref[...] = jnp.zeros_like(sums_ref)

    rate = rate_ref[...]
    entering_state = jnp.where(first == 0, start_ref[...], before_ref[7])

    def narrow(value):
        return functools.reduce(jnp.add, [value[:, c : c + 128] for c in range(0, chunk, 128)])

    def one(local, before, carried):
        state, decays = carried
        t = first + local
        masked = masked_ref[pl.ds(t, 1), :]
        grad = grad_scan_ref[pl.ds(t, 1), :]
        decay = jnp.exp2(masked * rate)
        state = state + grad * widen(out_lanes[t], chunk)
        at_out[local] = narrow(history_ref[local] * grad)
        at_in[local] = narrow(state * drive_ref[pl.ds(t, 1), :])
        grad_drive[pl.ds(t, 1), :] = jnp.sum(state * widen(in_lanes[t], chunk), axis=0, keepdims=True)
        state = decay * state
        pulled = state * before
        grad_steps[pl.ds(t, 1), :] = jnp.sum(pulled * rate, axis=0, keepdims=True)
        return state, decays + pulled * masked

    def eight(group, carried):
        for i in range(8):
            local = block - 1 - (group * 8 + i)
            carried = one(local, history_ref[local - 1], carried)
        return carried

    carried = lax.fori_loop(0, block // 8 - 1, eight, (carried_ref[...], decays_ref[...]))
    for local in range(7, 0, -1):
        carried = one(local, history_ref[local - 1], carried)
    carried_ref[...], decays_ref[...] = one(0, entering_state, carried)

    ones = jnp.ones((128, 128), BF16)
    lane = iota((states, 128), 1)
    for i, held in enumerate((at_in, at_out)):
        high, low = split(held[...].reshape(block * states, 128))
        spread = (dot(high, ones, NN) + dot(low, ones, NN)).reshape(block, states, 128)
        total = sums_ref[i]
        for local in range(block):
            total = jnp.where(lane == first + local, spread[local], total)
        sums_ref[i] = total

    @pl.when(step == blocks - 1)
    def _():
        grad_decay_ref[...] = decays_ref[...] * (rate * (1.0 / LOG2E))
        steps, act = steps_ref[...], act_ref[...]
        grad_act_ref[...] = skip_ref[...] * grad_scan_ref[...] + grad_drive[...] * steps
        grad_pre = (grad_steps[...] * (1.0 / LOG2E) + grad_drive[...] * act) * sigmoid(pre_ref[...])
        grad_pre_ref[...] = grad_pre
        grad_proj_ref[0:rank_n, :] = product(split(step_proj_ref[...]), split(grad_pre), NT)
        grad_proj_ref[rank_n : rank_n + states, :] = sums_ref[0]
        grad_proj_ref[rank_n + states : rank_n + 2 * states, :] = sums_ref[1]


def input_back_kernel(
    rank_n,
    states,
    core_ref,
    proj_a_ref,
    proj_b_ref,
    proj_c_ref,
    proj_ref,
    state_proj_ref,
    act_ref,
    grad_act_ref,
    grad_pre_ref,
    conv_ref,
    inner_ref,
    conv_w_ref,
    since_ref,
    weight_ref,
    x_ref,
    halo_ref,
    gain_ref,
    grad_gate_normed_ref,
    grad_resid_ref,
    grad_decay_ref,
    grad_skip_ref,
    small_ref,
    keep_ref,
    send_ref,
    input_ref,
    edge_ref,
    high,
    low,
    grad_inner,
    total,
):
    tokens, chunk = act_ref.shape
    depth = x_ref.shape[1]
    half = depth // 2
    taps = conv_w_ref.shape[0]
    step = pl.program_id(0)

    @pl.when(step == 0)
    def _():
        x = jnp.concatenate([halo_ref[...], x_ref[...]], axis=0)
        high[...], low[...] = split(x * scale_of(x) * gain_ref[...])
        total[...] = jnp.zeros_like(total)

    act, grad_pre = split(act_ref[...]), grad_pre_ref[...]
    grad_proj = split(proj_a_ref[...] + proj_b_ref[...] + proj_c_ref[...])
    grad_act = grad_act_ref[...] + product(grad_proj, split(state_proj_ref[...]), TN)
    _, slope = silu_parts(conv_ref[...])
    grad_conv = grad_act * slope
    since = since_ref[...]
    grad_inner[...] = jnp.zeros_like(grad_inner)
    rows = []
    for k in range(taps):
        valid = (since >= taps - 1 - k).astype(F32)
        first = HALO - taps + 1 + k
        held = grad_conv * valid
        rows.append(jnp.sum(held * inner_ref[first : first + tokens, :], axis=0, keepdims=True))
        grad_inner[first : first + tokens, :] += held * conv_w_ref[k : k + 1, :]
    rows.append(jnp.sum(grad_conv, axis=0, keepdims=True))
    rows.append(jnp.sum(grad_pre, axis=0, keepdims=True))
    rows.append(grad_skip_ref[...])
    grads = split(grad_inner[...])
    total[...] += product(grads, split(weight_ref[...]), NT)
    of_state_proj = product(grad_proj, act, NN)
    of_step_proj = product(split(proj_ref[0:rank_n, :]), split(grad_pre), NN)

    def first_half(out_ref):
        out_ref[0:half, :] = product((high[:, 0:half], low[:, 0:half]), grads, TN)
        at = half + 2 * states + rank_n
        out_ref[half:at, :] = of_state_proj
        out_ref[at : at + states, :] = grad_decay_ref[...]
        if at + states < out_ref.shape[0]:
            out_ref[at + states :, :] = jnp.zeros((out_ref.shape[0] - at - states, chunk), F32)

    def second_half(out_ref):
        out_ref[0:half, :] = product((high[:, half:], low[:, half:]), grads, TN)
        out_ref[half : half + rank_n, :] = of_step_proj
        at = half + rank_n
        out_ref[at:, :] = jnp.zeros((out_ref.shape[0] - at, chunk), F32)
        for i, row in enumerate(rows):
            out_ref[at + i : at + i + 1, :] = row

    @pl.when(core_ref[0] == 0)
    def _():
        first_half(keep_ref)
        second_half(send_ref)

    @pl.when(core_ref[0] == 1)
    def _():
        second_half(keep_ref)
        first_half(send_ref)

    @pl.when(step == pl.num_programs(0) - 1)
    def _():
        gain = gain_ref[...]

        def rows_back(x, grad):
            scale = scale_of(x)
            pulled = gain * grad
            back = scale * pulled - x * (scale * scale * scale) * jnp.mean(pulled * x, axis=1, keepdims=True)
            return back, jnp.sum(grad * x * scale, axis=0, keepdims=True)

        edge, edge_gain = rows_back(halo_ref[...], total[0:HALO, :])
        own, own_gain = rows_back(x_ref[...], total[HALO:, :] + grad_gate_normed_ref[...])
        edge_ref[...] = edge
        input_ref[...] = grad_resid_ref[...] + own
        small = jnp.concatenate([small_ref[0:10, :], edge_gain + own_gain], axis=0)

        def place_small(out_ref):
            at = half + rank_n + 8
            out_ref[at : at + 11, :] = small[:, 0:chunk]
            out_ref[at + 16 : at + 27, 0 : depth - chunk] = small[:, chunk:]

        @pl.when(core_ref[0] == 0)
        def _():
            place_small(send_ref)

        @pl.when(core_ref[0] == 1)
        def _():
            place_small(keep_ref)


def finish_late_kernel(core_ref, first_ref, second_ref, got_first_ref, got_second_ref, in_ref, out_ref):
    depth = out_ref.shape[2]
    step = pl.program_id(0)

    def write(gate, out):
        in_ref[...] = gate
        out_ref[0] = out[:, 0:depth]
        out_ref[1] = out[:, depth:]

    for i, (own, got) in enumerate(((first_ref, got_first_ref), (second_ref, got_second_ref))):

        @pl.when((core_ref[0] == 0) & (step == i))
        def _():
            write(own[...], got[...])

        @pl.when((core_ref[0] == 1) & (step == i))
        def _():
            write(got[...], own[...])


def finish_kernel(
    rank_n, states, taps, core_ref, first_ref, second_ref, got_first_ref, got_second_ref, _,
    in_ref, state_proj_ref, step_proj_ref, decay_ref, conv_w_ref, rows_ref, small_ref,
):
    depth = in_ref.shape[0]
    half, quarter = depth // 2, first_ref.shape[0]
    rest = half - quarter

    def first_half(one, two):
        in_ref[0:quarter, :] = one[...]
        in_ref[quarter:half, :] = two[0:rest, :]
        at = rest + 2 * states + rank_n
        state_proj_ref[...] = two[rest:at, :].T
        decay_ref[...] = two[at : at + states, :].T

    def second_half(one, two):
        in_ref[half : half + quarter, :] = one[...]
        in_ref[half + quarter :, :] = two[0:rest, :]
        step_proj_ref[...] = two[rest : rest + rank_n, :]
        at = rest + rank_n
        conv_w_ref[...] = two[at : at + taps, :]
        rows_ref[...] = two[at : at + 8, :]
        small_ref[...] = two[at + 8 : at + 40, :]

    @pl.when(core_ref[0] == 0)
    def _():
        first_half(first_ref, second_ref)
        second_half(got_first_ref, got_second_ref)

    @pl.when(core_ref[0] == 1)
    def _():
        first_half(got_first_ref, got_second_ref)
        second_half(first_ref, second_ref)


def per_device(
    block_input,
    seq_lengths,
    expert_ids,
    output_grad,
    mixer_gain,
    in_proj,
    conv_weight,
    conv_bias,
    state_proj,
    step_proj,
    step_bias,
    decay_log,
    skip_gain,
    out_proj,
    router_gain,
    router,
    expert_up,
    expert_down,
):
    grid = Grid()
    tokens, depth = block_input.shape
    taps, width = conv_weight.shape
    rank_n, states, experts = step_proj.shape[0], decay_log.shape[1], router.shape[1]
    cap = (5 * tokens + 4 * experts - 1) // (4 * experts)
    slots, hidden = experts * cap, expert_up.shape[2]
    chunk = 512
    chunks = width // chunk
    pieces, slices = grid.size["outer"], grid.size["inner"]
    token_block = 64
    blocks = tokens // token_block
    me = lax.axis_index("exp").astype(jnp.int32).reshape(1)
    ext = HALO + tokens

    halo = grid.along(block_input[tokens - HALO :], 1)

    count = seq_lengths.shape[0]
    earlier = jnp.arange(count)[:, None] > jnp.arange(count)[None, :]
    starts = jnp.sum(jnp.where(earlier, seq_lengths[None, :], 0), axis=1)
    position = grid.index * tokens + jnp.arange(tokens, dtype=jnp.int32)
    own_start = jnp.max(jnp.where(starts[None, :] <= position[:, None], starts[None, :], 0), axis=1)
    since = (position - own_start)[:, None]
    rate = -jnp.exp(decay_log.T) * LOG2E
    state_proj_t = state_proj.T
    router_t = pad_rows(router.T, 8)
    row = lambda vector: vector.reshape(1, -1)

    sent_grads, table, rank, loads = call(
        functools.partial(route_kernel, experts, cap),
        [shape(slots, depth), shape(slots, tokens, dtype=BF16), shape(tokens, 1), shape(8, depth)],
        (me, expert_ids, output_grad),
        in_specs=[SMEM] + [pl.BlockSpec(memory_space=pltpu.VMEM)] * 2,
        name="route",
    )
    halo, sent_grads = tie(halo, sent_grads)
    held_grads = core_first(grid, sent_grads, cap, False)
    up, down = expert_up[0], expert_down[0]
    up_rows = depth // 2
    downs = [down] + [grid.swap(down, "inner", s) for s in range(1, slices)]

    block = lambda c, *_: (0, c)
    joined = call(
        join_kernel,
        shape(ext, 2 * width),
        (block_input, halo, row(mixer_gain), in_proj),
        grid=(2 * chunks,),
        in_specs=[full(tokens, depth), full(HALO, depth), full(1, depth), pl.BlockSpec((depth, chunk), block)],
        out_specs=pl.BlockSpec((ext, chunk), block),
        scratch=[pltpu.VMEM((ext, depth), BF16)] * 2,
        name="join",
    )
    joined, *held_grads = tie(joined, *swap_y(grid, held_grads))
    own_grads = jnp.concatenate(held_grads, axis=0)
    joined, own_grads = tie(joined, own_grads)
    near_grads, far_grads = grid.swap(own_grads, "outer", 1), grid.swap(own_grads, "outer", 2)
    conv, act, pre, steps, masked, drive, proj, pair = call(
        functools.partial(features_kernel, rank_n, states),
        [shape(tokens, width)] * 6 + [shape(rank_n + 2 * states, tokens), shape(states + 1, width)],
        (joined, since, conv_weight, row(conv_bias), state_proj_t, step_proj, row(step_bias), rate),
        grid=(1,),
        in_specs=[
            full(ext, width),
            full(tokens, 1),
            full(taps, width),
            full(1, width),
            full(rank_n + 2 * states, width),
            full(rank_n, width),
            full(1, width),
            full(states, width),
        ],
        out_specs=[full(tokens, width)] * 6 + [full(rank_n + 2 * states, tokens), full(states + 1, width)],
        scratch=[pltpu.VMEM((tokens, states, 128), F32)],
        name="features",
    )
    pair, *downs = tie(pair, *downs)
    held = {}

    def third(total):
        total, held["near"], held["far"] = tie(total, near_grads, far_grads)
        return total

    start = entering(grid, pair, rate, False, {2: third})
    start, near_grads, far_grads = tie(start, held["near"], held["far"])
    up_top = [grid.swap(up[:up_rows], "inner", s) for s in range(1, slices)]
    last_grads = grid.swap(far_grads, "outer", 1)
    tok = pl.BlockSpec((tokens, chunk), block)
    gate_half = pl.BlockSpec((ext, chunk), lambda c, *_: (0, chunks + c))
    one_row = pl.BlockSpec((1, chunk), block)
    state_rows = pl.BlockSpec((states, chunk), block)
    history_block = pl.BlockSpec((tokens, states, chunk), lambda c: (0, 0, c))
    out_rows = pl.BlockSpec((chunk, depth), lambda c, *_: (c, 0))
    proj_full = full(rank_n + 2 * states, tokens)
    lanes = pltpu.VMEM((tokens, states, 128), F32)
    scan, history, resid, sent, probs, gate = call(
        functools.partial(scan_kernel, rank_n, states, experts, cap),
        [
            shape(tokens, width),
            shape(tokens, states, width),
            shape(tokens, depth),
            shape(slots + 8, depth),
            shape(tokens, 8),
            shape(tokens, 1),
        ],
        (
            me, masked, drive, act, joined, start, rate, row(skip_gain), proj, out_proj, block_input,
            row(router_gain), router_t, expert_ids, rank, table,
        ),
        grid=(chunks,),
        in_specs=[
            SMEM, tok, tok, tok, gate_half, state_rows, state_rows, one_row, proj_full, out_rows,
            full(tokens, depth), full(1, depth), full(8, depth), full(tokens, 1), full(tokens, 1),
            full(slots, tokens),
        ],
        out_specs=[
            tok, history_block, full(tokens, depth), full(slots + 8, depth), full(tokens, 8), full(tokens, 1),
        ],
        scratch=[lanes, lanes, pltpu.VMEM((tokens, depth), F32)],
        name="scan",
    )

    sent, last_grads, up_top, up_bottom = tie(sent, last_grads, up_top, up[up_rows:])
    up_bottom = [grid.swap(up_bottom, "inner", s) for s in range(1, slices)]
    own_tokens, last_grads = tie(core_first(grid, sent, cap, True), last_grads)
    grad_pieces = [own_grads, near_grads, far_grads, last_grads]
    pulled = call(
        functools.partial(early_kernel, pieces, slices),
        [shape(slices, slots, hidden)] * pieces,
        (*grad_pieces, *downs),
        name="early",
    )
    parts = grid.size["y"]
    outer_swap = lambda blocks, mask: [grid.swap(block, "outer", mask) for block in blocks]
    near_first, far_first = outer_swap(own_tokens[:1], 1), outer_swap(own_tokens[:1], 2)
    own_tokens, pulled, up_bottom = tie(swap_y(grid, own_tokens), pulled, up_bottom)
    ups = [up] + [jnp.concatenate(pair, axis=0) for pair in zip(up_top, up_bottom)]
    near_second, far_second = outer_swap(own_tokens[1:], 1), outer_swap(own_tokens[1:], 2)

    def expert(rows, pulled_rows):
        *outs, hidden_rows, pull_rows = call(
            functools.partial(expert_kernel, parts, slices, cap),
            [shape(2 * cap + 8, depth)] * parts + [shape(slices, slots, hidden)] * 2,
            (*rows, *ups, pulled_rows),
            name="expert",
        )
        return outs, hidden_rows, pull_rows

    own_outs = expert(own_tokens, pulled[0])
    near_first, far_first, own_outs = tie(near_first, far_first, own_outs)
    last_first = outer_swap(far_first, 1)
    near_second, far_second = tie(near_second, far_second)
    last_second = outer_swap(far_second, 1)
    near_tokens, far_tokens = near_first + near_second, far_first + far_second
    near_outs, far_outs = expert(near_tokens, pulled[1]), expert(far_tokens, pulled[2])
    last_first, last_second, near_outs, far_outs = tie(last_first, last_second, near_outs, far_outs)
    last_tokens = last_first + last_second
    last_outs = expert(last_tokens, pulled[3])
    token_pieces = [own_tokens, near_tokens, far_tokens, last_tokens]
    backs, hiddens, pulls = zip(own_outs, near_outs, far_outs, last_outs)
    back_through = outer_swap(backs[3][1:], 1)
    back_through, last_zero = tie(back_through, backs[3][0])
    zero_through = grid.swap(last_zero, "outer", 1)
    back_parts = [
        outer_reduce_rest(grid, [b[part] for b in backs], back_through[part - 1]) for part in range(1, parts)
    ]
    outs = call(
        functools.partial(expert_grads_kernel, pieces, parts, slices, cap),
        [shape(slots, depth)] * pieces + [shape(depth, hidden)] * slices + [shape(hidden, depth)] * slices,
        (*sum(token_pieces, []), *grad_pieces, *hiddens, *pulls, *downs),
        name="expert_grads",
    )
    back_parts, zero_through, zero, outs = tie(back_parts, zero_through, [b[0] for b in backs], outs)
    first_part = outer_reduce_rest(grid, zero, zero_through)
    back_parts = swap_y(grid, [None] + back_parts)[1:]
    first_part, back_parts = tie(first_part, back_parts)
    back = core_last(grid, [first_part] + back_parts, cap, True)
    results, up_grads, down_grads = outs[:pieces], outs[pieces : pieces + slices], outs[pieces + slices :]
    halves = lambda array: [array[: array.shape[0] // 2], array[array.shape[0] // 2 :]]
    ups_sent, downs_sent = ([halves(g) for g in grads[1:]] for grads in (up_grads, down_grads))

    def inner_swaps(sent, half):
        return [grid.swap(pair[half], "inner", s) for s, pair in enumerate(sent, 1)]

    up_first = inner_swaps(ups_sent, 0)
    back, last_result, ups_sent = tie(back, results[3], ups_sent)
    through = grid.swap(last_result, "outer", 1)
    up_second = inner_swaps(ups_sent, 1)

    grad_resid, small, grad_scan, grad_gate, grad_skip, back_pair = call(
        functools.partial(mixer_back_kernel, rank_n, states, experts, cap),
        [
            shape(tokens, depth),
            shape(16, depth),
            shape(tokens, width),
            shape(tokens, width),
            shape(1, width),
            shape(states + 1, width),
        ],
        (
            me, back, table, gate, probs, expert_ids, rank, resid, output_grad, row(router_gain), router_t,
            out_proj, joined, scan, act, row(skip_gain), masked, rate, proj, pair[states:],
        ),
        grid=(chunks,),
        in_specs=[
            SMEM, full(slots + 8, depth), full(slots, tokens), full(tokens, 1), full(tokens, 8),
            full(tokens, 1), full(tokens, 1), full(tokens, depth), full(tokens, depth), full(1, depth),
            full(8, depth), out_rows, gate_half, tok, tok, one_row, tok, state_rows, proj_full, one_row,
        ],
        out_specs=[
            full(tokens, depth), full(16, depth), tok, tok, one_row,
            pl.BlockSpec((states + 1, chunk), block),
        ],
        scratch=[lanes] + [pltpu.VMEM((tokens, depth), BF16)] * 2,
        name="mixer_back",
    )
    back_pair, downs_sent, *up_first = tie(back_pair, downs_sent, *up_first)
    core = grid.at["core"].astype(jnp.int32).reshape(1)
    wide = pl.BlockSpec((tokens, depth), block)

    def late(which, weight):
        return call(
            late_kernel,
            [shape(depth, width)] + [shape(tokens, depth)] * len(weight),
            (
                which, scan, act, row(skip_gain), joined, grad_resid, block_input, row(mixer_gain), grad_gate,
                *weight,
            ),
            grid=(2,),
            in_specs=[
                SMEM, wide, wide, pl.BlockSpec((1, depth), block), pl.BlockSpec((ext, depth), lambda c: (0, 2 + c)),
                full(tokens, depth), full(tokens, depth), full(1, depth), wide,
            ]
            + [pl.BlockSpec((depth, depth), lambda c: (0, 2 + c))] * len(weight),
            out_specs=[pl.BlockSpec((depth, depth), block)] + [full(tokens, depth)] * len(weight),
            scratch=[pltpu.VMEM((tokens, depth), BF16)] * 2,
            name="late",
        )

    (late_sent,) = late(core, ())
    late_kept, grad_gate_normed = late(1 - core, (in_proj,))
    late_got = grid.swap(late_sent, "core", 1)
    down_first = inner_swaps(downs_sent, 0)

    def first(total):
        total, held["through"], held["downs"], *held["up_second"] = tie(total, through, downs_sent, *up_second)
        return total

    def second(total):
        total, got, kept, held["normed"], *held["down_first"] = tie(
            total, late_got, late_kept, grad_gate_normed, *down_first
        )
        held["late"] = sum_first(grid, [kept, got])
        return total

    end = entering(grid, back_pair, rate, True, {1: first, 2: second})
    up_second = held["up_second"]
    end, near, far = tie(end, results[1], results[2] + held["through"])
    near, far = grid.swap(near, "outer", 1), grid.swap(far, "outer", 2)
    grad_gate_normed = held["normed"]
    late_first, late_second = held["late"]

    def with_others(own, firsts, seconds):
        for pair in zip(firsts, seconds):
            own = own + jnp.concatenate(pair, axis=0)
        return own

    def scan_back(c, before):
        at = lambda _: (0, c)
        tok, one_row = pl.BlockSpec((tokens, chunk), at), pl.BlockSpec((1, chunk), at)
        state_rows = pl.BlockSpec((states, chunk), at)
        return call(
            functools.partial(scan_back_kernel, rank_n, states),
            [
                shape(tokens, width), shape(tokens, width), shape(states, width),
                shape(rank_n + 2 * states, tokens),
            ],
            (
                masked, steps, drive, act, pre, grad_scan, row(skip_gain), history, history, start, end, rate, proj,
                step_proj, *before,
            ),
            grid=(blocks,),
            in_specs=[
                tok, tok, tok, tok, tok, tok, one_row,
                pl.BlockSpec((token_block, states, chunk), lambda i: (blocks - 1 - i, 0, c)),
                pl.BlockSpec(
                    (8, states, chunk),
                    lambda i: (jnp.maximum((blocks - 1 - i) * (token_block // 8) - 1, 0), 0, c),
                ),
                state_rows, state_rows, state_rows, proj_full, pl.BlockSpec((rank_n, chunk), at),
            ]
            + [pl.BlockSpec(memory_space=pl.ANY)] * len(before),
            out_specs=[tok, tok, state_rows, proj_full],
            scratch=[lanes, lanes]
            + [pltpu.VMEM((tokens, chunk), F32)] * 2
            + [pltpu.VMEM((token_block, states, 128), F32)] * 2
            + [pltpu.VMEM((states, chunk), F32)] * 2
            + [pltpu.VMEM((2, states, 128), F32)],
            name="scan_back",
            aliases={14 + i: i for i in range(len(before))},
        )

    *filled, grad_proj_a = scan_back(0, ())
    filled, late_first, late_second = tie(filled, late_first, late_second)
    late_both = sum_second(grid, late_first, late_second)
    *filled, grad_proj_b = scan_back(1, filled)
    filled, late_both, near, far, downs_sent = tie(filled, late_both, near, far, held["downs"])
    down_second = inner_swaps(downs_sent, 1)
    result = results[0] + near + far
    result_parts = swap_y(grid, [result[p * 2 * cap : (p + 1) * 2 * cap] for p in range(parts)])
    late_cut = cut_outer(grid, late_both)
    late_through = grid.swap(late_cut[3], "outer", 1)
    grad_act, grad_pre, grad_decay, grad_proj_c = scan_back(2, filled)
    grad_act, late_through, result_parts, down_second = tie(grad_act, late_through, result_parts, down_second)
    late_total = outer_reduce_rest(grid, late_cut, late_through)
    unit = 2 * grid.size["inner"] * grid.size["y"]
    half = -(-max(depth // 2 + 3 * states + rank_n, depth // 2 + rank_n + 40) // unit) * unit
    small = jnp.concatenate([small[:9], loads[0:1]], axis=0)
    kept, sent_half, input_grad, edge = call(
        functools.partial(input_back_kernel, rank_n, states),
        [shape(half, width), shape(half, width), shape(tokens, depth), shape(HALO, depth)],
        (
            core, grad_proj_a, grad_proj_b, grad_proj_c, proj, state_proj_t, act, grad_act, grad_pre, conv, joined,
            conv_weight, since, in_proj, block_input, halo, row(mixer_gain), grad_gate_normed, grad_resid,
            grad_decay, grad_skip, small,
        ),
        grid=(chunks,),
        in_specs=[
            SMEM, proj_full, proj_full, proj_full, proj_full, pl.BlockSpec((rank_n + 2 * states, chunk), block),
            tok, tok, tok, tok, pl.BlockSpec((ext, chunk), block), pl.BlockSpec((taps, chunk), block),
            full(tokens, 1), pl.BlockSpec((depth, chunk), block), full(tokens, depth), full(HALO, depth),
            full(1, depth), full(tokens, depth), full(tokens, depth), state_rows, one_row, full(10, depth),
        ],
        out_specs=[
            pl.BlockSpec((half, chunk), block), pl.BlockSpec((half, chunk), block), full(tokens, depth),
            full(HALO, depth),
        ],
        scratch=[pltpu.VMEM((ext, depth), BF16)] * 2
        + [pltpu.VMEM((ext, chunk), F32), pltpu.VMEM((ext, depth), F32)],
        name="input_back",
    )
    kept, sent_half, late_total = tie(kept, sent_half, late_total)
    late_near, late_far = grid.swap(late_total, "outer", 1), grid.swap(late_total, "outer", 2)
    sent_got = grid.swap(sent_half, "core", 1)
    kept, sent_got = tie(kept, sent_got)
    grads_first, grads_second = sum_first(grid, [kept, sent_got])
    late_near, late_far, grads_first, grads_second = tie(late_near, late_far, grads_first, grads_second)
    late_last = grid.swap(late_far, "outer", 1)
    grads = sum_second(grid, grads_first, grads_second)
    late_last, grads, edge, result_parts, up_parts, down_parts = tie(
        late_last, grads, edge, result_parts,
        [up_grads[0], up_first, up_second], [down_grads[0], held["down_first"], down_second],
    )
    from_next = grid.along(edge, -1)
    input_grad = jnp.concatenate([input_grad[: tokens - HALO], input_grad[tokens - HALO :] + from_next], axis=0)
    grad_up = with_others(*up_parts)
    result = core_last(grid, result_parts, cap, False)
    late_first, late_second = spread_second(grid, join_outer(grid, late_total, late_near, late_far, late_last))
    grads = sum_outer(grid, grads)
    late_first, late_second, grads, grad_up = tie(late_first, late_second, grads, grad_up)
    late_first, late_second = gather_rows(grid, late_first, "inner"), gather_rows(grid, late_second, "y")
    grads = spread_outer(grid, grads)
    late_first, late_second, grads, result, input_grad = tie(late_first, late_second, grads, result, input_grad)
    combined = jnp.dot(table.T, result.astype(F32), precision=lax.Precision.HIGHEST, preferred_element_type=F32)
    block_output = resid + gate * combined
    late_other = [grid.swap(late_first, "core", 1), grid.swap(late_second, "core", 1)]
    grads_first, grads_second = spread_second(grid, grads)
    grads_first, grads_second, down_parts, block_output, *late_other = tie(
        grads_first, grads_second, down_parts, block_output, *late_other
    )
    grad_down = with_others(*down_parts)
    grads_first, grads_second = gather_rows(grid, grads_first, "inner"), gather_rows(grid, grads_second, "y")
    quarter = pl.BlockSpec((half // 2, chunk), block)
    late_rows = full(depth // 2, width)
    grad_in_proj, grad_out_proj = call(
        finish_late_kernel,
        [shape(depth, 2 * width), shape(2, depth, depth)],
        (core, late_first, late_second, *late_other),
        grid=(2,),
        in_specs=[SMEM] + [late_rows] * 4,
        out_specs=[
            pl.BlockSpec((depth // 2, width), lambda r: (r, 1)),
            pl.BlockSpec((2, depth // 2, depth), lambda r: (0, r, 0)),
        ],
        name="finish_late",
    )
    grads_first, grads_second, grad_in_proj, grad_down = tie(grads_first, grads_second, grad_in_proj, grad_down)
    grads_other = [grid.swap(grads_first, "core", 1), grid.swap(grads_second, "core", 1)]
    tall = lambda columns: pl.BlockSpec((chunk, columns), lambda c: (c, 0))
    (
        grad_in_proj, grad_state_proj, grad_step_proj, grad_decay_log, grad_conv_weight, rows, small,
    ) = call(
        functools.partial(finish_kernel, rank_n, states, taps),
        [
            shape(depth, 2 * width), shape(width, rank_n + 2 * states), shape(rank_n, width),
            shape(width, states), shape(taps, width), shape(8, width), shape(32, chunk),
        ],
        (core, grads_first, grads_second, *grads_other, grad_in_proj),
        grid=(chunks,),
        in_specs=[SMEM] + [quarter] * 4 + [pl.BlockSpec(memory_space=pl.ANY)],
        out_specs=[
            pl.BlockSpec((depth, chunk), block), tall(rank_n + 2 * states), pl.BlockSpec((rank_n, chunk), block),
            tall(states), pl.BlockSpec((taps, chunk), block), pl.BlockSpec((8, chunk), block), full(32, chunk),
        ],
        name="finish",
        aliases={5: 0},
    )
    small = jnp.concatenate([small[:16], small[16:, : depth - chunk]], axis=1)
    return (
        block_output,
        input_grad,
        small[10],
        grad_in_proj,
        grad_conv_weight,
        rows[taps],
        grad_state_proj,
        grad_step_proj,
        rows[taps + 1],
        grad_decay_log,
        rows[taps + 2],
        grad_out_proj.reshape(width, depth),
        small[8],
        small[:experts].T,
        grad_up[None],
        grad_down[None],
        small[9, :experts].astype(jnp.int32),
        small[9, 128 : 128 + experts].astype(jnp.int32),
    )


def solution(mesh):
    rows, copied = P(("seq", "exp"), None), P()
    up, down = P("exp", None, "seq"), P("exp", "seq", None)
    in_specs = (rows, copied, rows, rows) + (copied,) * 12 + (up, down)
    out_specs = (rows, rows) + (copied,) * 12 + (up, down, copied, copied)
    return jax.shard_map(per_device, mesh=mesh, in_specs=in_specs, out_specs=out_specs, check_vma=False)
```

```python
import functools

import jax
import jax.numpy as jnp
from jax import lax
from jax.experimental import pallas as pl
from jax.experimental.pallas import tpu as pltpu
from jax.sharding import PartitionSpec as P

F32 = jnp.float32
BF16 = jnp.bfloat16
EPS = 1e-05
LOG2E = 1.4426950408889634
HALO = 16
RESET = 1e9
AXES = ("seq", "exp")
NN, NT, TN = ((1,), (0,)), ((1,), (1,)), ((0,), (0,))
VMEM_BYTES = 52 << 20
MICROSECONDS = {
    "route": 1, "join": 8, "features": 250, "join_states": 1, "scan": 200, "early": 200, "expert": 60,
    "expert_grads": 300, "mixer_back": 300, "late": 200, "scan_back": 10, "input_back": 11, "finish_late": 8, "finish": 6,
}


class Grid:
    def __init__(self):
        self.seq, self.exp = lax.axis_size("seq"), lax.axis_size("exp")
        self.outer = 4
        self.size = {
            "core": 2,
            "y": self.exp // 2,
            "inner": self.seq // self.outer,
            "outer": self.outer,
        }
        self.total = self.seq * self.exp
        index, step, self.step, self.at = lax.axis_index(AXES), 1, {}, {}
        for name in ("core", "y", "inner", "outer"):
            self.step[name] = step
            self.at[name] = (index // step) % self.size[name]
            step *= self.size[name]
        self.index = index

    def swap(self, block, name, mask):
        return self.swap_bits(block, mask * self.step[name])

    def swap_bits(self, block, bits):
        return lax.ppermute(block, AXES, [(i, i ^ bits) for i in range(self.total)])

    def along(self, block, distance):
        route = [(i - distance, i) for i in range(self.total) if 0 <= i - distance < self.total]
        return lax.ppermute(block, AXES, route)


def tie(*values):
    return lax.optimization_barrier(values)


def outer_reduce_rest(grid, parts, through):
    through, near = tie(through, parts[1])
    near = grid.swap(near, "outer", 1)
    far = grid.swap(parts[2] + through, "outer", 2)
    return parts[0] + near + far


def in_order(parts, place):
    bit = 1
    while bit < len(parts):
        turned = ((place // bit) % 2) == 1
        parts = [jnp.where(turned, parts[i ^ bit], parts[i]) for i in range(len(parts))]
        bit *= 2
    return parts


def rows_of(parts, first, rows):
    return functools.reduce(jnp.add, [lax.dynamic_slice_in_dim(part, first, rows, 0) for part in parts])


def scatter_rows(grid, parts, name, rows, start=0):
    count, place = grid.size[name], grid.at[name]
    rows = rows // count
    sent = [rows_of(parts, start + (place ^ s) * rows, rows) for s in range(1, count)]
    got = [grid.swap(block, name, s) for s, block in enumerate(sent, 1)]
    parts, _ = tie(list(parts), sent)
    return [rows_of(parts, start + place * rows, rows)] + got


def gather_rows(grid, block, name):
    count = grid.size[name]
    if count == 1:
        return block
    parts = [block] + [grid.swap(block, name, s) for s in range(1, count)]
    return jnp.concatenate(in_order(parts, grid.at[name]), axis=0)


def sum_first(grid, parts):
    rows = parts[0].shape[0] // 2
    return scatter_rows(grid, parts, "inner", rows), scatter_rows(grid, parts, "y", rows, rows)


def sum_second(grid, first, second):
    rows = first[0].shape[0]
    first, second = scatter_rows(grid, first, "y", rows), scatter_rows(grid, second, "inner", rows)
    return [jnp.concatenate(pair, axis=0) for pair in zip(first, second)]


def cut_outer(grid, parts):
    columns = parts[0].shape[1] // grid.outer

    def block(parts, s):
        cut = [lax.dynamic_slice_in_dim(p, (grid.at["outer"] ^ s) * columns, columns, 1) for p in parts]
        return functools.reduce(jnp.add, cut)

    others = [block(parts, s) for s in range(1, grid.outer)]
    parts, _ = tie(list(parts), others)
    return [block(parts, 0)] + others


def sum_outer(grid, parts):
    own, *others = cut_outer(grid, parts)
    return functools.reduce(jnp.add, [grid.swap(part, "outer", s) for s, part in enumerate(others, 1)], own)


def spread_outer(grid, total):
    count = grid.size["outer"]
    parts = [total] + [grid.swap(total, "outer", s) for s in range(1, count)]
    return jnp.concatenate(in_order(parts, grid.at["outer"]), axis=1)


def join_outer(grid, own, near, far, last):
    return jnp.concatenate(in_order([own, near, far, last], grid.at["outer"]), axis=1)


def spread_second(grid, both):
    own = both.shape[0] // 2
    return gather_rows(grid, both[:own], "y"), gather_rows(grid, both[own:], "inner")


def spread_first(grid, first, second):
    return jnp.concatenate([gather_rows(grid, first, "inner"), gather_rows(grid, second, "y")], axis=0)


def join_states_kernel(last, later_ref, total_ref, got_ref, ahead_ref, rate_ref, *outs):
    states = rate_ref.shape[0]
    rows, sums = slice(0, states), slice(states, states + 1)

    def follow(early, late, out):
        out[rows, :] = jnp.exp2(rate_ref[...] * late[sums, :]) * early[rows, :] + late[rows, :]
        out[sums, :] = early[sums, :] + late[sums, :]

    @pl.when(later_ref[0] == 1)
    def _():
        follow(got_ref, ahead_ref, outs[0])
        if not last:
            follow(got_ref, total_ref, outs[1])

    @pl.when(later_ref[0] == 0)
    def _():
        outs[0][...] = ahead_ref[...]
        if not last:
            follow(total_ref, got_ref, outs[1])


def entering(grid, pair, rate, backward, after):
    states = rate.shape[0]
    total, ahead, hop = pair, jnp.zeros_like(pair), 1
    bits = 1
    while bits < grid.total:
        got = grid.swap_bits(total, bits)
        later = ((grid.index // bits) % 2).astype(jnp.int32)
        later = (1 - later if backward else later).reshape(1)
        last = 2 * bits >= grid.total
        whole = pl.BlockSpec(memory_space=pltpu.VMEM)
        ahead, *rest = call(
            functools.partial(join_states_kernel, last),
            [shape(*pair.shape)] * (1 if last else 2),
            (later, total, got, ahead, rate),
            in_specs=[SMEM] + [whole] * 4,
            name="join_states",
        )
        total = rest[0] if rest else None
        if hop in after:
            total = after[hop](total)
        bits, hop = 2 * bits, hop + 1
    return ahead[:states]


def pad_rows(block, rows):
    return jnp.pad(block, ((0, rows - block.shape[0]), (0, 0)))


def core_first(grid, block, cap, tail):
    ny, width = grid.size["y"], 2 * cap
    slots = ny * width
    send = [block[s * width + cap : (s + 1) * width] for s in range(ny)] + ([block[slots:]] if tail else [])
    got = grid.swap(jnp.concatenate(send, axis=0), "core", 1)
    parts = []
    for s in range(ny):
        rows = [block[s * width : s * width + cap], got[s * cap : (s + 1) * cap]]
        if tail:
            ends = [block[slots + 2 * s : slots + 2 * s + 1], got[ny * cap + 2 * s + 1 : ny * cap + 2 * s + 2]]
            rows.append(pad_rows(jnp.concatenate(ends, axis=0), 8))
        parts.append(jnp.concatenate(rows, axis=0))
    return parts


def swap_y(grid, parts):
    return [parts[0]] + [grid.swap(part, "y", s) for s, part in enumerate(parts[1:], 1)]


def core_last(grid, parts, cap, tail):
    ny = grid.size["y"]
    send = [p[cap : 2 * cap] for p in parts]
    if tail:
        send.append(pad_rows(jnp.concatenate([p[2 * cap + 1 : 2 * cap + 2] for p in parts], axis=0), 8))
    got = grid.swap(jnp.concatenate(send, axis=0), "core", 1)
    rows, ends = [], []
    for s, p in enumerate(parts):
        rows += [p[:cap], got[s * cap : (s + 1) * cap]]
        if tail:
            ends += [p[2 * cap : 2 * cap + 1], got[ny * cap + s : ny * cap + s + 1]]
    if tail:
        rows.append(pad_rows(jnp.concatenate(ends, axis=0), 8))
    return jnp.concatenate(rows, axis=0)


def split(value):
    high = value.astype(BF16)
    return high, (value - high.astype(F32)).astype(BF16)


def dot(left, right, dims):
    return lax.dot_general(left, right, (dims, ((), ())), preferred_element_type=F32)


def product(left, right, dims):
    return dot(left[0], right[0], dims) + (dot(left[0], right[1], dims) + dot(left[1], right[0], dims))


def pick(exact, value, dims):
    high, low = split(value)
    return dot(exact, high, dims) + dot(exact, low, dims)


def sigmoid(value):
    return 1.0 / (1.0 + jnp.exp(-value))


def softplus(value):
    small = jnp.exp(-jnp.abs(value))
    series = small * (1.0 - small * (0.5 - small * (1.0 / 3.0 - small * (0.25 - small * 0.2))))
    return jnp.maximum(value, 0.0) + jnp.where(small < 0.03, series, jnp.log(1.0 + small))


def iota(shape, dim):
    return lax.broadcasted_iota(jnp.int32, shape, dim)


def scale_of(value):
    return lax.rsqrt(jnp.mean(value * value, axis=1, keepdims=True) + EPS)


def over_lanes(ref, columns):
    rows = columns.shape[0]
    for t in range(columns.shape[1]):
        ref[t] = jnp.broadcast_to(columns[:, t : t + 1], (rows, 128))


def widen(value, width):
    return jnp.concatenate([value] * (width // 128), axis=1)


def call(kernel, outs, ins, grid=None, in_specs=None, out_specs=None, scratch=(), name=None, aliases=None):
    whole = pl.BlockSpec(memory_space=pltpu.VMEM)
    return pl.pallas_call(
        kernel,
        out_shape=outs,
        grid=grid or (),
        in_specs=in_specs or [whole] * len(ins),
        out_specs=out_specs or jax.tree.map(lambda _: whole, outs),
        scratch_shapes=scratch,
        name=name,
        cost_estimate=pl.CostEstimate(
            flops=int(MICROSECONDS[name] * 1.1e9), transcendentals=0, bytes_accessed=int(MICROSECONDS[name] * 1e6)
        ),
        input_output_aliases=aliases or {},
        compiler_params=pltpu.CompilerParams(vmem_limit_bytes=VMEM_BYTES),
    )(*ins)


def shape(*dims, dtype=F32):
    return jax.ShapeDtypeStruct(dims, dtype)


SMEM = pl.BlockSpec(memory_space=pltpu.SMEM)


def full(*dims):
    return pl.BlockSpec(dims, lambda *_: (0,) * len(dims))


def route_kernel(experts, cap, me_ref, ids_ref, grad_ref, sent_ref, table_ref, rank_ref, load_ref):
    ids = ids_ref[...]
    tokens = ids.shape[0]
    chosen = (ids == iota((tokens, 128), 1)).astype(F32)
    before = (iota((tokens, tokens), 0) > iota((tokens, tokens), 1)).astype(BF16)
    rank = jnp.sum(dot(before, chosen.astype(BF16), NN) * chosen, axis=1, keepdims=True)
    kept = (rank < cap).astype(F32)
    place = jnp.where(rank < cap, ((ids ^ me_ref[0]) * cap).astype(F32) + rank, -1.0)
    row = jnp.broadcast_to(place, (tokens, tokens)).T
    slots = experts * cap
    table = (iota((slots, tokens), 0).astype(F32) == jnp.broadcast_to(row[0:1], (slots, tokens))).astype(F32)
    table = table.astype(BF16)
    table_ref[...] = table
    rank_ref[...] = rank
    sent_ref[...] = pick(table, grad_ref[...], NN)
    load_ref[...] = jnp.zeros_like(load_ref)
    load_ref[0:1, 0:128] = jnp.sum(chosen, axis=0, keepdims=True)
    load_ref[0:1, 128:256] = jnp.sum(chosen * (1.0 - kept), axis=0, keepdims=True)


def join_kernel(x_ref, halo_ref, gain_ref, weight_ref, joined_ref, high, low):
    @pl.when(pl.program_id(0) == 0)
    def _():
        x = jnp.concatenate([halo_ref[...], x_ref[...]], axis=0)
        high[...], low[...] = split(x * scale_of(x) * gain_ref[...])

    joined_ref[...] = product((high[...], low[...]), split(weight_ref[...]), NN)


def features_kernel(
    rank_n,
    states,
    inner_ref,
    since_ref,
    conv_w_ref,
    conv_b_ref,
    state_proj_ref,
    step_proj_ref,
    step_bias_ref,
    rate_ref,
    conv_ref,
    act_ref,
    pre_ref,
    steps_ref,
    masked_ref,
    drive_ref,
    proj_ref,
    pair_ref,
    in_lanes,
):
    tokens, width = act_ref.shape
    taps = conv_w_ref.shape[0]
    since = since_ref[...]
    conv = jnp.broadcast_to(conv_b_ref[...], (tokens, width))
    for k in range(taps):
        valid = (since >= taps - 1 - k).astype(F32)
        first = HALO - taps + 1 + k
        conv = conv + inner_ref[first : first + tokens, :] * valid * conv_w_ref[k : k + 1, :]
    act = conv * sigmoid(conv)
    conv_ref[...] = conv
    act_ref[...] = act
    proj = product(split(state_proj_ref[...]), split(act), NT)
    proj_ref[...] = proj
    pre = product(split(proj[:rank_n]), split(step_proj_ref[...]), TN) + step_bias_ref[...]
    pre_ref[...] = pre
    steps = softplus(pre)
    steps_ref[...] = steps
    masked = jnp.where(since == 0, RESET, steps)
    masked_ref[...] = masked
    drive_ref[...] = steps * act
    pair_ref[states : states + 1, :] = jnp.sum(masked, axis=0, keepdims=True)
    over_lanes(in_lanes, proj[rank_n : rank_n + states])
    chunk = 512
    for c in range(width // chunk):
        part = slice(c * chunk, (c + 1) * chunk)
        rate = rate_ref[:, part]

        def eight(group, state):
            for i in range(8):
                t = group * 8 + i
                decay = jnp.exp2(masked_ref[pl.ds(t, 1), part] * rate)
                state = decay * state + drive_ref[pl.ds(t, 1), part] * widen(in_lanes[t], chunk)
            return state

        pair_ref[0:states, part] = lax.fori_loop(0, tokens // 8, eight, jnp.zeros((states, chunk), F32))


def slot_tables(slots, cap, experts):
    slot = iota((slots, 8), 0)
    first = sum((slot >= cap * e).astype(jnp.int32) for e in range(1, experts))
    block = (first == iota((slots, 8), 1)).astype(F32)
    slot = iota((slots, 128), 0)
    first = sum(((slot >= cap * e).astype(jnp.int32) for e in range(1, experts)))
    within = (slot - first * cap == iota((slots, 128), 1)).astype(F32)
    return block, within


def scan_kernel(
    rank_n,
    states,
    experts,
    cap,
    me_ref,
    masked_ref,
    drive_ref,
    act_ref,
    gate_z_ref,
    start_ref,
    rate_ref,
    skip_ref,
    proj_ref,
    out_proj_ref,
    x_ref,
    gain_ref,
    router_ref,
    ids_ref,
    rank_ref,
    table_ref,
    scan_ref,
    history_ref,
    resid_ref,
    sent_ref,
    probs_ref,
    gate_ref,
    in_lanes,
    out_lanes,
    total,
):
    tokens, chunk = masked_ref.shape
    step = pl.program_id(0)

    @pl.when(step == 0)
    def _():
        over_lanes(in_lanes, proj_ref[rank_n : rank_n + states, :])
        over_lanes(out_lanes, proj_ref[rank_n + states : rank_n + 2 * states, :])
        total[...] = x_ref[...]

    rate = rate_ref[...]

    def eight(group, state):
        for i in range(8):
            t = group * 8 + i
            decay = jnp.exp2(masked_ref[pl.ds(t, 1), :] * rate)
            state = decay * state + drive_ref[pl.ds(t, 1), :] * widen(in_lanes[t], chunk)
            history_ref[t] = state
            scan_ref[pl.ds(t, 1), :] = jnp.sum(state * widen(out_lanes[t], chunk), axis=0, keepdims=True)
        return state

    lax.fori_loop(0, tokens // 8, eight, start_ref[...])
    gate_z = gate_z_ref[HALO:, :]
    mixed = (scan_ref[...] + skip_ref[...] * act_ref[...]) * (gate_z * sigmoid(gate_z))
    total[...] += product(split(mixed), split(out_proj_ref[...]), NN)

    @pl.when(step == pl.num_programs(0) - 1)
    def _():
        resid = total[...]
        resid_ref[...] = resid
        normed = resid * scale_of(resid) * gain_ref[...]
        logits = product(split(normed), split(router_ref[...]), NT)
        known = iota((tokens, 8), 1) < experts
        logits = jnp.where(known, logits, -1e30)
        raised = jnp.exp(logits - jnp.max(logits, axis=1, keepdims=True))
        raised = jnp.where(known, raised, 0.0)
        probs = raised / jnp.sum(raised, axis=1, keepdims=True)
        probs_ref[...] = probs
        ids = ids_ref[...]
        gate = jnp.sum(jnp.where(ids == iota((tokens, 8), 1), probs, 0.0), axis=1, keepdims=True)
        gate_ref[...] = gate
        slots = experts * cap
        sent_ref[0:slots, :] = pick(table_ref[...], normed, NN)
        sent_ref[slots:, :] = jnp.zeros((8, sent_ref.shape[1]), F32)
        rank = rank_ref[...].astype(jnp.int32)
        to_block = jnp.where(((ids ^ me_ref[0]) == iota((tokens, 8), 1)) & (rank < cap), gate, 0.0)
        at_rank = (rank == iota((tokens, 128), 1)).astype(BF16)
        high, low = split(to_block)
        rest = (to_block - high.astype(F32) - low.astype(F32)).astype(BF16)
        rows = dot(high, at_rank, TN) + (dot(low, at_rank, TN) + dot(rest, at_rank, TN))
        sent_ref[slots:, 0:128] = rows


def early_kernel(pieces, slices, *refs):
    grads, downs, outs = refs[:pieces], refs[pieces : pieces + slices], refs[pieces + slices :]
    downs = [split(d[...]) for d in downs]
    for p in range(pieces):
        grad = split(grads[p][...])
        for i in range(slices):
            outs[p][i] = product(grad, downs[i], NT)


def gelu_parts(value):
    inner = 0.7978845608 * (value + 0.044715 * value * value * value)
    tanh = jnp.tanh(inner)
    slope = 0.5 * (1.0 + tanh) + 0.5 * value * (1.0 - tanh * tanh) * 0.7978845608 * (
        1.0 + 3.0 * 0.044715 * value * value
    )
    return 0.5 * value * (1.0 + tanh), slope


def expert_kernel(parts, slices, cap, *refs):
    tokens, ups, pulled_ref = refs[:parts], refs[parts : parts + slices], refs[parts + slices]
    backs, hidden_ref, grad_ref = refs[parts + slices + 1 : -2], refs[-2], refs[-1]
    width = 2 * cap
    slots, depth = parts * width, tokens[0].shape[1]
    block, within = slot_tables(width, cap, 2)
    within = within.astype(BF16)
    rows = split(jnp.concatenate([t[0:width, :] for t in tokens], axis=0))
    back = jnp.zeros((slots, depth), F32)
    to_gate = jnp.zeros((slots, 1), F32)
    for i in range(slices):
        up = split(ups[i][...])
        hidden, slope = gelu_parts(product(rows, up, NN))
        pull = pulled_ref[i]
        grad = pull * slope
        hidden_ref[i] = hidden
        grad_ref[i] = grad
        to_gate += jnp.sum(hidden * pull, axis=1, keepdims=True)
        back += product(split(grad), up, NT)
    for p in range(parts):
        part = slice(p * width, (p + 1) * width)
        backs[p][0:width, :] = back[part]
        backs[p][width:, :] = jnp.zeros((8, depth), F32)
        mine = block * to_gate[part]
        high, low = split(mine)
        rest = (mine - high.astype(F32) - low.astype(F32)).astype(BF16)
        backs[p][width:, 0:128] = dot(high, within, TN) + (dot(low, within, TN) + dot(rest, within, TN))


def expert_grads_kernel(pieces, parts, slices, cap, *refs):
    tokens, refs = refs[: pieces * parts], refs[pieces * parts :]
    grads, hiddens, pulls = (refs[i * pieces : (i + 1) * pieces] for i in range(3))
    downs, outs = refs[3 * pieces : 3 * pieces + slices], refs[3 * pieces + slices :]
    results, up_outs, down_outs = outs[:pieces], outs[pieces : pieces + slices], outs[pieces + slices :]
    width = 2 * cap
    downs = [split(d[...]) for d in downs]
    block, within = slot_tables(width, cap, 2)
    within = within.astype(BF16)
    for p in range(pieces):
        rows, gates = [], []
        for token in tokens[p * parts : (p + 1) * parts]:
            ends = token[width:, 0:128]
            high, low = split(ends)
            rest = (ends - high.astype(F32) - low.astype(F32)).astype(BF16)
            spread = dot(within, high, NT) + (dot(within, low, NT) + dot(within, rest, NT))
            gates.append(jnp.sum(spread * block, axis=1, keepdims=True))
            rows.append(token[0:width, :] * gates[-1])
        rows = split(jnp.concatenate(rows, axis=0))
        gated = split(grads[p][...] * jnp.concatenate(gates, axis=0))
        total = None
        for i in range(slices):
            hidden = split(hiddens[p][i])
            part = product(hidden, downs[i], NN)
            total = part if total is None else total + part
            up = product(rows, split(pulls[p][i]), TN)
            down = product(hidden, gated, TN)
            if p == 0:
                up_outs[i][...] = up
                down_outs[i][...] = down
            else:
                up_outs[i][...] += up
                down_outs[i][...] += down
        results[p][...] = total


def silu_parts(value):
    sig = sigmoid(value)
    return value * sig, sig * (1.0 + value * (1.0 - sig))


def mixer_back_kernel(
    rank_n,
    states,
    experts,
    cap,
    me_ref,
    back_ref,
    table_ref,
    gate_ref,
    probs_ref,
    ids_ref,
    rank_ref,
    resid_ref,
    grad_ref,
    gain_ref,
    router_ref,
    out_proj_ref,
    gate_z_ref,
    scan_ref,
    act_ref,
    skip_ref,
    masked_ref,
    rate_ref,
    proj_ref,
    steps_row_ref,
    grad_resid_ref,
    small_ref,
    grad_scan_ref,
    grad_gate_ref,
    grad_skip_ref,
    pair_ref,
    out_lanes,
    high,
    low,
):
    tokens, chunk = masked_ref.shape

    @pl.when(pl.program_id(0) == 0)
    def _():
        over_lanes(out_lanes, proj_ref[rank_n + states : rank_n + 2 * states, :])
        slots = experts * cap
        ids, rank = ids_ref[...], rank_ref[...].astype(jnp.int32)
        back = pick(table_ref[...], back_ref[0:slots, :], TN)
        at_rank = (rank == iota((tokens, 128), 1)).astype(BF16)
        ends = back_ref[slots:, 0:128]
        first, second = split(ends)
        third = (ends - first.astype(F32) - second.astype(F32)).astype(BF16)
        spread = dot(at_rank, first, NT) + (dot(at_rank, second, NT) + dot(at_rank, third, NT))
        mine = ((ids ^ me_ref[0]) == iota((tokens, 8), 1)) & (rank < cap)
        grad_gate = jnp.sum(jnp.where(mine, spread, 0.0), axis=1, keepdims=True)
        probs = probs_ref[...]
        grad_probs = jnp.where(ids == iota((tokens, 8), 1), grad_gate, 0.0)
        grad_logits = probs * (grad_probs - jnp.sum(probs * grad_probs, axis=1, keepdims=True))
        resid, gain = resid_ref[...], gain_ref[...]
        scale = scale_of(resid)
        normed = resid * scale * gain
        logits_two = split(grad_logits)
        grad_normed = gate_ref[...] * back + product(logits_two, split(router_ref[...]), NN)
        small_ref[...] = jnp.zeros_like(small_ref)
        small_ref[0:8, :] = product(logits_two, split(normed), TN)
        small_ref[8:9, :] = jnp.sum(grad_normed * resid * scale, axis=0, keepdims=True)
        pulled = gain * grad_normed
        grad_resid = (
            grad_ref[...]
            + scale * pulled
            - resid * (scale * scale * scale) * jnp.mean(pulled * resid, axis=1, keepdims=True)
        )
        grad_resid_ref[...] = grad_resid
        high[...], low[...] = split(grad_resid)

    grad_mixed = product((high[...], low[...]), split(out_proj_ref[...]), NT)
    silu, slope = silu_parts(gate_z_ref[HALO:, :])
    act = act_ref[...]
    grad_scan = grad_mixed * silu
    grad_scan_ref[...] = grad_scan
    grad_gate_ref[...] = grad_mixed * (scan_ref[...] + skip_ref[...] * act) * slope
    grad_skip_ref[...] = jnp.sum(grad_scan * act, axis=0, keepdims=True)
    rate = rate_ref[...]

    def eight(group, state):
        for i in range(8):
            t = tokens - 1 - (group * 8 + i)
            decay = jnp.exp2(masked_ref[pl.ds(t, 1), :] * rate)
            state = decay * (state + grad_scan_ref[pl.ds(t, 1), :] * widen(out_lanes[t], chunk))
        return state

    pair_ref[0:states, :] = lax.fori_loop(0, tokens // 8, eight, jnp.zeros((states, chunk), F32))
    pair_ref[states : states + 1, :] = steps_row_ref[...]


def late_kernel(
    which_ref, scan_ref, act_ref, skip_ref, gate_z_ref, grad_resid_ref, x_ref, gain_ref, grad_gate_ref, *refs
):
    high, low = refs[-2:]
    if len(refs) == 5:
        weight_ref, out_ref, normed_ref = refs[:3]
    else:
        weight_ref, out_ref, normed_ref = None, refs[0], None

    @pl.when(pl.program_id(0) == 0)
    def _():
        @pl.when(which_ref[0] == 0)
        def _():
            high[...], low[...] = split(grad_resid_ref[...])

        @pl.when(which_ref[0] == 1)
        def _():
            x = x_ref[...]
            high[...], low[...] = split(x * scale_of(x) * gain_ref[...])

        if normed_ref is not None:
            normed_ref[...] = jnp.zeros_like(normed_ref)

    @pl.when(which_ref[0] == 0)
    def _():
        gate_z = gate_z_ref[HALO:, :]
        mixed = (scan_ref[...] + skip_ref[...] * act_ref[...]) * (gate_z * sigmoid(gate_z))
        out_ref[...] = product(split(mixed), (high[...], low[...]), TN)

    @pl.when(which_ref[0] == 1)
    def _():
        out_ref[...] = product((high[...], low[...]), split(grad_gate_ref[...]), TN)

    if normed_ref is not None:
        normed_ref[...] += product(split(grad_gate_ref[...]), split(weight_ref[...]), NT)


def scan_back_kernel(
    rank_n,
    states,
    masked_ref,
    steps_ref,
    drive_ref,
    act_ref,
    pre_ref,
    grad_scan_ref,
    skip_ref,
    history_ref,
    before_ref,
    start_ref,
    end_ref,
    rate_ref,
    proj_ref,
    step_proj_ref,
    *refs,
):
    (
        grad_act_ref, grad_pre_ref, grad_decay_ref, grad_proj_ref,
        in_lanes, out_lanes, grad_drive, grad_steps, at_in, at_out, carried_ref, decays_ref, sums_ref,
    ) = refs[-13:]
    tokens, chunk = masked_ref.shape
    block = history_ref.shape[0]
    step, blocks = pl.program_id(0), pl.num_programs(0)
    first = (blocks - 1 - step) * block

    @pl.when(step == 0)
    def _():
        over_lanes(in_lanes, proj_ref[rank_n : rank_n + states, :])
        over_lanes(out_lanes, proj_ref[rank_n + states : rank_n + 2 * states, :])
        carried_ref[...] = end_ref[...]
        decays_ref[...] = jnp.zeros_like(decays_ref)
        sums_ref[...] = jnp.zeros_like(sums_ref)

    rate = rate_ref[...]
    entering_state = jnp.where(first == 0, start_ref[...], before_ref[7])

    def narrow(value):
        return functools.reduce(jnp.add, [value[:, c : c + 128] for c in range(0, chunk, 128)])

    def one(local, before, carried):
        state, decays = carried
        t = first + local
        masked = masked_ref[pl.ds(t, 1), :]
        grad = grad_scan_ref[pl.ds(t, 1), :]
        decay = jnp.exp2(masked * rate)
        state = state + grad * widen(out_lanes[t], chunk)
        at_out[local] = narrow(history_ref[local] * grad)
        at_in[local] = narrow(state * drive_ref[pl.ds(t, 1), :])
        grad_drive[pl.ds(t, 1), :] = jnp.sum(state * widen(in_lanes[t], chunk), axis=0, keepdims=True)
        state = decay * state
        pulled = state * before
        grad_steps[pl.ds(t, 1), :] = jnp.sum(pulled * rate, axis=0, keepdims=True)
        return state, decays + pulled * masked

    def eight(group, carried):
        for i in range(8):
            local = block - 1 - (group * 8 + i)
            carried = one(local, history_ref[local - 1], carried)
        return carried

    carried = lax.fori_loop(0, block // 8 - 1, eight, (carried_ref[...], decays_ref[...]))
    for local in range(7, 0, -1):
        carried = one(local, history_ref[local - 1], carried)
    carried_ref[...], decays_ref[...] = one(0, entering_state, carried)

    ones = jnp.ones((128, 128), BF16)
    lane = iota((states, 128), 1)
    for i, held in enumerate((at_in, at_out)):
        high, low = split(held[...].reshape(block * states, 128))
        spread = (dot(high, ones, NN) + dot(low, ones, NN)).reshape(block, states, 128)
        total = sums_ref[i]
        for local in range(block):
            total = jnp.where(lane == first + local, spread[local], total)
        sums_ref[i] = total

    @pl.when(step == blocks - 1)
    def _():
        grad_decay_ref[...] = decays_ref[...] * (rate * (1.0 / LOG2E))
        steps, act = steps_ref[...], act_ref[...]
        grad_act_ref[...] = skip_ref[...] * grad_scan_ref[...] + grad_drive[...] * steps
        grad_pre = (grad_steps[...] * (1.0 / LOG2E) + grad_drive[...] * act) * sigmoid(pre_ref[...])
        grad_pre_ref[...] = grad_pre
        grad_proj_ref[0:rank_n, :] = product(split(step_proj_ref[...]), split(grad_pre), NT)
        grad_proj_ref[rank_n : rank_n + states, :] = sums_ref[0]
        grad_proj_ref[rank_n + states : rank_n + 2 * states, :] = sums_ref[1]


def input_back_kernel(
    rank_n,
    states,
    core_ref,
    proj_a_ref,
    proj_b_ref,
    proj_c_ref,
    proj_ref,
    state_proj_ref,
    act_ref,
    grad_act_ref,
    grad_pre_ref,
    conv_ref,
    inner_ref,
    conv_w_ref,
    since_ref,
    weight_ref,
    x_ref,
    halo_ref,
    gain_ref,
    grad_gate_normed_ref,
    grad_resid_ref,
    grad_decay_ref,
    grad_skip_ref,
    small_ref,
    keep_ref,
    send_ref,
    input_ref,
    edge_ref,
    high,
    low,
    grad_inner,
    total,
):
    tokens, chunk = act_ref.shape
    depth = x_ref.shape[1]
    half = depth // 2
    taps = conv_w_ref.shape[0]
    step = pl.program_id(0)

    @pl.when(step == 0)
    def _():
        x = jnp.concatenate([halo_ref[...], x_ref[...]], axis=0)
        high[...], low[...] = split(x * scale_of(x) * gain_ref[...])
        total[...] = jnp.zeros_like(total)

    act, grad_pre = split(act_ref[...]), grad_pre_ref[...]
    grad_proj = split(proj_a_ref[...] + proj_b_ref[...] + proj_c_ref[...])
    grad_act = grad_act_ref[...] + product(grad_proj, split(state_proj_ref[...]), TN)
    _, slope = silu_parts(conv_ref[...])
    grad_conv = grad_act * slope
    since = since_ref[...]
    grad_inner[...] = jnp.zeros_like(grad_inner)
    rows = []
    for k in range(taps):
        valid = (since >= taps - 1 - k).astype(F32)
        first = HALO - taps + 1 + k
        held = grad_conv * valid
        rows.append(jnp.sum(held * inner_ref[first : first + tokens, :], axis=0, keepdims=True))
        grad_inner[first : first + tokens, :] += held * conv_w_ref[k : k + 1, :]
    rows.append(jnp.sum(grad_conv, axis=0, keepdims=True))
    rows.append(jnp.sum(grad_pre, axis=0, keepdims=True))
    rows.append(grad_skip_ref[...])
    grads = split(grad_inner[...])
    total[...] += product(grads, split(weight_ref[...]), NT)
    of_state_proj = product(grad_proj, act, NN)
    of_step_proj = product(split(proj_ref[0:rank_n, :]), split(grad_pre), NN)

    def first_half(out_ref):
        out_ref[0:half, :] = product((high[:, 0:half], low[:, 0:half]), grads, TN)
        at = half + 2 * states + rank_n
        out_ref[half:at, :] = of_state_proj
        out_ref[at : at + states, :] = grad_decay_ref[...]
        if at + states < out_ref.shape[0]:
            out_ref[at + states :, :] = jnp.zeros((out_ref.shape[0] - at - states, chunk), F32)

    def second_half(out_ref):
        out_ref[0:half, :] = product((high[:, half:], low[:, half:]), grads, TN)
        out_ref[half : half + rank_n, :] = of_step_proj
        at = half + rank_n
        out_ref[at:, :] = jnp.zeros((out_ref.shape[0] - at, chunk), F32)
        for i, row in enumerate(rows):
            out_ref[at + i : at + i + 1, :] = row

    @pl.when(core_ref[0] == 0)
    def _():
        first_half(keep_ref)
        second_half(send_ref)

    @pl.when(core_ref[0] == 1)
    def _():
        second_half(keep_ref)
        first_half(send_ref)

    @pl.when(step == pl.num_programs(0) - 1)
    def _():
        gain = gain_ref[...]

        def rows_back(x, grad):
            scale = scale_of(x)
            pulled = gain * grad
            back = scale * pulled - x * (scale * scale * scale) * jnp.mean(pulled * x, axis=1, keepdims=True)
            return back, jnp.sum(grad * x * scale, axis=0, keepdims=True)

        edge, edge_gain = rows_back(halo_ref[...], total[0:HALO, :])
        own, own_gain = rows_back(x_ref[...], total[HALO:, :] + grad_gate_normed_ref[...])
        edge_ref[...] = edge
        input_ref[...] = grad_resid_ref[...] + own
        small = jnp.concatenate([small_ref[0:10, :], edge_gain + own_gain], axis=0)

        def place_small(out_ref):
            at = half + rank_n + 8
            out_ref[at : at + 11, :] = small[:, 0:chunk]
            out_ref[at + 16 : at + 27, 0 : depth - chunk] = small[:, chunk:]

        @pl.when(core_ref[0] == 0)
        def _():
            place_small(send_ref)

        @pl.when(core_ref[0] == 1)
        def _():
            place_small(keep_ref)


def finish_late_kernel(core_ref, first_ref, second_ref, got_first_ref, got_second_ref, in_ref, out_ref):
    depth = out_ref.shape[2]
    step = pl.program_id(0)

    def write(gate, out):
        in_ref[...] = gate
        out_ref[0] = out[:, 0:depth]
        out_ref[1] = out[:, depth:]

    for i, (own, got) in enumerate(((first_ref, got_first_ref), (second_ref, got_second_ref))):

        @pl.when((core_ref[0] == 0) & (step == i))
        def _():
            write(own[...], got[...])

        @pl.when((core_ref[0] == 1) & (step == i))
        def _():
            write(got[...], own[...])


def finish_kernel(
    rank_n, states, taps, core_ref, first_ref, second_ref, got_first_ref, got_second_ref, _,
    in_ref, state_proj_ref, step_proj_ref, decay_ref, conv_w_ref, rows_ref, small_ref,
):
    depth = in_ref.shape[0]
    half, quarter = depth // 2, first_ref.shape[0]
    rest = half - quarter

    def first_half(one, two):
        in_ref[0:quarter, :] = one[...]
        in_ref[quarter:half, :] = two[0:rest, :]
        at = rest + 2 * states + rank_n
        state_proj_ref[...] = two[rest:at, :]
        decay_ref[...] = two[at : at + states, :]

    def second_half(one, two):
        in_ref[half : half + quarter, :] = one[...]
        in_ref[half + quarter :, :] = two[0:rest, :]
        step_proj_ref[...] = two[rest : rest + rank_n, :]
        at = rest + rank_n
        conv_w_ref[...] = two[at : at + taps, :]
        rows_ref[...] = two[at : at + 8, :]
        small_ref[...] = two[at + 8 : at + 40, :]

    @pl.when(core_ref[0] == 0)
    def _():
        first_half(first_ref, second_ref)
        second_half(got_first_ref, got_second_ref)

    @pl.when(core_ref[0] == 1)
    def _():
        first_half(got_first_ref, got_second_ref)
        second_half(first_ref, second_ref)


def per_device(
    block_input,
    seq_lengths,
    expert_ids,
    output_grad,
    mixer_gain,
    in_proj,
    conv_weight,
    conv_bias,
    state_proj,
    step_proj,
    step_bias,
    decay_log,
    skip_gain,
    out_proj,
    router_gain,
    router,
    expert_up,
    expert_down,
):
    grid = Grid()
    tokens, depth = block_input.shape
    taps, width = conv_weight.shape
    rank_n, states, experts = step_proj.shape[0], decay_log.shape[1], router.shape[1]
    cap = (5 * tokens + 4 * experts - 1) // (4 * experts)
    slots, hidden = experts * cap, expert_up.shape[2]
    chunk = 512
    chunks = width // chunk
    pieces, slices = grid.size["outer"], grid.size["inner"]
    token_block = 64
    blocks = tokens // token_block
    me = lax.axis_index("exp").astype(jnp.int32).reshape(1)
    ext = HALO + tokens

    halo = grid.along(block_input[tokens - HALO :], 1)

    count = seq_lengths.shape[0]
    earlier = jnp.arange(count)[:, None] > jnp.arange(count)[None, :]
    starts = jnp.sum(jnp.where(earlier, seq_lengths[None, :], 0), axis=1)
    position = grid.index * tokens + jnp.arange(tokens, dtype=jnp.int32)
    own_start = jnp.max(jnp.where(starts[None, :] <= position[:, None], starts[None, :], 0), axis=1)
    since = (position - own_start)[:, None]
    rate = -jnp.exp(decay_log.T) * LOG2E
    state_proj_t = state_proj.T
    router_t = pad_rows(router.T, 8)
    row = lambda vector: vector.reshape(1, -1)

    sent_grads, table, rank, loads = call(
        functools.partial(route_kernel, experts, cap),
        [shape(slots, depth), shape(slots, tokens, dtype=BF16), shape(tokens, 1), shape(8, depth)],
        (me, expert_ids, output_grad),
        in_specs=[SMEM] + [pl.BlockSpec(memory_space=pltpu.VMEM)] * 2,
        name="route",
    )
    halo, sent_grads = tie(halo, sent_grads)
    held_grads = core_first(grid, sent_grads, cap, False)
    up, down = expert_up[0], expert_down[0]
    up_rows = depth // 2
    downs = [down] + [grid.swap(down, "inner", s) for s in range(1, slices)]

    block = lambda c, *_: (0, c)
    joined = call(
        join_kernel,
        shape(ext, 2 * width),
        (block_input, halo, row(mixer_gain), in_proj),
        grid=(2 * chunks,),
        in_specs=[full(tokens, depth), full(HALO, depth), full(1, depth), pl.BlockSpec((depth, chunk), block)],
        out_specs=pl.BlockSpec((ext, chunk), block),
        scratch=[pltpu.VMEM((ext, depth), BF16)] * 2,
        name="join",
    )
    joined, *held_grads = tie(joined, *swap_y(grid, held_grads))
    own_grads = jnp.concatenate(held_grads, axis=0)
    joined, own_grads = tie(joined, own_grads)
    near_grads, far_grads = grid.swap(own_grads, "outer", 1), grid.swap(own_grads, "outer", 2)
    conv, act, pre, steps, masked, drive, proj, pair = call(
        functools.partial(features_kernel, rank_n, states),
        [shape(tokens, width)] * 6 + [shape(rank_n + 2 * states, tokens), shape(states + 1, width)],
        (joined, since, conv_weight, row(conv_bias), state_proj_t, step_proj, row(step_bias), rate),
        grid=(1,),
        in_specs=[
            full(ext, width),
            full(tokens, 1),
            full(taps, width),
            full(1, width),
            full(rank_n + 2 * states, width),
            full(rank_n, width),
            full(1, width),
            full(states, width),
        ],
        out_specs=[full(tokens, width)] * 6 + [full(rank_n + 2 * states, tokens), full(states + 1, width)],
        scratch=[pltpu.VMEM((tokens, states, 128), F32)],
        name="features",
    )
    pair, *downs = tie(pair, *downs)
    held = {}

    def third(total):
        total, held["near"], held["far"] = tie(total, near_grads, far_grads)
        return total

    start = entering(grid, pair, rate, False, {2: third})
    start, near_grads, far_grads = tie(start, held["near"], held["far"])
    up_top = [grid.swap(up[:up_rows], "inner", s) for s in range(1, slices)]
    last_grads = grid.swap(far_grads, "outer", 1)
    tok = pl.BlockSpec((tokens, chunk), block)
    gate_half = pl.BlockSpec((ext, chunk), lambda c, *_: (0, chunks + c))
    one_row = pl.BlockSpec((1, chunk), block)
    state_rows = pl.BlockSpec((states, chunk), block)
    history_block = pl.BlockSpec((tokens, states, chunk), lambda c: (0, 0, c))
    out_rows = pl.BlockSpec((chunk, depth), lambda c, *_: (c, 0))
    proj_full = full(rank_n + 2 * states, tokens)
    lanes = pltpu.VMEM((tokens, states, 128), F32)
    scan, history, resid, sent, probs, gate = call(
        functools.partial(scan_kernel, rank_n, states, experts, cap),
        [
            shape(tokens, width),
            shape(tokens, states, width),
            shape(tokens, depth),
            shape(slots + 8, depth),
            shape(tokens, 8),
            shape(tokens, 1),
        ],
        (
            me, masked, drive, act, joined, start, rate, row(skip_gain), proj, out_proj, block_input,
            row(router_gain), router_t, expert_ids, rank, table,
        ),
        grid=(chunks,),
        in_specs=[
            SMEM, tok, tok, tok, gate_half, state_rows, state_rows, one_row, proj_full, out_rows,
            full(tokens, depth), full(1, depth), full(8, depth), full(tokens, 1), full(tokens, 1),
            full(slots, tokens),
        ],
        out_specs=[
            tok, history_block, full(tokens, depth), full(slots + 8, depth), full(tokens, 8), full(tokens, 1),
        ],
        scratch=[lanes, lanes, pltpu.VMEM((tokens, depth), F32)],
        name="scan",
    )

    sent, last_grads, up_top, up_bottom = tie(sent, last_grads, up_top, up[up_rows:])
    up_bottom = [grid.swap(up_bottom, "inner", s) for s in range(1, slices)]
    own_tokens, last_grads = tie(core_first(grid, sent, cap, True), last_grads)
    grad_pieces = [own_grads, near_grads, far_grads, last_grads]
    pulled = call(
        functools.partial(early_kernel, pieces, slices),
        [shape(slices, slots, hidden)] * pieces,
        (*grad_pieces, *downs),
        name="early",
    )
    parts = grid.size["y"]
    outer_swap = lambda blocks, mask: [grid.swap(block, "outer", mask) for block in blocks]
    near_first, far_first = outer_swap(own_tokens[:1], 1), outer_swap(own_tokens[:1], 2)
    own_tokens, pulled, up_bottom = tie(swap_y(grid, own_tokens), pulled, up_bottom)
    ups = [up] + [jnp.concatenate(pair, axis=0) for pair in zip(up_top, up_bottom)]
    near_second, far_second = outer_swap(own_tokens[1:], 1), outer_swap(own_tokens[1:], 2)

    def expert(rows, pulled_rows):
        *outs, hidden_rows, pull_rows = call(
            functools.partial(expert_kernel, parts, slices, cap),
            [shape(2 * cap + 8, depth)] * parts + [shape(slices, slots, hidden)] * 2,
            (*rows, *ups, pulled_rows),
            name="expert",
        )
        return outs, hidden_rows, pull_rows

    own_outs = expert(own_tokens, pulled[0])
    near_first, far_first, own_outs = tie(near_first, far_first, own_outs)
    last_first = outer_swap(far_first, 1)
    near_second, far_second = tie(near_second, far_second)
    last_second = outer_swap(far_second, 1)
    near_tokens, far_tokens = near_first + near_second, far_first + far_second
    near_outs, far_outs = expert(near_tokens, pulled[1]), expert(far_tokens, pulled[2])
    last_first, last_second, near_outs, far_outs = tie(last_first, last_second, near_outs, far_outs)
    last_tokens = last_first + last_second
    last_outs = expert(last_tokens, pulled[3])
    token_pieces = [own_tokens, near_tokens, far_tokens, last_tokens]
    backs, hiddens, pulls = zip(own_outs, near_outs, far_outs, last_outs)
    back_through = outer_swap(backs[3][1:], 1)
    back_through, last_zero = tie(back_through, backs[3][0])
    zero_through = grid.swap(last_zero, "outer", 1)
    back_parts = [
        outer_reduce_rest(grid, [b[part] for b in backs], back_through[part - 1]) for part in range(1, parts)
    ]
    outs = call(
        functools.partial(expert_grads_kernel, pieces, parts, slices, cap),
        [shape(slots, depth)] * pieces + [shape(depth, hidden)] * slices + [shape(hidden, depth)] * slices,
        (*sum(token_pieces, []), *grad_pieces, *hiddens, *pulls, *downs),
        name="expert_grads",
    )
    back_parts, zero_through, zero, outs = tie(back_parts, zero_through, [b[0] for b in backs], outs)
    first_part = outer_reduce_rest(grid, zero, zero_through)
    back_parts = swap_y(grid, [None] + back_parts)[1:]
    first_part, back_parts = tie(first_part, back_parts)
    back = core_last(grid, [first_part] + back_parts, cap, True)
    results, up_grads, down_grads = outs[:pieces], outs[pieces : pieces + slices], outs[pieces + slices :]
    halves = lambda array: [array[: array.shape[0] // 2], array[array.shape[0] // 2 :]]
    ups_sent, downs_sent = ([halves(g) for g in grads[1:]] for grads in (up_grads, down_grads))

    def inner_swaps(sent, half):
        return [grid.swap(pair[half], "inner", s) for s, pair in enumerate(sent, 1)]

    up_first = inner_swaps(ups_sent, 0)
    back, last_result, ups_sent = tie(back, results[3], ups_sent)
    through = grid.swap(last_result, "outer", 1)
    up_second = inner_swaps(ups_sent, 1)

    grad_resid, small, grad_scan, grad_gate, grad_skip, back_pair = call(
        functools.partial(mixer_back_kernel, rank_n, states, experts, cap),
        [
            shape(tokens, depth),
            shape(16, depth),
            shape(tokens, width),
            shape(tokens, width),
            shape(1, width),
            shape(states + 1, width),
        ],
        (
            me, back, table, gate, probs, expert_ids, rank, resid, output_grad, row(router_gain), router_t,
            out_proj, joined, scan, act, row(skip_gain), masked, rate, proj, pair[states:],
        ),
        grid=(chunks,),
        in_specs=[
            SMEM, full(slots + 8, depth), full(slots, tokens), full(tokens, 1), full(tokens, 8),
            full(tokens, 1), full(tokens, 1), full(tokens, depth), full(tokens, depth), full(1, depth),
            full(8, depth), out_rows, gate_half, tok, tok, one_row, tok, state_rows, proj_full, one_row,
        ],
        out_specs=[
            full(tokens, depth), full(16, depth), tok, tok, one_row,
            pl.BlockSpec((states + 1, chunk), block),
        ],
        scratch=[lanes] + [pltpu.VMEM((tokens, depth), BF16)] * 2,
        name="mixer_back",
    )
    back_pair, downs_sent, *up_first = tie(back_pair, downs_sent, *up_first)
    core = grid.at["core"].astype(jnp.int32).reshape(1)
    wide = pl.BlockSpec((tokens, depth), block)

    def late(which, weight):
        return call(
            late_kernel,
            [shape(depth, width)] + [shape(tokens, depth)] * len(weight),
            (
                which, scan, act, row(skip_gain), joined, grad_resid, block_input, row(mixer_gain), grad_gate,
                *weight,
            ),
            grid=(2,),
            in_specs=[
                SMEM, wide, wide, pl.BlockSpec((1, depth), block), pl.BlockSpec((ext, depth), lambda c: (0, 2 + c)),
                full(tokens, depth), full(tokens, depth), full(1, depth), wide,
            ]
            + [pl.BlockSpec((depth, depth), lambda c: (0, 2 + c))] * len(weight),
            out_specs=[pl.BlockSpec((depth, depth), block)] + [full(tokens, depth)] * len(weight),
            scratch=[pltpu.VMEM((tokens, depth), BF16)] * 2,
            name="late",
        )

    (late_sent,) = late(core, ())
    late_kept, grad_gate_normed = late(1 - core, (in_proj,))
    late_got = grid.swap(late_sent, "core", 1)
    down_first = inner_swaps(downs_sent, 0)

    def first(total):
        total, held["through"], held["downs"], *held["up_second"] = tie(total, through, downs_sent, *up_second)
        return total

    def second(total):
        total, got, kept, held["normed"], *held["down_first"] = tie(
            total, late_got, late_kept, grad_gate_normed, *down_first
        )
        held["late"] = sum_first(grid, [kept, got])
        return total

    end = entering(grid, back_pair, rate, True, {1: first, 2: second})
    up_second = held["up_second"]
    end, near, far = tie(end, results[1], results[2] + held["through"])
    near, far = grid.swap(near, "outer", 1), grid.swap(far, "outer", 2)
    grad_gate_normed = held["normed"]
    late_first, late_second = held["late"]

    def with_others(own, firsts, seconds):
        for pair in zip(firsts, seconds):
            own = own + jnp.concatenate(pair, axis=0)
        return own

    def scan_back(c, before):
        at = lambda _: (0, c)
        tok, one_row = pl.BlockSpec((tokens, chunk), at), pl.BlockSpec((1, chunk), at)
        state_rows = pl.BlockSpec((states, chunk), at)
        return call(
            functools.partial(scan_back_kernel, rank_n, states),
            [
                shape(tokens, width), shape(tokens, width), shape(states, width),
                shape(rank_n + 2 * states, tokens),
            ],
            (
                masked, steps, drive, act, pre, grad_scan, row(skip_gain), history, history, start, end, rate, proj,
                step_proj, *before,
            ),
            grid=(blocks,),
            in_specs=[
                tok, tok, tok, tok, tok, tok, one_row,
                pl.BlockSpec((token_block, states, chunk), lambda i: (blocks - 1 - i, 0, c)),
                pl.BlockSpec(
                    (8, states, chunk),
                    lambda i: (jnp.maximum((blocks - 1 - i) * (token_block // 8) - 1, 0), 0, c),
                ),
                state_rows, state_rows, state_rows, proj_full, pl.BlockSpec((rank_n, chunk), at),
            ]
            + [pl.BlockSpec(memory_space=pl.ANY)] * len(before),
            out_specs=[tok, tok, state_rows, proj_full],
            scratch=[lanes, lanes]
            + [pltpu.VMEM((tokens, chunk), F32)] * 2
            + [pltpu.VMEM((token_block, states, 128), F32)] * 2
            + [pltpu.VMEM((states, chunk), F32)] * 2
            + [pltpu.VMEM((2, states, 128), F32)],
            name="scan_back",
            aliases={14 + i: i for i in range(len(before))},
        )

    *filled, grad_proj_a = scan_back(0, ())
    filled, late_first, late_second = tie(filled, late_first, late_second)
    late_both = sum_second(grid, late_first, late_second)
    *filled, grad_proj_b = scan_back(1, filled)
    filled, late_both, near, far, downs_sent = tie(filled, late_both, near, far, held["downs"])
    down_second = inner_swaps(downs_sent, 1)
    result = results[0] + near + far
    result_parts = swap_y(grid, [result[p * 2 * cap : (p + 1) * 2 * cap] for p in range(parts)])
    late_cut = cut_outer(grid, late_both)
    late_through = grid.swap(late_cut[3], "outer", 1)
    grad_act, grad_pre, grad_decay, grad_proj_c = scan_back(2, filled)
    grad_act, late_through, result_parts, down_second = tie(grad_act, late_through, result_parts, down_second)
    late_total = outer_reduce_rest(grid, late_cut, late_through)
    unit = 2 * grid.size["inner"] * grid.size["y"]
    half = -(-max(depth // 2 + 3 * states + rank_n, depth // 2 + rank_n + 40) // unit) * unit
    small = jnp.concatenate([small[:9], loads[0:1]], axis=0)
    kept, sent_half, input_grad, edge = call(
        functools.partial(input_back_kernel, rank_n, states),
        [shape(half, width), shape(half, width), shape(tokens, depth), shape(HALO, depth)],
        (
            core, grad_proj_a, grad_proj_b, grad_proj_c, proj, state_proj_t, act, grad_act, grad_pre, conv, joined,
            conv_weight, since, in_proj, block_input, halo, row(mixer_gain), grad_gate_normed, grad_resid,
            grad_decay, grad_skip, small,
        ),
        grid=(chunks,),
        in_specs=[
            SMEM, proj_full, proj_full, proj_full, proj_full, pl.BlockSpec((rank_n + 2 * states, chunk), block),
            tok, tok, tok, tok, pl.BlockSpec((ext, chunk), block), pl.BlockSpec((taps, chunk), block),
            full(tokens, 1), pl.BlockSpec((depth, chunk), block), full(tokens, depth), full(HALO, depth),
            full(1, depth), full(tokens, depth), full(tokens, depth), state_rows, one_row, full(10, depth),
        ],
        out_specs=[
            pl.BlockSpec((half, chunk), block), pl.BlockSpec((half, chunk), block), full(tokens, depth),
            full(HALO, depth),
        ],
        scratch=[pltpu.VMEM((ext, depth), BF16)] * 2
        + [pltpu.VMEM((ext, chunk), F32), pltpu.VMEM((ext, depth), F32)],
        name="input_back",
    )
    kept, sent_half, late_total = tie(kept, sent_half, late_total)
    late_near, late_far = grid.swap(late_total, "outer", 1), grid.swap(late_total, "outer", 2)
    sent_got = grid.swap(sent_half, "core", 1)
    kept, sent_got = tie(kept, sent_got)
    grads_first, grads_second = sum_first(grid, [kept, sent_got])
    late_near, late_far, grads_first, grads_second = tie(late_near, late_far, grads_first, grads_second)
    late_last = grid.swap(late_far, "outer", 1)
    grads = sum_second(grid, grads_first, grads_second)
    late_last, grads, edge, result_parts, up_parts, down_parts = tie(
        late_last, grads, edge, result_parts,
        [up_grads[0], up_first, up_second], [down_grads[0], held["down_first"], down_second],
    )
    from_next = grid.along(edge, -1)
    input_grad = jnp.concatenate([input_grad[: tokens - HALO], input_grad[tokens - HALO :] + from_next], axis=0)
    grad_up = with_others(*up_parts)
    result = core_last(grid, result_parts, cap, False)
    late_first, late_second = spread_second(grid, join_outer(grid, late_total, late_near, late_far, late_last))
    grads = sum_outer(grid, grads)
    late_first, late_second, grads, grad_up = tie(late_first, late_second, grads, grad_up)
    late_first, late_second = gather_rows(grid, late_first, "inner"), gather_rows(grid, late_second, "y")
    grads = spread_outer(grid, grads)
    late_first, late_second, grads, result, input_grad = tie(late_first, late_second, grads, result, input_grad)
    combined = jnp.dot(table.T, result.astype(F32), precision=lax.Precision.HIGHEST, preferred_element_type=F32)
    block_output = resid + gate * combined
    late_other = [grid.swap(late_first, "core", 1), grid.swap(late_second, "core", 1)]
    grads_first, grads_second = spread_second(grid, grads)
    grads_first, grads_second, down_parts, block_output, *late_other = tie(
        grads_first, grads_second, down_parts, block_output, *late_other
    )
    grad_down = with_others(*down_parts)
    grads_first, grads_second = gather_rows(grid, grads_first, "inner"), gather_rows(grid, grads_second, "y")
    quarter = pl.BlockSpec((half // 2, chunk), block)
    late_rows = full(depth // 2, width)
    grad_in_proj, grad_out_proj = call(
        finish_late_kernel,
        [shape(depth, 2 * width), shape(2, depth, depth)],
        (core, late_first, late_second, *late_other),
        grid=(2,),
        in_specs=[SMEM] + [late_rows] * 4,
        out_specs=[
            pl.BlockSpec((depth // 2, width), lambda r: (r, 1)),
            pl.BlockSpec((2, depth // 2, depth), lambda r: (0, r, 0)),
        ],
        name="finish_late",
    )
    grads_first, grads_second, grad_in_proj, grad_down = tie(grads_first, grads_second, grad_in_proj, grad_down)
    grads_other = [grid.swap(grads_first, "core", 1), grid.swap(grads_second, "core", 1)]
    (
        grad_in_proj, grad_state_proj, grad_step_proj, grad_decay_log, grad_conv_weight, rows, small,
    ) = call(
        functools.partial(finish_kernel, rank_n, states, taps),
        [
            shape(depth, 2 * width), shape(rank_n + 2 * states, width), shape(rank_n, width),
            shape(states, width), shape(taps, width), shape(8, width), shape(32, chunk),
        ],
        (core, grads_first, grads_second, *grads_other, grad_in_proj),
        grid=(chunks,),
        in_specs=[SMEM] + [quarter] * 4 + [pl.BlockSpec(memory_space=pl.ANY)],
        out_specs=[
            pl.BlockSpec((depth, chunk), block), pl.BlockSpec((rank_n + 2 * states, chunk), block), pl.BlockSpec((rank_n, chunk), block),
            state_rows, pl.BlockSpec((taps, chunk), block), pl.BlockSpec((8, chunk), block), full(32, chunk),
        ],
        name="finish",
        aliases={5: 0},
    )
    small = jnp.concatenate([small[:16], small[16:, : depth - chunk]], axis=1)
    return (
        block_output,
        input_grad,
        small[10],
        grad_in_proj,
        grad_conv_weight,
        rows[taps],
        grad_state_proj.T,
        grad_step_proj,
        rows[taps + 1],
        grad_decay_log.T,
        rows[taps + 2],
        grad_out_proj.reshape(width, depth),
        small[8],
        small[:experts].T,
        grad_up[None],
        grad_down[None],
        small[9, :experts].astype(jnp.int32),
        small[9, 128 : 128 + experts].astype(jnp.int32),
    )


def solution(mesh):
    rows, copied = P(("seq", "exp"), None), P()
    up, down = P("exp", None, "seq"), P("exp", "seq", None)
    in_specs = (rows, copied, rows, rows) + (copied,) * 12 + (up, down)
    out_specs = (rows, rows) + (copied,) * 12 + (up, down, copied, copied)
    return jax.shard_map(per_device, mesh=mesh, in_specs=in_specs, out_specs=out_specs, check_vma=False)
```
